32 devices in a mesh: groups: 2 (over y), ctx: 4 (over z), chan: 4 (over x, core).
Axes of the slice: x: 2, y: 2, z: 4, core: 2. Of those that a mesh axis runs over, the one named last changes fastest.
Arguments:
- query_gate: float32 [4096, 1024], P(('groups', 'ctx'), 'chan'), parts along dimension 0, may hold values from -6 to 6
- key_gate: float32 [4096, 1024], P(('groups', 'ctx'), 'chan'), parts along dimension 0, may hold values from -6 to 6
- values: float32 [4096, 1024], P(('groups', 'ctx'), 'chan'), parts along dimension 0, may hold values from -6 to 6
- filter_taps: float32 [4096, 1024], P(None, 'chan'), may hold values from -0.125 to 0.125
- skip_gain: float32 [1024], P('chan'), may hold values from -1 to 1
- upstream: float32 [4096, 1024], P(('groups', 'ctx'), 'chan'), parts along dimension 0, may hold values from -6 to 6
Outputs:
- query_grad: float32 [4096, 1024], P(('groups', 'ctx'), 'chan'), parts along dimension 0
- key_grad: float32 [4096, 1024], P(('groups', 'ctx'), 'chan'), parts along dimension 0
- value_grad: float32 [4096, 1024], P(('groups', 'ctx'), 'chan'), parts along dimension 0
- filter_grad: float32 [8192, 1024], P(('groups', 'ctx'), 'chan'), parts along dimension 0
- skip_grad: float32 [2048], P(('groups', 'chan')), parts along dimension 0
The draws below stay inside these ranges and needn't reach their ends.
There are 2 independent parts, one for each index of `groups`. The reference program is written for one: setup_inputs(seed, part) draws one part's arguments, and reference() takes and returns one part's arrays. A program takes and returns all parts, laid end to end along the dimension named above; an argument that names none is the same for every part. Nothing has to cross between parts.
All inputs are finite; a program needn't handle non-finite values.
Results may differ from the reference program's by a relative error of at most 0.0001.
Values sent between devices are 32-bit elements; how exact they have to be, the bound alone decides.
No kernel may reach another device: no remote copies, remote signals or barrier semaphores. Data moves between devices by JAX's collectives and lax.ppermute only.
A program may use at most 128 MiB of HBM per device.

```python
import jax
import jax.numpy as jnp

WIDTH = 1024
HIST = 2048
LAGS = 4096


def steps_of(rng, shape, pieces, smallest, high):
    gain, own = 1.0, jax.random.fold_in(rng, 6)
    for position, blocks in pieces:
        draws = jnp.exp(jax.random.uniform(jax.random.fold_in(own, position), (blocks,), jnp.float32, smallest / len(pieces), high / len(pieces)))
        gain = gain * jnp.repeat(draws, shape[position] // blocks).reshape([-1 if axis == position else 1 for axis in range(len(shape))])
    return gain


def scatter_about(stream_key, extent, spread, most, split=(), held_as=jnp.bfloat16):
    values = spread * jax.random.normal(stream_key, extent, jnp.float32)
    if split:
        values = values * steps_of(stream_key, extent, split, -0.22, 0.18)
    return jnp.clip(values, -most, most).astype(held_as)


def setup_inputs(seed: int = 0, part: int = 0) -> dict:
    splits = jax.random.split(jax.random.key(seed), 7)
    part_splits = jax.random.split(jax.random.fold_in(splits[6], part), 7)
    return {
        "query_gate": scatter_about(part_splits[0], (HIST, WIDTH), 1.0, 6.0, ((0, 4), (1, 4)), jnp.float32),
        "key_gate": scatter_about(part_splits[1], (HIST, WIDTH), 1.0, 6.0, ((0, 4), (1, 4)), jnp.float32),
        "values": scatter_about(part_splits[2], (HIST, WIDTH), 1.0, 6.0, ((0, 4), (1, 4)), jnp.float32),
        "filter_taps": scatter_about(splits[3], (LAGS, WIDTH), HIST ** -0.5, 0.125, ((1, 4),), jnp.float32),
        "skip_gain": jnp.clip(jax.random.uniform(splits[4], (WIDTH,), jnp.float32, -1.0, 1.0) * steps_of(splits[4], (WIDTH,), ((0, 4),), -0.4, 0.0), -1.0, 1.0),
        "upstream": scatter_about(part_splits[5], (HIST, WIDTH), 1.0, 6.0, ((0, 4), (1, 4)), jnp.float32),
    }


def long_conv(gated, taps):
    hist = gated.shape[0]
    size = 4 * hist
    spec = jnp.fft.rfft(gated, n=size, axis=0) * jnp.fft.rfft(taps, n=size, axis=0)
    full = jnp.fft.irfft(spec, n=size, axis=0)
    return full[hist:2 * hist]

def reference(query_gate, key_gate, values, filter_taps, skip_gain, upstream):

    def forward(query_gate, key_gate, values, filter_taps, skip_gain):
        gated = key_gate * values
        mixed = long_conv(gated, filter_taps) + skip_gain[None, :] * gated
        return query_gate * mixed
    output, pullback = jax.vjp(forward, query_gate, key_gate, values, filter_taps, skip_gain)
    query_grad, key_grad, value_grad, filter_grad, skip_grad = pullback(upstream)
    return (query_grad, key_grad, value_grad, filter_grad, skip_grad)
```

```python
import functools
import math

import jax
import jax.numpy as jnp
import ml_dtypes
import numpy as np
from jax import lax
from jax.experimental import pallas as pl
from jax.experimental.pallas import tpu as pltpu
from jax.sharding import PartitionSpec as P

COS1, SIN1, HALF = math.cos(math.pi / 8), math.sin(math.pi / 8), math.sqrt(0.5)


def split_np(table):
    high = table.astype(ml_dtypes.bfloat16)
    low = (table - high.astype(np.float64)).astype(ml_dtypes.bfloat16)
    return np.stack([high, low])


def tables(seg):
    sub = seg // 4
    bins, pos = np.arange(sub)[:, None], np.arange(sub)[None, :]
    forward = []
    for group in range(4):
        angle = 2 * np.pi * pos * (8 * bins + group + 0.5) / (2 * seg)
        cos, sin = np.cos(angle), np.sin(angle)
        forward.append(np.block([[cos, -sin], [-sin, -cos]]))
    forward = np.stack(forward)
    inverse = forward.transpose(0, 2, 1) / seg
    return split_np(forward), split_np(inverse)


def split(x):
    high = x.astype(jnp.bfloat16)
    return high, (x - high.astype(jnp.float32)).astype(jnp.bfloat16)


def dot3(table_ref, group, high, low):
    t_high, t_low = table_ref[0, group], table_ref[1, group]
    dot = functools.partial(jnp.dot, preferred_element_type=jnp.float32)
    return dot(t_high, high) + dot(t_high, low) + dot(t_low, high)


def spread(x):
    sub = x.shape[0] // 4
    x0, x1, x2, x3 = (x[i * sub : (i + 1) * sub] for i in range(4))
    u, p, s, q, t = HALF * x2, COS1 * x1, SIN1 * x1, COS1 * x3, SIN1 * x3
    a, b, pt, sq, pmt, spq = x0 + u, x0 - u, p + t, s - q, p - t, s + q
    pairs = ((a + pt, spq + u), (b + sq, pmt + u), (b - sq, pmt - u), (a - pt, spq - u))
    return [jnp.concatenate(pair, axis=0) for pair in pairs]


def gather_quarters(re, im):
    e03, d03, e12, d12 = re[0] + re[3], re[0] - re[3], re[1] + re[2], re[1] - re[2]
    f03, g03, f12, g12 = im[0] + im[3], im[0] - im[3], im[1] + im[2], im[1] - im[2]
    return (
        e03 + e12,
        COS1 * (d03 + f12) + SIN1 * (d12 + f03),
        HALF * (e03 - e12 + g03 + g12),
        SIN1 * (d03 - f12) + COS1 * (f03 - d12),
    )


def transform(x, table_ref, store):
    for group, part in enumerate(spread(x)):
        store(group, dot3(table_ref, group, *split(part)))


def dft_kernel(table_ref, x_ref, out_ref):
    rows = out_ref.shape[1] // 4

    def store(group, value):
        out_ref[0, group * rows : (group + 1) * rows, :] = value

    transform(x_ref[...], table_ref, store)


def cost(flops, nbytes):
    return pl.CostEstimate(flops=int(flops), bytes_accessed=int(nbytes), transcendentals=0)


VMEM_LIMIT = 48 << 20


def params():
    return pltpu.CompilerParams(vmem_limit_bytes=VMEM_LIMIT)


def whole_spec(shape):
    return pl.BlockSpec(shape, lambda *_: (0,) * len(shape))


def dft(table, x, seg):
    width = x.shape[1]
    blocks = x.shape[0] // seg
    return pl.pallas_call(
        dft_kernel,
        grid=(blocks,),
        in_specs=[whole_spec(table.shape), pl.BlockSpec((seg, width), lambda i: (i, 0))],
        out_specs=pl.BlockSpec((1, 2 * seg, width), lambda i: (i, 0, 0)),
        out_shape=jax.ShapeDtypeStruct((blocks, 2 * seg, width), jnp.float32),
        compiler_params=params(),
        cost_estimate=cost(blocks * 3 * seg * seg * width * 2, blocks * 12 * seg * width),
        name="dft",
    )(table, x)


def taps_kernel(table_ref, x_ref, out_ref, last_ref):
    step = pl.program_id(0)
    rows = out_ref.shape[1] // 4
    sub = rows // 2

    def store(group, value):
        base = group * rows
        sign = 1.0 if group % 2 == 0 else -1.0
        re, im = slice(base, base + sub), slice(base + sub, base + rows)
        out_ref[0, re, :] = value[:sub] - sign * last_ref[im, :]
        out_ref[0, im, :] = value[sub:] + sign * last_ref[re, :]
        last_ref[base : base + rows, :] = value

    @pl.when(step == 0)
    def _():
        last_ref[...] = jnp.zeros_like(last_ref)

    transform(x_ref[...], table_ref, store)


def taps_spectra(table, taps, seg):
    width = taps.shape[1]
    blocks = taps.shape[0] // seg
    return pl.pallas_call(
        taps_kernel,
        grid=(blocks,),
        in_specs=[whole_spec(table.shape), pl.BlockSpec((seg, width), lambda i: (i, 0))],
        out_specs=pl.BlockSpec((1, 2 * seg, width), lambda i: (jnp.maximum(i - 1, 0), 0, 0)),
        out_shape=jax.ShapeDtypeStruct((blocks - 1, 2 * seg, width), jnp.float32),
        scratch_shapes=[pltpu.VMEM((2 * seg, width), jnp.float32)],
        compiler_params=params(),
        cost_estimate=cost(blocks * 3 * seg * seg * width * 2, blocks * 12 * seg * width),
        name="taps",
    )(table, taps)


def conj_mul(a, b):
    return a[0] * b[0] + a[1] * b[1], a[0] * b[1] - a[1] * b[0]


def mul(a, b):
    return a[0] * b[0] - a[1] * b[1], a[0] * b[1] + a[1] * b[0]


def add(a, b):
    return a[0] + b[0], a[1] + b[1]


def partial_kernel(pos_ref, table_ref, inverse_ref, win_near, win_far, near_ref, x_ref, far_ref, out_ref, z_ref):
    rows = far_ref.shape[0] // 4
    sub = rows // 2
    for group, part in enumerate(spread(x_ref[...])):
        base = group * rows
        far = dot3(table_ref, group, *split(part))
        far_ref[base : base + rows, :] = far
        re, im = slice(base, base + sub), slice(base + sub, base + rows)
        near = (near_ref[0, re, :], near_ref[0, im, :])
        total = add(
            conj_mul((win_near[0, re, :], win_near[0, im, :]), near),
            conj_mul((win_far[0, re, :], win_far[0, im, :]), (far[:sub], far[sub:])),
        )
        z_ref[group] = dot3(inverse_ref, group, *split(jnp.concatenate(total, axis=0)))
    quarters = gather_quarters([z_ref[g, :sub] for g in range(4)], [z_ref[g, sub:] for g in range(4)])
    for i, quarter in enumerate(quarters):
        out_ref[i * sub : (i + 1) * sub, :] = quarter


def back_partial(pos, table, inverse, windows, near, x, seg):
    width = x.shape[1]
    n = (windows.shape[0] + 1) // 2
    block = (1, 2 * seg, width)

    def window(distance):
        return pl.BlockSpec(block, lambda i, pos: (jnp.where(pos[0] == 1, n - 1 + distance, n - 1 - distance), 0, 0))

    return pl.pallas_call(
        partial_kernel,
        grid_spec=pltpu.PrefetchScalarGridSpec(
            num_scalar_prefetch=1,
            grid=(1,),
            in_specs=[
                whole_spec(table.shape),
                whole_spec(inverse.shape),
                window(2),
                window(3),
                pl.BlockSpec(block, lambda i, pos: (jnp.where(pos[0] == 1, 3, 1), 0, 0)),
                whole_spec((seg, width)),
            ],
            out_specs=[whole_spec((2 * seg, width)), whole_spec((seg, width))],
            scratch_shapes=[pltpu.VMEM((4, seg // 2, width), jnp.float32)],
        ),
        out_shape=[
            jax.ShapeDtypeStruct((2 * seg, width), jnp.float32),
            jax.ShapeDtypeStruct((seg, width), jnp.float32),
        ],
        compiler_params=params(),
        cost_estimate=cost(6 * seg * seg * width * 2, 24 * seg * width),
        name="partial",
    )(pos, table, inverse, windows, windows, near, x)


OWN, LEFT, RIGHT, TWO, THREE = range(5)
PAIRS = (
    ((), ((OWN, THREE),), ((OWN, TWO), (RIGHT, THREE))),
    (
        ((LEFT, RIGHT), (OWN, TWO)),
        ((LEFT, OWN), (OWN, RIGHT), (RIGHT, TWO)),
        ((LEFT, LEFT), (OWN, OWN), (RIGHT, RIGHT), (TWO, TWO)),
    ),
    (
        ((TWO, TWO), (LEFT, LEFT), (OWN, OWN), (RIGHT, RIGHT)),
        ((LEFT, TWO), (OWN, LEFT), (RIGHT, OWN)),
        ((OWN, TWO), (RIGHT, LEFT)),
    ),
    (((LEFT, THREE), (OWN, TWO)), ((OWN, THREE),), ()),
)


def final_kernel(
    pos_ref, inverse_ref, win_ref, own_ref, near_ref, two_g, two_m, three_g, gm_ref, skip_ref, up_ref,
    query_out, filter_out, back_out, x_high, x_low, z_ref,
):
    group = pl.program_id(0)
    pos = pos_ref[0]
    rows = own_ref.shape[1]
    sub = rows // 2
    width = own_ref.shape[2]
    seg = 4 * sub
    mid = win_ref.shape[0] // 2
    sign = jnp.where(group % 2 == 0, 1.0, -1.0)
    step = 8
    two_off = jnp.where(pos < 2, -2, 2)
    three_off = jnp.where(pos == 0, -3, 3)

    def put(slot, tile, value):
        for half in range(2):
            high, low = split(value[half])
            at = pl.ds(pl.multiple_of(half * sub + tile * step * 2, 16), 2 * step)
            x_high[at, slot * width : (slot + 1) * width] = high
            x_low[at, slot * width : (slot + 1) * width] = low

    def tiles(tile):
        re = pl.ds(pl.multiple_of(tile * step * 2, 16), 2 * step)
        im = pl.ds(pl.multiple_of(sub + tile * step * 2, 16), 2 * step)

        def read(ref, *lead):
            return ref[(*lead, re, slice(None))], ref[(*lead, im, slice(None))]

        gated = (
            lambda: read(own_ref, 0), lambda: read(near_ref, 0), lambda: read(near_ref, 2),
            lambda: read(two_g, 0), lambda: read(three_g, 0),
        )
        mixed = (lambda: read(own_ref, 1), lambda: read(near_ref, 1), lambda: read(near_ref, 3), lambda: read(two_m))
        return read, gated, mixed

    def sums(tile, _):
        read, gated, mixed = tiles(tile)
        conv = mul(read(win_ref, mid), gated[OWN]())
        conv = add(conv, mul(read(win_ref, mid + 1), gated[LEFT]()))
        conv = add(conv, mul(read(win_ref, mid - 1), gated[RIGHT]()))
        conv = add(conv, mul(read(win_ref, mid + two_off), gated[TWO]()))
        conv = add(conv, mul(read(win_ref, mid + three_off), gated[THREE]()))
        put(0, tile, conv)
        back = conj_mul(read(win_ref, mid), mixed[OWN]())
        back = add(back, conj_mul(read(win_ref, mid - 1), mixed[LEFT]()))
        back = add(back, conj_mul(read(win_ref, mid + 1), mixed[RIGHT]()))
        back = add(back, conj_mul(read(win_ref, mid - two_off), mixed[TWO]()))
        put(1, tile, back)
        return _

    count = sub // (2 * step)
    lax.fori_loop(0, count, sums, 0)

    for where, distances in enumerate(PAIRS):

        @pl.when(pos == where)
        def _():
            def lags(tile, _):
                read, gated, mixed = tiles(tile)
                total = []
                for pairs in distances:
                    value = None
                    for m, g in pairs:
                        term = conj_mul(gated[g](), mixed[m]())
                        value = term if value is None else add(value, term)
                    total.append(value)
                for slot in range(2):
                    low, high = total[slot], total[slot + 1]
                    if high is None:
                        value = low
                    else:
                        turned = (sign * high[1], -sign * high[0])
                        value = turned if low is None else add(low, turned)
                    put(2 + slot, tile, value)
                return _

            lax.fori_loop(0, count, lags, 0)

    dot = functools.partial(jnp.dot, preferred_element_type=jnp.float32)
    t_high, t_low = inverse_ref[0, 0], inverse_ref[1, 0]
    for slot in range(4):
        cols = slice(slot * width, (slot + 1) * width)
        z_ref[group, :, cols] = (
            dot(t_high, x_high[:, cols]) + dot(t_high, x_low[:, cols]) + dot(t_low, x_high[:, cols])
        )

    @pl.when(group == 3)
    def _():
        for slot in range(4):
            cols = slice(slot * width, (slot + 1) * width)
            quarters = gather_quarters(
                [z_ref[g, :sub, cols] for g in range(4)], [z_ref[g, sub:, cols] for g in range(4)]
            )
            for i, quarter in enumerate(quarters):
                at = slice(i * sub, (i + 1) * sub)
                if slot == 0:
                    query_out[at, :] = up_ref[at, :] * (quarter + skip_ref[...] * gm_ref[at, :])
                elif slot == 1:
                    back_out[at, :] = quarter + skip_ref[...] * gm_ref[seg + i * sub : seg + (i + 1) * sub, :]
                else:
                    base = (slot - 2) * seg + i * sub
                    filter_out[base : base + sub, :] = quarter


def final(pos, inverse, windows, own, near, two_g, two_m, three_g, gm, skip, upstream, seg):
    width = gm.shape[1]
    rows = seg // 2

    def groups(lead):
        return pl.BlockSpec((lead, rows, width), lambda i, pos: (0, i, 0))

    return pl.pallas_call(
        final_kernel,
        grid_spec=pltpu.PrefetchScalarGridSpec(
            num_scalar_prefetch=1,
            grid=(4,),
            in_specs=[
                pl.BlockSpec((2, 1, rows, rows), lambda i, pos: (0, i, 0, 0)),
                groups(windows.shape[0]),
                groups(2),
                groups(4),
                groups(1),
                pl.BlockSpec((rows, width), lambda i, pos: (i, 0)),
                groups(1),
                whole_spec((2 * seg, width)),
                whole_spec((1, width)),
                whole_spec((seg, width)),
            ],
            out_specs=[whole_spec((seg, width)), whole_spec((2 * seg, width)), whole_spec((seg, width))],
            scratch_shapes=[
                pltpu.VMEM((rows, 4 * width), jnp.bfloat16),
                pltpu.VMEM((rows, 4 * width), jnp.bfloat16),
                pltpu.VMEM((4, rows, 4 * width), jnp.float32),
            ],
        ),
        out_shape=[
            jax.ShapeDtypeStruct((seg, width), jnp.float32),
            jax.ShapeDtypeStruct((2 * seg, width), jnp.float32),
            jax.ShapeDtypeStruct((seg, width), jnp.float32),
        ],
        compiler_params=params(),
        cost_estimate=cost(12 * seg * seg * width * 2, 150 * seg * width),
        name="final",
    )(pos, inverse, windows, own, near, two_g, two_m, three_g, gm, skip, upstream)


def local_line(query_gate, key_gate, values, filter_taps, skip_gain, upstream):
    seg, width = values.shape
    forward_np, inverse_np = tables(seg)
    table, inverse = jnp.asarray(forward_np), jnp.asarray(inverse_np)
    position = lax.axis_index("ctx")
    pos = position.astype(jnp.int32).reshape(1)
    gm = jnp.concatenate([key_gate * values, upstream * query_gate], axis=0)
    skip_grad = lax.psum(jnp.sum(gm[:seg] * gm[seg:], axis=0), "ctx")
    from_left = lax.ppermute(gm, "ctx", [(0, 1), (1, 2), (2, 3)])
    from_right = lax.ppermute(gm, "ctx", [(1, 0), (2, 1), (3, 2)])
    windows = taps_spectra(table, filter_taps, seg)
    own = dft(table, gm, seg)
    two_g = lax.ppermute(from_left[:seg], "ctx", [(1, 2), (2, 3)]) + lax.ppermute(
        from_right[:seg], "ctx", [(2, 1), (1, 0)]
    )
    far_m = jnp.where(position == 1, from_left[seg:], from_right[seg:])
    near = dft(table, jnp.concatenate([from_left, from_right], axis=0), seg)
    far_m, two_g = lax.optimization_barrier((far_m, two_g))
    three_g = lax.ppermute(two_g, "ctx", [(1, 0), (2, 3)])
    two_m = lax.ppermute(far_m, "ctx", [(1, 2), (2, 1)])
    two_g = dft(table, two_g, seg)
    two_m, partial = back_partial(pos, table, inverse, windows, near, two_m, seg)
    partial = lax.ppermute(partial, "ctx", [(1, 0), (2, 3)])
    three_g = dft(table, three_g, seg)
    query_grad, filter_grad, back = final(
        pos, inverse, windows, own, near, two_g, two_m, three_g, gm, skip_gain[None, :], upstream, seg
    )
    back = back + partial
    return (query_grad, back * values, back * key_gate, filter_grad, skip_grad)


def matmul(left, right):
    return jnp.dot(left, right, preferred_element_type=jnp.float32, precision=lax.Precision.HIGHEST)


def forward_table(seg_len, count, offset):
    num_bins = seg_len + 1
    period = 2 * seg_len
    bin_index = lax.broadcasted_iota(jnp.int32, (num_bins, count), 0)
    pos_index = lax.broadcasted_iota(jnp.int32, (num_bins, count), 1) + offset
    angles = (bin_index * pos_index % period).astype(jnp.float32) * (2.0 * math.pi / period)
    return jnp.concatenate([jnp.cos(angles), -jnp.sin(angles)], axis=0)


def inverse_table(seg_len, count, offset):
    num_bins = seg_len + 1
    period = 2 * seg_len
    pos_index = lax.broadcasted_iota(jnp.int32, (count, num_bins), 0) + offset
    bin_index = lax.broadcasted_iota(jnp.int32, (count, num_bins), 1)
    angles = (bin_index * pos_index % period).astype(jnp.float32) * (2.0 * math.pi / period)
    weights = jnp.where((bin_index == 0) | (bin_index == seg_len), 1.0, 2.0) / period
    return jnp.concatenate([weights * jnp.cos(angles), -weights * jnp.sin(angles)], axis=1)


def times_spec(first, second):
    num_bins = first.shape[0] // 2
    real_a, imag_a = (first[:num_bins], first[num_bins:])
    real_b, imag_b = (second[:num_bins], second[num_bins:])
    return jnp.concatenate(
        [real_a * real_b - imag_a * imag_b, real_a * imag_b + imag_a * real_b], axis=0
    )


def conj_times(first, second):
    num_bins = first.shape[0] // 2
    real_a, imag_a = (first[:num_bins], first[num_bins:])
    real_b, imag_b = (second[:num_bins], second[num_bins:])
    return jnp.concatenate(
        [real_a * real_b + imag_a * imag_b, real_a * imag_b - imag_a * real_b], axis=0
    )


def pick(stack, index):
    return lax.dynamic_index_in_dim(stack, index, 0, keepdims=False)


def local(query_gate, key_gate, values, filter_taps, skip_gain, upstream):
    seg_len, width_dev = values.shape
    cycle_size = lax.axis_size("ctx")
    position = lax.axis_index("ctx")
    history = seg_len * cycle_size
    gated = key_gate * values
    mixed_grad = upstream * query_gate
    table_low = forward_table(seg_len, seg_len, 0)
    table_high = forward_table(seg_len, seg_len, seg_len)
    table_taps = forward_table(seg_len, 2 * seg_len, 0)
    back_low = inverse_table(seg_len, seg_len, 0)
    back_high = inverse_table(seg_len, seg_len, seg_len)
    back_full = inverse_table(seg_len, 2 * seg_len, 0)
    own_grad_spec = matmul(table_high, mixed_grad)
    spec_rows = 2 * (seg_len + 1)

    def taps_spec(lag_block):
        start_row = (lag_block - 1) * seg_len + history
        window = lax.dynamic_slice_in_dim(filter_taps, start_row, 2 * seg_len, 0)
        return matmul(table_taps, window)

    def visit(carry, gated_spec, grad_spec, source):
        acc_conv, acc_back, partial_value = carry
        lag_block = position - source
        acc_conv = acc_conv + times_spec(taps_spec(lag_block), gated_spec)
        acc_back = acc_back + conj_times(taps_spec(-lag_block), grad_spec)
        segment = matmul(back_full, conj_times(gated_spec, own_grad_spec))
        start_row = (lag_block - 1) * seg_len + history
        current = lax.dynamic_slice_in_dim(partial_value, start_row, 2 * seg_len, 0)
        partial_value = lax.dynamic_update_slice_in_dim(
            partial_value, current + segment, start_row, 0
        )
        return (acc_conv, acc_back, partial_value)

    initial = (
        jnp.zeros((spec_rows, width_dev), jnp.float32),
        jnp.zeros((spec_rows, width_dev), jnp.float32),
        jnp.zeros((2 * history, width_dev), jnp.float32),
    )
    own_gated_spec = matmul(table_low, gated)
    pieces = (
        lax.all_gather(own_gated_spec[None], "ctx", axis=0, tiled=True),
        lax.all_gather(own_grad_spec[None], "ctx", axis=0, tiled=True),
    )

    def advance(member, state):
        return visit(state, pick(pieces[0], member), pick(pieces[1], member), member)

    folded = lax.fori_loop(0, pieces[0].shape[0], advance, initial)
    acc_conv, acc_back, partial_value = folded
    filter_grad = lax.psum_scatter(partial_value, "ctx", scatter_dimension=0, tiled=True)
    conv = matmul(back_high, acc_conv)
    back = matmul(back_low, acc_back) + skip_gain[None, :] * mixed_grad
    query_grad = upstream * (conv + skip_gain[None, :] * gated)
    key_grad = back * values
    value_grad = back * key_gate
    skip_grad = lax.psum(jnp.sum(mixed_grad * gated, axis=0), "ctx")
    return (query_grad, key_grad, value_grad, filter_grad, skip_grad)


def solution(mesh):
    in_specs = (
        P(("groups", "ctx"), "chan"),
        P(("groups", "ctx"), "chan"),
        P(("groups", "ctx"), "chan"),
        P(None, "chan"),
        P("chan"),
        P(("groups", "ctx"), "chan"),
    )
    out_specs = (
        P(("groups", "ctx"), "chan"),
        P(("groups", "ctx"), "chan"),
        P(("groups", "ctx"), "chan"),
        P(("groups", "ctx"), "chan"),
        P(("groups", "chan")),
    )
    body = local_line if mesh.shape["ctx"] == 4 else local
    return jax.shard_map(body, mesh=mesh, in_specs=in_specs, out_specs=out_specs, check_vma=False)
```

```python
import functools
import math

import jax
import jax.numpy as jnp
import ml_dtypes
import numpy as np
from jax import lax
from jax.experimental import pallas as pl
from jax.experimental.pallas import tpu as pltpu
from jax.sharding import PartitionSpec as P

COS1, SIN1, HALF = math.cos(math.pi / 8), math.sin(math.pi / 8), math.sqrt(0.5)


def split_np(table):
    high = table.astype(ml_dtypes.bfloat16)
    low = (table - high.astype(np.float64)).astype(ml_dtypes.bfloat16)
    return np.stack([high, low])


def tables(seg):
    sub = seg // 4
    bins, pos = np.arange(sub)[:, None], np.arange(sub)[None, :]
    forward = []
    for group in range(4):
        angle = 2 * np.pi * pos * (8 * bins + group + 0.5) / (2 * seg)
        cos, sin = np.cos(angle), np.sin(angle)
        forward.append(np.block([[cos, -sin], [-sin, -cos]]))
    forward = np.stack(forward)
    inverse = forward.transpose(0, 2, 1) / seg
    return split_np(forward), split_np(inverse)


def split(x):
    high = x.astype(jnp.bfloat16)
    return high, (x - high.astype(jnp.float32)).astype(jnp.bfloat16)


def dot3(table_ref, group, high, low):
    t_high, t_low = table_ref[0, group], table_ref[1, group]
    dot = functools.partial(jnp.dot, preferred_element_type=jnp.float32)
    return dot(t_high, high) + dot(t_high, low) + dot(t_low, high)


def spread(x):
    sub = x.shape[0] // 4
    x0, x1, x2, x3 = (x[i * sub : (i + 1) * sub] for i in range(4))
    u, p, s, q, t = HALF * x2, COS1 * x1, SIN1 * x1, COS1 * x3, SIN1 * x3
    a, b, pt, sq, pmt, spq = x0 + u, x0 - u, p + t, s - q, p - t, s + q
    pairs = ((a + pt, spq + u), (b + sq, pmt + u), (b - sq, pmt - u), (a - pt, spq - u))
    return [jnp.concatenate(pair, axis=0) for pair in pairs]


def gather_quarters(re, im):
    e03, d03, e12, d12 = re[0] + re[3], re[0] - re[3], re[1] + re[2], re[1] - re[2]
    f03, g03, f12, g12 = im[0] + im[3], im[0] - im[3], im[1] + im[2], im[1] - im[2]
    return (
        e03 + e12,
        COS1 * (d03 + f12) + SIN1 * (d12 + f03),
        HALF * (e03 - e12 + g03 + g12),
        SIN1 * (d03 - f12) + COS1 * (f03 - d12),
    )


def transform(x, table_ref, store):
    for group, part in enumerate(spread(x)):
        store(group, dot3(table_ref, group, *split(part)))


def cost(flops, nbytes):
    return pl.CostEstimate(flops=int(flops), bytes_accessed=int(nbytes), transcendentals=0)


def params(mib):
    return pltpu.CompilerParams(vmem_limit_bytes=mib << 20)


def whole_spec(shape):
    return pl.BlockSpec(shape, lambda *_: (0,) * len(shape))


def f32(*shape):
    return jax.ShapeDtypeStruct(shape, jnp.float32)


def prepare_kernel(query_ref, key_ref, values_ref, up_ref, gated_ref, *rest):
    mixed_refs, sum_ref = rest[:-1], rest[-1]
    step = pl.program_id(0)
    rows, width = key_ref.shape
    half = width // len(mixed_refs)
    gated = key_ref[...] * values_ref[...]
    mixed = up_ref[...] * query_ref[...]
    gated_ref[pl.ds(pl.multiple_of(step * rows, rows), rows), :] = gated
    for i, ref in enumerate(mixed_refs):
        ref[...] = mixed[:, i * half : (i + 1) * half]
    part = jnp.sum((gated * mixed).reshape(rows // 8, 8, width), axis=0)

    @pl.when(step == 0)
    def _():
        sum_ref[...] = part

    @pl.when(step > 0)
    def _():
        sum_ref[...] += part

    @pl.when(step == pl.num_programs(0) - 1)
    def _():
        seg = gated_ref.shape[0] - 8
        gated_ref[seg:, :] = sum_ref[...]


def prepare(query_gate, key_gate, values, upstream, halves):
    seg, width = values.shape
    steps = 4
    rows = seg // steps
    block = pl.BlockSpec((rows, width), lambda i: (i, 0))
    half = pl.BlockSpec((rows, width // halves), lambda i: (i, 0))
    return pl.pallas_call(
        prepare_kernel,
        grid=(steps,),
        in_specs=[block] * 4,
        out_specs=[whole_spec((seg + 8, width))] + [half] * halves,
        out_shape=[f32(seg + 8, width)] + [f32(seg, width // halves)] * halves,
        scratch_shapes=[pltpu.VMEM((8, width), jnp.float32)],
        compiler_params=params(8),
        cost_estimate=cost(4 * seg * width, 24 * seg * width),
        name="prepare",
    )(query_gate, key_gate, values, upstream)


def dft_kernel(table_ref, *refs):
    *x_refs, out_ref = refs
    rows = out_ref.shape[0] // 4

    def store(group, value):
        out_ref[group * rows : (group + 1) * rows, :] = value

    parts = [ref[...] for ref in x_refs]
    transform(parts[0] if len(parts) == 1 else jnp.concatenate(parts, axis=1), table_ref, store)


def dft(table, seg, *xs):
    width = sum(x.shape[1] for x in xs)
    return pl.pallas_call(
        dft_kernel,
        grid=(1,),
        in_specs=[whole_spec(table.shape)] + [whole_spec((seg, x.shape[1])) for x in xs],
        out_specs=whole_spec((2 * seg, width)),
        out_shape=f32(2 * seg, width),
        compiler_params=params(12),
        cost_estimate=cost(3 * seg * seg * width * 2, 12 * seg * width),
        name="dft",
    )(table, *xs)


def taps_kernel(table_ref, x_ref, out_ref, last_ref):
    step = pl.program_id(0)
    rows = out_ref.shape[1] // 4
    sub = rows // 2

    def store(group, value):
        base = group * rows
        sign = 1.0 if group % 2 == 0 else -1.0
        re, im = slice(base, base + sub), slice(base + sub, base + rows)
        out_ref[0, re, :] = value[:sub] - sign * last_ref[im, :]
        out_ref[0, im, :] = value[sub:] + sign * last_ref[re, :]
        last_ref[base : base + rows, :] = value

    @pl.when(step == 0)
    def _():
        last_ref[...] = jnp.zeros_like(last_ref)

    transform(x_ref[...], table_ref, store)


def taps_spectra(table, taps, seg):
    width = taps.shape[1]
    blocks = taps.shape[0] // seg
    return pl.pallas_call(
        taps_kernel,
        grid=(blocks,),
        in_specs=[whole_spec(table.shape), pl.BlockSpec((seg, width), lambda i: (i, 0))],
        out_specs=pl.BlockSpec((1, 2 * seg, width), lambda i: (jnp.maximum(i - 1, 0), 0, 0)),
        out_shape=jax.ShapeDtypeStruct((blocks - 1, 2 * seg, width), jnp.float32),
        scratch_shapes=[pltpu.VMEM((2 * seg, width), jnp.float32)],
        compiler_params=params(14),
        cost_estimate=cost(blocks * 3 * seg * seg * width * 2, blocks * 12 * seg * width),
        name="taps",
    )(table, taps)


def conj_mul(a, b):
    return a[0] * b[0] + a[1] * b[1], a[0] * b[1] - a[1] * b[0]


def mul(a, b):
    return a[0] * b[0] - a[1] * b[1], a[0] * b[1] + a[1] * b[0]


def add(a, b):
    return a[0] + b[0], a[1] + b[1]


def partial_kernel(
    pos_ref, table_ref, inverse_ref, win_near, win_far, left_ref, right_ref, x_ref, far_ref, out_ref, z_ref
):
    rows = far_ref.shape[0] // 4
    sub = rows // 2
    is_left = pos_ref[0] != 1
    for group, part in enumerate(spread(x_ref[...])):
        base = group * rows
        far = dot3(table_ref, group, *split(part))
        far_ref[base : base + rows, :] = far
        re, im = slice(base, base + sub), slice(base + sub, base + rows)
        near = tuple(jnp.where(is_left, left_ref[at, :], right_ref[at, :]) for at in (re, im))
        total = add(
            conj_mul((win_near[0, re, :], win_near[0, im, :]), near),
            conj_mul((win_far[0, re, :], win_far[0, im, :]), (far[:sub], far[sub:])),
        )
        z_ref[group] = dot3(inverse_ref, group, *split(jnp.concatenate(total, axis=0)))
    quarters = gather_quarters([z_ref[g, :sub] for g in range(4)], [z_ref[g, sub:] for g in range(4)])
    for i, quarter in enumerate(quarters):
        out_ref[i * sub : (i + 1) * sub, :] = quarter


def back_partial(pos, table, inverse, windows, left, right, x, half, seg):
    width = x.shape[1]
    n = (windows.shape[0] + 1) // 2

    def window(distance):
        return pl.BlockSpec(
            (1, 2 * seg, width),
            lambda i, pos: (jnp.where(pos[0] == 1, n - 1 + distance, n - 1 - distance), 0, half),
        )

    near = pl.BlockSpec((2 * seg, width), lambda i, pos: (0, half))
    return pl.pallas_call(
        partial_kernel,
        grid_spec=pltpu.PrefetchScalarGridSpec(
            num_scalar_prefetch=1,
            grid=(1,),
            in_specs=[
                whole_spec(table.shape),
                whole_spec(inverse.shape),
                window(2),
                window(3),
                near,
                near,
                whole_spec((seg, width)),
            ],
            out_specs=[whole_spec((2 * seg, width)), whole_spec((seg, width))],
            scratch_shapes=[pltpu.VMEM((4, seg // 2, width), jnp.float32)],
        ),
        out_shape=[f32(2 * seg, width), f32(seg, width)],
        compiler_params=params(20),
        cost_estimate=cost(6 * seg * seg * width * 2, 24 * seg * width),
        name="partial",
    )(pos, table, inverse, windows, windows, left, right, x)


OWN, LEFT, RIGHT, TWO, THREE = range(5)
PAIRS = (
    ((), ((OWN, THREE),), ((OWN, TWO), (RIGHT, THREE))),
    (
        ((LEFT, RIGHT), (OWN, TWO)),
        ((LEFT, OWN), (OWN, RIGHT), (RIGHT, TWO)),
        ((LEFT, LEFT), (OWN, OWN), (RIGHT, RIGHT), (TWO, TWO)),
    ),
    (
        ((TWO, TWO), (LEFT, LEFT), (OWN, OWN), (RIGHT, RIGHT)),
        ((LEFT, TWO), (OWN, LEFT), (RIGHT, OWN)),
        ((OWN, TWO), (RIGHT, LEFT)),
    ),
    (((LEFT, THREE), (OWN, TWO)), ((OWN, THREE),), ()),
)


def is_late(pair):
    return pair[0] == TWO or pair[1] == THREE


def pair_sums(distances, gated, mixed, sign, late):
    total = []
    for pairs in distances:
        value = None
        for m, g in pairs:
            if is_late((m, g)) == late:
                term = conj_mul(gated[g](), mixed[m]())
                value = term if value is None else add(value, term)
        total.append(value)
    out = []
    for low, high in zip(total[:2], total[1:]):
        if high is not None:
            turned = (sign * high[1], -sign * high[0])
            low = turned if low is None else add(low, turned)
        out.append(low)
    return out


TILE = 16


def tile_reader(tile, sub):
    re = pl.ds(pl.multiple_of(tile * TILE, TILE), TILE)
    im = pl.ds(pl.multiple_of(sub + tile * TILE, TILE), TILE)

    def read(ref, *lead):
        return ref[(*lead, re, slice(None))], ref[(*lead, im, slice(None))]

    return re, im, read


def group_sign():
    return jnp.where(pl.program_id(0) % 2 == 0, 1.0, -1.0)


def early_kernel(
    pos_ref, win_own, win_left, win_right, win_two, own_g, left_g, right_g, two_g, own_m, left_m, right_m, out_ref
):
    pos, sign = pos_ref[0], group_sign()
    rows = own_g.shape[0]
    sub = rows // 2
    count = sub // TILE

    def put(at, slot, value):
        re, im = at
        out_ref[slot, re, :] = value[0]
        out_ref[slot, im, :] = value[1]

    def sums(tile, _):
        re, im, read = tile_reader(tile, sub)
        own, left, right = read(win_own, 0), read(win_left, 0), read(win_right, 0)
        conv = add(mul(own, read(own_g)), mul(left, read(left_g)))
        conv = add(conv, add(mul(right, read(right_g)), mul(read(win_two, 0), read(two_g))))
        put((re, im), 0, conv)
        back = add(conj_mul(own, read(own_m)), conj_mul(right, read(left_m)))
        put((re, im), 1, add(back, conj_mul(left, read(right_m))))
        return _

    lax.fori_loop(0, count, sums, 0)
    for where, distances in enumerate(PAIRS):

        @pl.when(pos == where)
        def _():
            def lags(tile, _):
                re, im, read = tile_reader(tile, sub)
                gated = [functools.partial(read, ref) for ref in (own_g, left_g, right_g, two_g)]
                mixed = [functools.partial(read, ref) for ref in (own_m, left_m, right_m)]
                for slot, value in enumerate(pair_sums(distances, gated, mixed, sign, False)):
                    if value is None:
                        value = (jnp.zeros_like(own_g[re, :]),) * 2
                    put((re, im), 2 + slot, value)
                return _

            lax.fori_loop(0, count, lags, 0)


def early(pos, windows, gated, mixed, seg):
    width = gated[0].shape[1]
    rows = seg // 2
    mid = windows.shape[0] // 2

    def window(index):
        return pl.BlockSpec((1, rows, width), lambda i, pos: (index(pos[0]), i, 0))

    group = pl.BlockSpec((rows, width), lambda i, pos: (i, 0))
    return pl.pallas_call(
        early_kernel,
        grid_spec=pltpu.PrefetchScalarGridSpec(
            num_scalar_prefetch=1,
            grid=(4,),
            in_specs=[
                window(lambda p: mid),
                window(lambda p: mid + 1),
                window(lambda p: mid - 1),
                window(lambda p: jnp.where(p < 2, mid - 2, mid + 2)),
            ]
            + [group] * 7,
            out_specs=pl.BlockSpec((4, rows, width), lambda i, pos: (0, i, 0)),
        ),
        out_shape=f32(4, 2 * seg, width),
        compiler_params=params(14),
        cost_estimate=cost(200 * seg * width, 120 * seg * width),
        name="early",
    )(pos, *[windows] * 4, *gated, *mixed)


def late_kernel(
    pos_ref, inverse_ref, acc_ref, win_ref, three_g, two_g, own_m, left_m, right_m, *rest
):
    two_m, (gated_ref, mixed, strips), (skip_ref, up_ref, query_out, filter_out, back_out, skip_out) = (
        rest[:2], (rest[2], rest[3:5], rest[5:10]), rest[10:16])
    x_high, x_low, z_ref = rest[16:]
    group = pl.program_id(0)
    pos, sign = pos_ref[0], group_sign()
    rows, width = own_m.shape
    half = width // 2
    sub = rows // 2

    def put(at, slot, value):
        for rows_at, part in zip(at, value):
            high, low = split(part)
            x_high[rows_at, slot * width : (slot + 1) * width] = high
            x_low[rows_at, slot * width : (slot + 1) * width] = low

    for where, distances in enumerate(PAIRS):

        @pl.when(pos == where)
        def _():
            def lags(tile, _):
                re, im, read = tile_reader(tile, sub)

                def read_two():
                    parts = [read(ref) for ref in two_m]
                    return tuple(jnp.concatenate([p[i] for p in parts], axis=1) for i in range(2))

                gated = [None, None, None, functools.partial(read, two_g), functools.partial(read, three_g)]
                mixed = [functools.partial(read, ref) for ref in (own_m, left_m, right_m)] + [read_two]
                total = [read(acc_ref, slot) for slot in range(4)]
                if where in (0, 3):
                    total[0] = add(total[0], mul(read(win_ref, 0), gated[THREE]()))
                else:
                    total[1] = add(total[1], conj_mul(read(win_ref, 0), mixed[TWO]()))
                for slot, value in enumerate(pair_sums(distances, gated, mixed, sign, True)):
                    if value is not None:
                        total[2 + slot] = add(total[2 + slot], value)
                for slot, value in enumerate(total):
                    put((re, im), slot, value)
                return _

            lax.fori_loop(0, sub // TILE, lags, 0)

    dot = functools.partial(jnp.dot, preferred_element_type=jnp.float32)
    t_high, t_low = inverse_ref[0, 0], inverse_ref[1, 0]
    for slot in range(4):
        cols = slice(slot * width, (slot + 1) * width)
        z_ref[group, :, cols] = (
            dot(t_high, x_high[:, cols]) + dot(t_high, x_low[:, cols]) + dot(t_low, x_high[:, cols])
        )

    @pl.when(group == 3)
    def _():
        seg = 4 * sub
        for slot in range(4):
            cols = slice(slot * width, (slot + 1) * width)
            quarters = gather_quarters(
                [z_ref[g, :sub, cols] for g in range(4)], [z_ref[g, sub:, cols] for g in range(4)]
            )
            for i, quarter in enumerate(quarters):
                at = slice(i * sub, (i + 1) * sub)
                if slot == 0:
                    query_out[at, :] = up_ref[at, :] * (quarter + skip_ref[...] * gated_ref[at, :])
                elif slot == 1:
                    for h in range(2):
                        lanes = slice(h * half, (h + 1) * half)
                        back_out[at, lanes] = quarter[:, lanes] + skip_ref[:, lanes] * mixed[h][at, :]
                else:
                    base = (slot - 2) * seg + i * sub
                    filter_out[base : base + sub, :] = quarter
        sources = (pos, pos - 1, pos + 1, jnp.where(pos < 2, pos + 2, pos - 2), 3 - pos)
        total = jnp.zeros((8, width), jnp.float32)
        for block in range(4):
            value = jnp.zeros((8, width), jnp.float32)
            for where, (ref, source) in enumerate(zip(strips, sources)):
                hit = source == block
                if where == THREE:
                    hit = jnp.logical_and(hit, jnp.logical_or(pos == 0, pos == 3))
                value = value + jnp.where(hit, ref[...], 0.0)
            total = total + value
        skip_out[...] = jnp.sum(total, axis=0, keepdims=True)


def late(pos, inverse, acc, windows, three_g, two_g, own_m, left_m, right_m, two_m, blocks, mixed, skip, upstream):
    seg, width = upstream.shape
    rows = seg // 2
    mid = windows.shape[0] // 2

    def win_at(i, pos):
        p = pos[0]
        ends = jnp.where(p == 0, mid - 3, mid + 3)
        return jnp.where(p == 1, mid + 2, jnp.where(p == 2, mid - 2, ends)), i, 0

    group = pl.BlockSpec((rows, width), lambda i, pos: (i, 0))
    group_half = pl.BlockSpec((rows, width // 2), lambda i, pos: (i, 0))
    strip = pl.BlockSpec((8, width), lambda i, pos: (seg // 8, 0))
    return pl.pallas_call(
        late_kernel,
        grid_spec=pltpu.PrefetchScalarGridSpec(
            num_scalar_prefetch=1,
            grid=(4,),
            in_specs=[
                pl.BlockSpec((2, 1, rows, rows), lambda i, pos: (0, i, 0, 0)),
                pl.BlockSpec((4, rows, width), lambda i, pos: (0, i, 0)),
                pl.BlockSpec((1, rows, width), win_at),
                *[group] * 5,
                *[group_half] * 2,
                whole_spec((seg, width)),
                *[whole_spec((seg, width // 2))] * 2,
                *[strip] * 5,
                whole_spec((1, width)),
                whole_spec((seg, width)),
            ],
            out_specs=[
                whole_spec((seg, width)), whole_spec((2 * seg, width)), whole_spec((seg, width)), whole_spec((1, width)),
            ],
            scratch_shapes=[
                pltpu.VMEM((rows, 4 * width), jnp.bfloat16),
                pltpu.VMEM((rows, 4 * width), jnp.bfloat16),
                pltpu.VMEM((4, rows, 4 * width), jnp.float32),
            ],
        ),
        out_shape=[f32(seg, width), f32(2 * seg, width), f32(seg, width), f32(1, width)],
        compiler_params=params(32),
        cost_estimate=cost(12 * seg * seg * width * 2, 100 * seg * width),
        name="late",
    )(pos, inverse, acc, windows, three_g, two_g, own_m, left_m, right_m, *two_m, blocks[0], *mixed, *blocks, skip, upstream)


def send(x, *pairs):
    return lax.ppermute(x, "ctx", list(pairs))


def to_right(x):
    return send(x, (0, 1), (1, 2), (2, 3))


def to_left(x):
    return send(x, (1, 0), (2, 1), (3, 2))


def local_line(query_gate, key_gate, values, filter_taps, skip_gain, upstream):
    seg, width = values.shape
    forward_np, inverse_np = tables(seg)
    table, inverse = jnp.asarray(forward_np), jnp.asarray(inverse_np)
    position = lax.axis_index("ctx")
    pos = position.astype(jnp.int32).reshape(1)
    after = lax.optimization_barrier

    gated, *mixed = prepare(query_gate, key_gate, values, upstream, 2)
    left, right = to_right(gated), to_left(gated)
    left_m0, right_m0 = to_right(mixed[0]), to_left(mixed[0])
    windows = taps_spectra(table, filter_taps, seg)
    own_g, own_m = dft(table, seg, gated), dft(table, seg, *mixed)
    left, right, windows, own_g, own_m = after((left, right, windows, own_g, own_m))

    two_l, two_r = send(left, (1, 2), (2, 3)), send(right, (2, 1), (1, 0))
    left_g, right_g = dft(table, seg, left), dft(table, seg, right)
    left_m0, right_m0, mixed_1, left_g, right_g = after((left_m0, right_m0, mixed[1], left_g, right_g))
    left_m1, right_m1 = to_right(mixed_1), to_left(mixed_1)
    far_0 = jnp.where(position == 1, left_m0, right_m0)
    two_l, two_r, far_0 = after((two_l, two_r, far_0))
    two = two_l + two_r
    three = send(two, (1, 0), (2, 3))
    two_m0 = send(far_0, (1, 2), (2, 1))
    two_g = dft(table, seg, two)

    left_m1, right_m1, two_g = after((left_m1, right_m1, two_g))
    far_1 = jnp.where(position == 1, left_m1, right_m1)
    two_m1 = send(far_1, (1, 2), (2, 1))
    left_m, right_m = dft(table, seg, left_m0, left_m1), dft(table, seg, right_m0, right_m1)
    acc = early(pos, windows, (own_g, left_g, right_g, two_g), (own_m, left_m, right_m), seg)
    two_m0, left_m, right_m = after((two_m0, left_m, right_m))
    spec_0, partial_0 = back_partial(pos, table, inverse, windows, left_m, right_m, two_m0, 0, seg)
    two_m1, partial_0 = after((two_m1, partial_0))
    partial_0 = send(partial_0, (1, 0), (2, 3))
    spec_1, partial_1 = back_partial(pos, table, inverse, windows, left_m, right_m, two_m1, 1, seg)
    partial_1 = send(partial_1, (1, 0), (2, 3))
    three_g = dft(table, seg, three)
    query_grad, filter_grad, back, skip_grad = late(
        pos, inverse, acc, windows, three_g, two_g, own_m, left_m, right_m, (spec_0, spec_1),
        (gated, left, right, two, three), mixed, skip_gain[None, :], upstream,
    )
    partial_0, partial_1, back = after((partial_0, partial_1, back))
    back = back + jnp.concatenate([partial_0, partial_1], axis=1)
    return (query_grad, back * values, back * key_gate, filter_grad, skip_grad[0])


def matmul(left, right):
    return jnp.dot(left, right, preferred_element_type=jnp.float32, precision=lax.Precision.HIGHEST)


def forward_table(seg_len, count, offset):
    num_bins = seg_len + 1
    period = 2 * seg_len
    bin_index = lax.broadcasted_iota(jnp.int32, (num_bins, count), 0)
    pos_index = lax.broadcasted_iota(jnp.int32, (num_bins, count), 1) + offset
    angles = (bin_index * pos_index % period).astype(jnp.float32) * (2.0 * math.pi / period)
    return jnp.concatenate([jnp.cos(angles), -jnp.sin(angles)], axis=0)


def inverse_table(seg_len, count, offset):
    num_bins = seg_len + 1
    period = 2 * seg_len
    pos_index = lax.broadcasted_iota(jnp.int32, (count, num_bins), 0) + offset
    bin_index = lax.broadcasted_iota(jnp.int32, (count, num_bins), 1)
    angles = (bin_index * pos_index % period).astype(jnp.float32) * (2.0 * math.pi / period)
    weights = jnp.where((bin_index == 0) | (bin_index == seg_len), 1.0, 2.0) / period
    return jnp.concatenate([weights * jnp.cos(angles), -weights * jnp.sin(angles)], axis=1)


def times_spec(first, second):
    num_bins = first.shape[0] // 2
    real_a, imag_a = (first[:num_bins], first[num_bins:])
    real_b, imag_b = (second[:num_bins], second[num_bins:])
    return jnp.concatenate(
        [real_a * real_b - imag_a * imag_b, real_a * imag_b + imag_a * real_b], axis=0
    )


def conj_times(first, second):
    num_bins = first.shape[0] // 2
    real_a, imag_a = (first[:num_bins], first[num_bins:])
    real_b, imag_b = (second[:num_bins], second[num_bins:])
    return jnp.concatenate(
        [real_a * real_b + imag_a * imag_b, real_a * imag_b - imag_a * real_b], axis=0
    )


def pick(stack, index):
    return lax.dynamic_index_in_dim(stack, index, 0, keepdims=False)


def local(query_gate, key_gate, values, filter_taps, skip_gain, upstream):
    seg_len, width_dev = values.shape
    cycle_size = lax.axis_size("ctx")
    position = lax.axis_index("ctx")
    history = seg_len * cycle_size
    gated = key_gate * values
    mixed_grad = upstream * query_gate
    table_low = forward_table(seg_len, seg_len, 0)
    table_high = forward_table(seg_len, seg_len, seg_len)
    table_taps = forward_table(seg_len, 2 * seg_len, 0)
    back_low = inverse_table(seg_len, seg_len, 0)
    back_high = inverse_table(seg_len, seg_len, seg_len)
    back_full = inverse_table(seg_len, 2 * seg_len, 0)
    own_grad_spec = matmul(table_high, mixed_grad)
    spec_rows = 2 * (seg_len + 1)

    def taps_spec(lag_block):
        start_row = (lag_block - 1) * seg_len + history
        window = lax.dynamic_slice_in_dim(filter_taps, start_row, 2 * seg_len, 0)
        return matmul(table_taps, window)

    def visit(carry, gated_spec, grad_spec, source):
        acc_conv, acc_back, partial_value = carry
        lag_block = position - source
        acc_conv = acc_conv + times_spec(taps_spec(lag_block), gated_spec)
        acc_back = acc_back + conj_times(taps_spec(-lag_block), grad_spec)
        segment = matmul(back_full, conj_times(gated_spec, own_grad_spec))
        start_row = (lag_block - 1) * seg_len + history
        current = lax.dynamic_slice_in_dim(partial_value, start_row, 2 * seg_len, 0)
        partial_value = lax.dynamic_update_slice_in_dim(
            partial_value, current + segment, start_row, 0
        )
        return (acc_conv, acc_back, partial_value)

    initial = (
        jnp.zeros((spec_rows, width_dev), jnp.float32),
        jnp.zeros((spec_rows, width_dev), jnp.float32),
        jnp.zeros((2 * history, width_dev), jnp.float32),
    )
    own_gated_spec = matmul(table_low, gated)
    pieces = (
        lax.all_gather(own_gated_spec[None], "ctx", axis=0, tiled=True),
        lax.all_gather(own_grad_spec[None], "ctx", axis=0, tiled=True),
    )

    def advance(member, state):
        return visit(state, pick(pieces[0], member), pick(pieces[1], member), member)

    folded = lax.fori_loop(0, pieces[0].shape[0], advance, initial)
    acc_conv, acc_back, partial_value = folded
    filter_grad = lax.psum_scatter(partial_value, "ctx", scatter_dimension=0, tiled=True)
    conv = matmul(back_high, acc_conv)
    back = matmul(back_low, acc_back) + skip_gain[None, :] * mixed_grad
    query_grad = upstream * (conv + skip_gain[None, :] * gated)
    key_grad = back * values
    value_grad = back * key_gate
    skip_grad = lax.psum(jnp.sum(mixed_grad * gated, axis=0), "ctx")
    return (query_grad, key_grad, value_grad, filter_grad, skip_grad)


def solution(mesh):
    in_specs = (
        P(("groups", "ctx"), "chan"),
        P(("groups", "ctx"), "chan"),
        P(("groups", "ctx"), "chan"),
        P(None, "chan"),
        P("chan"),
        P(("groups", "ctx"), "chan"),
    )
    out_specs = (
        P(("groups", "ctx"), "chan"),
        P(("groups", "ctx"), "chan"),
        P(("groups", "ctx"), "chan"),
        P(("groups", "ctx"), "chan"),
        P(("groups", "chan")),
    )
    body = local_line if mesh.shape["ctx"] == 4 else local
    return jax.shard_map(body, mesh=mesh, in_specs=in_specs, out_specs=out_specs, check_vma=False)
```

```python
import functools
import math

import jax
import jax.numpy as jnp
import ml_dtypes
import numpy as np
from jax import lax
from jax.experimental import pallas as pl
from jax.experimental.pallas import tpu as pltpu
from jax.sharding import PartitionSpec as P

COS1, SIN1, HALF = math.cos(math.pi / 8), math.sin(math.pi / 8), math.sqrt(0.5)


def split_np(table):
    high = table.astype(ml_dtypes.bfloat16)
    low = (table - high.astype(np.float64)).astype(ml_dtypes.bfloat16)
    return np.stack([high, low])


def tables(seg):
    sub = seg // 4
    bins, pos = np.arange(sub)[:, None], np.arange(sub)[None, :]
    forward = []
    for group in range(4):
        angle = 2 * np.pi * pos * (8 * bins + group + 0.5) / (2 * seg)
        cos, sin = np.cos(angle), np.sin(angle)
        forward.append(np.block([[cos, -sin], [-sin, -cos]]))
    forward = np.stack(forward)
    inverse = forward.transpose(0, 2, 1) / seg
    return split_np(forward), split_np(inverse)


def split(x):
    high = x.astype(jnp.bfloat16)
    return high, (x - high.astype(jnp.float32)).astype(jnp.bfloat16)


def dot3(table_ref, group, high, low):
    t_high, t_low = table_ref[0, group], table_ref[1, group]
    dot = functools.partial(jnp.dot, preferred_element_type=jnp.float32)
    return dot(t_high, high) + dot(t_high, low) + dot(t_low, high)


def spread(x):
    sub = x.shape[0] // 4
    x0, x1, x2, x3 = (x[i * sub : (i + 1) * sub] for i in range(4))
    u, p, s, q, t = HALF * x2, COS1 * x1, SIN1 * x1, COS1 * x3, SIN1 * x3
    a, b, pt, sq, pmt, spq = x0 + u, x0 - u, p + t, s - q, p - t, s + q
    pairs = ((a + pt, spq + u), (b + sq, pmt + u), (b - sq, pmt - u), (a - pt, spq - u))
    return [jnp.concatenate(pair, axis=0) for pair in pairs]


def gather_quarters(re, im):
    e03, d03, e12, d12 = re[0] + re[3], re[0] - re[3], re[1] + re[2], re[1] - re[2]
    f03, g03, f12, g12 = im[0] + im[3], im[0] - im[3], im[1] + im[2], im[1] - im[2]
    return (
        e03 + e12,
        COS1 * (d03 + f12) + SIN1 * (d12 + f03),
        HALF * (e03 - e12 + g03 + g12),
        SIN1 * (d03 - f12) + COS1 * (f03 - d12),
    )


def transform(x, table_ref, store):
    for group, part in enumerate(spread(x)):
        store(group, dot3(table_ref, group, *split(part)))


def cost(flops, nbytes):
    return pl.CostEstimate(flops=int(flops), bytes_accessed=int(nbytes), transcendentals=0)


def params(mib):
    return pltpu.CompilerParams(vmem_limit_bytes=mib << 20)


def whole_spec(shape):
    return pl.BlockSpec(shape, lambda *_: (0,) * len(shape))


def f32(*shape):
    return jax.ShapeDtypeStruct(shape, jnp.float32)


def prepare_kernel(query_ref, key_ref, values_ref, up_ref, gated_ref, mixed_ref, sum_ref):
    step = pl.program_id(0)
    rows, width = key_ref.shape
    gated = key_ref[...] * values_ref[...]
    mixed = up_ref[...] * query_ref[...]
    gated_ref[pl.ds(pl.multiple_of(step * rows, rows), rows), :] = gated
    mixed_ref[...] = mixed
    part = jnp.sum((gated * mixed).reshape(rows // 8, 8, width), axis=0)

    @pl.when(step == 0)
    def _():
        sum_ref[...] = part

    @pl.when(step > 0)
    def _():
        sum_ref[...] += part

    @pl.when(step == pl.num_programs(0) - 1)
    def _():
        seg = gated_ref.shape[0] - 8
        gated_ref[seg:, :] = sum_ref[...]


def prepare(query_gate, key_gate, values, upstream):
    seg, width = values.shape
    steps = 4
    rows = seg // steps
    block = pl.BlockSpec((rows, width), lambda i: (i, 0))
    return pl.pallas_call(
        prepare_kernel,
        grid=(steps,),
        in_specs=[block] * 4,
        out_specs=[whole_spec((seg + 8, width)), block],
        out_shape=[f32(seg + 8, width), f32(seg, width)],
        scratch_shapes=[pltpu.VMEM((8, width), jnp.float32)],
        compiler_params=params(56),
        cost_estimate=cost(4 * seg * width, 24 * seg * width),
        name="prepare",
    )(query_gate, key_gate, values, upstream)


def dft_kernel(table_ref, *refs):
    *x_refs, out_ref = refs
    rows = out_ref.shape[0] // 4

    def store(group, value):
        out_ref[group * rows : (group + 1) * rows, :] = value

    parts = [ref[...] for ref in x_refs]
    transform(parts[0] if len(parts) == 1 else jnp.concatenate(parts, axis=1), table_ref, store)


def dft(table, seg, *xs):
    width = sum(x.shape[1] for x in xs)
    return pl.pallas_call(
        dft_kernel,
        grid=(1,),
        in_specs=[whole_spec(table.shape)] + [whole_spec((seg, x.shape[1])) for x in xs],
        out_specs=whole_spec((2 * seg, width)),
        out_shape=f32(2 * seg, width),
        compiler_params=params(12),
        cost_estimate=cost(3 * seg * seg * width * 2, 12 * seg * width),
        name="dft",
    )(table, *xs)


def taps_kernel(table_ref, x_ref, out_ref, last_ref):
    step = pl.program_id(0)
    rows = out_ref.shape[1] // 4
    sub = rows // 2

    def store(group, value):
        base = group * rows
        sign = 1.0 if group % 2 == 0 else -1.0
        re, im = slice(base, base + sub), slice(base + sub, base + rows)
        out_ref[0, re, :] = value[:sub] - sign * last_ref[im, :]
        out_ref[0, im, :] = value[sub:] + sign * last_ref[re, :]
        last_ref[base : base + rows, :] = value

    @pl.when(step == 0)
    def _():
        last_ref[...] = jnp.zeros_like(last_ref)

    transform(x_ref[...], table_ref, store)


def taps_spectra(table, taps, seg):
    width = taps.shape[1]
    blocks = taps.shape[0] // seg
    return pl.pallas_call(
        taps_kernel,
        grid=(blocks,),
        in_specs=[whole_spec(table.shape), pl.BlockSpec((seg, width), lambda i: (i, 0))],
        out_specs=pl.BlockSpec((1, 2 * seg, width), lambda i: (jnp.maximum(i - 1, 0), 0, 0)),
        out_shape=jax.ShapeDtypeStruct((blocks - 1, 2 * seg, width), jnp.float32),
        scratch_shapes=[pltpu.VMEM((2 * seg, width), jnp.float32)],
        compiler_params=params(14),
        cost_estimate=cost(blocks * 3 * seg * seg * width * 2, blocks * 12 * seg * width),
        name="taps",
    )(table, taps)


def conj_mul(a, b):
    return a[0] * b[0] + a[1] * b[1], a[0] * b[1] - a[1] * b[0]


def mul(a, b):
    return a[0] * b[0] - a[1] * b[1], a[0] * b[1] + a[1] * b[0]


def add(a, b):
    return a[0] + b[0], a[1] + b[1]


def partial_kernel(
    pos_ref, table_ref, inverse_ref, win_near, win_far, left_ref, right_ref, x_ref, far_ref, out_ref, z_ref
):
    rows = far_ref.shape[0] // 4
    sub = rows // 2
    is_left = pos_ref[0] != 1
    for group, part in enumerate(spread(x_ref[...])):
        base = group * rows
        far = dot3(table_ref, group, *split(part))
        far_ref[base : base + rows, :] = far
        re, im = slice(base, base + sub), slice(base + sub, base + rows)
        near = tuple(jnp.where(is_left, left_ref[at, :], right_ref[at, :]) for at in (re, im))
        total = add(
            conj_mul((win_near[0, re, :], win_near[0, im, :]), near),
            conj_mul((win_far[0, re, :], win_far[0, im, :]), (far[:sub], far[sub:])),
        )
        z_ref[group] = dot3(inverse_ref, group, *split(jnp.concatenate(total, axis=0)))
    quarters = gather_quarters([z_ref[g, :sub] for g in range(4)], [z_ref[g, sub:] for g in range(4)])
    for i, quarter in enumerate(quarters):
        out_ref[i * sub : (i + 1) * sub, :] = quarter


def back_partial(pos, table, inverse, windows, left, right, x, half, seg):
    width = x.shape[1]
    n = (windows.shape[0] + 1) // 2

    def window(distance):
        return pl.BlockSpec(
            (1, 2 * seg, width),
            lambda i, pos: (jnp.where(pos[0] == 1, n - 1 + distance, n - 1 - distance), 0, half),
        )

    near = pl.BlockSpec((2 * seg, width), lambda i, pos: (0, half))
    return pl.pallas_call(
        partial_kernel,
        grid_spec=pltpu.PrefetchScalarGridSpec(
            num_scalar_prefetch=1,
            grid=(1,),
            in_specs=[
                whole_spec(table.shape),
                whole_spec(inverse.shape),
                window(2),
                window(3),
                near,
                near,
                whole_spec((seg, width)),
            ],
            out_specs=[whole_spec((2 * seg, width)), whole_spec((seg, width))],
            scratch_shapes=[pltpu.VMEM((4, seg // 2, width), jnp.float32)],
        ),
        out_shape=[f32(2 * seg, width), f32(seg, width)],
        compiler_params=params(20),
        cost_estimate=cost(6 * seg * seg * width * 2, 24 * seg * width),
        name="partial",
    )(pos, table, inverse, windows, windows, left, right, x)


OWN, LEFT, RIGHT, TWO, THREE = range(5)
PAIRS = (
    ((), ((OWN, THREE),), ((OWN, TWO), (RIGHT, THREE))),
    (
        ((LEFT, RIGHT), (OWN, TWO)),
        ((LEFT, OWN), (OWN, RIGHT), (RIGHT, TWO)),
        ((LEFT, LEFT), (OWN, OWN), (RIGHT, RIGHT), (TWO, TWO)),
    ),
    (
        ((TWO, TWO), (LEFT, LEFT), (OWN, OWN), (RIGHT, RIGHT)),
        ((LEFT, TWO), (OWN, LEFT), (RIGHT, OWN)),
        ((OWN, TWO), (RIGHT, LEFT)),
    ),
    (((LEFT, THREE), (OWN, TWO)), ((OWN, THREE),), ()),
)


def is_late(pair):
    return pair[0] == TWO or pair[1] == THREE


def pair_sums(distances, gated, mixed, sign, late):
    total = []
    for pairs in distances:
        value = None
        for m, g in pairs:
            if is_late((m, g)) == late:
                term = conj_mul(gated[g](), mixed[m]())
                value = term if value is None else add(value, term)
        total.append(value)
    out = []
    for low, high in zip(total[:2], total[1:]):
        if high is not None:
            turned = (sign * high[1], -sign * high[0])
            low = turned if low is None else add(low, turned)
        out.append(low)
    return out


TILE = 16


def tile_reader(tile, sub):
    re = pl.ds(pl.multiple_of(tile * TILE, TILE), TILE)
    im = pl.ds(pl.multiple_of(sub + tile * TILE, TILE), TILE)

    def read(ref, *lead):
        return ref[(*lead, re, slice(None))], ref[(*lead, im, slice(None))]

    return re, im, read


def group_sign():
    return jnp.where(pl.program_id(0) % 2 == 0, 1.0, -1.0)


def early_kernel(
    pos_ref, win_own, win_left, win_right, win_two, own_g, left_g, right_g, two_g, own_m, left_m, right_m, out_ref
):
    pos, sign = pos_ref[0], group_sign()
    rows = own_g.shape[0]
    sub = rows // 2
    count = sub // TILE

    def put(at, slot, value):
        re, im = at
        out_ref[slot, re, :] = value[0]
        out_ref[slot, im, :] = value[1]

    def sums(tile, _):
        re, im, read = tile_reader(tile, sub)
        own, left, right = read(win_own, 0), read(win_left, 0), read(win_right, 0)
        conv = add(mul(own, read(own_g)), mul(left, read(left_g)))
        conv = add(conv, add(mul(right, read(right_g)), mul(read(win_two, 0), read(two_g))))
        put((re, im), 0, conv)
        back = add(conj_mul(own, read(own_m)), conj_mul(right, read(left_m)))
        put((re, im), 1, add(back, conj_mul(left, read(right_m))))
        return _

    lax.fori_loop(0, count, sums, 0)
    for where, distances in enumerate(PAIRS):

        @pl.when(pos == where)
        def _():
            def lags(tile, _):
                re, im, read = tile_reader(tile, sub)
                gated = [functools.partial(read, ref) for ref in (own_g, left_g, right_g, two_g)]
                mixed = [functools.partial(read, ref) for ref in (own_m, left_m, right_m)]
                for slot, value in enumerate(pair_sums(distances, gated, mixed, sign, False)):
                    if value is None:
                        value = (jnp.zeros_like(own_g[re, :]),) * 2
                    put((re, im), 2 + slot, value)
                return _

            lax.fori_loop(0, count, lags, 0)


def early(pos, windows, gated, mixed, seg):
    width = gated[0].shape[1]
    rows = seg // 2
    mid = windows.shape[0] // 2

    def window(index):
        return pl.BlockSpec((1, rows, width), lambda i, pos: (index(pos[0]), i, 0))

    group = pl.BlockSpec((rows, width), lambda i, pos: (i, 0))
    return pl.pallas_call(
        early_kernel,
        grid_spec=pltpu.PrefetchScalarGridSpec(
            num_scalar_prefetch=1,
            grid=(4,),
            in_specs=[
                window(lambda p: mid),
                window(lambda p: mid + 1),
                window(lambda p: mid - 1),
                window(lambda p: jnp.where(p < 2, mid - 2, mid + 2)),
            ]
            + [group] * 7,
            out_specs=pl.BlockSpec((4, rows, width), lambda i, pos: (0, i, 0)),
        ),
        out_shape=f32(4, 2 * seg, width),
        compiler_params=params(14),
        cost_estimate=cost(200 * seg * width, 120 * seg * width),
        name="early",
    )(pos, *[windows] * 4, *gated, *mixed)


def late_kernel(
    pos_ref, inverse_ref, acc_ref, win_ref, three_g, two_g, own_m, left_m, right_m, *rest
):
    two_m, (gated_ref, mixed_ref, partial_ref), strips = rest[:2], rest[2:5], rest[5:10]
    skip_ref, up_ref, query_out, filter_out, back_out, skip_out, x_high, x_low, z_ref = rest[10:]
    group = pl.program_id(0)
    pos, sign = pos_ref[0], group_sign()
    rows, width = own_m.shape
    half = width // 2
    sub = rows // 2

    def put(at, slot, value):
        for rows_at, part in zip(at, value):
            high, low = split(part)
            x_high[rows_at, slot * width : (slot + 1) * width] = high
            x_low[rows_at, slot * width : (slot + 1) * width] = low

    for where, distances in enumerate(PAIRS):

        @pl.when(pos == where)
        def _():
            def lags(tile, _):
                re, im, read = tile_reader(tile, sub)

                def read_two():
                    parts = [read(ref) for ref in two_m]
                    return tuple(jnp.concatenate([p[i] for p in parts], axis=1) for i in range(2))

                gated = [None, None, None, functools.partial(read, two_g), functools.partial(read, three_g)]
                mixed = [functools.partial(read, ref) for ref in (own_m, left_m, right_m)] + [read_two]
                total = [read(acc_ref, slot) for slot in range(4)]
                if where in (0, 3):
                    total[0] = add(total[0], mul(read(win_ref, 0), gated[THREE]()))
                else:
                    total[1] = add(total[1], conj_mul(read(win_ref, 0), mixed[TWO]()))
                for slot, value in enumerate(pair_sums(distances, gated, mixed, sign, True)):
                    if value is not None:
                        total[2 + slot] = add(total[2 + slot], value)
                for slot, value in enumerate(total):
                    put((re, im), slot, value)
                return _

            lax.fori_loop(0, sub // TILE, lags, 0)

    dot = functools.partial(jnp.dot, preferred_element_type=jnp.float32)
    t_high, t_low = inverse_ref[0, 0], inverse_ref[1, 0]
    for slot in range(4):
        cols = slice(slot * width, (slot + 1) * width)
        z_ref[group, :, cols] = (
            dot(t_high, x_high[:, cols]) + dot(t_high, x_low[:, cols]) + dot(t_low, x_high[:, cols])
        )

    @pl.when(group == 3)
    def _():
        seg = 4 * sub
        for slot in range(4):
            cols = slice(slot * width, (slot + 1) * width)
            quarters = gather_quarters(
                [z_ref[g, :sub, cols] for g in range(4)], [z_ref[g, sub:, cols] for g in range(4)]
            )
            for i, quarter in enumerate(quarters):
                at = slice(i * sub, (i + 1) * sub)
                if slot == 0:
                    query_out[at, :] = up_ref[at, :] * (quarter + skip_ref[...] * gated_ref[at, :])
                elif slot == 1:
                    back = quarter + skip_ref[...] * mixed_ref[at, :]
                    back_out[at, :half] = back[:, :half] + partial_ref[at, :]
                    back_out[at, half:] = back[:, half:]
                else:
                    base = (slot - 2) * seg + i * sub
                    filter_out[base : base + sub, :] = quarter
        sources = (pos, pos - 1, pos + 1, jnp.where(pos < 2, pos + 2, pos - 2), 3 - pos)
        total = jnp.zeros((8, width), jnp.float32)
        for block in range(4):
            value = jnp.zeros((8, width), jnp.float32)
            for where, (ref, source) in enumerate(zip(strips, sources)):
                hit = source == block
                if where == THREE:
                    hit = jnp.logical_and(hit, jnp.logical_or(pos == 0, pos == 3))
                value = value + jnp.where(hit, ref[...], 0.0)
            total = total + value
        skip_out[...] = jnp.sum(total, axis=0, keepdims=True)


def late(pos, inverse, acc, windows, three_g, two_g, own_m, left_m, right_m, two_m, blocks, mixed, partial, skip, upstream):
    seg, width = upstream.shape
    rows = seg // 2
    mid = windows.shape[0] // 2

    def win_at(i, pos):
        p = pos[0]
        ends = jnp.where(p == 0, mid - 3, mid + 3)
        return jnp.where(p == 1, mid + 2, jnp.where(p == 2, mid - 2, ends)), i, 0

    group = pl.BlockSpec((rows, width), lambda i, pos: (i, 0))
    group_half = pl.BlockSpec((rows, width // 2), lambda i, pos: (i, 0))
    strip = pl.BlockSpec((8, width), lambda i, pos: (seg // 8, 0))
    return pl.pallas_call(
        late_kernel,
        grid_spec=pltpu.PrefetchScalarGridSpec(
            num_scalar_prefetch=1,
            grid=(4,),
            in_specs=[
                pl.BlockSpec((2, 1, rows, rows), lambda i, pos: (0, i, 0, 0)),
                pl.BlockSpec((4, rows, width), lambda i, pos: (0, i, 0)),
                pl.BlockSpec((1, rows, width), win_at),
                *[group] * 5,
                *[group_half] * 2,
                whole_spec((seg, width)),
                whole_spec((seg, width)),
                whole_spec((seg, width // 2)),
                *[strip] * 5,
                whole_spec((1, width)),
                whole_spec((seg, width)),
            ],
            out_specs=[
                whole_spec((seg, width)), whole_spec((2 * seg, width)), whole_spec((seg, width)), whole_spec((1, width)),
            ],
            scratch_shapes=[
                pltpu.VMEM((rows, 4 * width), jnp.bfloat16),
                pltpu.VMEM((rows, 4 * width), jnp.bfloat16),
                pltpu.VMEM((4, rows, 4 * width), jnp.float32),
            ],
        ),
        out_shape=[f32(seg, width), f32(2 * seg, width), f32(seg, width), f32(1, width)],
        compiler_params=params(20),
        cost_estimate=cost(12 * seg * seg * width * 2, 100 * seg * width),
        name="late",
    )(pos, inverse, acc, windows, three_g, two_g, own_m, left_m, right_m, *two_m, blocks[0], mixed, partial, *blocks, skip, upstream)


def send(x, *pairs):
    return lax.ppermute(x, "ctx", list(pairs))


def to_right(x):
    return send(x, (0, 1), (1, 2), (2, 3))


def to_left(x):
    return send(x, (1, 0), (2, 1), (3, 2))


def local_line(query_gate, key_gate, values, filter_taps, skip_gain, upstream):
    seg, width = values.shape
    forward_np, inverse_np = tables(seg)
    table, inverse = jnp.asarray(forward_np), jnp.asarray(inverse_np)
    half = width // 2
    position = lax.axis_index("ctx")
    pos = position.astype(jnp.int32).reshape(1)
    after = lax.optimization_barrier

    gated, mixed = prepare(query_gate, key_gate, values, upstream)
    left, right = to_right(gated), to_left(gated)
    left_x, right_x = to_right(mixed), to_left(mixed)
    windows = taps_spectra(table, filter_taps, seg)
    own_g = dft(table, seg, gated)
    left, right, windows, own_g = after((left, right, windows, own_g))

    two_l, two_r = send(left, (1, 2), (2, 3)), send(right, (2, 1), (1, 0))
    own_m, left_g, right_g = dft(table, seg, mixed), dft(table, seg, left), dft(table, seg, right)
    left_x, right_x, own_m, left_g, right_g = after((left_x, right_x, own_m, left_g, right_g))

    far = [jnp.where(position == 1, left_x[:, at], right_x[:, at]) for at in (slice(half), slice(half, None))]
    two_m0, two_m1 = [send(x, (1, 2), (2, 1)) for x in far]
    left_m, right_m = dft(table, seg, left_x), dft(table, seg, right_x)
    two_l, two_r, left_m, right_m = after((two_l, two_r, left_m, right_m))

    two = two_l + two_r
    three = send(two, (1, 0), (2, 3))
    two_g = dft(table, seg, two)
    acc = early(pos, windows, (own_g, left_g, right_g, two_g), (own_m, left_m, right_m), seg)
    two_m0, acc = after((two_m0, acc))

    spec_0, partial_0 = back_partial(pos, table, inverse, windows, left_m, right_m, two_m0, 0, seg)
    two_m1, partial_0 = after((two_m1, partial_0))
    partial_0 = send(partial_0, (1, 0), (2, 3))
    spec_1, partial_1 = back_partial(pos, table, inverse, windows, left_m, right_m, two_m1, 1, seg)
    partial_1 = send(partial_1, (1, 0), (2, 3))
    three_g = dft(table, seg, three)
    query_grad, filter_grad, back, skip_grad = late(
        pos, inverse, acc, windows, three_g, two_g, own_m, left_m, right_m, (spec_0, spec_1),
        (gated, left, right, two, three), mixed, partial_0, skip_gain[None, :], upstream,
    )
    back, partial_1 = after((back, partial_1))
    back = jnp.concatenate([back[:, :half], back[:, half:] + partial_1], axis=1)
    return (query_grad, back * values, back * key_gate, filter_grad, skip_grad[0])


def matmul(left, right):
    return jnp.dot(left, right, preferred_element_type=jnp.float32, precision=lax.Precision.HIGHEST)


def forward_table(seg_len, count, offset):
    num_bins = seg_len + 1
    period = 2 * seg_len
    bin_index = lax.broadcasted_iota(jnp.int32, (num_bins, count), 0)
    pos_index = lax.broadcasted_iota(jnp.int32, (num_bins, count), 1) + offset
    angles = (bin_index * pos_index % period).astype(jnp.float32) * (2.0 * math.pi / period)
    return jnp.concatenate([jnp.cos(angles), -jnp.sin(angles)], axis=0)


def inverse_table(seg_len, count, offset):
    num_bins = seg_len + 1
    period = 2 * seg_len
    pos_index = lax.broadcasted_iota(jnp.int32, (count, num_bins), 0) + offset
    bin_index = lax.broadcasted_iota(jnp.int32, (count, num_bins), 1)
    angles = (bin_index * pos_index % period).astype(jnp.float32) * (2.0 * math.pi / period)
    weights = jnp.where((bin_index == 0) | (bin_index == seg_len), 1.0, 2.0) / period
    return jnp.concatenate([weights * jnp.cos(angles), -weights * jnp.sin(angles)], axis=1)


def times_spec(first, second):
    num_bins = first.shape[0] // 2
    real_a, imag_a = (first[:num_bins], first[num_bins:])
    real_b, imag_b = (second[:num_bins], second[num_bins:])
    return jnp.concatenate(
        [real_a * real_b - imag_a * imag_b, real_a * imag_b + imag_a * real_b], axis=0
    )


def conj_times(first, second):
    num_bins = first.shape[0] // 2
    real_a, imag_a = (first[:num_bins], first[num_bins:])
    real_b, imag_b = (second[:num_bins], second[num_bins:])
    return jnp.concatenate(
        [real_a * real_b + imag_a * imag_b, real_a * imag_b - imag_a * real_b], axis=0
    )


def pick(stack, index):
    return lax.dynamic_index_in_dim(stack, index, 0, keepdims=False)


def local(query_gate, key_gate, values, filter_taps, skip_gain, upstream):
    seg_len, width_dev = values.shape
    cycle_size = lax.axis_size("ctx")
    position = lax.axis_index("ctx")
    history = seg_len * cycle_size
    gated = key_gate * values
    mixed_grad = upstream * query_gate
    table_low = forward_table(seg_len, seg_len, 0)
    table_high = forward_table(seg_len, seg_len, seg_len)
    table_taps = forward_table(seg_len, 2 * seg_len, 0)
    back_low = inverse_table(seg_len, seg_len, 0)
    back_high = inverse_table(seg_len, seg_len, seg_len)
    back_full = inverse_table(seg_len, 2 * seg_len, 0)
    own_grad_spec = matmul(table_high, mixed_grad)
    spec_rows = 2 * (seg_len + 1)

    def taps_spec(lag_block):
        start_row = (lag_block - 1) * seg_len + history
        window = lax.dynamic_slice_in_dim(filter_taps, start_row, 2 * seg_len, 0)
        return matmul(table_taps, window)

    def visit(carry, gated_spec, grad_spec, source):
        acc_conv, acc_back, partial_value = carry
        lag_block = position - source
        acc_conv = acc_conv + times_spec(taps_spec(lag_block), gated_spec)
        acc_back = acc_back + conj_times(taps_spec(-lag_block), grad_spec)
        segment = matmul(back_full, conj_times(gated_spec, own_grad_spec))
        start_row = (lag_block - 1) * seg_len + history
        current = lax.dynamic_slice_in_dim(partial_value, start_row, 2 * seg_len, 0)
        partial_value = lax.dynamic_update_slice_in_dim(
            partial_value, current + segment, start_row, 0
        )
        return (acc_conv, acc_back, partial_value)

    initial = (
        jnp.zeros((spec_rows, width_dev), jnp.float32),
        jnp.zeros((spec_rows, width_dev), jnp.float32),
        jnp.zeros((2 * history, width_dev), jnp.float32),
    )
    own_gated_spec = matmul(table_low, gated)
    pieces = (
        lax.all_gather(own_gated_spec[None], "ctx", axis=0, tiled=True),
        lax.all_gather(own_grad_spec[None], "ctx", axis=0, tiled=True),
    )

    def advance(member, state):
        return visit(state, pick(pieces[0], member), pick(pieces[1], member), member)

    folded = lax.fori_loop(0, pieces[0].shape[0], advance, initial)
    acc_conv, acc_back, partial_value = folded
    filter_grad = lax.psum_scatter(partial_value, "ctx", scatter_dimension=0, tiled=True)
    conv = matmul(back_high, acc_conv)
    back = matmul(back_low, acc_back) + skip_gain[None, :] * mixed_grad
    query_grad = upstream * (conv + skip_gain[None, :] * gated)
    key_grad = back * values
    value_grad = back * key_gate
    skip_grad = lax.psum(jnp.sum(mixed_grad * gated, axis=0), "ctx")
    return (query_grad, key_grad, value_grad, filter_grad, skip_grad)


def solution(mesh):
    in_specs = (
        P(("groups", "ctx"), "chan"),
        P(("groups", "ctx"), "chan"),
        P(("groups", "ctx"), "chan"),
        P(None, "chan"),
        P("chan"),
        P(("groups", "ctx"), "chan"),
    )
    out_specs = (
        P(("groups", "ctx"), "chan"),
        P(("groups", "ctx"), "chan"),
        P(("groups", "ctx"), "chan"),
        P(("groups", "ctx"), "chan"),
        P(("groups", "chan")),
    )
    body = local_line if mesh.shape["ctx"] == 4 else local
    return jax.shard_map(body, mesh=mesh, in_specs=in_specs, out_specs=out_specs, check_vma=False)
```

```python
import functools
import math

import jax
import jax.numpy as jnp
import ml_dtypes
import numpy as np
from jax import lax
from jax.experimental import pallas as pl
from jax.experimental.pallas import tpu as pltpu
from jax.sharding import PartitionSpec as P

COS1, SIN1, HALF = math.cos(math.pi / 8), math.sin(math.pi / 8), math.sqrt(0.5)


def split_np(table):
    high = table.astype(ml_dtypes.bfloat16)
    low = (table - high.astype(np.float64)).astype(ml_dtypes.bfloat16)
    return np.stack([high, low])


def tables(seg):
    sub = seg // 4
    bins, pos = np.arange(sub)[:, None], np.arange(sub)[None, :]
    forward = []
    for group in range(4):
        angle = 2 * np.pi * pos * (8 * bins + group + 0.5) / (2 * seg)
        cos, sin = np.cos(angle), np.sin(angle)
        forward.append(np.block([[cos, -sin], [-sin, -cos]]))
    forward = np.stack(forward)
    inverse = forward.transpose(0, 2, 1) / seg
    return split_np(forward), split_np(inverse)


def split(x):
    high = x.astype(jnp.bfloat16)
    return high, (x - high.astype(jnp.float32)).astype(jnp.bfloat16)


def dot3(table_ref, group, high, low):
    t_high, t_low = table_ref[0, group], table_ref[1, group]
    dot = functools.partial(jnp.dot, preferred_element_type=jnp.float32)
    return dot(t_high, high) + dot(t_high, low) + dot(t_low, high)


def spread(x):
    sub = x.shape[0] // 4
    x0, x1, x2, x3 = (x[i * sub : (i + 1) * sub] for i in range(4))
    u, p, s, q, t = HALF * x2, COS1 * x1, SIN1 * x1, COS1 * x3, SIN1 * x3
    a, b, pt, sq, pmt, spq = x0 + u, x0 - u, p + t, s - q, p - t, s + q
    pairs = ((a + pt, spq + u), (b + sq, pmt + u), (b - sq, pmt - u), (a - pt, spq - u))
    return [jnp.concatenate(pair, axis=0) for pair in pairs]


def gather_quarters(re, im):
    e03, d03, e12, d12 = re[0] + re[3], re[0] - re[3], re[1] + re[2], re[1] - re[2]
    f03, g03, f12, g12 = im[0] + im[3], im[0] - im[3], im[1] + im[2], im[1] - im[2]
    return (
        e03 + e12,
        COS1 * (d03 + f12) + SIN1 * (d12 + f03),
        HALF * (e03 - e12 + g03 + g12),
        SIN1 * (d03 - f12) + COS1 * (f03 - d12),
    )


def transform(x, table_ref, store):
    for group, part in enumerate(spread(x)):
        store(group, dot3(table_ref, group, *split(part)))


def cost(flops, nbytes):
    return pl.CostEstimate(flops=int(flops), bytes_accessed=int(nbytes), transcendentals=0)


def params(mib):
    return pltpu.CompilerParams(vmem_limit_bytes=mib << 20)


def whole_spec(shape):
    return pl.BlockSpec(shape, lambda *_: (0,) * len(shape))


def f32(*shape):
    return jax.ShapeDtypeStruct(shape, jnp.float32)


def prepare_kernel(query_ref, key_ref, values_ref, up_ref, gated_ref, mixed_ref, sum_ref):
    step = pl.program_id(0)
    rows, width = key_ref.shape
    gated = key_ref[...] * values_ref[...]
    mixed = up_ref[...] * query_ref[...]
    gated_ref[pl.ds(pl.multiple_of(step * rows, rows), rows), :] = gated
    mixed_ref[...] = mixed
    part = jnp.sum((gated * mixed).reshape(rows // 8, 8, width), axis=0)

    @pl.when(step == 0)
    def _():
        sum_ref[...] = part

    @pl.when(step > 0)
    def _():
        sum_ref[...] += part

    @pl.when(step == pl.num_programs(0) - 1)
    def _():
        seg = gated_ref.shape[0] - 8
        gated_ref[seg:, :] = sum_ref[...]


def prepare(query_gate, key_gate, values, upstream):
    seg, width = values.shape
    steps = 4
    rows = seg // steps
    block = pl.BlockSpec((rows, width), lambda i: (i, 0))
    return pl.pallas_call(
        prepare_kernel,
        grid=(steps,),
        in_specs=[block] * 4,
        out_specs=[whole_spec((seg + 8, width)), block],
        out_shape=[f32(seg + 8, width), f32(seg, width)],
        scratch_shapes=[pltpu.VMEM((8, width), jnp.float32)],
        compiler_params=params(56),
        cost_estimate=cost(4 * seg * width, 24 * seg * width),
        name="prepare",
    )(query_gate, key_gate, values, upstream)


def dft_kernel(table_ref, *refs):
    *x_refs, out_ref = refs
    rows = out_ref.shape[0] // 4

    def store(group, value):
        out_ref[group * rows : (group + 1) * rows, :] = value

    x = x_refs[0][...]
    for ref in x_refs[1:]:
        x = x + ref[...]
    transform(x, table_ref, store)


def dft(table, seg, *xs):
    width = xs[0].shape[1]
    return pl.pallas_call(
        dft_kernel,
        grid=(1,),
        in_specs=[whole_spec(table.shape)] + [whole_spec((seg, x.shape[1])) for x in xs],
        out_specs=whole_spec((2 * seg, width)),
        out_shape=f32(2 * seg, width),
        compiler_params=params(12),
        cost_estimate=cost(3 * seg * seg * width * 2, 12 * seg * width),
        name="dft",
    )(table, *xs)


def taps_kernel(table_ref, x_ref, out_ref, last_ref):
    step = pl.program_id(0)
    rows = out_ref.shape[1] // 4
    sub = rows // 2

    def store(group, value):
        base = group * rows
        sign = 1.0 if group % 2 == 0 else -1.0
        re, im = slice(base, base + sub), slice(base + sub, base + rows)
        out_ref[0, re, :] = value[:sub] - sign * last_ref[im, :]
        out_ref[0, im, :] = value[sub:] + sign * last_ref[re, :]
        last_ref[base : base + rows, :] = value

    @pl.when(step == 0)
    def _():
        last_ref[...] = jnp.zeros_like(last_ref)

    transform(x_ref[...], table_ref, store)


def taps_spectra(table, taps, seg):
    width = taps.shape[1]
    blocks = taps.shape[0] // seg
    return pl.pallas_call(
        taps_kernel,
        grid=(blocks,),
        in_specs=[whole_spec(table.shape), pl.BlockSpec((seg, width), lambda i: (i, 0))],
        out_specs=pl.BlockSpec((1, 2 * seg, width), lambda i: (jnp.maximum(i - 1, 0), 0, 0)),
        out_shape=jax.ShapeDtypeStruct((blocks - 1, 2 * seg, width), jnp.float32),
        scratch_shapes=[pltpu.VMEM((2 * seg, width), jnp.float32)],
        compiler_params=params(14),
        cost_estimate=cost(blocks * 3 * seg * seg * width * 2, blocks * 12 * seg * width),
        name="taps",
    )(table, taps)


def conj_mul(a, b):
    return a[0] * b[0] + a[1] * b[1], a[0] * b[1] - a[1] * b[0]


def mul(a, b):
    return a[0] * b[0] - a[1] * b[1], a[0] * b[1] + a[1] * b[0]


def add(a, b):
    return a[0] + b[0], a[1] + b[1]


def partial_kernel(
    pos_ref, table_ref, inverse_ref, win_near, win_far, left_ref, right_ref, x_ref, far_ref, out_ref, z_ref
):
    rows = far_ref.shape[0] // 4
    sub = rows // 2
    is_left = pos_ref[0] != 1
    for group, part in enumerate(spread(x_ref[...])):
        base = group * rows
        far = dot3(table_ref, group, *split(part))
        far_ref[base : base + rows, :] = far
        re, im = slice(base, base + sub), slice(base + sub, base + rows)
        near = tuple(jnp.where(is_left, left_ref[at, :], right_ref[at, :]) for at in (re, im))
        total = add(
            conj_mul((win_near[0, re, :], win_near[0, im, :]), near),
            conj_mul((win_far[0, re, :], win_far[0, im, :]), (far[:sub], far[sub:])),
        )
        z_ref[group] = dot3(inverse_ref, group, *split(jnp.concatenate(total, axis=0)))
    quarters = gather_quarters([z_ref[g, :sub] for g in range(4)], [z_ref[g, sub:] for g in range(4)])
    for i, quarter in enumerate(quarters):
        out_ref[i * sub : (i + 1) * sub, :] = quarter


def back_partial(pos, table, inverse, windows, left, right, x, seg):
    width = x.shape[1]
    n = (windows.shape[0] + 1) // 2

    def window(distance):
        return pl.BlockSpec(
            (1, 2 * seg, width),
            lambda i, pos: (jnp.where(pos[0] == 1, n - 1 + distance, n - 1 - distance), 0, 0),
        )

    near = whole_spec((2 * seg, width))
    return pl.pallas_call(
        partial_kernel,
        grid_spec=pltpu.PrefetchScalarGridSpec(
            num_scalar_prefetch=1,
            grid=(1,),
            in_specs=[
                whole_spec(table.shape),
                whole_spec(inverse.shape),
                window(2),
                window(3),
                near,
                near,
                whole_spec((seg, width)),
            ],
            out_specs=[whole_spec((2 * seg, width)), whole_spec((seg, width))],
            scratch_shapes=[pltpu.VMEM((4, seg // 2, width), jnp.float32)],
        ),
        out_shape=[f32(2 * seg, width), f32(seg, width)],
        compiler_params=params(24),
        cost_estimate=cost(6 * seg * seg * width * 2, 24 * seg * width),
        name="partial",
    )(pos, table, inverse, windows, windows, left, right, x)


OWN, LEFT, RIGHT, TWO, THREE = range(5)
PAIRS = (
    ((), ((OWN, THREE),), ((OWN, TWO), (RIGHT, THREE))),
    (
        ((LEFT, RIGHT), (OWN, TWO)),
        ((LEFT, OWN), (OWN, RIGHT), (RIGHT, TWO)),
        ((LEFT, LEFT), (OWN, OWN), (RIGHT, RIGHT), (TWO, TWO)),
    ),
    (
        ((TWO, TWO), (LEFT, LEFT), (OWN, OWN), (RIGHT, RIGHT)),
        ((LEFT, TWO), (OWN, LEFT), (RIGHT, OWN)),
        ((OWN, TWO), (RIGHT, LEFT)),
    ),
    (((LEFT, THREE), (OWN, TWO)), ((OWN, THREE),), ()),
)


def is_late(pair):
    return pair[0] == TWO or pair[1] == THREE


def pair_sums(distances, gated, mixed, sign, late):
    total = []
    for pairs in distances:
        value = None
        for m, g in pairs:
            if is_late((m, g)) == late:
                term = conj_mul(gated[g](), mixed[m]())
                value = term if value is None else add(value, term)
        total.append(value)
    out = []
    for low, high in zip(total[:2], total[1:]):
        if high is not None:
            turned = (sign * high[1], -sign * high[0])
            low = turned if low is None else add(low, turned)
        out.append(low)
    return out


TILE = 16


def tile_reader(tile, sub):
    re = pl.ds(pl.multiple_of(tile * TILE, TILE), TILE)
    im = pl.ds(pl.multiple_of(sub + tile * TILE, TILE), TILE)

    def read(ref, *lead):
        return ref[(*lead, re, slice(None))], ref[(*lead, im, slice(None))]

    return re, im, read


def group_sign():
    return jnp.where(pl.program_id(0) % 2 == 0, 1.0, -1.0)


def early_kernel(
    pos_ref, win_own, win_left, win_right, win_two, own_g, left_g, right_g, two_g, own_m, left_m, right_m, out_ref
):
    pos, sign = pos_ref[0], group_sign()
    rows = own_g.shape[0]
    sub = rows // 2
    count = sub // TILE

    def put(at, slot, value):
        re, im = at
        out_ref[slot, re, :] = value[0]
        out_ref[slot, im, :] = value[1]

    def sums(tile, _):
        re, im, read = tile_reader(tile, sub)
        own, left, right = read(win_own, 0), read(win_left, 0), read(win_right, 0)
        conv = add(mul(own, read(own_g)), mul(left, read(left_g)))
        conv = add(conv, add(mul(right, read(right_g)), mul(read(win_two, 0), read(two_g))))
        put((re, im), 0, conv)
        back = add(conj_mul(own, read(own_m)), conj_mul(right, read(left_m)))
        put((re, im), 1, add(back, conj_mul(left, read(right_m))))
        return _

    lax.fori_loop(0, count, sums, 0)
    for where, distances in enumerate(PAIRS):

        @pl.when(pos == where)
        def _():
            def lags(tile, _):
                re, im, read = tile_reader(tile, sub)
                gated = [functools.partial(read, ref) for ref in (own_g, left_g, right_g, two_g)]
                mixed = [functools.partial(read, ref) for ref in (own_m, left_m, right_m)]
                for slot, value in enumerate(pair_sums(distances, gated, mixed, sign, False)):
                    if value is None:
                        value = (jnp.zeros_like(own_g[re, :]),) * 2
                    put((re, im), 2 + slot, value)
                return _

            lax.fori_loop(0, count, lags, 0)


def early(pos, windows, gated, mixed, seg):
    width = gated[0].shape[1]
    rows = seg // 2
    mid = windows.shape[0] // 2

    def window(index):
        return pl.BlockSpec((1, rows, width), lambda i, pos: (index(pos[0]), i, 0))

    group = pl.BlockSpec((rows, width), lambda i, pos: (i, 0))
    return pl.pallas_call(
        early_kernel,
        grid_spec=pltpu.PrefetchScalarGridSpec(
            num_scalar_prefetch=1,
            grid=(4,),
            in_specs=[
                window(lambda p: mid),
                window(lambda p: mid + 1),
                window(lambda p: mid - 1),
                window(lambda p: jnp.where(p < 2, mid - 2, mid + 2)),
            ]
            + [group] * 7,
            out_specs=pl.BlockSpec((4, rows, width), lambda i, pos: (0, i, 0)),
        ),
        out_shape=f32(4, 2 * seg, width),
        compiler_params=params(14),
        cost_estimate=cost(200 * seg * width, 120 * seg * width),
        name="early",
    )(pos, *[windows] * 4, *gated, *mixed)


def late_kernel(
    pos_ref, inverse_ref, acc_ref, win_ref, three_g, two_g, own_m, left_m, right_m, *rest
):
    two_m, gated_ref, mixed_ref = rest[:3]
    strips, rest = rest[3:10], rest[10:]
    skip_ref, up_ref, query_out, filter_out, back_out, skip_out, x_high, x_low, z_ref = rest
    group = pl.program_id(0)
    pos, sign = pos_ref[0], group_sign()
    rows, width = own_m.shape
    sub = rows // 2

    def put(at, slot, value):
        for rows_at, part in zip(at, value):
            high, low = split(part)
            x_high[rows_at, slot * width : (slot + 1) * width] = high
            x_low[rows_at, slot * width : (slot + 1) * width] = low

    for where, distances in enumerate(PAIRS):

        @pl.when(pos == where)
        def _():
            def lags(tile, _):
                re, im, read = tile_reader(tile, sub)

                gated = [None, None, None, functools.partial(read, two_g), functools.partial(read, three_g)]
                mixed = [functools.partial(read, ref) for ref in (own_m, left_m, right_m, two_m)]
                total = [read(acc_ref, slot) for slot in range(4)]
                if where in (0, 3):
                    total[0] = add(total[0], mul(read(win_ref, 0), gated[THREE]()))
                else:
                    total[1] = add(total[1], conj_mul(read(win_ref, 0), mixed[TWO]()))
                for slot, value in enumerate(pair_sums(distances, gated, mixed, sign, True)):
                    if value is not None:
                        total[2 + slot] = add(total[2 + slot], value)
                for slot, value in enumerate(total):
                    put((re, im), slot, value)
                return _

            lax.fori_loop(0, sub // TILE, lags, 0)

    dot = functools.partial(jnp.dot, preferred_element_type=jnp.float32)
    t_high, t_low = inverse_ref[0, 0], inverse_ref[1, 0]
    for slot in range(4):
        cols = slice(slot * width, (slot + 1) * width)
        z_ref[group, :, cols] = (
            dot(t_high, x_high[:, cols]) + dot(t_high, x_low[:, cols]) + dot(t_low, x_high[:, cols])
        )

    @pl.when(group == 3)
    def _():
        seg = 4 * sub
        for slot in range(4):
            cols = slice(slot * width, (slot + 1) * width)
            quarters = gather_quarters(
                [z_ref[g, :sub, cols] for g in range(4)], [z_ref[g, sub:, cols] for g in range(4)]
            )
            for i, quarter in enumerate(quarters):
                at = slice(i * sub, (i + 1) * sub)
                if slot == 0:
                    query_out[at, :] = up_ref[at, :] * (quarter + skip_ref[...] * gated_ref[at, :])
                elif slot == 1:
                    back_out[at, :] = quarter + skip_ref[...] * mixed_ref[at, :]
                else:
                    base = (slot - 2) * seg + i * sub
                    filter_out[base : base + sub, :] = quarter
        own, left, right, *far = (ref[...] for ref in strips)
        blocks = (own, left, right, far[0] + far[1], far[2] + far[3])
        sources = (pos, pos - 1, pos + 1, jnp.where(pos < 2, pos + 2, pos - 2), 3 - pos)
        total = jnp.zeros((8, width), jnp.float32)
        for block in range(4):
            value = jnp.zeros((8, width), jnp.float32)
            for where, (strip, source) in enumerate(zip(blocks, sources)):
                hit = source == block
                if where == THREE:
                    hit = jnp.logical_and(hit, jnp.logical_or(pos == 0, pos == 3))
                value = value + jnp.where(hit, strip, 0.0)
            total = total + value
        skip_out[...] = jnp.sum(total, axis=0, keepdims=True)


def late(pos, inverse, acc, windows, three_g, two_g, own_m, left_m, right_m, two_m, blocks, mixed, skip, upstream):
    seg, width = upstream.shape
    rows = seg // 2
    mid = windows.shape[0] // 2

    def win_at(i, pos):
        p = pos[0]
        ends = jnp.where(p == 0, mid - 3, mid + 3)
        return jnp.where(p == 1, mid + 2, jnp.where(p == 2, mid - 2, ends)), i, 0

    group = pl.BlockSpec((rows, width), lambda i, pos: (i, 0))
    strip = pl.BlockSpec((8, width), lambda i, pos: (seg // 8, 0))
    return pl.pallas_call(
        late_kernel,
        grid_spec=pltpu.PrefetchScalarGridSpec(
            num_scalar_prefetch=1,
            grid=(4,),
            in_specs=[
                pl.BlockSpec((2, 1, rows, rows), lambda i, pos: (0, i, 0, 0)),
                pl.BlockSpec((4, rows, width), lambda i, pos: (0, i, 0)),
                pl.BlockSpec((1, rows, width), win_at),
                *[group] * 6,
                whole_spec((seg, width)),
                whole_spec((seg, width)),
                *[strip] * 7,
                whole_spec((1, width)),
                whole_spec((seg, width)),
            ],
            out_specs=[
                whole_spec((seg, width)), whole_spec((2 * seg, width)), whole_spec((seg, width)), whole_spec((1, width)),
            ],
            scratch_shapes=[
                pltpu.VMEM((rows, 4 * width), jnp.bfloat16),
                pltpu.VMEM((rows, 4 * width), jnp.bfloat16),
                pltpu.VMEM((4, rows, 4 * width), jnp.float32),
            ],
        ),
        out_shape=[f32(seg, width), f32(2 * seg, width), f32(seg, width), f32(1, width)],
        compiler_params=params(20),
        cost_estimate=cost(12 * seg * seg * width * 2, 100 * seg * width),
        name="late",
    )(pos, inverse, acc, windows, three_g, two_g, own_m, left_m, right_m, two_m, blocks[0], mixed, *blocks, skip, upstream)


def send(x, *pairs):
    return lax.ppermute(x, "ctx", list(pairs))


def to_right(x):
    return send(x, (0, 1), (1, 2), (2, 3))


def to_left(x):
    return send(x, (1, 0), (2, 1), (3, 2))


def local_line(query_gate, key_gate, values, filter_taps, skip_gain, upstream):
    seg, width = values.shape
    forward_np, inverse_np = tables(seg)
    table, inverse = jnp.asarray(forward_np), jnp.asarray(inverse_np)
    position = lax.axis_index("ctx")
    pos = position.astype(jnp.int32).reshape(1)
    after = lax.optimization_barrier

    gated, mixed = prepare(query_gate, key_gate, values, upstream)
    left, right = to_right(gated), to_left(gated)
    left_x, right_x = to_right(mixed), to_left(mixed)
    windows = taps_spectra(table, filter_taps, seg)
    own_g = dft(table, seg, gated)
    left, right, windows, own_g = after((left, right, windows, own_g))

    two = send(left, (1, 2), (2, 3)), send(right, (2, 1), (1, 0))
    own_m, left_g, right_g = dft(table, seg, mixed), dft(table, seg, left), dft(table, seg, right)
    left_x, right_x, own_m, left_g, right_g = after((left_x, right_x, own_m, left_g, right_g))

    two_x = send(jnp.where(position == 1, left_x, right_x), (1, 2), (2, 1))
    left_m, right_m = dft(table, seg, left_x), dft(table, seg, right_x)
    *two, left_m, right_m = after((*two, left_m, right_m))

    three = send(two[0], (2, 3)), send(two[1], (1, 0))
    two_m, partial = back_partial(pos, table, inverse, windows, left_m, right_m, two_x, seg)
    *two, partial = after((*two, partial))
    partial = send(partial, (1, 0), (2, 3))
    two_g = dft(table, seg, *two)
    acc = early(pos, windows, (own_g, left_g, right_g, two_g), (own_m, left_m, right_m), seg)
    *three, acc = after((*three, acc))

    three_g = dft(table, seg, *three)
    query_grad, filter_grad, back, skip_grad = late(
        pos, inverse, acc, windows, three_g, two_g, own_m, left_m, right_m, two_m,
        (gated, left, right, *two, *three), mixed, skip_gain[None, :], upstream,
    )
    back, partial = after((back, partial))
    back = back + partial
    return (query_grad, back * values, back * key_gate, filter_grad, skip_grad[0])


def matmul(left, right):
    return jnp.dot(left, right, preferred_element_type=jnp.float32, precision=lax.Precision.HIGHEST)


def forward_table(seg_len, count, offset):
    num_bins = seg_len + 1
    period = 2 * seg_len
    bin_index = lax.broadcasted_iota(jnp.int32, (num_bins, count), 0)
    pos_index = lax.broadcasted_iota(jnp.int32, (num_bins, count), 1) + offset
    angles = (bin_index * pos_index % period).astype(jnp.float32) * (2.0 * math.pi / period)
    return jnp.concatenate([jnp.cos(angles), -jnp.sin(angles)], axis=0)


def inverse_table(seg_len, count, offset):
    num_bins = seg_len + 1
    period = 2 * seg_len
    pos_index = lax.broadcasted_iota(jnp.int32, (count, num_bins), 0) + offset
    bin_index = lax.broadcasted_iota(jnp.int32, (count, num_bins), 1)
    angles = (bin_index * pos_index % period).astype(jnp.float32) * (2.0 * math.pi / period)
    weights = jnp.where((bin_index == 0) | (bin_index == seg_len), 1.0, 2.0) / period
    return jnp.concatenate([weights * jnp.cos(angles), -weights * jnp.sin(angles)], axis=1)


def times_spec(first, second):
    num_bins = first.shape[0] // 2
    real_a, imag_a = (first[:num_bins], first[num_bins:])
    real_b, imag_b = (second[:num_bins], second[num_bins:])
    return jnp.concatenate(
        [real_a * real_b - imag_a * imag_b, real_a * imag_b + imag_a * real_b], axis=0
    )


def conj_times(first, second):
    num_bins = first.shape[0] // 2
    real_a, imag_a = (first[:num_bins], first[num_bins:])
    real_b, imag_b = (second[:num_bins], second[num_bins:])
    return jnp.concatenate(
        [real_a * real_b + imag_a * imag_b, real_a * imag_b - imag_a * real_b], axis=0
    )


def pick(stack, index):
    return lax.dynamic_index_in_dim(stack, index, 0, keepdims=False)


def local(query_gate, key_gate, values, filter_taps, skip_gain, upstream):
    seg_len, width_dev = values.shape
    cycle_size = lax.axis_size("ctx")
    position = lax.axis_index("ctx")
    history = seg_len * cycle_size
    gated = key_gate * values
    mixed_grad = upstream * query_gate
    table_low = forward_table(seg_len, seg_len, 0)
    table_high = forward_table(seg_len, seg_len, seg_len)
    table_taps = forward_table(seg_len, 2 * seg_len, 0)
    back_low = inverse_table(seg_len, seg_len, 0)
    back_high = inverse_table(seg_len, seg_len, seg_len)
    back_full = inverse_table(seg_len, 2 * seg_len, 0)
    own_grad_spec = matmul(table_high, mixed_grad)
    spec_rows = 2 * (seg_len + 1)

    def taps_spec(lag_block):
        start_row = (lag_block - 1) * seg_len + history
        window = lax.dynamic_slice_in_dim(filter_taps, start_row, 2 * seg_len, 0)
        return matmul(table_taps, window)

    def visit(carry, gated_spec, grad_spec, source):
        acc_conv, acc_back, partial_value = carry
        lag_block = position - source
        acc_conv = acc_conv + times_spec(taps_spec(lag_block), gated_spec)
        acc_back = acc_back + conj_times(taps_spec(-lag_block), grad_spec)
        segment = matmul(back_full, conj_times(gated_spec, own_grad_spec))
        start_row = (lag_block - 1) * seg_len + history
        current = lax.dynamic_slice_in_dim(partial_value, start_row, 2 * seg_len, 0)
        partial_value = lax.dynamic_update_slice_in_dim(
            partial_value, current + segment, start_row, 0
        )
        return (acc_conv, acc_back, partial_value)

    initial = (
        jnp.zeros((spec_rows, width_dev), jnp.float32),
        jnp.zeros((spec_rows, width_dev), jnp.float32),
        jnp.zeros((2 * history, width_dev), jnp.float32),
    )
    own_gated_spec = matmul(table_low, gated)
    pieces = (
        lax.all_gather(own_gated_spec[None], "ctx", axis=0, tiled=True),
        lax.all_gather(own_grad_spec[None], "ctx", axis=0, tiled=True),
    )

    def advance(member, state):
        return visit(state, pick(pieces[0], member), pick(pieces[1], member), member)

    folded = lax.fori_loop(0, pieces[0].shape[0], advance, initial)
    acc_conv, acc_back, partial_value = folded
    filter_grad = lax.psum_scatter(partial_value, "ctx", scatter_dimension=0, tiled=True)
    conv = matmul(back_high, acc_conv)
    back = matmul(back_low, acc_back) + skip_gain[None, :] * mixed_grad
    query_grad = upstream * (conv + skip_gain[None, :] * gated)
    key_grad = back * values
    value_grad = back * key_gate
    skip_grad = lax.psum(jnp.sum(mixed_grad * gated, axis=0), "ctx")
    return (query_grad, key_grad, value_grad, filter_grad, skip_grad)


def solution(mesh):
    in_specs = (
        P(("groups", "ctx"), "chan"),
        P(("groups", "ctx"), "chan"),
        P(("groups", "ctx"), "chan"),
        P(None, "chan"),
        P("chan"),
        P(("groups", "ctx"), "chan"),
    )
    out_specs = (
        P(("groups", "ctx"), "chan"),
        P(("groups", "ctx"), "chan"),
        P(("groups", "ctx"), "chan"),
        P(("groups", "ctx"), "chan"),
        P(("groups", "chan")),
    )
    body = local_line if mesh.shape["ctx"] == 4 else local
    return jax.shard_map(body, mesh=mesh, in_specs=in_specs, out_specs=out_specs, check_vma=False)
```

```python
import functools
import math

import jax
import jax.numpy as jnp
import ml_dtypes
import numpy as np
from jax import lax
from jax.experimental import pallas as pl
from jax.experimental.pallas import tpu as pltpu
from jax.sharding import PartitionSpec as P

COS1, SIN1, HALF = math.cos(math.pi / 8), math.sin(math.pi / 8), math.sqrt(0.5)


def split_np(table):
    high = table.astype(ml_dtypes.bfloat16)
    low = (table - high.astype(np.float64)).astype(ml_dtypes.bfloat16)
    return np.stack([high, low])


def tables(seg):
    sub = seg // 4
    bins, pos = np.arange(sub)[:, None], np.arange(sub)[None, :]
    forward = []
    for group in range(4):
        angle = 2 * np.pi * pos * (8 * bins + group + 0.5) / (2 * seg)
        cos, sin = np.cos(angle), np.sin(angle)
        forward.append(np.block([[cos, -sin], [-sin, -cos]]))
    forward = np.stack(forward)
    inverse = forward.transpose(0, 2, 1) / seg
    return split_np(forward), split_np(inverse)


def split(x):
    high = x.astype(jnp.bfloat16)
    return high, (x - high.astype(jnp.float32)).astype(jnp.bfloat16)


def dot3(table_ref, group, high, low):
    t_high, t_low = table_ref[0, group], table_ref[1, group]
    dot = functools.partial(jnp.dot, preferred_element_type=jnp.float32)
    return dot(t_high, high) + dot(t_high, low) + dot(t_low, high)


def spread(x):
    sub = x.shape[0] // 4
    x0, x1, x2, x3 = (x[i * sub : (i + 1) * sub] for i in range(4))
    u, p, s, q, t = HALF * x2, COS1 * x1, SIN1 * x1, COS1 * x3, SIN1 * x3
    a, b, pt, sq, pmt, spq = x0 + u, x0 - u, p + t, s - q, p - t, s + q
    pairs = ((a + pt, spq + u), (b + sq, pmt + u), (b - sq, pmt - u), (a - pt, spq - u))
    return [jnp.concatenate(pair, axis=0) for pair in pairs]


def gather_quarters(re, im):
    e03, d03, e12, d12 = re[0] + re[3], re[0] - re[3], re[1] + re[2], re[1] - re[2]
    f03, g03, f12, g12 = im[0] + im[3], im[0] - im[3], im[1] + im[2], im[1] - im[2]
    return (
        e03 + e12,
        COS1 * (d03 + f12) + SIN1 * (d12 + f03),
        HALF * (e03 - e12 + g03 + g12),
        SIN1 * (d03 - f12) + COS1 * (f03 - d12),
    )


def transform(x, table_ref, store):
    for group, part in enumerate(spread(x)):
        store(group, dot3(table_ref, group, *split(part)))


def cost(flops, nbytes):
    return pl.CostEstimate(flops=int(flops), bytes_accessed=int(nbytes), transcendentals=0)


def params(mib):
    return pltpu.CompilerParams(vmem_limit_bytes=mib << 20)


def whole_spec(shape):
    return pl.BlockSpec(shape, lambda *_: (0,) * len(shape))


def f32(*shape):
    return jax.ShapeDtypeStruct(shape, jnp.float32)


def mix_kernel(gated_ref, up_ref, query_ref, mixed_ref):
    seg, width = gated_ref.shape
    mixed = up_ref[...] * query_ref[...]
    mixed_ref[:seg, :] = mixed
    mixed_ref[seg:, :] = jnp.sum((gated_ref[...] * mixed).reshape(seg // 8, 8, width), axis=0)


def mix(gated, upstream, query_gate):
    seg, width = gated.shape
    return pl.pallas_call(
        mix_kernel,
        grid=(1,),
        in_specs=[whole_spec((seg, width))] * 3,
        out_specs=whole_spec((seg + 8, width)),
        out_shape=f32(seg + 8, width),
        compiler_params=params(12),
        cost_estimate=cost(4 * seg * width, 16 * seg * width),
        name="mix",
    )(gated, upstream, query_gate)


def strip_spec(seg, width):
    return pl.BlockSpec((8, width), lambda *_: (seg // 8, 0))


def dft_kernel(table_ref, *refs):
    *x_refs, out_ref = refs
    rows = out_ref.shape[0] // 4

    def store(group, value):
        out_ref[group * rows : (group + 1) * rows, :] = value

    x = x_refs[0][...]
    for ref in x_refs[1:]:
        x = x + ref[...]
    transform(x, table_ref, store)


def dft(table, seg, *xs):
    width = xs[0].shape[1]
    return pl.pallas_call(
        dft_kernel,
        grid=(1,),
        in_specs=[whole_spec(table.shape)] + [whole_spec((seg, x.shape[1])) for x in xs],
        out_specs=whole_spec((2 * seg, width)),
        out_shape=f32(2 * seg, width),
        compiler_params=params(12),
        cost_estimate=cost(3 * seg * seg * width * 2, 12 * seg * width),
        name="dft",
    )(table, *xs)


def taps_kernel(table_ref, x_ref, out_ref, last_ref):
    step = pl.program_id(0)
    rows = out_ref.shape[1] // 4
    sub = rows // 2

    def store(group, value):
        base = group * rows
        sign = 1.0 if group % 2 == 0 else -1.0
        re, im = slice(base, base + sub), slice(base + sub, base + rows)
        out_ref[0, re, :] = value[:sub] - sign * last_ref[im, :]
        out_ref[0, im, :] = value[sub:] + sign * last_ref[re, :]
        last_ref[base : base + rows, :] = value

    @pl.when(step == 0)
    def _():
        last_ref[...] = jnp.zeros_like(last_ref)

    transform(x_ref[...], table_ref, store)


def taps_spectra(table, taps, seg):
    width = taps.shape[1]
    blocks = taps.shape[0] // seg
    return pl.pallas_call(
        taps_kernel,
        grid=(blocks,),
        in_specs=[whole_spec(table.shape), pl.BlockSpec((seg, width), lambda i: (i, 0))],
        out_specs=pl.BlockSpec((1, 2 * seg, width), lambda i: (jnp.maximum(i - 1, 0), 0, 0)),
        out_shape=jax.ShapeDtypeStruct((blocks - 1, 2 * seg, width), jnp.float32),
        scratch_shapes=[pltpu.VMEM((2 * seg, width), jnp.float32)],
        compiler_params=params(14),
        cost_estimate=cost(blocks * 3 * seg * seg * width * 2, blocks * 12 * seg * width),
        name="taps",
    )(table, taps)


def conj_mul(a, b):
    return a[0] * b[0] + a[1] * b[1], a[0] * b[1] - a[1] * b[0]


def mul(a, b):
    return a[0] * b[0] - a[1] * b[1], a[0] * b[1] + a[1] * b[0]


def add(a, b):
    return a[0] + b[0], a[1] + b[1]


def partial_kernel(
    pos_ref, table_ref, inverse_ref, win_near, win_far, left_ref, right_ref, x_ref,
    left_strip, right_strip, far_strip, far_ref, out_ref, z_ref
):
    rows = far_ref.shape[0] // 4
    sub = rows // 2
    is_left = pos_ref[0] != 1
    for group, part in enumerate(spread(x_ref[...])):
        base = group * rows
        far = dot3(table_ref, group, *split(part))
        far_ref[base : base + rows, :] = far
        re, im = slice(base, base + sub), slice(base + sub, base + rows)
        near = tuple(jnp.where(is_left, left_ref[at, :], right_ref[at, :]) for at in (re, im))
        total = add(
            conj_mul((win_near[0, re, :], win_near[0, im, :]), near),
            conj_mul((win_far[0, re, :], win_far[0, im, :]), (far[:sub], far[sub:])),
        )
        z_ref[group] = dot3(inverse_ref, group, *split(jnp.concatenate(total, axis=0)))
    quarters = gather_quarters([z_ref[g, :sub] for g in range(4)], [z_ref[g, sub:] for g in range(4)])
    for i, quarter in enumerate(quarters):
        out_ref[i * sub : (i + 1) * sub, :] = quarter
    out_ref[4 * sub : 4 * sub + 8, :] = jnp.where(is_left, left_strip[...], right_strip[...])
    out_ref[4 * sub + 8 :, :] = far_strip[...]


def back_partial(pos, table, inverse, windows, left, right, left_x, right_x, x, seg):
    width = x.shape[1]
    n = (windows.shape[0] + 1) // 2

    def window(distance):
        return pl.BlockSpec(
            (1, 2 * seg, width),
            lambda i, pos: (jnp.where(pos[0] == 1, n - 1 + distance, n - 1 - distance), 0, 0),
        )

    near = whole_spec((2 * seg, width))
    return pl.pallas_call(
        partial_kernel,
        grid_spec=pltpu.PrefetchScalarGridSpec(
            num_scalar_prefetch=1,
            grid=(1,),
            in_specs=[
                whole_spec(table.shape),
                whole_spec(inverse.shape),
                window(2),
                window(3),
                near,
                near,
                whole_spec((seg, width)),
                *[strip_spec(seg, width)] * 3,
            ],
            out_specs=[whole_spec((2 * seg, width)), whole_spec((seg + 16, width))],
            scratch_shapes=[pltpu.VMEM((4, seg // 2, width), jnp.float32)],
        ),
        out_shape=[f32(2 * seg, width), f32(seg + 16, width)],
        compiler_params=params(24),
        cost_estimate=cost(6 * seg * seg * width * 2, 24 * seg * width),
        name="partial",
    )(pos, table, inverse, windows, windows, left, right, x, left_x, right_x, x)


OWN, LEFT, RIGHT, TWO, THREE = range(5)
PAIRS = (
    ((), ((OWN, THREE),), ((OWN, TWO), (RIGHT, THREE))),
    (
        ((LEFT, RIGHT), (OWN, TWO)),
        ((LEFT, OWN), (OWN, RIGHT), (RIGHT, TWO)),
        ((LEFT, LEFT), (OWN, OWN), (RIGHT, RIGHT), (TWO, TWO)),
    ),
    (
        ((TWO, TWO), (LEFT, LEFT), (OWN, OWN), (RIGHT, RIGHT)),
        ((LEFT, TWO), (OWN, LEFT), (RIGHT, OWN)),
        ((OWN, TWO), (RIGHT, LEFT)),
    ),
    (((LEFT, THREE), (OWN, TWO)), ((OWN, THREE),), ()),
)


def is_late(pair):
    return pair[0] == TWO or pair[1] == THREE


def pair_sums(distances, gated, mixed, sign, late):
    total = []
    for pairs in distances:
        value = None
        for m, g in pairs:
            if is_late((m, g)) == late:
                term = conj_mul(gated[g](), mixed[m]())
                value = term if value is None else add(value, term)
        total.append(value)
    out = []
    for low, high in zip(total[:2], total[1:]):
        if high is not None:
            turned = (sign * high[1], -sign * high[0])
            low = turned if low is None else add(low, turned)
        out.append(low)
    return out


TILE = 16


def tile_reader(tile, sub):
    re = pl.ds(pl.multiple_of(tile * TILE, TILE), TILE)
    im = pl.ds(pl.multiple_of(sub + tile * TILE, TILE), TILE)

    def read(ref, *lead):
        return ref[(*lead, re, slice(None))], ref[(*lead, im, slice(None))]

    return re, im, read


def group_sign():
    return jnp.where(pl.program_id(0) % 2 == 0, 1.0, -1.0)


def early_kernel(
    pos_ref, win_own, win_left, win_right, win_two, own_g, left_g, right_g, two_g, own_m, left_m, right_m, out_ref
):
    pos, sign = pos_ref[0], group_sign()
    rows = own_g.shape[0]
    sub = rows // 2
    count = sub // TILE

    def put(at, slot, value):
        re, im = at
        out_ref[slot, re, :] = value[0]
        out_ref[slot, im, :] = value[1]

    def sums(tile, _):
        re, im, read = tile_reader(tile, sub)
        own, left, right = read(win_own, 0), read(win_left, 0), read(win_right, 0)
        conv = add(mul(own, read(own_g)), mul(left, read(left_g)))
        conv = add(conv, add(mul(right, read(right_g)), mul(read(win_two, 0), read(two_g))))
        put((re, im), 0, conv)
        back = add(conj_mul(own, read(own_m)), conj_mul(right, read(left_m)))
        put((re, im), 1, add(back, conj_mul(left, read(right_m))))
        return _

    lax.fori_loop(0, count, sums, 0)
    for where, distances in enumerate(PAIRS):

        @pl.when(pos == where)
        def _():
            def lags(tile, _):
                re, im, read = tile_reader(tile, sub)
                gated = [functools.partial(read, ref) for ref in (own_g, left_g, right_g, two_g)]
                mixed = [functools.partial(read, ref) for ref in (own_m, left_m, right_m)]
                for slot, value in enumerate(pair_sums(distances, gated, mixed, sign, False)):
                    if value is None:
                        value = (jnp.zeros_like(own_g[re, :]),) * 2
                    put((re, im), 2 + slot, value)
                return _

            lax.fori_loop(0, count, lags, 0)


def early(pos, windows, gated, mixed, seg):
    width = gated[0].shape[1]
    rows = seg // 2
    mid = windows.shape[0] // 2

    def window(index):
        return pl.BlockSpec((1, rows, width), lambda i, pos: (index(pos[0]), i, 0))

    group = pl.BlockSpec((rows, width), lambda i, pos: (i, 0))
    return pl.pallas_call(
        early_kernel,
        grid_spec=pltpu.PrefetchScalarGridSpec(
            num_scalar_prefetch=1,
            grid=(4,),
            in_specs=[
                window(lambda p: mid),
                window(lambda p: mid + 1),
                window(lambda p: mid - 1),
                window(lambda p: jnp.where(p < 2, mid - 2, mid + 2)),
            ]
            + [group] * 7,
            out_specs=pl.BlockSpec((4, rows, width), lambda i, pos: (0, i, 0)),
        ),
        out_shape=f32(4, 2 * seg, width),
        compiler_params=params(14),
        cost_estimate=cost(200 * seg * width, 120 * seg * width),
        name="early",
    )(pos, *[windows] * 4, *gated, *mixed)


def late_kernel(
    pos_ref, inverse_ref, acc_ref, win_ref, three_g, two_g, own_m, left_m, right_m, *rest
):
    two_m, gated_ref, mixed_ref, skip_ref, up_ref, query_out, filter_out, back_out, x_high, x_low, z_ref = rest
    group = pl.program_id(0)
    pos, sign = pos_ref[0], group_sign()
    rows, width = own_m.shape
    sub = rows // 2

    def put(at, slot, value):
        for rows_at, part in zip(at, value):
            high, low = split(part)
            x_high[rows_at, slot * width : (slot + 1) * width] = high
            x_low[rows_at, slot * width : (slot + 1) * width] = low

    for where, distances in enumerate(PAIRS):

        @pl.when(pos == where)
        def _():
            def lags(tile, _):
                re, im, read = tile_reader(tile, sub)

                gated = [None, None, None, functools.partial(read, two_g), functools.partial(read, three_g)]
                mixed = [functools.partial(read, ref) for ref in (own_m, left_m, right_m, two_m)]
                total = [read(acc_ref, slot) for slot in range(4)]
                if where in (0, 3):
                    total[0] = add(total[0], mul(read(win_ref, 0), gated[THREE]()))
                else:
                    total[1] = add(total[1], conj_mul(read(win_ref, 0), mixed[TWO]()))
                for slot, value in enumerate(pair_sums(distances, gated, mixed, sign, True)):
                    if value is not None:
                        total[2 + slot] = add(total[2 + slot], value)
                for slot, value in enumerate(total):
                    put((re, im), slot, value)
                return _

            lax.fori_loop(0, sub // TILE, lags, 0)

    dot = functools.partial(jnp.dot, preferred_element_type=jnp.float32)
    t_high, t_low = inverse_ref[0, 0], inverse_ref[1, 0]
    for slot in range(4):
        cols = slice(slot * width, (slot + 1) * width)
        z_ref[group, :, cols] = (
            dot(t_high, x_high[:, cols]) + dot(t_high, x_low[:, cols]) + dot(t_low, x_high[:, cols])
        )

    @pl.when(group == 3)
    def _():
        seg = 4 * sub
        for slot in range(4):
            cols = slice(slot * width, (slot + 1) * width)
            quarters = gather_quarters(
                [z_ref[g, :sub, cols] for g in range(4)], [z_ref[g, sub:, cols] for g in range(4)]
            )
            for i, quarter in enumerate(quarters):
                at = slice(i * sub, (i + 1) * sub)
                if slot == 0:
                    query_out[at, :] = up_ref[at, :] * (quarter + skip_ref[...] * gated_ref[at, :])
                elif slot == 1:
                    back_out[at, :] = quarter + skip_ref[...] * mixed_ref[at, :]
                else:
                    base = (slot - 2) * seg + i * sub
                    filter_out[base : base + sub, :] = quarter


def late(pos, inverse, acc, windows, three_g, two_g, own_m, left_m, right_m, two_m, gated, mixed, skip, upstream):
    seg, width = upstream.shape
    rows = seg // 2
    mid = windows.shape[0] // 2

    def win_at(i, pos):
        p = pos[0]
        ends = jnp.where(p == 0, mid - 3, mid + 3)
        return jnp.where(p == 1, mid + 2, jnp.where(p == 2, mid - 2, ends)), i, 0

    group = pl.BlockSpec((rows, width), lambda i, pos: (i, 0))
    return pl.pallas_call(
        late_kernel,
        grid_spec=pltpu.PrefetchScalarGridSpec(
            num_scalar_prefetch=1,
            grid=(4,),
            in_specs=[
                pl.BlockSpec((2, 1, rows, rows), lambda i, pos: (0, i, 0, 0)),
                pl.BlockSpec((4, rows, width), lambda i, pos: (0, i, 0)),
                pl.BlockSpec((1, rows, width), win_at),
                *[group] * 6,
                whole_spec((seg, width)),
                whole_spec((seg, width)),
                whole_spec((1, width)),
                whole_spec((seg, width)),
            ],
            out_specs=[whole_spec((seg, width)), whole_spec((2 * seg, width)), whole_spec((seg, width))],
            scratch_shapes=[
                pltpu.VMEM((rows, 4 * width), jnp.bfloat16),
                pltpu.VMEM((rows, 4 * width), jnp.bfloat16),
                pltpu.VMEM((4, rows, 4 * width), jnp.float32),
            ],
        ),
        out_shape=[f32(seg, width), f32(2 * seg, width), f32(seg, width)],
        compiler_params=params(20),
        cost_estimate=cost(12 * seg * seg * width * 2, 100 * seg * width),
        name="late",
    )(pos, inverse, acc, windows, three_g, two_g, own_m, left_m, right_m, two_m, gated, mixed, skip, upstream)


def finish_kernel(
    pos_ref, back_ref, key_ref, values_ref, partial_ref, own_strip, left_strip, right_strip, two_strip,
    key_out, value_out, skip_out,
):
    pos = pos_ref[0]
    seg = back_ref.shape[0]
    back = back_ref[...] + partial_ref[:seg, :]
    key_out[...] = back * values_ref[...]
    value_out[...] = back * key_ref[...]
    far = jnp.where(pos < 2, pos + 2, pos - 2)
    strips = (
        (own_strip[...], pos),
        (left_strip[...], pos - 1),
        (right_strip[...], pos + 1),
        (two_strip[...] + partial_ref[seg : seg + 8, :], far),
        (partial_ref[seg + 8 :, :], 3 - pos),
    )
    total = None
    for block in range(4):
        value = jnp.zeros_like(own_strip[...])
        for where, (strip, source) in enumerate(strips):
            hit = source == block
            if where == THREE:
                hit = jnp.logical_and(hit, jnp.logical_or(pos == 0, pos == 3))
            value = value + jnp.where(hit, strip, 0.0)
        total = value if total is None else total + value
    skip_out[...] = jnp.sum(total, axis=0, keepdims=True)


def finish(pos, back, key_gate, values, partial, mixed, left_x, right_x, two_x):
    seg, width = back.shape
    block = whole_spec((seg, width))
    return pl.pallas_call(
        finish_kernel,
        grid_spec=pltpu.PrefetchScalarGridSpec(
            num_scalar_prefetch=1,
            grid=(1,),
            in_specs=[block] * 3 + [whole_spec(partial.shape)] + [strip_spec(seg, width)] * 4,
            out_specs=[block, block, whole_spec((1, width))],
        ),
        out_shape=[f32(seg, width), f32(seg, width), f32(1, width)],
        compiler_params=params(12),
        cost_estimate=cost(3 * seg * width, 24 * seg * width),
        name="finish",
    )(pos, back, key_gate, values, partial, mixed, left_x, right_x, two_x)


def send(x, *pairs):
    return lax.ppermute(x, "ctx", list(pairs))


def to_right(x):
    return send(x, (0, 1), (1, 2), (2, 3))


def to_left(x):
    return send(x, (1, 0), (2, 1), (3, 2))


def local_line(query_gate, key_gate, values, filter_taps, skip_gain, upstream):
    seg, width = values.shape
    forward_np, inverse_np = tables(seg)
    table, inverse = jnp.asarray(forward_np), jnp.asarray(inverse_np)
    position = lax.axis_index("ctx")
    pos = position.astype(jnp.int32).reshape(1)
    after = lax.optimization_barrier

    gated = key_gate * values
    left, right = to_right(gated), to_left(gated)
    mixed = mix(gated, upstream, query_gate)
    left_x, right_x = to_right(mixed), to_left(mixed)
    own_g, own_m = dft(table, seg, gated), dft(table, seg, mixed)
    left, right, filter_taps, own_g, own_m = after((left, right, filter_taps, own_g, own_m))

    two = send(left, (1, 2), (2, 3)), send(right, (2, 1), (1, 0))
    left_g, right_g = dft(table, seg, left), dft(table, seg, right)
    windows = taps_spectra(table, filter_taps, seg)
    left_x, right_x, windows, left_g, right_g = after((left_x, right_x, windows, left_g, right_g))

    two_x = send(jnp.where(position == 1, left_x, right_x), (1, 2), (2, 1))
    left_m, right_m = dft(table, seg, left_x), dft(table, seg, right_x)
    *two, left_m, right_m = after((*two, left_m, right_m))

    three = send(two[0], (2, 3)), send(two[1], (1, 0))
    two_m, partial = back_partial(pos, table, inverse, windows, left_m, right_m, left_x, right_x, two_x, seg)
    *two, partial = after((*two, partial))
    partial = send(partial, (1, 0), (2, 3))
    two_g = dft(table, seg, *two)
    acc = early(pos, windows, (own_g, left_g, right_g, two_g), (own_m, left_m, right_m), seg)
    *three, acc = after((*three, acc))

    three_g = dft(table, seg, *three)
    query_grad, filter_grad, back = late(
        pos, inverse, acc, windows, three_g, two_g, own_m, left_m, right_m, two_m,
        gated, mixed, skip_gain[None, :], upstream,
    )
    key_grad, value_grad, skip_grad = finish(
        pos, back, key_gate, values, partial, mixed, left_x, right_x, two_x
    )
    return (query_grad, key_grad, value_grad, filter_grad, skip_grad[0])


def matmul(left, right):
    return jnp.dot(left, right, preferred_element_type=jnp.float32, precision=lax.Precision.HIGHEST)


def forward_table(seg_len, count, offset):
    num_bins = seg_len + 1
    period = 2 * seg_len
    bin_index = lax.broadcasted_iota(jnp.int32, (num_bins, count), 0)
    pos_index = lax.broadcasted_iota(jnp.int32, (num_bins, count), 1) + offset
    angles = (bin_index * pos_index % period).astype(jnp.float32) * (2.0 * math.pi / period)
    return jnp.concatenate([jnp.cos(angles), -jnp.sin(angles)], axis=0)


def inverse_table(seg_len, count, offset):
    num_bins = seg_len + 1
    period = 2 * seg_len
    pos_index = lax.broadcasted_iota(jnp.int32, (count, num_bins), 0) + offset
    bin_index = lax.broadcasted_iota(jnp.int32, (count, num_bins), 1)
    angles = (bin_index * pos_index % period).astype(jnp.float32) * (2.0 * math.pi / period)
    weights = jnp.where((bin_index == 0) | (bin_index == seg_len), 1.0, 2.0) / period
    return jnp.concatenate([weights * jnp.cos(angles), -weights * jnp.sin(angles)], axis=1)


def times_spec(first, second):
    num_bins = first.shape[0] // 2
    real_a, imag_a = (first[:num_bins], first[num_bins:])
    real_b, imag_b = (second[:num_bins], second[num_bins:])
    return jnp.concatenate(
        [real_a * real_b - imag_a * imag_b, real_a * imag_b + imag_a * real_b], axis=0
    )


def conj_times(first, second):
    num_bins = first.shape[0] // 2
    real_a, imag_a = (first[:num_bins], first[num_bins:])
    real_b, imag_b = (second[:num_bins], second[num_bins:])
    return jnp.concatenate(
        [real_a * real_b + imag_a * imag_b, real_a * imag_b - imag_a * real_b], axis=0
    )


def pick(stack, index):
    return lax.dynamic_index_in_dim(stack, index, 0, keepdims=False)


def local(query_gate, key_gate, values, filter_taps, skip_gain, upstream):
    seg_len, width_dev = values.shape
    cycle_size = lax.axis_size("ctx")
    position = lax.axis_index("ctx")
    history = seg_len * cycle_size
    gated = key_gate * values
    mixed_grad = upstream * query_gate
    table_low = forward_table(seg_len, seg_len, 0)
    table_high = forward_table(seg_len, seg_len, seg_len)
    table_taps = forward_table(seg_len, 2 * seg_len, 0)
    back_low = inverse_table(seg_len, seg_len, 0)
    back_high = inverse_table(seg_len, seg_len, seg_len)
    back_full = inverse_table(seg_len, 2 * seg_len, 0)
    own_grad_spec = matmul(table_high, mixed_grad)
    spec_rows = 2 * (seg_len + 1)

    def taps_spec(lag_block):
        start_row = (lag_block - 1) * seg_len + history
        window = lax.dynamic_slice_in_dim(filter_taps, start_row, 2 * seg_len, 0)
        return matmul(table_taps, window)

    def visit(carry, gated_spec, grad_spec, source):
        acc_conv, acc_back, partial_value = carry
        lag_block = position - source
        acc_conv = acc_conv + times_spec(taps_spec(lag_block), gated_spec)
        acc_back = acc_back + conj_times(taps_spec(-lag_block), grad_spec)
        segment = matmul(back_full, conj_times(gated_spec, own_grad_spec))
        start_row = (lag_block - 1) * seg_len + history
        current = lax.dynamic_slice_in_dim(partial_value, start_row, 2 * seg_len, 0)
        partial_value = lax.dynamic_update_slice_in_dim(
            partial_value, current + segment, start_row, 0
        )
        return (acc_conv, acc_back, partial_value)

    initial = (
        jnp.zeros((spec_rows, width_dev), jnp.float32),
        jnp.zeros((spec_rows, width_dev), jnp.float32),
        jnp.zeros((2 * history, width_dev), jnp.float32),
    )
    own_gated_spec = matmul(table_low, gated)
    pieces = (
        lax.all_gather(own_gated_spec[None], "ctx", axis=0, tiled=True),
        lax.all_gather(own_grad_spec[None], "ctx", axis=0, tiled=True),
    )

    def advance(member, state):
        return visit(state, pick(pieces[0], member), pick(pieces[1], member), member)

    folded = lax.fori_loop(0, pieces[0].shape[0], advance, initial)
    acc_conv, acc_back, partial_value = folded
    filter_grad = lax.psum_scatter(partial_value, "ctx", scatter_dimension=0, tiled=True)
    conv = matmul(back_high, acc_conv)
    back = matmul(back_low, acc_back) + skip_gain[None, :] * mixed_grad
    query_grad = upstream * (conv + skip_gain[None, :] * gated)
    key_grad = back * values
    value_grad = back * key_gate
    skip_grad = lax.psum(jnp.sum(mixed_grad * gated, axis=0), "ctx")
    return (query_grad, key_grad, value_grad, filter_grad, skip_grad)


def solution(mesh):
    in_specs = (
        P(("groups", "ctx"), "chan"),
        P(("groups", "ctx"), "chan"),
        P(("groups", "ctx"), "chan"),
        P(None, "chan"),
        P("chan"),
        P(("groups", "ctx"), "chan"),
    )
    out_specs = (
        P(("groups", "ctx"), "chan"),
        P(("groups", "ctx"), "chan"),
        P(("groups", "ctx"), "chan"),
        P(("groups", "ctx"), "chan"),
        P(("groups", "chan")),
    )
    body = local_line if mesh.shape["ctx"] == 4 else local
    return jax.shard_map(body, mesh=mesh, in_specs=in_specs, out_specs=out_specs, check_vma=False)
```

```python
import functools
import math

import jax
import jax.numpy as jnp
import ml_dtypes
import numpy as np
from jax import lax
from jax.experimental import pallas as pl
from jax.experimental.pallas import tpu as pltpu
from jax.sharding import PartitionSpec as P

COS1, SIN1, HALF = math.cos(math.pi / 8), math.sin(math.pi / 8), math.sqrt(0.5)


def split_np(table):
    high = table.astype(ml_dtypes.bfloat16)
    low = (table - high.astype(np.float64)).astype(ml_dtypes.bfloat16)
    return np.stack([high, low])


def tables(seg):
    sub = seg // 4
    bins, pos = np.arange(sub)[:, None], np.arange(sub)[None, :]
    forward = []
    for group in range(4):
        angle = 2 * np.pi * pos * (8 * bins + group + 0.5) / (2 * seg)
        cos, sin = np.cos(angle), np.sin(angle)
        forward.append(np.block([[cos, -sin], [-sin, -cos]]))
    forward = np.stack(forward)
    inverse = forward.transpose(0, 2, 1) / seg
    return split_np(forward), split_np(inverse)


def split(x):
    high = x.astype(jnp.bfloat16)
    return high, (x - high.astype(jnp.float32)).astype(jnp.bfloat16)


def dot3(table_ref, group, high, low):
    t_high, t_low = table_ref[0, group], table_ref[1, group]
    dot = functools.partial(jnp.dot, preferred_element_type=jnp.float32)
    return dot(t_high, high) + dot(t_high, low) + dot(t_low, high)


def spread(x):
    sub = x.shape[0] // 4
    x0, x1, x2, x3 = (x[i * sub : (i + 1) * sub] for i in range(4))
    u, p, s, q, t = HALF * x2, COS1 * x1, SIN1 * x1, COS1 * x3, SIN1 * x3
    a, b, pt, sq, pmt, spq = x0 + u, x0 - u, p + t, s - q, p - t, s + q
    pairs = ((a + pt, spq + u), (b + sq, pmt + u), (b - sq, pmt - u), (a - pt, spq - u))
    return [jnp.concatenate(pair, axis=0) for pair in pairs]


def gather_quarters(re, im):
    e03, d03, e12, d12 = re[0] + re[3], re[0] - re[3], re[1] + re[2], re[1] - re[2]
    f03, g03, f12, g12 = im[0] + im[3], im[0] - im[3], im[1] + im[2], im[1] - im[2]
    return (
        e03 + e12,
        COS1 * (d03 + f12) + SIN1 * (d12 + f03),
        HALF * (e03 - e12 + g03 + g12),
        SIN1 * (d03 - f12) + COS1 * (f03 - d12),
    )


def transform(x, table_ref, store):
    for group, part in enumerate(spread(x)):
        store(group, dot3(table_ref, group, *split(part)))


def cost(flops, nbytes):
    return pl.CostEstimate(flops=int(flops), bytes_accessed=int(nbytes), transcendentals=0)


def params(mib):
    return pltpu.CompilerParams(vmem_limit_bytes=mib << 20)


def whole_spec(shape):
    return pl.BlockSpec(shape, lambda *_: (0,) * len(shape))


def f32(*shape):
    return jax.ShapeDtypeStruct(shape, jnp.float32)


def mix_kernel(gated_ref, up_ref, query_ref, mixed_ref):
    seg, width = gated_ref.shape
    mixed = up_ref[...] * query_ref[...]
    mixed_ref[:seg, :] = mixed
    mixed_ref[seg:, :] = jnp.sum((gated_ref[...] * mixed).reshape(seg // 8, 8, width), axis=0)


def mix(gated, upstream, query_gate):
    seg, width = gated.shape
    return pl.pallas_call(
        mix_kernel,
        grid=(1,),
        in_specs=[whole_spec((seg, width))] * 3,
        out_specs=whole_spec((seg + 8, width)),
        out_shape=f32(seg + 8, width),
        compiler_params=params(12),
        cost_estimate=cost(4 * seg * width, 16 * seg * width),
        name="mix",
    )(gated, upstream, query_gate)


def strip_spec(seg, width):
    return pl.BlockSpec((8, width), lambda *_: (seg // 8, 0))


def dft_kernel(table_ref, *refs):
    *x_refs, out_ref = refs
    rows = out_ref.shape[0] // 4

    def store(group, value):
        out_ref[group * rows : (group + 1) * rows, :] = value

    x = x_refs[0][...]
    for ref in x_refs[1:]:
        x = x + ref[...]
    transform(x, table_ref, store)


def dft(table, seg, *xs):
    width = xs[0].shape[1]
    return pl.pallas_call(
        dft_kernel,
        grid=(1,),
        in_specs=[whole_spec(table.shape)] + [whole_spec((seg, x.shape[1])) for x in xs],
        out_specs=whole_spec((2 * seg, width)),
        out_shape=f32(2 * seg, width),
        compiler_params=params(12),
        cost_estimate=cost(3 * seg * seg * width * 2, 12 * seg * width),
        name="dft",
    )(table, *xs)


def taps_kernel(table_ref, x_ref, out_ref, last_ref):
    step = pl.program_id(0)
    rows = out_ref.shape[1] // 4
    sub = rows // 2

    def store(group, value):
        base = group * rows
        sign = 1.0 if group % 2 == 0 else -1.0
        re, im = slice(base, base + sub), slice(base + sub, base + rows)
        out_ref[0, re, :] = value[:sub] - sign * last_ref[im, :]
        out_ref[0, im, :] = value[sub:] + sign * last_ref[re, :]
        last_ref[base : base + rows, :] = value

    @pl.when(step == 0)
    def _():
        last_ref[...] = jnp.zeros_like(last_ref)

    transform(x_ref[...], table_ref, store)


def taps_spectra(table, taps, seg):
    width = taps.shape[1]
    blocks = taps.shape[0] // seg
    return pl.pallas_call(
        taps_kernel,
        grid=(blocks,),
        in_specs=[whole_spec(table.shape), pl.BlockSpec((seg, width), lambda i: (i, 0))],
        out_specs=pl.BlockSpec((1, 2 * seg, width), lambda i: (jnp.maximum(i - 1, 0), 0, 0)),
        out_shape=jax.ShapeDtypeStruct((blocks - 1, 2 * seg, width), jnp.float32),
        scratch_shapes=[pltpu.VMEM((2 * seg, width), jnp.float32)],
        compiler_params=params(14),
        cost_estimate=cost(blocks * 3 * seg * seg * width * 2, blocks * 12 * seg * width),
        name="taps",
    )(table, taps)


def conj_mul(a, b):
    return a[0] * b[0] + a[1] * b[1], a[0] * b[1] - a[1] * b[0]


def mul(a, b):
    return a[0] * b[0] - a[1] * b[1], a[0] * b[1] + a[1] * b[0]


def add(a, b):
    return a[0] + b[0], a[1] + b[1]


def partial_kernel(
    pos_ref, table_ref, inverse_ref, win_near, win_far, next_ref, x_ref, next_strip, far_strip, far_ref, out_ref, z_ref
):
    rows = far_ref.shape[0] // 4
    sub = rows // 2
    for group, part in enumerate(spread(x_ref[...])):
        base = group * rows
        far = dot3(table_ref, group, *split(part))
        far_ref[base : base + rows, :] = far
        re, im = slice(base, base + sub), slice(base + sub, base + rows)
        near = (next_ref[re, :], next_ref[im, :])
        total = add(
            conj_mul((win_near[0, re, :], win_near[0, im, :]), near),
            conj_mul((win_far[0, re, :], win_far[0, im, :]), (far[:sub], far[sub:])),
        )
        z_ref[group] = dot3(inverse_ref, group, *split(jnp.concatenate(total, axis=0)))
    quarters = gather_quarters([z_ref[g, :sub] for g in range(4)], [z_ref[g, sub:] for g in range(4)])
    for i, quarter in enumerate(quarters):
        out_ref[i * sub : (i + 1) * sub, :] = quarter
    out_ref[4 * sub : 4 * sub + 8, :] = next_strip[...]
    out_ref[4 * sub + 8 :, :] = far_strip[...]


def back_partial(pos, table, inverse, windows, next_m, next_x, x, seg):
    width = x.shape[1]
    n = (windows.shape[0] + 1) // 2

    def window(distance):
        return pl.BlockSpec(
            (1, 2 * seg, width),
            lambda i, pos: (jnp.where(pos[0] == 1, n - 1 + distance, n - 1 - distance), 0, 0),
        )

    return pl.pallas_call(
        partial_kernel,
        grid_spec=pltpu.PrefetchScalarGridSpec(
            num_scalar_prefetch=1,
            grid=(1,),
            in_specs=[
                whole_spec(table.shape),
                whole_spec(inverse.shape),
                window(2),
                window(3),
                whole_spec((2 * seg, width)),
                whole_spec((seg, width)),
                *[strip_spec(seg, width)] * 2,
            ],
            out_specs=[whole_spec((2 * seg, width)), whole_spec((seg + 16, width))],
            scratch_shapes=[pltpu.VMEM((4, seg // 2, width), jnp.float32)],
        ),
        out_shape=[f32(2 * seg, width), f32(seg + 16, width)],
        compiler_params=params(24),
        cost_estimate=cost(6 * seg * seg * width * 2, 24 * seg * width),
        name="partial",
    )(pos, table, inverse, windows, windows, next_m, x, next_x, x)


OWN, OUTER, NEXT, TWO, THREE = range(5)
PAIRS = (
    ((), ((OWN, THREE),), ((OWN, TWO), (NEXT, THREE))),
    (
        ((OUTER, NEXT), (OWN, TWO)),
        ((OUTER, OWN), (OWN, NEXT), (NEXT, TWO)),
        ((OUTER, OUTER), (OWN, OWN), (NEXT, NEXT), (TWO, TWO)),
    ),
    (
        ((TWO, TWO), (NEXT, NEXT), (OWN, OWN), (OUTER, OUTER)),
        ((NEXT, TWO), (OWN, NEXT), (OUTER, OWN)),
        ((OWN, TWO), (OUTER, NEXT)),
    ),
    (((NEXT, THREE), (OWN, TWO)), ((OWN, THREE),), ()),
)


def is_late(pair):
    return pair[0] == TWO or pair[1] == THREE


def pair_sums(distances, gated, mixed, sign, late):
    total = []
    for pairs in distances:
        value = None
        for m, g in pairs:
            if is_late((m, g)) == late:
                term = conj_mul(gated[g](), mixed[m]())
                value = term if value is None else add(value, term)
        total.append(value)
    out = []
    for low, high in zip(total[:2], total[1:]):
        if high is not None:
            turned = (sign * high[1], -sign * high[0])
            low = turned if low is None else add(low, turned)
        out.append(low)
    return out


TILE = 16


def tile_reader(tile, sub):
    re = pl.ds(pl.multiple_of(tile * TILE, TILE), TILE)
    im = pl.ds(pl.multiple_of(sub + tile * TILE, TILE), TILE)

    def read(ref, *lead):
        return ref[(*lead, re, slice(None))], ref[(*lead, im, slice(None))]

    return re, im, read


def group_sign():
    return jnp.where(pl.program_id(0) % 2 == 0, 1.0, -1.0)


def early_kernel(
    pos_ref, win_own, win_outer, win_next, win_two, own_g, outer_g, next_g, two_g, own_m, outer_m, next_m, out_ref
):
    pos, sign = pos_ref[0], group_sign()
    rows = own_g.shape[0]
    sub = rows // 2
    count = sub // TILE

    def put(at, slot, value):
        re, im = at
        out_ref[slot, re, :] = value[0]
        out_ref[slot, im, :] = value[1]

    def sums(tile, _):
        re, im, read = tile_reader(tile, sub)
        own, outer, ahead = read(win_own, 0), read(win_outer, 0), read(win_next, 0)
        conv = add(mul(own, read(own_g)), mul(outer, read(outer_g)))
        conv = add(conv, add(mul(ahead, read(next_g)), mul(read(win_two, 0), read(two_g))))
        put((re, im), 0, conv)
        back = add(conj_mul(own, read(own_m)), conj_mul(ahead, read(outer_m)))
        put((re, im), 1, add(back, conj_mul(outer, read(next_m))))
        return _

    lax.fori_loop(0, count, sums, 0)
    for where, distances in enumerate(PAIRS):

        @pl.when(pos == where)
        def _():
            def lags(tile, _):
                re, im, read = tile_reader(tile, sub)
                gated = [functools.partial(read, ref) for ref in (own_g, outer_g, next_g, two_g)]
                mixed = [functools.partial(read, ref) for ref in (own_m, outer_m, next_m)]
                for slot, value in enumerate(pair_sums(distances, gated, mixed, sign, False)):
                    if value is None:
                        value = (jnp.zeros_like(own_g[re, :]),) * 2
                    put((re, im), 2 + slot, value)
                return _

            lax.fori_loop(0, count, lags, 0)


def early(pos, windows, gated, mixed, seg):
    width = gated[0].shape[1]
    rows = seg // 2
    mid = windows.shape[0] // 2

    def window(index):
        return pl.BlockSpec((1, rows, width), lambda i, pos: (index(pos[0]), i, 0))

    group = pl.BlockSpec((rows, width), lambda i, pos: (i, 0))
    return pl.pallas_call(
        early_kernel,
        grid_spec=pltpu.PrefetchScalarGridSpec(
            num_scalar_prefetch=1,
            grid=(4,),
            in_specs=[
                window(lambda p: mid),
                window(lambda p: jnp.where(p < 2, mid + 1, mid - 1)),
                window(lambda p: jnp.where(p < 2, mid - 1, mid + 1)),
                window(lambda p: jnp.where(p < 2, mid - 2, mid + 2)),
            ]
            + [group] * 7,
            out_specs=pl.BlockSpec((4, rows, width), lambda i, pos: (0, i, 0)),
        ),
        out_shape=f32(4, 2 * seg, width),
        compiler_params=params(14),
        cost_estimate=cost(200 * seg * width, 120 * seg * width),
        name="early",
    )(pos, *[windows] * 4, *gated, *mixed)


def late_kernel(
    pos_ref, inverse_ref, acc_ref, win_ref, three_g, two_g, own_m, outer_m, next_m, *rest
):
    two_m, gated_ref, mixed_ref, skip_ref, up_ref, query_out, filter_out, back_out, x_high, x_low, z_ref = rest
    group = pl.program_id(0)
    pos, sign = pos_ref[0], group_sign()
    rows, width = own_m.shape
    sub = rows // 2

    def put(at, slot, value):
        for rows_at, part in zip(at, value):
            high, low = split(part)
            x_high[rows_at, slot * width : (slot + 1) * width] = high
            x_low[rows_at, slot * width : (slot + 1) * width] = low

    for where, distances in enumerate(PAIRS):

        @pl.when(pos == where)
        def _():
            def lags(tile, _):
                re, im, read = tile_reader(tile, sub)

                gated = [None, None, None, functools.partial(read, two_g), functools.partial(read, three_g)]
                mixed = [functools.partial(read, ref) for ref in (own_m, outer_m, next_m, two_m)]
                total = [read(acc_ref, slot) for slot in range(4)]
                if where in (0, 3):
                    total[0] = add(total[0], mul(read(win_ref, 0), gated[THREE]()))
                else:
                    total[1] = add(total[1], conj_mul(read(win_ref, 0), mixed[TWO]()))
                for slot, value in enumerate(pair_sums(distances, gated, mixed, sign, True)):
                    if value is not None:
                        total[2 + slot] = add(total[2 + slot], value)
                for slot, value in enumerate(total):
                    put((re, im), slot, value)
                return _

            lax.fori_loop(0, sub // TILE, lags, 0)

    dot = functools.partial(jnp.dot, preferred_element_type=jnp.float32)
    t_high, t_low = inverse_ref[0, 0], inverse_ref[1, 0]
    for slot in range(4):
        cols = slice(slot * width, (slot + 1) * width)
        z_ref[group, :, cols] = (
            dot(t_high, x_high[:, cols]) + dot(t_high, x_low[:, cols]) + dot(t_low, x_high[:, cols])
        )

    @pl.when(group == 3)
    def _():
        seg = 4 * sub
        for slot in range(4):
            cols = slice(slot * width, (slot + 1) * width)
            quarters = gather_quarters(
                [z_ref[g, :sub, cols] for g in range(4)], [z_ref[g, sub:, cols] for g in range(4)]
            )
            for i, quarter in enumerate(quarters):
                at = slice(i * sub, (i + 1) * sub)
                if slot == 0:
                    query_out[at, :] = up_ref[at, :] * (quarter + skip_ref[...] * gated_ref[at, :])
                elif slot == 1:
                    back_out[at, :] = quarter + skip_ref[...] * mixed_ref[at, :]
                else:
                    base = (slot - 2) * seg + i * sub
                    filter_out[base : base + sub, :] = quarter


def late(pos, inverse, acc, windows, three_g, two_g, own_m, outer_m, next_m, two_m, gated, mixed, skip, upstream):
    seg, width = upstream.shape
    rows = seg // 2
    mid = windows.shape[0] // 2

    def win_at(i, pos):
        p = pos[0]
        ends = jnp.where(p == 0, mid - 3, mid + 3)
        return jnp.where(p == 1, mid + 2, jnp.where(p == 2, mid - 2, ends)), i, 0

    group = pl.BlockSpec((rows, width), lambda i, pos: (i, 0))
    return pl.pallas_call(
        late_kernel,
        grid_spec=pltpu.PrefetchScalarGridSpec(
            num_scalar_prefetch=1,
            grid=(4,),
            in_specs=[
                pl.BlockSpec((2, 1, rows, rows), lambda i, pos: (0, i, 0, 0)),
                pl.BlockSpec((4, rows, width), lambda i, pos: (0, i, 0)),
                pl.BlockSpec((1, rows, width), win_at),
                *[group] * 6,
                whole_spec((seg, width)),
                whole_spec((seg, width)),
                whole_spec((1, width)),
                whole_spec((seg, width)),
            ],
            out_specs=[whole_spec((seg, width)), whole_spec((2 * seg, width)), whole_spec((seg, width))],
            scratch_shapes=[
                pltpu.VMEM((rows, 4 * width), jnp.bfloat16),
                pltpu.VMEM((rows, 4 * width), jnp.bfloat16),
                pltpu.VMEM((4, rows, 4 * width), jnp.float32),
            ],
        ),
        out_shape=[f32(seg, width), f32(2 * seg, width), f32(seg, width)],
        compiler_params=params(20),
        cost_estimate=cost(12 * seg * seg * width * 2, 100 * seg * width),
        name="late",
    )(pos, inverse, acc, windows, three_g, two_g, own_m, outer_m, next_m, two_m, gated, mixed, skip, upstream)


def finish_kernel(
    pos_ref, back_ref, key_ref, values_ref, partial_ref, own_strip, outer_strip, out_strip, across_strip, two_strip,
    key_out, value_out, skip_out,
):
    pos = pos_ref[0]
    seg = back_ref.shape[0]
    back = back_ref[...] + partial_ref[:seg, :]
    key_out[...] = back * values_ref[...]
    value_out[...] = back * key_ref[...]
    far = jnp.where(pos < 2, pos + 2, pos - 2)
    strips = (
        (own_strip[...], pos),
        (outer_strip[...], jnp.where(pos < 2, 0, 3)),
        (out_strip[...] + across_strip[...], jnp.where(pos < 2, pos + 1, pos - 1)),
        (two_strip[...] + partial_ref[seg : seg + 8, :], far),
        (partial_ref[seg + 8 :, :], 3 - pos),
    )
    total = None
    for block in range(4):
        value = jnp.zeros_like(own_strip[...])
        for strip, source in strips:
            value = value + jnp.where(source == block, strip, 0.0)
        total = value if total is None else total + value
    skip_out[...] = jnp.sum(total, axis=0, keepdims=True)


def finish(pos, back, key_gate, values, partial, *mixed):
    seg, width = back.shape
    block = whole_spec((seg, width))
    return pl.pallas_call(
        finish_kernel,
        grid_spec=pltpu.PrefetchScalarGridSpec(
            num_scalar_prefetch=1,
            grid=(1,),
            in_specs=[block] * 3 + [whole_spec(partial.shape)] + [strip_spec(seg, width)] * len(mixed),
            out_specs=[block, block, whole_spec((1, width))],
        ),
        out_shape=[f32(seg, width), f32(seg, width), f32(1, width)],
        compiler_params=params(12),
        cost_estimate=cost(3 * seg * width, 24 * seg * width),
        name="finish",
    )(pos, back, key_gate, values, partial, *mixed)


def send(x, *pairs):
    return lax.ppermute(x, "ctx", list(pairs))


def across(x):
    return send(x, (1, 2), (2, 1))


def outward(x):
    return send(x, (1, 0), (2, 3))


def inward(x):
    return send(x, (0, 1), (3, 2))


def local_line(query_gate, key_gate, values, filter_taps, skip_gain, upstream):
    seg, width = values.shape
    forward_np, inverse_np = tables(seg)
    table, inverse = jnp.asarray(forward_np), jnp.asarray(inverse_np)
    pos = lax.axis_index("ctx").astype(jnp.int32).reshape(1)
    after = lax.optimization_barrier

    gated = key_gate * values
    outer = inward(gated)
    next_g = (outward(gated), across(gated))
    mixed = mix(gated, upstream, query_gate)
    outer_x = inward(mixed)
    next_x = (outward(mixed), across(mixed))
    own_g, own_m = dft(table, seg, gated), dft(table, seg, mixed)
    outer, *next_g, filter_taps, own_g, own_m = after((outer, *next_g, filter_taps, own_g, own_m))

    two = outward(next_g[1]), across(outer)
    outer_g, next_g = dft(table, seg, outer), dft(table, seg, *next_g)
    windows = taps_spectra(table, filter_taps, seg)
    outer_x, *next_x, windows, outer_g, next_g = after((outer_x, *next_x, windows, outer_g, next_g))

    two_x = across(outer_x)
    outer_m, next_m = dft(table, seg, outer_x), dft(table, seg, *next_x)
    *two, outer_m, next_m = after((*two, outer_m, next_m))

    three = outward(two[1])
    two_m, partial = back_partial(pos, table, inverse, windows, next_m, next_x[1], two_x, seg)
    *two, partial = after((*two, partial))
    partial = outward(partial)
    two_g = dft(table, seg, *two)
    acc = early(pos, windows, (own_g, outer_g, next_g, two_g), (own_m, outer_m, next_m), seg)
    three, acc = after((three, acc))

    three_g = dft(table, seg, three)
    query_grad, filter_grad, back = late(
        pos, inverse, acc, windows, three_g, two_g, own_m, outer_m, next_m, two_m,
        gated, mixed, skip_gain[None, :], upstream,
    )
    key_grad, value_grad, skip_grad = finish(
        pos, back, key_gate, values, partial, mixed, outer_x, *next_x, two_x
    )
    return (query_grad, key_grad, value_grad, filter_grad, skip_grad[0])


def matmul(left, right):
    return jnp.dot(left, right, preferred_element_type=jnp.float32, precision=lax.Precision.HIGHEST)


def forward_table(seg_len, count, offset):
    num_bins = seg_len + 1
    period = 2 * seg_len
    bin_index = lax.broadcasted_iota(jnp.int32, (num_bins, count), 0)
    pos_index = lax.broadcasted_iota(jnp.int32, (num_bins, count), 1) + offset
    angles = (bin_index * pos_index % period).astype(jnp.float32) * (2.0 * math.pi / period)
    return jnp.concatenate([jnp.cos(angles), -jnp.sin(angles)], axis=0)


def inverse_table(seg_len, count, offset):
    num_bins = seg_len + 1
    period = 2 * seg_len
    pos_index = lax.broadcasted_iota(jnp.int32, (count, num_bins), 0) + offset
    bin_index = lax.broadcasted_iota(jnp.int32, (count, num_bins), 1)
    angles = (bin_index * pos_index % period).astype(jnp.float32) * (2.0 * math.pi / period)
    weights = jnp.where((bin_index == 0) | (bin_index == seg_len), 1.0, 2.0) / period
    return jnp.concatenate([weights * jnp.cos(angles), -weights * jnp.sin(angles)], axis=1)


def times_spec(first, second):
    num_bins = first.shape[0] // 2
    real_a, imag_a = (first[:num_bins], first[num_bins:])
    real_b, imag_b = (second[:num_bins], second[num_bins:])
    return jnp.concatenate(
        [real_a * real_b - imag_a * imag_b, real_a * imag_b + imag_a * real_b], axis=0
    )


def conj_times(first, second):
    num_bins = first.shape[0] // 2
    real_a, imag_a = (first[:num_bins], first[num_bins:])
    real_b, imag_b = (second[:num_bins], second[num_bins:])
    return jnp.concatenate(
        [real_a * real_b + imag_a * imag_b, real_a * imag_b - imag_a * real_b], axis=0
    )


def pick(stack, index):
    return lax.dynamic_index_in_dim(stack, index, 0, keepdims=False)


def local(query_gate, key_gate, values, filter_taps, skip_gain, upstream):
    seg_len, width_dev = values.shape
    cycle_size = lax.axis_size("ctx")
    position = lax.axis_index("ctx")
    history = seg_len * cycle_size
    gated = key_gate * values
    mixed_grad = upstream * query_gate
    table_low = forward_table(seg_len, seg_len, 0)
    table_high = forward_table(seg_len, seg_len, seg_len)
    table_taps = forward_table(seg_len, 2 * seg_len, 0)
    back_low = inverse_table(seg_len, seg_len, 0)
    back_high = inverse_table(seg_len, seg_len, seg_len)
    back_full = inverse_table(seg_len, 2 * seg_len, 0)
    own_grad_spec = matmul(table_high, mixed_grad)
    spec_rows = 2 * (seg_len + 1)

    def taps_spec(lag_block):
        start_row = (lag_block - 1) * seg_len + history
        window = lax.dynamic_slice_in_dim(filter_taps, start_row, 2 * seg_len, 0)
        return matmul(table_taps, window)

    def visit(carry, gated_spec, grad_spec, source):
        acc_conv, acc_back, partial_value = carry
        lag_block = position - source
        acc_conv = acc_conv + times_spec(taps_spec(lag_block), gated_spec)
        acc_back = acc_back + conj_times(taps_spec(-lag_block), grad_spec)
        segment = matmul(back_full, conj_times(gated_spec, own_grad_spec))
        start_row = (lag_block - 1) * seg_len + history
        current = lax.dynamic_slice_in_dim(partial_value, start_row, 2 * seg_len, 0)
        partial_value = lax.dynamic_update_slice_in_dim(
            partial_value, current + segment, start_row, 0
        )
        return (acc_conv, acc_back, partial_value)

    initial = (
        jnp.zeros((spec_rows, width_dev), jnp.float32),
        jnp.zeros((spec_rows, width_dev), jnp.float32),
        jnp.zeros((2 * history, width_dev), jnp.float32),
    )
    own_gated_spec = matmul(table_low, gated)
    pieces = (
        lax.all_gather(own_gated_spec[None], "ctx", axis=0, tiled=True),
        lax.all_gather(own_grad_spec[None], "ctx", axis=0, tiled=True),
    )

    def advance(member, state):
        return visit(state, pick(pieces[0], member), pick(pieces[1], member), member)

    folded = lax.fori_loop(0, pieces[0].shape[0], advance, initial)
    acc_conv, acc_back, partial_value = folded
    filter_grad = lax.psum_scatter(partial_value, "ctx", scatter_dimension=0, tiled=True)
    conv = matmul(back_high, acc_conv)
    back = matmul(back_low, acc_back) + skip_gain[None, :] * mixed_grad
    query_grad = upstream * (conv + skip_gain[None, :] * gated)
    key_grad = back * values
    value_grad = back * key_gate
    skip_grad = lax.psum(jnp.sum(mixed_grad * gated, axis=0), "ctx")
    return (query_grad, key_grad, value_grad, filter_grad, skip_grad)


def solution(mesh):
    in_specs = (
        P(("groups", "ctx"), "chan"),
        P(("groups", "ctx"), "chan"),
        P(("groups", "ctx"), "chan"),
        P(None, "chan"),
        P("chan"),
        P(("groups", "ctx"), "chan"),
    )
    out_specs = (
        P(("groups", "ctx"), "chan"),
        P(("groups", "ctx"), "chan"),
        P(("groups", "ctx"), "chan"),
        P(("groups", "ctx"), "chan"),
        P(("groups", "chan")),
    )
    body = local_line if mesh.shape["ctx"] == 4 else local
    return jax.shard_map(body, mesh=mesh, in_specs=in_specs, out_specs=out_specs, check_vma=False)
```

```python
import functools
import math

import jax
import jax.numpy as jnp
import ml_dtypes
import numpy as np
from jax import lax
from jax.experimental import pallas as pl
from jax.experimental.pallas import tpu as pltpu
from jax.sharding import PartitionSpec as P

COS1, SIN1, HALF = math.cos(math.pi / 8), math.sin(math.pi / 8), math.sqrt(0.5)


def split_np(table):
    high = table.astype(ml_dtypes.bfloat16)
    low = (table - high.astype(np.float64)).astype(ml_dtypes.bfloat16)
    return np.stack([high, low])


def tables(seg):
    sub = seg // 4
    bins, pos = np.arange(sub)[:, None], np.arange(sub)[None, :]
    forward = []
    for group in range(4):
        angle = 2 * np.pi * pos * (8 * bins + group + 0.5) / (2 * seg)
        cos, sin = np.cos(angle), np.sin(angle)
        forward.append(np.block([[cos, -sin], [-sin, -cos]]))
    forward = np.stack(forward)
    inverse = forward.transpose(0, 2, 1) / seg
    return split_np(forward), split_np(inverse)


def split(x):
    high = x.astype(jnp.bfloat16)
    return high, (x - high.astype(jnp.float32)).astype(jnp.bfloat16)


def dot3(table_ref, group, high, low):
    t_high, t_low = table_ref[0, group], table_ref[1, group]
    dot = functools.partial(jnp.dot, preferred_element_type=jnp.float32)
    return dot(t_high, high) + dot(t_high, low) + dot(t_low, high)


def spread(x):
    sub = x.shape[0] // 4
    x0, x1, x2, x3 = (x[i * sub : (i + 1) * sub] for i in range(4))
    u, p, s, q, t = HALF * x2, COS1 * x1, SIN1 * x1, COS1 * x3, SIN1 * x3
    a, b, pt, sq, pmt, spq = x0 + u, x0 - u, p + t, s - q, p - t, s + q
    pairs = ((a + pt, spq + u), (b + sq, pmt + u), (b - sq, pmt - u), (a - pt, spq - u))
    return [jnp.concatenate(pair, axis=0) for pair in pairs]


def gather_quarters(re, im):
    e03, d03, e12, d12 = re[0] + re[3], re[0] - re[3], re[1] + re[2], re[1] - re[2]
    f03, g03, f12, g12 = im[0] + im[3], im[0] - im[3], im[1] + im[2], im[1] - im[2]
    return (
        e03 + e12,
        COS1 * (d03 + f12) + SIN1 * (d12 + f03),
        HALF * (e03 - e12 + g03 + g12),
        SIN1 * (d03 - f12) + COS1 * (f03 - d12),
    )


def transform(x, table_ref, store):
    for group, part in enumerate(spread(x)):
        store(group, dot3(table_ref, group, *split(part)))


def cost(flops, nbytes):
    return pl.CostEstimate(flops=int(flops), bytes_accessed=int(nbytes), transcendentals=0)


def params(mib):
    return pltpu.CompilerParams(vmem_limit_bytes=mib << 20)


def whole_spec(shape):
    return pl.BlockSpec(shape, lambda *_: (0,) * len(shape))


def f32(*shape):
    return jax.ShapeDtypeStruct(shape, jnp.float32)


def mix_kernel(gated_ref, up_ref, query_ref, mixed_ref):
    seg, width = gated_ref.shape
    mixed = up_ref[...] * query_ref[...]
    mixed_ref[:seg, :] = mixed
    mixed_ref[seg:, :] = jnp.sum((gated_ref[...] * mixed).reshape(seg // 8, 8, width), axis=0)


def mix(gated, upstream, query_gate):
    seg, width = gated.shape
    return pl.pallas_call(
        mix_kernel,
        grid=(1,),
        in_specs=[whole_spec((seg, width))] * 3,
        out_specs=whole_spec((seg + 8, width)),
        out_shape=f32(seg + 8, width),
        compiler_params=params(12),
        cost_estimate=cost(4 * seg * width, 16 * seg * width),
        name="mix",
    )(gated, upstream, query_gate)


def strip_spec(seg, width):
    return pl.BlockSpec((8, width), lambda *_: (seg // 8, 0))


def dft_kernel(choose, pos_ref, table_ref, *refs):
    *x_refs, out_ref = refs
    rows = out_ref.shape[0] // 4
    inner = jnp.logical_or(pos_ref[0] == 1, pos_ref[0] == 2)

    def store(group, value):
        out_ref[group * rows : (group + 1) * rows, :] = value

    x = x_refs[0][...]
    if choose:
        x = jnp.where(inner, x, x_refs[1][...] if len(x_refs) == 2 else 0.0)
    elif len(x_refs) == 2:
        x = x + x_refs[1][...]
    transform(x, table_ref, store)


def dft(pos, table, seg, *xs, choose=False):
    width = xs[0].shape[1]
    return pl.pallas_call(
        functools.partial(dft_kernel, choose),
        grid_spec=pltpu.PrefetchScalarGridSpec(
            num_scalar_prefetch=1,
            grid=(1,),
            in_specs=[whole_spec(table.shape)] + [whole_spec((seg, width))] * len(xs),
            out_specs=whole_spec((2 * seg, width)),
        ),
        out_shape=f32(2 * seg, width),
        compiler_params=params(12),
        cost_estimate=cost(3 * seg * seg * width * 2, 12 * seg * width),
        name="dft",
    )(pos, table, *xs)


def taps_kernel(table_ref, x_ref, out_ref, last_ref):
    step = pl.program_id(0)
    rows = out_ref.shape[1] // 4
    sub = rows // 2

    def store(group, value):
        base = group * rows
        sign = 1.0 if group % 2 == 0 else -1.0
        re, im = slice(base, base + sub), slice(base + sub, base + rows)
        out_ref[0, re, :] = value[:sub] - sign * last_ref[im, :]
        out_ref[0, im, :] = value[sub:] + sign * last_ref[re, :]
        last_ref[base : base + rows, :] = value

    @pl.when(step == 0)
    def _():
        last_ref[...] = jnp.zeros_like(last_ref)

    transform(x_ref[...], table_ref, store)


def taps_spectra(table, taps, seg):
    width = taps.shape[1]
    blocks = taps.shape[0] // seg
    return pl.pallas_call(
        taps_kernel,
        grid=(blocks,),
        in_specs=[whole_spec(table.shape), pl.BlockSpec((seg, width), lambda i: (i, 0))],
        out_specs=pl.BlockSpec((1, 2 * seg, width), lambda i: (jnp.maximum(i - 1, 0), 0, 0)),
        out_shape=jax.ShapeDtypeStruct((blocks - 1, 2 * seg, width), jnp.float32),
        scratch_shapes=[pltpu.VMEM((2 * seg, width), jnp.float32)],
        compiler_params=params(14),
        cost_estimate=cost(blocks * 3 * seg * seg * width * 2, blocks * 12 * seg * width),
        name="taps",
    )(table, taps)


def conj_mul(a, b):
    return a[0] * b[0] + a[1] * b[1], a[0] * b[1] - a[1] * b[0]


def mul(a, b):
    return a[0] * b[0] - a[1] * b[1], a[0] * b[1] + a[1] * b[0]


def add(a, b):
    return a[0] + b[0], a[1] + b[1]


def partial_kernel(
    pos_ref, table_ref, inverse_ref, win_near, win_far, next_ref, x_ref, next_strip, far_strip, far_ref, out_ref, z_ref
):
    rows = far_ref.shape[0] // 4
    sub = rows // 2
    for group, part in enumerate(spread(x_ref[...])):
        base = group * rows
        far = dot3(table_ref, group, *split(part))
        far_ref[base : base + rows, :] = far
        re, im = slice(base, base + sub), slice(base + sub, base + rows)
        near = (next_ref[re, :], next_ref[im, :])
        total = add(
            conj_mul((win_near[0, re, :], win_near[0, im, :]), near),
            conj_mul((win_far[0, re, :], win_far[0, im, :]), (far[:sub], far[sub:])),
        )
        z_ref[group] = dot3(inverse_ref, group, *split(jnp.concatenate(total, axis=0)))
    quarters = gather_quarters([z_ref[g, :sub] for g in range(4)], [z_ref[g, sub:] for g in range(4)])
    for i, quarter in enumerate(quarters):
        out_ref[i * sub : (i + 1) * sub, :] = quarter
    out_ref[4 * sub : 4 * sub + 8, :] = next_strip[...]
    out_ref[4 * sub + 8 :, :] = far_strip[...]


def back_partial(pos, table, inverse, windows, next_m, next_x, x, seg):
    width = x.shape[1]
    n = (windows.shape[0] + 1) // 2

    def window(distance):
        return pl.BlockSpec(
            (1, 2 * seg, width),
            lambda i, pos: (jnp.where(pos[0] == 1, n - 1 + distance, n - 1 - distance), 0, 0),
        )

    return pl.pallas_call(
        partial_kernel,
        grid_spec=pltpu.PrefetchScalarGridSpec(
            num_scalar_prefetch=1,
            grid=(1,),
            in_specs=[
                whole_spec(table.shape),
                whole_spec(inverse.shape),
                window(2),
                window(3),
                whole_spec((2 * seg, width)),
                whole_spec((seg, width)),
                *[strip_spec(seg, width)] * 2,
            ],
            out_specs=[whole_spec((2 * seg, width)), whole_spec((seg + 16, width))],
            scratch_shapes=[pltpu.VMEM((4, seg // 2, width), jnp.float32)],
        ),
        out_shape=[f32(2 * seg, width), f32(seg + 16, width)],
        compiler_params=params(24),
        cost_estimate=cost(6 * seg * seg * width * 2, 24 * seg * width),
        name="partial",
    )(pos, table, inverse, windows, windows, next_m, x, next_x, x)


OWN, OUTER, NEXT, TWO, THREE = range(5)
PAIRS = (
    ((), ((OWN, THREE),), ((OWN, TWO), (NEXT, THREE))),
    (
        ((OUTER, NEXT), (OWN, TWO)),
        ((OUTER, OWN), (OWN, NEXT), (NEXT, TWO)),
        ((OUTER, OUTER), (OWN, OWN), (NEXT, NEXT), (TWO, TWO)),
    ),
    (
        ((TWO, TWO), (NEXT, NEXT), (OWN, OWN), (OUTER, OUTER)),
        ((NEXT, TWO), (OWN, NEXT), (OUTER, OWN)),
        ((OWN, TWO), (OUTER, NEXT)),
    ),
    (((NEXT, THREE), (OWN, TWO)), ((OWN, THREE),), ()),
)


def is_late(pair):
    return pair[0] == TWO or pair[1] == THREE


def pair_sums(distances, gated, mixed, sign, late):
    total = []
    for pairs in distances:
        value = None
        for m, g in pairs:
            if is_late((m, g)) == late:
                term = conj_mul(gated[g](), mixed[m]())
                value = term if value is None else add(value, term)
        total.append(value)
    out = []
    for low, high in zip(total[:2], total[1:]):
        if high is not None:
            turned = (sign * high[1], -sign * high[0])
            low = turned if low is None else add(low, turned)
        out.append(low)
    return out


TILE = 16


def tile_reader(tile, sub):
    re = pl.ds(pl.multiple_of(tile * TILE, TILE), TILE)
    im = pl.ds(pl.multiple_of(sub + tile * TILE, TILE), TILE)

    def read(ref, *lead):
        return ref[(*lead, re, slice(None))], ref[(*lead, im, slice(None))]

    return re, im, read


def group_sign():
    return jnp.where(pl.program_id(0) % 2 == 0, 1.0, -1.0)


def early_kernel(
    pos_ref, win_own, win_outer, win_next, win_two, own_g, outer_g, next_g, two_g, own_m, outer_m, next_m, out_ref
):
    pos, sign = pos_ref[0], group_sign()
    rows = own_g.shape[0]
    sub = rows // 2
    count = sub // TILE

    def put(at, slot, value):
        re, im = at
        out_ref[slot, re, :] = value[0]
        out_ref[slot, im, :] = value[1]

    def sums(tile, _):
        re, im, read = tile_reader(tile, sub)
        own, outer, ahead = read(win_own, 0), read(win_outer, 0), read(win_next, 0)
        conv = add(mul(own, read(own_g)), mul(outer, read(outer_g)))
        conv = add(conv, add(mul(ahead, read(next_g)), mul(read(win_two, 0), read(two_g))))
        put((re, im), 0, conv)
        back = add(conj_mul(own, read(own_m)), conj_mul(ahead, read(outer_m)))
        put((re, im), 1, add(back, conj_mul(outer, read(next_m))))
        return _

    lax.fori_loop(0, count, sums, 0)
    for where, distances in enumerate(PAIRS):

        @pl.when(pos == where)
        def _():
            def lags(tile, _):
                re, im, read = tile_reader(tile, sub)
                gated = [functools.partial(read, ref) for ref in (own_g, outer_g, next_g, two_g)]
                mixed = [functools.partial(read, ref) for ref in (own_m, outer_m, next_m)]
                for slot, value in enumerate(pair_sums(distances, gated, mixed, sign, False)):
                    if value is None:
                        value = (jnp.zeros_like(own_g[re, :]),) * 2
                    put((re, im), 2 + slot, value)
                return _

            lax.fori_loop(0, count, lags, 0)


def early(pos, windows, gated, mixed, seg):
    width = gated[0].shape[1]
    rows = seg // 2
    mid = windows.shape[0] // 2

    def window(index):
        return pl.BlockSpec((1, rows, width), lambda i, pos: (index(pos[0]), i, 0))

    group = pl.BlockSpec((rows, width), lambda i, pos: (i, 0))
    return pl.pallas_call(
        early_kernel,
        grid_spec=pltpu.PrefetchScalarGridSpec(
            num_scalar_prefetch=1,
            grid=(4,),
            in_specs=[
                window(lambda p: mid),
                window(lambda p: jnp.where(p < 2, mid + 1, mid - 1)),
                window(lambda p: jnp.where(p < 2, mid - 1, mid + 1)),
                window(lambda p: jnp.where(p < 2, mid - 2, mid + 2)),
            ]
            + [group] * 7,
            out_specs=pl.BlockSpec((4, rows, width), lambda i, pos: (0, i, 0)),
        ),
        out_shape=f32(4, 2 * seg, width),
        compiler_params=params(14),
        cost_estimate=cost(200 * seg * width, 120 * seg * width),
        name="early",
    )(pos, *[windows] * 4, *gated, *mixed)


def late_kernel(
    pos_ref, inverse_ref, acc_ref, win_ref, three_g, two_g, own_m, outer_m, next_m, *rest
):
    two_m, gated_ref, mixed_ref, skip_ref, up_ref, query_out, filter_out, back_out, x_high, x_low, z_ref = rest
    group = pl.program_id(0)
    pos, sign = pos_ref[0], group_sign()
    rows, width = own_m.shape
    sub = rows // 2

    def put(at, slot, value):
        for rows_at, part in zip(at, value):
            high, low = split(part)
            x_high[rows_at, slot * width : (slot + 1) * width] = high
            x_low[rows_at, slot * width : (slot + 1) * width] = low

    for where, distances in enumerate(PAIRS):

        @pl.when(pos == where)
        def _():
            def lags(tile, _):
                re, im, read = tile_reader(tile, sub)

                gated = [None, None, None, functools.partial(read, two_g), functools.partial(read, three_g)]
                mixed = [functools.partial(read, ref) for ref in (own_m, outer_m, next_m, two_m)]
                total = [read(acc_ref, slot) for slot in range(4)]
                if where in (0, 3):
                    total[0] = add(total[0], mul(read(win_ref, 0), gated[THREE]()))
                else:
                    total[1] = add(total[1], conj_mul(read(win_ref, 0), mixed[TWO]()))
                for slot, value in enumerate(pair_sums(distances, gated, mixed, sign, True)):
                    if value is not None:
                        total[2 + slot] = add(total[2 + slot], value)
                for slot, value in enumerate(total):
                    put((re, im), slot, value)
                return _

            lax.fori_loop(0, sub // TILE, lags, 0)

    dot = functools.partial(jnp.dot, preferred_element_type=jnp.float32)
    t_high, t_low = inverse_ref[0, 0], inverse_ref[1, 0]
    for slot in range(4):
        cols = slice(slot * width, (slot + 1) * width)
        z_ref[group, :, cols] = (
            dot(t_high, x_high[:, cols]) + dot(t_high, x_low[:, cols]) + dot(t_low, x_high[:, cols])
        )

    @pl.when(group == 3)
    def _():
        seg = 4 * sub
        for slot in range(4):
            cols = slice(slot * width, (slot + 1) * width)
            quarters = gather_quarters(
                [z_ref[g, :sub, cols] for g in range(4)], [z_ref[g, sub:, cols] for g in range(4)]
            )
            for i, quarter in enumerate(quarters):
                at = slice(i * sub, (i + 1) * sub)
                if slot == 0:
                    query_out[at, :] = up_ref[at, :] * (quarter + skip_ref[...] * gated_ref[at, :])
                elif slot == 1:
                    back_out[at, :] = quarter + skip_ref[...] * mixed_ref[at, :]
                else:
                    base = (slot - 2) * seg + i * sub
                    filter_out[base : base + sub, :] = quarter


def late(pos, inverse, acc, windows, three_g, two_g, own_m, outer_m, next_m, two_m, gated, mixed, skip, upstream):
    seg, width = upstream.shape
    rows = seg // 2
    mid = windows.shape[0] // 2

    def win_at(i, pos):
        p = pos[0]
        ends = jnp.where(p == 0, mid - 3, mid + 3)
        return jnp.where(p == 1, mid + 2, jnp.where(p == 2, mid - 2, ends)), i, 0

    group = pl.BlockSpec((rows, width), lambda i, pos: (i, 0))
    return pl.pallas_call(
        late_kernel,
        grid_spec=pltpu.PrefetchScalarGridSpec(
            num_scalar_prefetch=1,
            grid=(4,),
            in_specs=[
                pl.BlockSpec((2, 1, rows, rows), lambda i, pos: (0, i, 0, 0)),
                pl.BlockSpec((4, rows, width), lambda i, pos: (0, i, 0)),
                pl.BlockSpec((1, rows, width), win_at),
                *[group] * 6,
                whole_spec((seg, width)),
                whole_spec((seg, width)),
                whole_spec((1, width)),
                whole_spec((seg, width)),
            ],
            out_specs=[whole_spec((seg, width)), whole_spec((2 * seg, width)), whole_spec((seg, width))],
            scratch_shapes=[
                pltpu.VMEM((rows, 4 * width), jnp.bfloat16),
                pltpu.VMEM((rows, 4 * width), jnp.bfloat16),
                pltpu.VMEM((4, rows, 4 * width), jnp.float32),
            ],
        ),
        out_shape=[f32(seg, width), f32(2 * seg, width), f32(seg, width)],
        compiler_params=params(20),
        cost_estimate=cost(12 * seg * seg * width * 2, 100 * seg * width),
        name="late",
    )(pos, inverse, acc, windows, three_g, two_g, own_m, outer_m, next_m, two_m, gated, mixed, skip, upstream)


def finish_kernel(
    pos_ref, back_ref, key_ref, values_ref, partial_ref, own_strip, beside_strip, across_strip, two_strip,
    key_out, value_out, skip_out,
):
    pos = pos_ref[0]
    seg = back_ref.shape[0]
    back = back_ref[...] + partial_ref[:seg, :]
    key_out[...] = back * values_ref[...]
    value_out[...] = back * key_ref[...]
    far = jnp.where(pos < 2, pos + 2, pos - 2)
    strips = (
        (own_strip[...], pos),
        (beside_strip[...], jnp.where(pos % 2 == 0, pos + 1, pos - 1)),
        (across_strip[...], 3 - pos),
        (two_strip[...] + partial_ref[seg : seg + 8, :], far),
        (partial_ref[seg + 8 :, :], 3 - pos),
    )
    total = None
    for block in range(4):
        value = jnp.zeros_like(own_strip[...])
        for strip, source in strips:
            value = value + jnp.where(source == block, strip, 0.0)
        total = value if total is None else total + value
    skip_out[...] = jnp.sum(total, axis=0, keepdims=True)


def finish(pos, back, key_gate, values, partial, *mixed):
    seg, width = back.shape
    block = whole_spec((seg, width))
    return pl.pallas_call(
        finish_kernel,
        grid_spec=pltpu.PrefetchScalarGridSpec(
            num_scalar_prefetch=1,
            grid=(1,),
            in_specs=[block] * 3 + [whole_spec(partial.shape)] + [strip_spec(seg, width)] * len(mixed),
            out_specs=[block, block, whole_spec((1, width))],
        ),
        out_shape=[f32(seg, width), f32(seg, width), f32(1, width)],
        compiler_params=params(12),
        cost_estimate=cost(3 * seg * width, 24 * seg * width),
        name="finish",
    )(pos, back, key_gate, values, partial, *mixed)


def send(x, *pairs):
    return lax.ppermute(x, "ctx", list(pairs))


def across(x):
    return send(x, (1, 2), (2, 1))


def outward(x):
    return send(x, (1, 0), (2, 3))


def beside(x):
    return send(x, (0, 1), (1, 0), (2, 3), (3, 2))


def local_line(query_gate, key_gate, values, filter_taps, skip_gain, upstream):
    seg, width = values.shape
    forward_np, inverse_np = tables(seg)
    table, inverse = jnp.asarray(forward_np), jnp.asarray(inverse_np)
    pos = lax.axis_index("ctx").astype(jnp.int32).reshape(1)
    after = lax.optimization_barrier

    gated = key_gate * values
    side, over = beside(gated), across(gated)
    mixed = mix(gated, upstream, query_gate)
    side_x, over_x = beside(mixed), across(mixed)
    own_g, own_m = dft(pos, table, seg, gated), dft(pos, table, seg, mixed)
    side, over, filter_taps, own_g, own_m = after((side, over, filter_taps, own_g, own_m))

    two = across(side), outward(over)
    outer_g = dft(pos, table, seg, side, choose=True)
    next_g = dft(pos, table, seg, over, side, choose=True)
    windows = taps_spectra(table, filter_taps, seg)
    side_x, over_x, windows, outer_g, next_g = after((side_x, over_x, windows, outer_g, next_g))

    two_x = across(side_x)
    outer_m = dft(pos, table, seg, side_x, choose=True)
    next_m = dft(pos, table, seg, over_x, side_x, choose=True)
    *two, outer_m, next_m = after((*two, outer_m, next_m))

    three = outward(two[0])
    two_m, partial = back_partial(pos, table, inverse, windows, next_m, over_x, two_x, seg)
    *two, partial = after((*two, partial))
    partial = outward(partial)
    two_g = dft(pos, table, seg, *two)
    acc = early(pos, windows, (own_g, outer_g, next_g, two_g), (own_m, outer_m, next_m), seg)
    three, acc = after((three, acc))

    three_g = dft(pos, table, seg, three)
    query_grad, filter_grad, back = late(
        pos, inverse, acc, windows, three_g, two_g, own_m, outer_m, next_m, two_m,
        gated, mixed, skip_gain[None, :], upstream,
    )
    key_grad, value_grad, skip_grad = finish(
        pos, back, key_gate, values, partial, mixed, side_x, over_x, two_x
    )
    return (query_grad, key_grad, value_grad, filter_grad, skip_grad[0])


def matmul(left, right):
    return jnp.dot(left, right, preferred_element_type=jnp.float32, precision=lax.Precision.HIGHEST)


def forward_table(seg_len, count, offset):
    num_bins = seg_len + 1
    period = 2 * seg_len
    bin_index = lax.broadcasted_iota(jnp.int32, (num_bins, count), 0)
    pos_index = lax.broadcasted_iota(jnp.int32, (num_bins, count), 1) + offset
    angles = (bin_index * pos_index % period).astype(jnp.float32) * (2.0 * math.pi / period)
    return jnp.concatenate([jnp.cos(angles), -jnp.sin(angles)], axis=0)


def inverse_table(seg_len, count, offset):
    num_bins = seg_len + 1
    period = 2 * seg_len
    pos_index = lax.broadcasted_iota(jnp.int32, (count, num_bins), 0) + offset
    bin_index = lax.broadcasted_iota(jnp.int32, (count, num_bins), 1)
    angles = (bin_index * pos_index % period).astype(jnp.float32) * (2.0 * math.pi / period)
    weights = jnp.where((bin_index == 0) | (bin_index == seg_len), 1.0, 2.0) / period
    return jnp.concatenate([weights * jnp.cos(angles), -weights * jnp.sin(angles)], axis=1)


def times_spec(first, second):
    num_bins = first.shape[0] // 2
    real_a, imag_a = (first[:num_bins], first[num_bins:])
    real_b, imag_b = (second[:num_bins], second[num_bins:])
    return jnp.concatenate(
        [real_a * real_b - imag_a * imag_b, real_a * imag_b + imag_a * real_b], axis=0
    )


def conj_times(first, second):
    num_bins = first.shape[0] // 2
    real_a, imag_a = (first[:num_bins], first[num_bins:])
    real_b, imag_b = (second[:num_bins], second[num_bins:])
    return jnp.concatenate(
        [real_a * real_b + imag_a * imag_b, real_a * imag_b - imag_a * real_b], axis=0
    )


def pick(stack, index):
    return lax.dynamic_index_in_dim(stack, index, 0, keepdims=False)


def local(query_gate, key_gate, values, filter_taps, skip_gain, upstream):
    seg_len, width_dev = values.shape
    cycle_size = lax.axis_size("ctx")
    position = lax.axis_index("ctx")
    history = seg_len * cycle_size
    gated = key_gate * values
    mixed_grad = upstream * query_gate
    table_low = forward_table(seg_len, seg_len, 0)
    table_high = forward_table(seg_len, seg_len, seg_len)
    table_taps = forward_table(seg_len, 2 * seg_len, 0)
    back_low = inverse_table(seg_len, seg_len, 0)
    back_high = inverse_table(seg_len, seg_len, seg_len)
    back_full = inverse_table(seg_len, 2 * seg_len, 0)
    own_grad_spec = matmul(table_high, mixed_grad)
    spec_rows = 2 * (seg_len + 1)

    def taps_spec(lag_block):
        start_row = (lag_block - 1) * seg_len + history
        window = lax.dynamic_slice_in_dim(filter_taps, start_row, 2 * seg_len, 0)
        return matmul(table_taps, window)

    def visit(carry, gated_spec, grad_spec, source):
        acc_conv, acc_back, partial_value = carry
        lag_block = position - source
        acc_conv = acc_conv + times_spec(taps_spec(lag_block), gated_spec)
        acc_back = acc_back + conj_times(taps_spec(-lag_block), grad_spec)
        segment = matmul(back_full, conj_times(gated_spec, own_grad_spec))
        start_row = (lag_block - 1) * seg_len + history
        current = lax.dynamic_slice_in_dim(partial_value, start_row, 2 * seg_len, 0)
        partial_value = lax.dynamic_update_slice_in_dim(
            partial_value, current + segment, start_row, 0
        )
        return (acc_conv, acc_back, partial_value)

    initial = (
        jnp.zeros((spec_rows, width_dev), jnp.float32),
        jnp.zeros((spec_rows, width_dev), jnp.float32),
        jnp.zeros((2 * history, width_dev), jnp.float32),
    )
    own_gated_spec = matmul(table_low, gated)
    pieces = (
        lax.all_gather(own_gated_spec[None], "ctx", axis=0, tiled=True),
        lax.all_gather(own_grad_spec[None], "ctx", axis=0, tiled=True),
    )

    def advance(member, state):
        return visit(state, pick(pieces[0], member), pick(pieces[1], member), member)

    folded = lax.fori_loop(0, pieces[0].shape[0], advance, initial)
    acc_conv, acc_back, partial_value = folded
    filter_grad = lax.psum_scatter(partial_value, "ctx", scatter_dimension=0, tiled=True)
    conv = matmul(back_high, acc_conv)
    back = matmul(back_low, acc_back) + skip_gain[None, :] * mixed_grad
    query_grad = upstream * (conv + skip_gain[None, :] * gated)
    key_grad = back * values
    value_grad = back * key_gate
    skip_grad = lax.psum(jnp.sum(mixed_grad * gated, axis=0), "ctx")
    return (query_grad, key_grad, value_grad, filter_grad, skip_grad)


def solution(mesh):
    in_specs = (
        P(("groups", "ctx"), "chan"),
        P(("groups", "ctx"), "chan"),
        P(("groups", "ctx"), "chan"),
        P(None, "chan"),
        P("chan"),
        P(("groups", "ctx"), "chan"),
    )
    out_specs = (
        P(("groups", "ctx"), "chan"),
        P(("groups", "ctx"), "chan"),
        P(("groups", "ctx"), "chan"),
        P(("groups", "ctx"), "chan"),
        P(("groups", "chan")),
    )
    body = local_line if mesh.shape["ctx"] == 4 else local
    return jax.shard_map(body, mesh=mesh, in_specs=in_specs, out_specs=out_specs, check_vma=False)
```

```python
import functools
import math

import jax
import jax.numpy as jnp
import ml_dtypes
import numpy as np
from jax import lax
from jax.experimental import pallas as pl
from jax.experimental.pallas import tpu as pltpu
from jax.sharding import PartitionSpec as P

COS1, SIN1, HALF = math.cos(math.pi / 8), math.sin(math.pi / 8), math.sqrt(0.5)


def split_np(table):
    high = table.astype(ml_dtypes.bfloat16)
    low = (table - high.astype(np.float64)).astype(ml_dtypes.bfloat16)
    return np.stack([high, low])


def tables(seg):
    sub = seg // 4
    bins, pos = np.arange(sub)[:, None], np.arange(sub)[None, :]
    forward = []
    for group in range(4):
        angle = 2 * np.pi * pos * (8 * bins + group + 0.5) / (2 * seg)
        cos, sin = np.cos(angle), np.sin(angle)
        forward.append(np.block([[cos, -sin], [-sin, -cos]]))
    forward = np.stack(forward)
    inverse = forward.transpose(0, 2, 1) / seg
    return split_np(forward), split_np(inverse)


def split(x):
    high = x.astype(jnp.bfloat16)
    return high, (x - high.astype(jnp.float32)).astype(jnp.bfloat16)


def dot3(table_ref, group, high, low):
    t_high, t_low = table_ref[0, group], table_ref[1, group]
    dot = functools.partial(jnp.dot, preferred_element_type=jnp.float32)
    return dot(t_high, high) + dot(t_high, low) + dot(t_low, high)


def spread(x):
    sub = x.shape[0] // 4
    x0, x1, x2, x3 = (x[i * sub : (i + 1) * sub] for i in range(4))
    u, p, s, q, t = HALF * x2, COS1 * x1, SIN1 * x1, COS1 * x3, SIN1 * x3
    a, b, pt, sq, pmt, spq = x0 + u, x0 - u, p + t, s - q, p - t, s + q
    pairs = ((a + pt, spq + u), (b + sq, pmt + u), (b - sq, pmt - u), (a - pt, spq - u))
    return [jnp.concatenate(pair, axis=0) for pair in pairs]


def gather_quarters(re, im):
    e03, d03, e12, d12 = re[0] + re[3], re[0] - re[3], re[1] + re[2], re[1] - re[2]
    f03, g03, f12, g12 = im[0] + im[3], im[0] - im[3], im[1] + im[2], im[1] - im[2]
    return (
        e03 + e12,
        COS1 * (d03 + f12) + SIN1 * (d12 + f03),
        HALF * (e03 - e12 + g03 + g12),
        SIN1 * (d03 - f12) + COS1 * (f03 - d12),
    )


def transform(x, table_ref, store):
    for group, part in enumerate(spread(x)):
        store(group, dot3(table_ref, group, *split(part)))


def cost(flops, nbytes):
    return pl.CostEstimate(flops=int(flops), bytes_accessed=int(nbytes), transcendentals=0)


def params(mib):
    return pltpu.CompilerParams(vmem_limit_bytes=mib << 20)


def whole_spec(shape):
    return pl.BlockSpec(shape, lambda *_: (0,) * len(shape))


def f32(*shape):
    return jax.ShapeDtypeStruct(shape, jnp.float32)


def mix_kernel(gated_ref, up_ref, query_ref, mixed_ref):
    seg, width = gated_ref.shape
    mixed = up_ref[...] * query_ref[...]
    mixed_ref[:seg, :] = mixed
    mixed_ref[seg:, :] = jnp.sum((gated_ref[...] * mixed).reshape(seg // 8, 8, width), axis=0)


def mix(gated, upstream, query_gate):
    seg, width = gated.shape
    return pl.pallas_call(
        mix_kernel,
        grid=(1,),
        in_specs=[whole_spec((seg, width))] * 3,
        out_specs=whole_spec((seg + 8, width)),
        out_shape=f32(seg + 8, width),
        compiler_params=params(12),
        cost_estimate=cost(4 * seg * width, 16 * seg * width),
        name="mix",
    )(gated, upstream, query_gate)


def strip_spec(seg, width):
    return pl.BlockSpec((8, width), lambda *_: (seg // 8, 0))


def dft_kernel(choose, pos_ref, table_ref, *refs):
    *x_refs, out_ref = refs
    rows = out_ref.shape[0] // 4
    inner = jnp.logical_or(pos_ref[0] == 1, pos_ref[0] == 2)

    def store(group, value):
        out_ref[group * rows : (group + 1) * rows, :] = value

    x = x_refs[0][...]
    if choose:
        x = jnp.where(inner, x, x_refs[1][...] if len(x_refs) == 2 else 0.0)
    elif len(x_refs) == 2:
        x = x + x_refs[1][...]
    transform(x, table_ref, store)


def dft(pos, table, seg, *xs, choose=False):
    width = xs[0].shape[1]
    return pl.pallas_call(
        functools.partial(dft_kernel, choose),
        grid_spec=pltpu.PrefetchScalarGridSpec(
            num_scalar_prefetch=1,
            grid=(1,),
            in_specs=[whole_spec(table.shape)] + [whole_spec((seg, width))] * len(xs),
            out_specs=whole_spec((2 * seg, width)),
        ),
        out_shape=f32(2 * seg, width),
        compiler_params=params(12),
        cost_estimate=cost(3 * seg * seg * width * 2, 12 * seg * width),
        name="dft",
    )(pos, table, *xs)


def taps_kernel(table_ref, x_ref, out_ref, last_ref):
    step = pl.program_id(0)
    rows = out_ref.shape[1] // 4
    sub = rows // 2

    def store(group, value):
        base = group * rows
        sign = 1.0 if group % 2 == 0 else -1.0
        re, im = slice(base, base + sub), slice(base + sub, base + rows)
        out_ref[0, re, :] = value[:sub] - sign * last_ref[im, :]
        out_ref[0, im, :] = value[sub:] + sign * last_ref[re, :]
        last_ref[base : base + rows, :] = value

    @pl.when(step == 0)
    def _():
        last_ref[...] = jnp.zeros_like(last_ref)

    transform(x_ref[...], table_ref, store)


def taps_spectra(table, taps, seg):
    width = taps.shape[1]
    blocks = taps.shape[0] // seg
    return pl.pallas_call(
        taps_kernel,
        grid=(blocks,),
        in_specs=[whole_spec(table.shape), pl.BlockSpec((seg, width), lambda i: (i, 0))],
        out_specs=pl.BlockSpec((1, 2 * seg, width), lambda i: (jnp.maximum(i - 1, 0), 0, 0)),
        out_shape=jax.ShapeDtypeStruct((blocks - 1, 2 * seg, width), jnp.float32),
        scratch_shapes=[pltpu.VMEM((2 * seg, width), jnp.float32)],
        compiler_params=params(14),
        cost_estimate=cost(blocks * 3 * seg * seg * width * 2, blocks * 12 * seg * width),
        name="taps",
    )(table, taps)


def conj_mul(a, b):
    return a[0] * b[0] + a[1] * b[1], a[0] * b[1] - a[1] * b[0]


def mul(a, b):
    return a[0] * b[0] - a[1] * b[1], a[0] * b[1] + a[1] * b[0]


def add(a, b):
    return a[0] + b[0], a[1] + b[1]


def partial_kernel(
    pos_ref, inverse_ref, win_own, win_outer, own_ref, outer_ref, own_strip, outer_strip, out_ref, z_ref
):
    rows = own_ref.shape[0] // 4
    sub = rows // 2
    for group in range(4):
        base = group * rows
        re, im = slice(base, base + sub), slice(base + sub, base + rows)
        total = add(
            conj_mul((win_own[0, re, :], win_own[0, im, :]), (own_ref[re, :], own_ref[im, :])),
            conj_mul((win_outer[0, re, :], win_outer[0, im, :]), (outer_ref[re, :], outer_ref[im, :])),
        )
        z_ref[group] = dot3(inverse_ref, group, *split(jnp.concatenate(total, axis=0)))
    quarters = gather_quarters([z_ref[g, :sub] for g in range(4)], [z_ref[g, sub:] for g in range(4)])
    for i, quarter in enumerate(quarters):
        out_ref[i * sub : (i + 1) * sub, :] = quarter
    out_ref[4 * sub : 4 * sub + 8, :] = own_strip[...]
    out_ref[4 * sub + 8 :, :] = outer_strip[...]


def back_partial(pos, inverse, windows, own_m, outer_m, own_x, outer_x, seg):
    width = own_m.shape[1]
    n = (windows.shape[0] + 1) // 2

    def window(distance):
        return pl.BlockSpec(
            (1, 2 * seg, width),
            lambda i, pos: (jnp.where(pos[0] == 2, n - 1 + distance, n - 1 - distance), 0, 0),
        )

    return pl.pallas_call(
        partial_kernel,
        grid_spec=pltpu.PrefetchScalarGridSpec(
            num_scalar_prefetch=1,
            grid=(1,),
            in_specs=[
                whole_spec(inverse.shape),
                window(2),
                window(3),
                *[whole_spec((2 * seg, width))] * 2,
                *[strip_spec(seg, width)] * 2,
            ],
            out_specs=whole_spec((seg + 16, width)),
            scratch_shapes=[pltpu.VMEM((4, seg // 2, width), jnp.float32)],
        ),
        out_shape=f32(seg + 16, width),
        compiler_params=params(24),
        cost_estimate=cost(3 * seg * seg * width * 2, 24 * seg * width),
        name="partial",
    )(pos, inverse, windows, windows, own_m, outer_m, own_x, outer_x)


OWN, OUTER, NEXT, TWO, THREE = range(5)
PAIRS = (
    ((), ((OWN, THREE),), ((OWN, TWO), (NEXT, THREE))),
    (
        ((OUTER, NEXT), (OWN, TWO)),
        ((OUTER, OWN), (OWN, NEXT), (NEXT, TWO)),
        ((OUTER, OUTER), (OWN, OWN), (NEXT, NEXT), (TWO, TWO)),
    ),
    (
        ((TWO, TWO), (NEXT, NEXT), (OWN, OWN), (OUTER, OUTER)),
        ((NEXT, TWO), (OWN, NEXT), (OUTER, OWN)),
        ((OWN, TWO), (OUTER, NEXT)),
    ),
    (((NEXT, THREE), (OWN, TWO)), ((OWN, THREE),), ()),
)


def is_late(pair):
    return pair[0] == TWO or pair[1] == THREE


def pair_sums(distances, gated, mixed, sign, late):
    total = []
    for pairs in distances:
        value = None
        for m, g in pairs:
            if is_late((m, g)) == late:
                term = conj_mul(gated[g](), mixed[m]())
                value = term if value is None else add(value, term)
        total.append(value)
    out = []
    for low, high in zip(total[:2], total[1:]):
        if high is not None:
            turned = (sign * high[1], -sign * high[0])
            low = turned if low is None else add(low, turned)
        out.append(low)
    return out


TILE = 16


def tile_reader(tile, sub):
    re = pl.ds(pl.multiple_of(tile * TILE, TILE), TILE)
    im = pl.ds(pl.multiple_of(sub + tile * TILE, TILE), TILE)

    def read(ref, *lead):
        return ref[(*lead, re, slice(None))], ref[(*lead, im, slice(None))]

    return re, im, read


def group_sign():
    return jnp.where(pl.program_id(0) % 2 == 0, 1.0, -1.0)


def early_kernel(
    pos_ref, win_own, win_outer, win_next, win_two, own_g, outer_g, next_g, two_g, own_m, outer_m, next_m, out_ref
):
    pos, sign = pos_ref[0], group_sign()
    rows = own_g.shape[0]
    sub = rows // 2
    count = sub // TILE

    def put(at, slot, value):
        re, im = at
        out_ref[slot, re, :] = value[0]
        out_ref[slot, im, :] = value[1]

    def sums(tile, _):
        re, im, read = tile_reader(tile, sub)
        own, outer, ahead = read(win_own, 0), read(win_outer, 0), read(win_next, 0)
        conv = add(mul(own, read(own_g)), mul(outer, read(outer_g)))
        conv = add(conv, add(mul(ahead, read(next_g)), mul(read(win_two, 0), read(two_g))))
        put((re, im), 0, conv)
        back = add(conj_mul(own, read(own_m)), conj_mul(ahead, read(outer_m)))
        put((re, im), 1, add(back, conj_mul(outer, read(next_m))))
        return _

    lax.fori_loop(0, count, sums, 0)
    for where, distances in enumerate(PAIRS):

        @pl.when(pos == where)
        def _():
            def lags(tile, _):
                re, im, read = tile_reader(tile, sub)
                gated = [functools.partial(read, ref) for ref in (own_g, outer_g, next_g, two_g)]
                mixed = [functools.partial(read, ref) for ref in (own_m, outer_m, next_m)]
                for slot, value in enumerate(pair_sums(distances, gated, mixed, sign, False)):
                    if value is None:
                        value = (jnp.zeros_like(own_g[re, :]),) * 2
                    put((re, im), 2 + slot, value)
                return _

            lax.fori_loop(0, count, lags, 0)


def early(pos, windows, gated, mixed, seg):
    width = gated[0].shape[1]
    rows = seg // 2
    mid = windows.shape[0] // 2

    def window(index):
        return pl.BlockSpec((1, rows, width), lambda i, pos: (index(pos[0]), i, 0))

    group = pl.BlockSpec((rows, width), lambda i, pos: (i, 0))
    return pl.pallas_call(
        early_kernel,
        grid_spec=pltpu.PrefetchScalarGridSpec(
            num_scalar_prefetch=1,
            grid=(4,),
            in_specs=[
                window(lambda p: mid),
                window(lambda p: jnp.where(p < 2, mid + 1, mid - 1)),
                window(lambda p: jnp.where(p < 2, mid - 1, mid + 1)),
                window(lambda p: jnp.where(p < 2, mid - 2, mid + 2)),
            ]
            + [group] * 7,
            out_specs=pl.BlockSpec((4, rows, width), lambda i, pos: (0, i, 0)),
        ),
        out_shape=f32(4, 2 * seg, width),
        compiler_params=params(14),
        cost_estimate=cost(200 * seg * width, 120 * seg * width),
        name="early",
    )(pos, *[windows] * 4, *gated, *mixed)


def late_kernel(
    pos_ref, inverse_ref, acc_ref, win_ref, three_g, two_g, own_m, outer_m, next_m, *rest
):
    two_m, gated_ref, mixed_ref, skip_ref, up_ref, query_out, filter_out, back_out, x_high, x_low, z_ref = rest
    group = pl.program_id(0)
    pos, sign = pos_ref[0], group_sign()
    rows, width = own_m.shape
    sub = rows // 2

    def put(at, slot, value):
        for rows_at, part in zip(at, value):
            high, low = split(part)
            x_high[rows_at, slot * width : (slot + 1) * width] = high
            x_low[rows_at, slot * width : (slot + 1) * width] = low

    for where, distances in enumerate(PAIRS):

        @pl.when(pos == where)
        def _():
            def lags(tile, _):
                re, im, read = tile_reader(tile, sub)

                gated = [None, None, None, functools.partial(read, two_g), functools.partial(read, three_g)]
                mixed = [functools.partial(read, ref) for ref in (own_m, outer_m, next_m, two_m)]
                total = [read(acc_ref, slot) for slot in range(4)]
                if where in (0, 3):
                    total[0] = add(total[0], mul(read(win_ref, 0), gated[THREE]()))
                else:
                    total[1] = add(total[1], conj_mul(read(win_ref, 0), mixed[TWO]()))
                for slot, value in enumerate(pair_sums(distances, gated, mixed, sign, True)):
                    if value is not None:
                        total[2 + slot] = add(total[2 + slot], value)
                for slot, value in enumerate(total):
                    put((re, im), slot, value)
                return _

            lax.fori_loop(0, sub // TILE, lags, 0)

    dot = functools.partial(jnp.dot, preferred_element_type=jnp.float32)
    t_high, t_low = inverse_ref[0, 0], inverse_ref[1, 0]
    for slot in range(4):
        cols = slice(slot * width, (slot + 1) * width)
        z_ref[group, :, cols] = (
            dot(t_high, x_high[:, cols]) + dot(t_high, x_low[:, cols]) + dot(t_low, x_high[:, cols])
        )

    @pl.when(group == 3)
    def _():
        seg = 4 * sub
        for slot in range(4):
            cols = slice(slot * width, (slot + 1) * width)
            quarters = gather_quarters(
                [z_ref[g, :sub, cols] for g in range(4)], [z_ref[g, sub:, cols] for g in range(4)]
            )
            for i, quarter in enumerate(quarters):
                at = slice(i * sub, (i + 1) * sub)
                if slot == 0:
                    query_out[at, :] = up_ref[at, :] * (quarter + skip_ref[...] * gated_ref[at, :])
                elif slot == 1:
                    back_out[at, :] = quarter + skip_ref[...] * mixed_ref[at, :]
                else:
                    base = (slot - 2) * seg + i * sub
                    filter_out[base : base + sub, :] = quarter


def late(pos, inverse, acc, windows, three_g, two_g, own_m, outer_m, next_m, two_m, gated, mixed, skip, upstream):
    seg, width = upstream.shape
    rows = seg // 2
    mid = windows.shape[0] // 2

    def win_at(i, pos):
        p = pos[0]
        ends = jnp.where(p == 0, mid - 3, mid + 3)
        return jnp.where(p == 1, mid + 2, jnp.where(p == 2, mid - 2, ends)), i, 0

    group = pl.BlockSpec((rows, width), lambda i, pos: (i, 0))
    return pl.pallas_call(
        late_kernel,
        grid_spec=pltpu.PrefetchScalarGridSpec(
            num_scalar_prefetch=1,
            grid=(4,),
            in_specs=[
                pl.BlockSpec((2, 1, rows, rows), lambda i, pos: (0, i, 0, 0)),
                pl.BlockSpec((4, rows, width), lambda i, pos: (0, i, 0)),
                pl.BlockSpec((1, rows, width), win_at),
                *[group] * 6,
                whole_spec((seg, width)),
                whole_spec((seg, width)),
                whole_spec((1, width)),
                whole_spec((seg, width)),
            ],
            out_specs=[whole_spec((seg, width)), whole_spec((2 * seg, width)), whole_spec((seg, width))],
            scratch_shapes=[
                pltpu.VMEM((rows, 4 * width), jnp.bfloat16),
                pltpu.VMEM((rows, 4 * width), jnp.bfloat16),
                pltpu.VMEM((4, rows, 4 * width), jnp.float32),
            ],
        ),
        out_shape=[f32(seg, width), f32(2 * seg, width), f32(seg, width)],
        compiler_params=params(20),
        cost_estimate=cost(12 * seg * seg * width * 2, 100 * seg * width),
        name="late",
    )(pos, inverse, acc, windows, three_g, two_g, own_m, outer_m, next_m, two_m, gated, mixed, skip, upstream)


def finish_kernel(
    pos_ref, back_ref, key_ref, values_ref, partial_ref, own_strip, beside_strip, across_strip, two_strip,
    key_out, value_out, skip_out,
):
    pos = pos_ref[0]
    seg = back_ref.shape[0]
    back = back_ref[...] + partial_ref[:seg, :]
    key_out[...] = back * values_ref[...]
    value_out[...] = back * key_ref[...]
    far = jnp.where(pos < 2, pos + 2, pos - 2)
    strips = (
        (own_strip[...], pos),
        (beside_strip[...], jnp.where(pos % 2 == 0, pos + 1, pos - 1)),
        (across_strip[...], 3 - pos),
        (two_strip[...] + partial_ref[seg : seg + 8, :], far),
        (partial_ref[seg + 8 :, :], 3 - pos),
    )
    total = None
    for block in range(4):
        value = jnp.zeros_like(own_strip[...])
        for strip, source in strips:
            value = value + jnp.where(source == block, strip, 0.0)
        total = value if total is None else total + value
    skip_out[...] = jnp.sum(total, axis=0, keepdims=True)


def finish(pos, back, key_gate, values, partial, *mixed):
    seg, width = back.shape
    block = whole_spec((seg, width))
    return pl.pallas_call(
        finish_kernel,
        grid_spec=pltpu.PrefetchScalarGridSpec(
            num_scalar_prefetch=1,
            grid=(1,),
            in_specs=[block] * 3 + [whole_spec(partial.shape)] + [strip_spec(seg, width)] * len(mixed),
            out_specs=[block, block, whole_spec((1, width))],
        ),
        out_shape=[f32(seg, width), f32(seg, width), f32(1, width)],
        compiler_params=params(12),
        cost_estimate=cost(3 * seg * width, 24 * seg * width),
        name="finish",
    )(pos, back, key_gate, values, partial, *mixed)


def send(x, *pairs):
    return lax.ppermute(x, "ctx", list(pairs))


def across(x):
    return send(x, (1, 2), (2, 1))


def outward(x):
    return send(x, (1, 0), (2, 3))


def beside(x):
    return send(x, (0, 1), (1, 0), (2, 3), (3, 2))


def local_line(query_gate, key_gate, values, filter_taps, skip_gain, upstream):
    seg, width = values.shape
    forward_np, inverse_np = tables(seg)
    table, inverse = jnp.asarray(forward_np), jnp.asarray(inverse_np)
    pos = lax.axis_index("ctx").astype(jnp.int32).reshape(1)
    after = lax.optimization_barrier

    gated = key_gate * values
    side, over = beside(gated), across(gated)
    mixed = mix(gated, upstream, query_gate)
    side_x, over_x = beside(mixed), across(mixed)
    own_g, own_m = dft(pos, table, seg, gated), dft(pos, table, seg, mixed)
    side, over, filter_taps, own_g, own_m = after((side, over, filter_taps, own_g, own_m))

    over_two, out_two = across(side), outward(over)
    outer_g = dft(pos, table, seg, side, choose=True)
    next_g = dft(pos, table, seg, over, side, choose=True)
    windows = taps_spectra(table, filter_taps, seg)
    side_x, over_x, windows, outer_g, next_g = after((side_x, over_x, windows, outer_g, next_g))

    two_x = across(side_x)
    outer_m = dft(pos, table, seg, side_x, choose=True)
    next_m = dft(pos, table, seg, over_x, side_x, choose=True)
    partial = back_partial(pos, inverse, windows, own_m, outer_m, mixed, side_x, seg)
    over_two, next_m, partial = after((over_two, next_m, partial))

    three = outward(over_two)
    two_g = dft(pos, table, seg, over_two, out_two)
    acc = early(pos, windows, (own_g, outer_g, next_g, two_g), (own_m, outer_m, next_m), seg)
    partial, acc = after((partial, acc))
    partial = send(partial, (2, 0), (1, 3))
    two_m = dft(pos, table, seg, two_x)
    three, two_m = after((three, two_m))

    three_g = dft(pos, table, seg, three)
    query_grad, filter_grad, back = late(
        pos, inverse, acc, windows, three_g, two_g, own_m, outer_m, next_m, two_m,
        gated, mixed, skip_gain[None, :], upstream,
    )
    key_grad, value_grad, skip_grad = finish(
        pos, back, key_gate, values, partial, mixed, side_x, over_x, two_x
    )
    return (query_grad, key_grad, value_grad, filter_grad, skip_grad[0])


def matmul(left, right):
    return jnp.dot(left, right, preferred_element_type=jnp.float32, precision=lax.Precision.HIGHEST)


def forward_table(seg_len, count, offset):
    num_bins = seg_len + 1
    period = 2 * seg_len
    bin_index = lax.broadcasted_iota(jnp.int32, (num_bins, count), 0)
    pos_index = lax.broadcasted_iota(jnp.int32, (num_bins, count), 1) + offset
    angles = (bin_index * pos_index % period).astype(jnp.float32) * (2.0 * math.pi / period)
    return jnp.concatenate([jnp.cos(angles), -jnp.sin(angles)], axis=0)


def inverse_table(seg_len, count, offset):
    num_bins = seg_len + 1
    period = 2 * seg_len
    pos_index = lax.broadcasted_iota(jnp.int32, (count, num_bins), 0) + offset
    bin_index = lax.broadcasted_iota(jnp.int32, (count, num_bins), 1)
    angles = (bin_index * pos_index % period).astype(jnp.float32) * (2.0 * math.pi / period)
    weights = jnp.where((bin_index == 0) | (bin_index == seg_len), 1.0, 2.0) / period
    return jnp.concatenate([weights * jnp.cos(angles), -weights * jnp.sin(angles)], axis=1)


def times_spec(first, second):
    num_bins = first.shape[0] // 2
    real_a, imag_a = (first[:num_bins], first[num_bins:])
    real_b, imag_b = (second[:num_bins], second[num_bins:])
    return jnp.concatenate(
        [real_a * real_b - imag_a * imag_b, real_a * imag_b + imag_a * real_b], axis=0
    )


def conj_times(first, second):
    num_bins = first.shape[0] // 2
    real_a, imag_a = (first[:num_bins], first[num_bins:])
    real_b, imag_b = (second[:num_bins], second[num_bins:])
    return jnp.concatenate(
        [real_a * real_b + imag_a * imag_b, real_a * imag_b - imag_a * real_b], axis=0
    )


def pick(stack, index):
    return lax.dynamic_index_in_dim(stack, index, 0, keepdims=False)


def local(query_gate, key_gate, values, filter_taps, skip_gain, upstream):
    seg_len, width_dev = values.shape
    cycle_size = lax.axis_size("ctx")
    position = lax.axis_index("ctx")
    history = seg_len * cycle_size
    gated = key_gate * values
    mixed_grad = upstream * query_gate
    table_low = forward_table(seg_len, seg_len, 0)
    table_high = forward_table(seg_len, seg_len, seg_len)
    table_taps = forward_table(seg_len, 2 * seg_len, 0)
    back_low = inverse_table(seg_len, seg_len, 0)
    back_high = inverse_table(seg_len, seg_len, seg_len)
    back_full = inverse_table(seg_len, 2 * seg_len, 0)
    own_grad_spec = matmul(table_high, mixed_grad)
    spec_rows = 2 * (seg_len + 1)

    def taps_spec(lag_block):
        start_row = (lag_block - 1) * seg_len + history
        window = lax.dynamic_slice_in_dim(filter_taps, start_row, 2 * seg_len, 0)
        return matmul(table_taps, window)

    def visit(carry, gated_spec, grad_spec, source):
        acc_conv, acc_back, partial_value = carry
        lag_block = position - source
        acc_conv = acc_conv + times_spec(taps_spec(lag_block), gated_spec)
        acc_back = acc_back + conj_times(taps_spec(-lag_block), grad_spec)
        segment = matmul(back_full, conj_times(gated_spec, own_grad_spec))
        start_row = (lag_block - 1) * seg_len + history
        current = lax.dynamic_slice_in_dim(partial_value, start_row, 2 * seg_len, 0)
        partial_value = lax.dynamic_update_slice_in_dim(
            partial_value, current + segment, start_row, 0
        )
        return (acc_conv, acc_back, partial_value)

    initial = (
        jnp.zeros((spec_rows, width_dev), jnp.float32),
        jnp.zeros((spec_rows, width_dev), jnp.float32),
        jnp.zeros((2 * history, width_dev), jnp.float32),
    )
    own_gated_spec = matmul(table_low, gated)
    pieces = (
        lax.all_gather(own_gated_spec[None], "ctx", axis=0, tiled=True),
        lax.all_gather(own_grad_spec[None], "ctx", axis=0, tiled=True),
    )

    def advance(member, state):
        return visit(state, pick(pieces[0], member), pick(pieces[1], member), member)

    folded = lax.fori_loop(0, pieces[0].shape[0], advance, initial)
    acc_conv, acc_back, partial_value = folded
    filter_grad = lax.psum_scatter(partial_value, "ctx", scatter_dimension=0, tiled=True)
    conv = matmul(back_high, acc_conv)
    back = matmul(back_low, acc_back) + skip_gain[None, :] * mixed_grad
    query_grad = upstream * (conv + skip_gain[None, :] * gated)
    key_grad = back * values
    value_grad = back * key_gate
    skip_grad = lax.psum(jnp.sum(mixed_grad * gated, axis=0), "ctx")
    return (query_grad, key_grad, value_grad, filter_grad, skip_grad)


def solution(mesh):
    in_specs = (
        P(("groups", "ctx"), "chan"),
        P(("groups", "ctx"), "chan"),
        P(("groups", "ctx"), "chan"),
        P(None, "chan"),
        P("chan"),
        P(("groups", "ctx"), "chan"),
    )
    out_specs = (
        P(("groups", "ctx"), "chan"),
        P(("groups", "ctx"), "chan"),
        P(("groups", "ctx"), "chan"),
        P(("groups", "ctx"), "chan"),
        P(("groups", "chan")),
    )
    body = local_line if mesh.shape["ctx"] == 4 else local
    return jax.shard_map(body, mesh=mesh, in_specs=in_specs, out_specs=out_specs, check_vma=False)
```

```python
import functools
import math

import jax
import jax.numpy as jnp
import ml_dtypes
import numpy as np
from jax import lax
from jax.experimental import pallas as pl
from jax.experimental.pallas import tpu as pltpu
from jax.sharding import PartitionSpec as P

COS1, SIN1, HALF = math.cos(math.pi / 8), math.sin(math.pi / 8), math.sqrt(0.5)


def split_np(table):
    high = table.astype(ml_dtypes.bfloat16)
    low = (table - high.astype(np.float64)).astype(ml_dtypes.bfloat16)
    return np.stack([high, low])


def tables(seg):
    sub = seg // 4
    bins, pos = np.arange(sub)[:, None], np.arange(sub)[None, :]
    forward = []
    for group in range(4):
        angle = 2 * np.pi * pos * (8 * bins + group + 0.5) / (2 * seg)
        cos, sin = np.cos(angle), np.sin(angle)
        forward.append(np.block([[cos, -sin], [-sin, -cos]]))
    forward = np.stack(forward)
    inverse = forward.transpose(0, 2, 1) / seg
    return split_np(forward), split_np(inverse)


def split(x):
    high = x.astype(jnp.bfloat16)
    return high, (x - high.astype(jnp.float32)).astype(jnp.bfloat16)


def dot3(table_ref, group, high, low):
    t_high, t_low = table_ref[0, group], table_ref[1, group]
    dot = functools.partial(jnp.dot, preferred_element_type=jnp.float32)
    return dot(t_high, high) + dot(t_high, low) + dot(t_low, high)


def spread(x):
    sub = x.shape[0] // 4
    x0, x1, x2, x3 = (x[i * sub : (i + 1) * sub] for i in range(4))
    u, p, s, q, t = HALF * x2, COS1 * x1, SIN1 * x1, COS1 * x3, SIN1 * x3
    a, b, pt, sq, pmt, spq = x0 + u, x0 - u, p + t, s - q, p - t, s + q
    pairs = ((a + pt, spq + u), (b + sq, pmt + u), (b - sq, pmt - u), (a - pt, spq - u))
    return [jnp.concatenate(pair, axis=0) for pair in pairs]


def gather_quarters(re, im):
    e03, d03, e12, d12 = re[0] + re[3], re[0] - re[3], re[1] + re[2], re[1] - re[2]
    f03, g03, f12, g12 = im[0] + im[3], im[0] - im[3], im[1] + im[2], im[1] - im[2]
    return (
        e03 + e12,
        COS1 * (d03 + f12) + SIN1 * (d12 + f03),
        HALF * (e03 - e12 + g03 + g12),
        SIN1 * (d03 - f12) + COS1 * (f03 - d12),
    )


def transform(x, table_ref, store):
    for group, part in enumerate(spread(x)):
        store(group, dot3(table_ref, group, *split(part)))


def cost(flops, nbytes):
    return pl.CostEstimate(flops=int(flops), bytes_accessed=int(nbytes), transcendentals=0)


def params(mib):
    return pltpu.CompilerParams(vmem_limit_bytes=mib << 20)


def whole_spec(shape):
    return pl.BlockSpec(shape, lambda *_: (0,) * len(shape))


def f32(*shape):
    return jax.ShapeDtypeStruct(shape, jnp.float32)


def mix_kernel(gated_ref, up_ref, query_ref, mixed_ref, sum_ref):
    seg, width = gated_ref.shape
    mixed = up_ref[...] * query_ref[...]
    mixed_ref[...] = mixed
    sum_ref[...] = jnp.sum((gated_ref[...] * mixed).reshape(seg // 8, 8, width), axis=0)


def mix(gated, upstream, query_gate):
    seg, width = gated.shape
    block = whole_spec((seg, width))
    return pl.pallas_call(
        mix_kernel,
        grid=(1,),
        in_specs=[block] * 3,
        out_specs=[block, whole_spec((8, width))],
        out_shape=[f32(seg, width), f32(8, width)],
        compiler_params=params(12),
        cost_estimate=cost(4 * seg * width, 16 * seg * width),
        name="mix",
    )(gated, upstream, query_gate)


def dft_kernel(choose, pos_ref, table_ref, *refs):
    *x_refs, out_ref = refs
    rows = out_ref.shape[0] // 4
    inner = jnp.logical_or(pos_ref[0] == 1, pos_ref[0] == 2)

    def store(group, value):
        out_ref[group * rows : (group + 1) * rows, :] = value

    x = x_refs[0][...]
    if choose:
        x = jnp.where(inner, x, x_refs[1][...] if len(x_refs) == 2 else 0.0)
    elif len(x_refs) == 2:
        x = x + x_refs[1][...]
    transform(x, table_ref, store)


def dft(pos, table, seg, *xs, choose=False):
    width = xs[0].shape[1]
    return pl.pallas_call(
        functools.partial(dft_kernel, choose),
        grid_spec=pltpu.PrefetchScalarGridSpec(
            num_scalar_prefetch=1,
            grid=(1,),
            in_specs=[whole_spec(table.shape)] + [whole_spec((seg, width))] * len(xs),
            out_specs=whole_spec((2 * seg, width)),
        ),
        out_shape=f32(2 * seg, width),
        compiler_params=params(12),
        cost_estimate=cost(3 * seg * seg * width * 2, 12 * seg * width),
        name="dft",
    )(pos, table, *xs)


def taps_kernel(table_ref, x_ref, out_ref, last_ref):
    step = pl.program_id(0)
    rows = out_ref.shape[1] // 4
    sub = rows // 2

    def store(group, value):
        base = group * rows
        sign = 1.0 if group % 2 == 0 else -1.0
        re, im = slice(base, base + sub), slice(base + sub, base + rows)
        out_ref[0, re, :] = value[:sub] - sign * last_ref[im, :]
        out_ref[0, im, :] = value[sub:] + sign * last_ref[re, :]
        last_ref[base : base + rows, :] = value

    @pl.when(step == 0)
    def _():
        last_ref[...] = jnp.zeros_like(last_ref)

    transform(x_ref[...], table_ref, store)


def taps_spectra(table, taps, seg):
    width = taps.shape[1]
    blocks = taps.shape[0] // seg
    return pl.pallas_call(
        taps_kernel,
        grid=(blocks,),
        in_specs=[whole_spec(table.shape), pl.BlockSpec((seg, width), lambda i: (i, 0))],
        out_specs=pl.BlockSpec((1, 2 * seg, width), lambda i: (jnp.maximum(i - 1, 0), 0, 0)),
        out_shape=jax.ShapeDtypeStruct((blocks - 1, 2 * seg, width), jnp.float32),
        scratch_shapes=[pltpu.VMEM((2 * seg, width), jnp.float32)],
        compiler_params=params(14),
        cost_estimate=cost(blocks * 3 * seg * seg * width * 2, blocks * 12 * seg * width),
        name="taps",
    )(table, taps)


def conj_mul(a, b):
    return a[0] * b[0] + a[1] * b[1], a[0] * b[1] - a[1] * b[0]


def mul(a, b):
    return a[0] * b[0] - a[1] * b[1], a[0] * b[1] + a[1] * b[0]


def add(a, b):
    return a[0] + b[0], a[1] + b[1]


def partial_kernel(
    pos_ref, table_ref, inverse_ref, win_near, win_far, next_ref, x_ref, far_ref, out_ref, z_ref
):
    rows = far_ref.shape[0] // 4
    sub = rows // 2
    for group, part in enumerate(spread(x_ref[...])):
        base = group * rows
        far = dot3(table_ref, group, *split(part))
        far_ref[base : base + rows, :] = far
        re, im = slice(base, base + sub), slice(base + sub, base + rows)
        near = (next_ref[re, :], next_ref[im, :])
        total = add(
            conj_mul((win_near[0, re, :], win_near[0, im, :]), near),
            conj_mul((win_far[0, re, :], win_far[0, im, :]), (far[:sub], far[sub:])),
        )
        z_ref[group] = dot3(inverse_ref, group, *split(jnp.concatenate(total, axis=0)))
    quarters = gather_quarters([z_ref[g, :sub] for g in range(4)], [z_ref[g, sub:] for g in range(4)])
    for i, quarter in enumerate(quarters):
        out_ref[i * sub : (i + 1) * sub, :] = quarter


def back_partial(pos, table, inverse, windows, next_m, x, seg):
    width = x.shape[1]
    n = (windows.shape[0] + 1) // 2

    def window(distance):
        return pl.BlockSpec(
            (1, 2 * seg, width),
            lambda i, pos: (jnp.where(pos[0] == 1, n - 1 + distance, n - 1 - distance), 0, 0),
        )

    return pl.pallas_call(
        partial_kernel,
        grid_spec=pltpu.PrefetchScalarGridSpec(
            num_scalar_prefetch=1,
            grid=(1,),
            in_specs=[
                whole_spec(table.shape),
                whole_spec(inverse.shape),
                window(2),
                window(3),
                whole_spec((2 * seg, width)),
                whole_spec((seg, width)),
            ],
            out_specs=[whole_spec((2 * seg, width)), whole_spec((seg, width))],
            scratch_shapes=[pltpu.VMEM((4, seg // 2, width), jnp.float32)],
        ),
        out_shape=[f32(2 * seg, width), f32(seg, width)],
        compiler_params=params(24),
        cost_estimate=cost(6 * seg * seg * width * 2, 24 * seg * width),
        name="partial",
    )(pos, table, inverse, windows, windows, next_m, x)


OWN, OUTER, NEXT, TWO, THREE = range(5)
PAIRS = (
    ((), ((OWN, THREE),), ((OWN, TWO), (NEXT, THREE))),
    (
        ((OUTER, NEXT), (OWN, TWO)),
        ((OUTER, OWN), (OWN, NEXT), (NEXT, TWO)),
        ((OUTER, OUTER), (OWN, OWN), (NEXT, NEXT), (TWO, TWO)),
    ),
    (
        ((TWO, TWO), (NEXT, NEXT), (OWN, OWN), (OUTER, OUTER)),
        ((NEXT, TWO), (OWN, NEXT), (OUTER, OWN)),
        ((OWN, TWO), (OUTER, NEXT)),
    ),
    (((NEXT, THREE), (OWN, TWO)), ((OWN, THREE),), ()),
)


def is_late(pair):
    return pair[0] == TWO or pair[1] == THREE


def pair_sums(distances, gated, mixed, sign, late):
    total = []
    for pairs in distances:
        value = None
        for m, g in pairs:
            if is_late((m, g)) == late:
                term = conj_mul(gated[g](), mixed[m]())
                value = term if value is None else add(value, term)
        total.append(value)
    out = []
    for low, high in zip(total[:2], total[1:]):
        if high is not None:
            turned = (sign * high[1], -sign * high[0])
            low = turned if low is None else add(low, turned)
        out.append(low)
    return out


TILE = 16


def tile_reader(tile, sub):
    re = pl.ds(pl.multiple_of(tile * TILE, TILE), TILE)
    im = pl.ds(pl.multiple_of(sub + tile * TILE, TILE), TILE)

    def read(ref, *lead):
        return ref[(*lead, re, slice(None))], ref[(*lead, im, slice(None))]

    return re, im, read


def group_sign():
    return jnp.where(pl.program_id(0) % 2 == 0, 1.0, -1.0)


def early_kernel(
    pos_ref, win_own, win_outer, win_next, win_two, own_g, outer_g, next_g, two_g, own_m, outer_m, next_m, out_ref
):
    pos, sign = pos_ref[0], group_sign()
    rows = own_g.shape[0]
    sub = rows // 2
    count = sub // TILE

    def put(at, slot, value):
        re, im = at
        out_ref[slot, re, :] = value[0]
        out_ref[slot, im, :] = value[1]

    def sums(tile, _):
        re, im, read = tile_reader(tile, sub)
        own, outer, ahead = read(win_own, 0), read(win_outer, 0), read(win_next, 0)
        conv = add(mul(own, read(own_g)), mul(outer, read(outer_g)))
        conv = add(conv, add(mul(ahead, read(next_g)), mul(read(win_two, 0), read(two_g))))
        put((re, im), 0, conv)
        back = add(conj_mul(own, read(own_m)), conj_mul(ahead, read(outer_m)))
        put((re, im), 1, add(back, conj_mul(outer, read(next_m))))
        return _

    lax.fori_loop(0, count, sums, 0)
    for where, distances in enumerate(PAIRS):

        @pl.when(pos == where)
        def _():
            def lags(tile, _):
                re, im, read = tile_reader(tile, sub)
                gated = [functools.partial(read, ref) for ref in (own_g, outer_g, next_g, two_g)]
                mixed = [functools.partial(read, ref) for ref in (own_m, outer_m, next_m)]
                for slot, value in enumerate(pair_sums(distances, gated, mixed, sign, False)):
                    if value is None:
                        value = (jnp.zeros_like(own_g[re, :]),) * 2
                    put((re, im), 2 + slot, value)
                return _

            lax.fori_loop(0, count, lags, 0)


def early(pos, windows, gated, mixed, seg):
    width = gated[0].shape[1]
    rows = seg // 2
    mid = windows.shape[0] // 2

    def window(index):
        return pl.BlockSpec((1, rows, width), lambda i, pos: (index(pos[0]), i, 0))

    group = pl.BlockSpec((rows, width), lambda i, pos: (i, 0))
    return pl.pallas_call(
        early_kernel,
        grid_spec=pltpu.PrefetchScalarGridSpec(
            num_scalar_prefetch=1,
            grid=(4,),
            in_specs=[
                window(lambda p: mid),
                window(lambda p: jnp.where(p < 2, mid + 1, mid - 1)),
                window(lambda p: jnp.where(p < 2, mid - 1, mid + 1)),
                window(lambda p: jnp.where(p < 2, mid - 2, mid + 2)),
            ]
            + [group] * 7,
            out_specs=pl.BlockSpec((4, rows, width), lambda i, pos: (0, i, 0)),
        ),
        out_shape=f32(4, 2 * seg, width),
        compiler_params=params(14),
        cost_estimate=cost(200 * seg * width, 120 * seg * width),
        name="early",
    )(pos, *[windows] * 4, *gated, *mixed)


def late_kernel(
    pos_ref, inverse_ref, acc_ref, win_ref, three_g, two_g, own_m, outer_m, next_m, *rest
):
    two_m, gated_ref, mixed_ref, skip_ref, up_ref, query_out, filter_out, back_out, x_high, x_low, z_ref = rest
    group = pl.program_id(0)
    pos, sign = pos_ref[0], group_sign()
    rows, width = own_m.shape
    sub = rows // 2

    def put(at, slot, value):
        for rows_at, part in zip(at, value):
            high, low = split(part)
            x_high[rows_at, slot * width : (slot + 1) * width] = high
            x_low[rows_at, slot * width : (slot + 1) * width] = low

    for where, distances in enumerate(PAIRS):

        @pl.when(pos == where)
        def _():
            def lags(tile, _):
                re, im, read = tile_reader(tile, sub)

                gated = [None, None, None, functools.partial(read, two_g), functools.partial(read, three_g)]
                mixed = [functools.partial(read, ref) for ref in (own_m, outer_m, next_m, two_m)]
                total = [read(acc_ref, slot) for slot in range(4)]
                if where in (0, 3):
                    total[0] = add(total[0], mul(read(win_ref, 0), gated[THREE]()))
                else:
                    total[1] = add(total[1], conj_mul(read(win_ref, 0), mixed[TWO]()))
                for slot, value in enumerate(pair_sums(distances, gated, mixed, sign, True)):
                    if value is not None:
                        total[2 + slot] = add(total[2 + slot], value)
                for slot, value in enumerate(total):
                    put((re, im), slot, value)
                return _

            lax.fori_loop(0, sub // TILE, lags, 0)

    dot = functools.partial(jnp.dot, preferred_element_type=jnp.float32)
    t_high, t_low = inverse_ref[0, 0], inverse_ref[1, 0]
    for slot in range(4):
        cols = slice(slot * width, (slot + 1) * width)
        z_ref[group, :, cols] = (
            dot(t_high, x_high[:, cols]) + dot(t_high, x_low[:, cols]) + dot(t_low, x_high[:, cols])
        )

    @pl.when(group == 3)
    def _():
        seg = 4 * sub
        for slot in range(4):
            cols = slice(slot * width, (slot + 1) * width)
            quarters = gather_quarters(
                [z_ref[g, :sub, cols] for g in range(4)], [z_ref[g, sub:, cols] for g in range(4)]
            )
            for i, quarter in enumerate(quarters):
                at = slice(i * sub, (i + 1) * sub)
                if slot == 0:
                    query_out[at, :] = up_ref[at, :] * (quarter + skip_ref[...] * gated_ref[at, :])
                elif slot == 1:
                    back_out[at, :] = quarter + skip_ref[...] * mixed_ref[at, :]
                else:
                    base = (slot - 2) * seg + i * sub
                    filter_out[base : base + sub, :] = quarter


def late(pos, inverse, acc, windows, three_g, two_g, own_m, outer_m, next_m, two_m, gated, mixed, skip, upstream):
    seg, width = upstream.shape
    rows = seg // 2
    mid = windows.shape[0] // 2

    def win_at(i, pos):
        p = pos[0]
        ends = jnp.where(p == 0, mid - 3, mid + 3)
        return jnp.where(p == 1, mid + 2, jnp.where(p == 2, mid - 2, ends)), i, 0

    group = pl.BlockSpec((rows, width), lambda i, pos: (i, 0))
    return pl.pallas_call(
        late_kernel,
        grid_spec=pltpu.PrefetchScalarGridSpec(
            num_scalar_prefetch=1,
            grid=(4,),
            in_specs=[
                pl.BlockSpec((2, 1, rows, rows), lambda i, pos: (0, i, 0, 0)),
                pl.BlockSpec((4, rows, width), lambda i, pos: (0, i, 0)),
                pl.BlockSpec((1, rows, width), win_at),
                *[group] * 6,
                whole_spec((seg, width)),
                whole_spec((seg, width)),
                whole_spec((1, width)),
                whole_spec((seg, width)),
            ],
            out_specs=[whole_spec((seg, width)), whole_spec((2 * seg, width)), whole_spec((seg, width))],
            scratch_shapes=[
                pltpu.VMEM((rows, 4 * width), jnp.bfloat16),
                pltpu.VMEM((rows, 4 * width), jnp.bfloat16),
                pltpu.VMEM((4, rows, 4 * width), jnp.float32),
            ],
        ),
        out_shape=[f32(seg, width), f32(2 * seg, width), f32(seg, width)],
        compiler_params=params(20),
        cost_estimate=cost(12 * seg * seg * width * 2, 100 * seg * width),
        name="late",
    )(pos, inverse, acc, windows, three_g, two_g, own_m, outer_m, next_m, two_m, gated, mixed, skip, upstream)


def finish_kernel(back_ref, key_ref, values_ref, partial_ref, pair_ref, other_ref, key_out, value_out, skip_out):
    back = back_ref[...] + partial_ref[...]
    key_out[...] = back * values_ref[...]
    value_out[...] = back * key_ref[...]
    skip_out[...] = jnp.sum(pair_ref[...] + other_ref[...], axis=0, keepdims=True)


def finish(back, key_gate, values, partial, pair, other):
    seg, width = back.shape
    steps = 2
    block = pl.BlockSpec((seg // steps, width), lambda i: (i, 0))
    strip = whole_spec((8, width))
    return pl.pallas_call(
        finish_kernel,
        grid=(steps,),
        in_specs=[block] * 4 + [strip] * 2,
        out_specs=[block, block, whole_spec((1, width))],
        out_shape=[f32(seg, width), f32(seg, width), f32(1, width)],
        compiler_params=params(12),
        cost_estimate=cost(3 * seg * width, 24 * seg * width),
        name="finish",
    )(back, key_gate, values, partial, pair, other)


def send(x, *pairs):
    return lax.ppermute(x, "ctx", list(pairs))


def across(x):
    return send(x, (1, 2), (2, 1))


def outward(x):
    return send(x, (1, 0), (2, 3))


def beside(x):
    return send(x, (0, 1), (1, 0), (2, 3), (3, 2))


def local_line(query_gate, key_gate, values, filter_taps, skip_gain, upstream):
    seg, width = values.shape
    forward_np, inverse_np = tables(seg)
    table, inverse = jnp.asarray(forward_np), jnp.asarray(inverse_np)
    pos = lax.axis_index("ctx").astype(jnp.int32).reshape(1)
    after = lax.optimization_barrier

    gated = key_gate * values
    side, over = beside(gated), across(gated)
    mixed, strip = mix(gated, upstream, query_gate)
    side_x, over_x = beside(mixed), across(mixed)
    own_g, own_m = dft(pos, table, seg, gated), dft(pos, table, seg, mixed)
    side, over, filter_taps, own_g, own_m = after((side, over, filter_taps, own_g, own_m))

    over_two, out_two = across(side), outward(over)
    outer_g = dft(pos, table, seg, side, choose=True)
    next_g = dft(pos, table, seg, over, side, choose=True)
    windows = taps_spectra(table, filter_taps, seg)
    side_x, over_x, windows, outer_g, next_g, strip = after((side_x, over_x, windows, outer_g, next_g, strip))

    two_x = across(side_x)
    beside_strip = beside(strip)
    outer_m = dft(pos, table, seg, side_x, choose=True)
    next_m = dft(pos, table, seg, over_x, side_x, choose=True)
    over_two, outer_m, next_m, beside_strip = after((over_two, outer_m, next_m, beside_strip))

    three = outward(over_two)
    pair = strip + beside_strip
    two_g = dft(pos, table, seg, over_two, out_two)
    acc = early(pos, windows, (own_g, outer_g, next_g, two_g), (own_m, outer_m, next_m), seg)
    two_x, acc = after((two_x, acc))

    two_m, partial = back_partial(pos, table, inverse, windows, next_m, two_x, seg)
    partial, pair = after((partial, pair))
    partial = outward(partial)
    other = send(pair, (0, 2), (2, 0), (1, 3), (3, 1))
    three_g = dft(pos, table, seg, three)
    query_grad, filter_grad, back = late(
        pos, inverse, acc, windows, three_g, two_g, own_m, outer_m, next_m, two_m,
        gated, mixed, skip_gain[None, :], upstream,
    )
    key_grad, value_grad, skip_grad = finish(back, key_gate, values, partial, pair, other)
    return (query_grad, key_grad, value_grad, filter_grad, skip_grad[0])


def matmul(left, right):
    return jnp.dot(left, right, preferred_element_type=jnp.float32, precision=lax.Precision.HIGHEST)


def forward_table(seg_len, count, offset):
    num_bins = seg_len + 1
    period = 2 * seg_len
    bin_index = lax.broadcasted_iota(jnp.int32, (num_bins, count), 0)
    pos_index = lax.broadcasted_iota(jnp.int32, (num_bins, count), 1) + offset
    angles = (bin_index * pos_index % period).astype(jnp.float32) * (2.0 * math.pi / period)
    return jnp.concatenate([jnp.cos(angles), -jnp.sin(angles)], axis=0)


def inverse_table(seg_len, count, offset):
    num_bins = seg_len + 1
    period = 2 * seg_len
    pos_index = lax.broadcasted_iota(jnp.int32, (count, num_bins), 0) + offset
    bin_index = lax.broadcasted_iota(jnp.int32, (count, num_bins), 1)
    angles = (bin_index * pos_index % period).astype(jnp.float32) * (2.0 * math.pi / period)
    weights = jnp.where((bin_index == 0) | (bin_index == seg_len), 1.0, 2.0) / period
    return jnp.concatenate([weights * jnp.cos(angles), -weights * jnp.sin(angles)], axis=1)


def times_spec(first, second):
    num_bins = first.shape[0] // 2
    real_a, imag_a = (first[:num_bins], first[num_bins:])
    real_b, imag_b = (second[:num_bins], second[num_bins:])
    return jnp.concatenate(
        [real_a * real_b - imag_a * imag_b, real_a * imag_b + imag_a * real_b], axis=0
    )


def conj_times(first, second):
    num_bins = first.shape[0] // 2
    real_a, imag_a = (first[:num_bins], first[num_bins:])
    real_b, imag_b = (second[:num_bins], second[num_bins:])
    return jnp.concatenate(
        [real_a * real_b + imag_a * imag_b, real_a * imag_b - imag_a * real_b], axis=0
    )


def pick(stack, index):
    return lax.dynamic_index_in_dim(stack, index, 0, keepdims=False)


def local(query_gate, key_gate, values, filter_taps, skip_gain, upstream):
    seg_len, width_dev = values.shape
    cycle_size = lax.axis_size("ctx")
    position = lax.axis_index("ctx")
    history = seg_len * cycle_size
    gated = key_gate * values
    mixed_grad = upstream * query_gate
    table_low = forward_table(seg_len, seg_len, 0)
    table_high = forward_table(seg_len, seg_len, seg_len)
    table_taps = forward_table(seg_len, 2 * seg_len, 0)
    back_low = inverse_table(seg_len, seg_len, 0)
    back_high = inverse_table(seg_len, seg_len, seg_len)
    back_full = inverse_table(seg_len, 2 * seg_len, 0)
    own_grad_spec = matmul(table_high, mixed_grad)
    spec_rows = 2 * (seg_len + 1)

    def taps_spec(lag_block):
        start_row = (lag_block - 1) * seg_len + history
        window = lax.dynamic_slice_in_dim(filter_taps, start_row, 2 * seg_len, 0)
        return matmul(table_taps, window)

    def visit(carry, gated_spec, grad_spec, source):
        acc_conv, acc_back, partial_value = carry
        lag_block = position - source
        acc_conv = acc_conv + times_spec(taps_spec(lag_block), gated_spec)
        acc_back = acc_back + conj_times(taps_spec(-lag_block), grad_spec)
        segment = matmul(back_full, conj_times(gated_spec, own_grad_spec))
        start_row = (lag_block - 1) * seg_len + history
        current = lax.dynamic_slice_in_dim(partial_value, start_row, 2 * seg_len, 0)
        partial_value = lax.dynamic_update_slice_in_dim(
            partial_value, current + segment, start_row, 0
        )
        return (acc_conv, acc_back, partial_value)

    initial = (
        jnp.zeros((spec_rows, width_dev), jnp.float32),
        jnp.zeros((spec_rows, width_dev), jnp.float32),
        jnp.zeros((2 * history, width_dev), jnp.float32),
    )
    own_gated_spec = matmul(table_low, gated)
    pieces = (
        lax.all_gather(own_gated_spec[None], "ctx", axis=0, tiled=True),
        lax.all_gather(own_grad_spec[None], "ctx", axis=0, tiled=True),
    )

    def advance(member, state):
        return visit(state, pick(pieces[0], member), pick(pieces[1], member), member)

    folded = lax.fori_loop(0, pieces[0].shape[0], advance, initial)
    acc_conv, acc_back, partial_value = folded
    filter_grad = lax.psum_scatter(partial_value, "ctx", scatter_dimension=0, tiled=True)
    conv = matmul(back_high, acc_conv)
    back = matmul(back_low, acc_back) + skip_gain[None, :] * mixed_grad
    query_grad = upstream * (conv + skip_gain[None, :] * gated)
    key_grad = back * values
    value_grad = back * key_gate
    skip_grad = lax.psum(jnp.sum(mixed_grad * gated, axis=0), "ctx")
    return (query_grad, key_grad, value_grad, filter_grad, skip_grad)


def solution(mesh):
    in_specs = (
        P(("groups", "ctx"), "chan"),
        P(("groups", "ctx"), "chan"),
        P(("groups", "ctx"), "chan"),
        P(None, "chan"),
        P("chan"),
        P(("groups", "ctx"), "chan"),
    )
    out_specs = (
        P(("groups", "ctx"), "chan"),
        P(("groups", "ctx"), "chan"),
        P(("groups", "ctx"), "chan"),
        P(("groups", "ctx"), "chan"),
        P(("groups", "chan")),
    )
    body = local_line if mesh.shape["ctx"] == 4 else local
    return jax.shard_map(body, mesh=mesh, in_specs=in_specs, out_specs=out_specs, check_vma=False)
```

```python
import functools
import math

import jax
import jax.numpy as jnp
import ml_dtypes
import numpy as np
from jax import lax
from jax.experimental import pallas as pl
from jax.experimental.pallas import tpu as pltpu
from jax.sharding import PartitionSpec as P

COS1, SIN1, HALF = math.cos(math.pi / 8), math.sin(math.pi / 8), math.sqrt(0.5)


def split_np(table):
    high = table.astype(ml_dtypes.bfloat16)
    low = (table - high.astype(np.float64)).astype(ml_dtypes.bfloat16)
    return np.stack([high, low])


def tables(seg):
    sub = seg // 4
    bins, pos = np.arange(sub)[:, None], np.arange(sub)[None, :]
    forward = []
    for group in range(4):
        angle = 2 * np.pi * pos * (8 * bins + group + 0.5) / (2 * seg)
        cos, sin = np.cos(angle), np.sin(angle)
        forward.append(np.block([[cos, -sin], [-sin, -cos]]))
    forward = np.stack(forward)
    inverse = forward.transpose(0, 2, 1) / seg
    return split_np(forward), split_np(inverse)


def split(x):
    high = x.astype(jnp.bfloat16)
    return high, (x - high.astype(jnp.float32)).astype(jnp.bfloat16)


def dot3(table_ref, group, high, low):
    t_high, t_low = table_ref[0, group], table_ref[1, group]
    dot = functools.partial(jnp.dot, preferred_element_type=jnp.float32)
    return dot(t_high, high) + dot(t_high, low) + dot(t_low, high)


def spread(x):
    sub = x.shape[0] // 4
    x0, x1, x2, x3 = (x[i * sub : (i + 1) * sub] for i in range(4))
    u, p, s, q, t = HALF * x2, COS1 * x1, SIN1 * x1, COS1 * x3, SIN1 * x3
    a, b, pt, sq, pmt, spq = x0 + u, x0 - u, p + t, s - q, p - t, s + q
    pairs = ((a + pt, spq + u), (b + sq, pmt + u), (b - sq, pmt - u), (a - pt, spq - u))
    return [jnp.concatenate(pair, axis=0) for pair in pairs]


def gather_quarters(re, im):
    e03, d03, e12, d12 = re[0] + re[3], re[0] - re[3], re[1] + re[2], re[1] - re[2]
    f03, g03, f12, g12 = im[0] + im[3], im[0] - im[3], im[1] + im[2], im[1] - im[2]
    return (
        e03 + e12,
        COS1 * (d03 + f12) + SIN1 * (d12 + f03),
        HALF * (e03 - e12 + g03 + g12),
        SIN1 * (d03 - f12) + COS1 * (f03 - d12),
    )


def transform(x, table_ref, store):
    for group, part in enumerate(spread(x)):
        store(group, dot3(table_ref, group, *split(part)))


def cost(flops, nbytes):
    return pl.CostEstimate(flops=int(flops), bytes_accessed=int(nbytes), transcendentals=0)


def params(mib):
    return pltpu.CompilerParams(vmem_limit_bytes=mib << 20)


def whole_spec(shape):
    return pl.BlockSpec(shape, lambda *_: (0,) * len(shape))


def f32(*shape):
    return jax.ShapeDtypeStruct(shape, jnp.float32)


def mix_kernel(gated_ref, up_ref, query_ref, mixed_ref, sum_ref):
    seg, width = gated_ref.shape
    mixed = up_ref[...] * query_ref[...]
    mixed_ref[...] = mixed
    sum_ref[...] = jnp.sum((gated_ref[...] * mixed).reshape(seg // 8, 8, width), axis=0)


def mix(gated, upstream, query_gate):
    seg, width = gated.shape
    block = whole_spec((seg, width))
    return pl.pallas_call(
        mix_kernel,
        grid=(1,),
        in_specs=[block] * 3,
        out_specs=[block, whole_spec((8, width))],
        out_shape=[f32(seg, width), f32(8, width)],
        compiler_params=params(12),
        cost_estimate=cost(4 * seg * width, 16 * seg * width),
        name="mix",
    )(gated, upstream, query_gate)


def dft_kernel(choose, pos_ref, table_ref, *refs):
    *x_refs, out_ref = refs
    rows = out_ref.shape[0] // 4
    inner = jnp.logical_or(pos_ref[0] == 1, pos_ref[0] == 2)

    def store(group, value):
        out_ref[group * rows : (group + 1) * rows, :] = value

    x = x_refs[0][...]
    if choose:
        x = jnp.where(inner, x, x_refs[1][...] if len(x_refs) == 2 else 0.0)
    elif len(x_refs) == 2:
        x = x + x_refs[1][...]
    transform(x, table_ref, store)


def dft(pos, table, seg, *xs, choose=False):
    width = xs[0].shape[1]
    return pl.pallas_call(
        functools.partial(dft_kernel, choose),
        grid_spec=pltpu.PrefetchScalarGridSpec(
            num_scalar_prefetch=1,
            grid=(1,),
            in_specs=[whole_spec(table.shape)] + [whole_spec((seg, width))] * len(xs),
            out_specs=whole_spec((2 * seg, width)),
        ),
        out_shape=f32(2 * seg, width),
        compiler_params=params(12),
        cost_estimate=cost(3 * seg * seg * width * 2, 12 * seg * width),
        name="dft",
    )(pos, table, *xs)


def taps_kernel(table_ref, x_ref, out_ref, last_ref):
    step = pl.program_id(0)
    rows = out_ref.shape[1] // 4
    sub = rows // 2

    def store(group, value):
        base = group * rows
        sign = 1.0 if group % 2 == 0 else -1.0
        re, im = slice(base, base + sub), slice(base + sub, base + rows)
        out_ref[0, re, :] = value[:sub] - sign * last_ref[im, :]
        out_ref[0, im, :] = value[sub:] + sign * last_ref[re, :]
        last_ref[base : base + rows, :] = value

    @pl.when(step == 0)
    def _():
        last_ref[...] = jnp.zeros_like(last_ref)

    transform(x_ref[...], table_ref, store)


def taps_spectra(table, taps, seg):
    width = taps.shape[1]
    blocks = taps.shape[0] // seg
    return pl.pallas_call(
        taps_kernel,
        grid=(blocks,),
        in_specs=[whole_spec(table.shape), pl.BlockSpec((seg, width), lambda i: (i, 0))],
        out_specs=pl.BlockSpec((1, 2 * seg, width), lambda i: (jnp.maximum(i - 1, 0), 0, 0)),
        out_shape=jax.ShapeDtypeStruct((blocks - 1, 2 * seg, width), jnp.float32),
        scratch_shapes=[pltpu.VMEM((2 * seg, width), jnp.float32)],
        compiler_params=params(14),
        cost_estimate=cost(blocks * 3 * seg * seg * width * 2, blocks * 12 * seg * width),
        name="taps",
    )(table, taps)


def conj_mul(a, b):
    return a[0] * b[0] + a[1] * b[1], a[0] * b[1] - a[1] * b[0]


def mul(a, b):
    return a[0] * b[0] - a[1] * b[1], a[0] * b[1] + a[1] * b[0]


def add(a, b):
    return a[0] + b[0], a[1] + b[1]


def partial_kernel(
    pos_ref, table_ref, inverse_ref, win_near, win_far, next_ref, x_ref, far_ref, out_ref, z_ref
):
    rows = far_ref.shape[0] // 4
    sub = rows // 2
    for group, part in enumerate(spread(x_ref[...])):
        base = group * rows
        far = dot3(table_ref, group, *split(part))
        far_ref[base : base + rows, :] = far
        re, im = slice(base, base + sub), slice(base + sub, base + rows)
        near = (next_ref[re, :], next_ref[im, :])
        total = add(
            conj_mul((win_near[0, re, :], win_near[0, im, :]), near),
            conj_mul((win_far[0, re, :], win_far[0, im, :]), (far[:sub], far[sub:])),
        )
        z_ref[group] = dot3(inverse_ref, group, *split(jnp.concatenate(total, axis=0)))
    quarters = gather_quarters([z_ref[g, :sub] for g in range(4)], [z_ref[g, sub:] for g in range(4)])
    for i, quarter in enumerate(quarters):
        out_ref[i * sub : (i + 1) * sub, :] = quarter


def back_partial(pos, table, inverse, windows, next_m, x, seg):
    width = x.shape[1]
    n = (windows.shape[0] + 1) // 2

    def window(distance):
        return pl.BlockSpec(
            (1, 2 * seg, width),
            lambda i, pos: (jnp.where(pos[0] == 1, n - 1 + distance, n - 1 - distance), 0, 0),
        )

    return pl.pallas_call(
        partial_kernel,
        grid_spec=pltpu.PrefetchScalarGridSpec(
            num_scalar_prefetch=1,
            grid=(1,),
            in_specs=[
                whole_spec(table.shape),
                whole_spec(inverse.shape),
                window(2),
                window(3),
                whole_spec((2 * seg, width)),
                whole_spec((seg, width)),
            ],
            out_specs=[whole_spec((2 * seg, width)), whole_spec((seg, width))],
            scratch_shapes=[pltpu.VMEM((4, seg // 2, width), jnp.float32)],
        ),
        out_shape=[f32(2 * seg, width), f32(seg, width)],
        compiler_params=params(24),
        cost_estimate=cost(6 * seg * seg * width * 2, 24 * seg * width),
        name="partial",
    )(pos, table, inverse, windows, windows, next_m, x)


OWN, OUTER, NEXT, TWO, THREE = range(5)
PAIRS = (
    ((), ((OWN, THREE),), ((OWN, TWO), (NEXT, THREE))),
    (
        ((OUTER, NEXT), (OWN, TWO)),
        ((OUTER, OWN), (OWN, NEXT), (NEXT, TWO)),
        ((OUTER, OUTER), (OWN, OWN), (NEXT, NEXT), (TWO, TWO)),
    ),
    (
        ((TWO, TWO), (NEXT, NEXT), (OWN, OWN), (OUTER, OUTER)),
        ((NEXT, TWO), (OWN, NEXT), (OUTER, OWN)),
        ((OWN, TWO), (OUTER, NEXT)),
    ),
    (((NEXT, THREE), (OWN, TWO)), ((OWN, THREE),), ()),
)


def is_late(pair):
    return pair[0] == TWO or pair[1] == THREE


def pair_sums(distances, gated, mixed, sign, late):
    total = []
    for pairs in distances:
        value = None
        for m, g in pairs:
            if is_late((m, g)) == late:
                term = conj_mul(gated[g](), mixed[m]())
                value = term if value is None else add(value, term)
        total.append(value)
    out = []
    for low, high in zip(total[:2], total[1:]):
        if high is not None:
            turned = (sign * high[1], -sign * high[0])
            low = turned if low is None else add(low, turned)
        out.append(low)
    return out


TILE = 16


def tile_reader(tile, sub):
    re = pl.ds(pl.multiple_of(tile * TILE, TILE), TILE)
    im = pl.ds(pl.multiple_of(sub + tile * TILE, TILE), TILE)

    def read(ref, *lead):
        return ref[(*lead, re, slice(None))], ref[(*lead, im, slice(None))]

    return re, im, read


def group_sign():
    return jnp.where(pl.program_id(0) % 2 == 0, 1.0, -1.0)


def early_kernel(
    pos_ref, win_own, win_outer, win_next, win_two, own_g, outer_g, next_g, two_g, own_m, outer_m, next_m, out_ref
):
    pos, sign = pos_ref[0], group_sign()
    rows = own_g.shape[0]
    sub = rows // 2
    count = sub // TILE

    def put(at, slot, value):
        re, im = at
        out_ref[slot, re, :] = value[0]
        out_ref[slot, im, :] = value[1]

    def sums(tile, _):
        re, im, read = tile_reader(tile, sub)
        own, outer, ahead = read(win_own, 0), read(win_outer, 0), read(win_next, 0)
        conv = add(mul(own, read(own_g)), mul(outer, read(outer_g)))
        conv = add(conv, add(mul(ahead, read(next_g)), mul(read(win_two, 0), read(two_g))))
        put((re, im), 0, conv)
        back = add(conj_mul(own, read(own_m)), conj_mul(ahead, read(outer_m)))
        put((re, im), 1, add(back, conj_mul(outer, read(next_m))))
        return _

    lax.fori_loop(0, count, sums, 0)
    for where, distances in enumerate(PAIRS):

        @pl.when(pos == where)
        def _():
            def lags(tile, _):
                re, im, read = tile_reader(tile, sub)
                gated = [functools.partial(read, ref) for ref in (own_g, outer_g, next_g, two_g)]
                mixed = [functools.partial(read, ref) for ref in (own_m, outer_m, next_m)]
                for slot, value in enumerate(pair_sums(distances, gated, mixed, sign, False)):
                    if value is None:
                        value = (jnp.zeros_like(own_g[re, :]),) * 2
                    put((re, im), 2 + slot, value)
                return _

            lax.fori_loop(0, count, lags, 0)


def early(pos, windows, gated, mixed, seg):
    width = gated[0].shape[1]
    rows = seg // 2
    mid = windows.shape[0] // 2

    def window(index):
        return pl.BlockSpec((1, rows, width), lambda i, pos: (index(pos[0]), i, 0))

    group = pl.BlockSpec((rows, width), lambda i, pos: (i, 0))
    return pl.pallas_call(
        early_kernel,
        grid_spec=pltpu.PrefetchScalarGridSpec(
            num_scalar_prefetch=1,
            grid=(4,),
            in_specs=[
                window(lambda p: mid),
                window(lambda p: jnp.where(p < 2, mid + 1, mid - 1)),
                window(lambda p: jnp.where(p < 2, mid - 1, mid + 1)),
                window(lambda p: jnp.where(p < 2, mid - 2, mid + 2)),
            ]
            + [group] * 7,
            out_specs=pl.BlockSpec((4, rows, width), lambda i, pos: (0, i, 0)),
        ),
        out_shape=f32(4, 2 * seg, width),
        compiler_params=params(14),
        cost_estimate=cost(200 * seg * width, 120 * seg * width),
        name="early",
    )(pos, *[windows] * 4, *gated, *mixed)


def late_kernel(
    pos_ref, inverse_ref, acc_ref, win_ref, three_g, two_g, own_m, outer_m, next_m, *rest
):
    two_m, gated_ref, mixed_ref, skip_ref, up_ref, query_out, filter_out, back_out, x_high, x_low, z_ref = rest
    group = pl.program_id(0)
    pos, sign = pos_ref[0], group_sign()
    rows, width = own_m.shape
    sub = rows // 2

    def put(at, slot, value):
        for rows_at, part in zip(at, value):
            high, low = split(part)
            x_high[rows_at, slot * width : (slot + 1) * width] = high
            x_low[rows_at, slot * width : (slot + 1) * width] = low

    for where, distances in enumerate(PAIRS):

        @pl.when(pos == where)
        def _():
            def lags(tile, _):
                re, im, read = tile_reader(tile, sub)

                gated = [None, None, None, functools.partial(read, two_g), functools.partial(read, three_g)]
                mixed = [functools.partial(read, ref) for ref in (own_m, outer_m, next_m, two_m)]
                total = [read(acc_ref, slot) for slot in range(4)]
                if where in (0, 3):
                    total[0] = add(total[0], mul(read(win_ref, 0), gated[THREE]()))
                else:
                    total[1] = add(total[1], conj_mul(read(win_ref, 0), mixed[TWO]()))
                for slot, value in enumerate(pair_sums(distances, gated, mixed, sign, True)):
                    if value is not None:
                        total[2 + slot] = add(total[2 + slot], value)
                for slot, value in enumerate(total):
                    put((re, im), slot, value)
                return _

            lax.fori_loop(0, sub // TILE, lags, 0)

    dot = functools.partial(jnp.dot, preferred_element_type=jnp.float32)
    t_high, t_low = inverse_ref[0, 0], inverse_ref[1, 0]
    for slot in range(4):
        cols = slice(slot * width, (slot + 1) * width)
        z_ref[group, :, cols] = (
            dot(t_high, x_high[:, cols]) + dot(t_high, x_low[:, cols]) + dot(t_low, x_high[:, cols])
        )

    @pl.when(group == 3)
    def _():
        seg = 4 * sub
        for slot in range(4):
            cols = slice(slot * width, (slot + 1) * width)
            quarters = gather_quarters(
                [z_ref[g, :sub, cols] for g in range(4)], [z_ref[g, sub:, cols] for g in range(4)]
            )
            for i, quarter in enumerate(quarters):
                at = slice(i * sub, (i + 1) * sub)
                if slot == 0:
                    query_out[at, :] = up_ref[at, :] * (quarter + skip_ref[...] * gated_ref[at, :])
                elif slot == 1:
                    back_out[at, :] = quarter + skip_ref[...] * mixed_ref[at, :]
                else:
                    base = (slot - 2) * seg + i * sub
                    filter_out[base : base + sub, :] = quarter


def late(pos, inverse, acc, windows, three_g, two_g, own_m, outer_m, next_m, two_m, gated, mixed, skip, upstream):
    seg, width = upstream.shape
    rows = seg // 2
    mid = windows.shape[0] // 2

    def win_at(i, pos):
        p = pos[0]
        ends = jnp.where(p == 0, mid - 3, mid + 3)
        return jnp.where(p == 1, mid + 2, jnp.where(p == 2, mid - 2, ends)), i, 0

    group = pl.BlockSpec((rows, width), lambda i, pos: (i, 0))
    return pl.pallas_call(
        late_kernel,
        grid_spec=pltpu.PrefetchScalarGridSpec(
            num_scalar_prefetch=1,
            grid=(4,),
            in_specs=[
                pl.BlockSpec((2, 1, rows, rows), lambda i, pos: (0, i, 0, 0)),
                pl.BlockSpec((4, rows, width), lambda i, pos: (0, i, 0)),
                pl.BlockSpec((1, rows, width), win_at),
                *[group] * 6,
                whole_spec((seg, width)),
                whole_spec((seg, width)),
                whole_spec((1, width)),
                whole_spec((seg, width)),
            ],
            out_specs=[whole_spec((seg, width)), whole_spec((2 * seg, width)), whole_spec((seg, width))],
            scratch_shapes=[
                pltpu.VMEM((rows, 4 * width), jnp.bfloat16),
                pltpu.VMEM((rows, 4 * width), jnp.bfloat16),
                pltpu.VMEM((4, rows, 4 * width), jnp.float32),
            ],
        ),
        out_shape=[f32(seg, width), f32(2 * seg, width), f32(seg, width)],
        compiler_params=params(20),
        cost_estimate=cost(12 * seg * seg * width * 2, 100 * seg * width),
        name="late",
    )(pos, inverse, acc, windows, three_g, two_g, own_m, outer_m, next_m, two_m, gated, mixed, skip, upstream)


def finish_kernel(back_ref, key_ref, values_ref, partial_ref, pair_ref, other_ref, key_out, value_out, skip_out):
    back = back_ref[...] + partial_ref[...]
    key_out[...] = back * values_ref[...]
    value_out[...] = back * key_ref[...]
    skip_out[...] = jnp.sum(pair_ref[...] + other_ref[...], axis=0, keepdims=True)


def finish(back, key_gate, values, partial, pair, other):
    seg, width = back.shape
    steps = 2
    block = pl.BlockSpec((seg // steps, width), lambda i: (i, 0))
    strip = whole_spec((8, width))
    return pl.pallas_call(
        finish_kernel,
        grid=(steps,),
        in_specs=[block] * 4 + [strip] * 2,
        out_specs=[block, block, whole_spec((1, width))],
        out_shape=[f32(seg, width), f32(seg, width), f32(1, width)],
        compiler_params=params(12),
        cost_estimate=cost(3 * seg * width, 24 * seg * width),
        name="finish",
    )(back, key_gate, values, partial, pair, other)


def send(x, *pairs):
    return lax.ppermute(x, "ctx", list(pairs))


def across(x):
    return send(x, (1, 2), (2, 1))


def outward(x):
    return send(x, (1, 0), (2, 3))


def beside(x):
    return send(x, (0, 1), (1, 0), (2, 3), (3, 2))


def local_line(query_gate, key_gate, values, filter_taps, skip_gain, upstream):
    seg, width = values.shape
    forward_np, inverse_np = tables(seg)
    table, inverse = jnp.asarray(forward_np), jnp.asarray(inverse_np)
    pos = lax.axis_index("ctx").astype(jnp.int32).reshape(1)
    after = lax.optimization_barrier

    gated = key_gate * values
    side, over = beside(gated), across(gated)
    mixed, strip = mix(gated, upstream, query_gate)
    side_x, over_x = beside(mixed), across(mixed)
    own_g, own_m = dft(pos, table, seg, gated), dft(pos, table, seg, mixed)
    side, over, filter_taps, own_g, own_m = after((side, over, filter_taps, own_g, own_m))

    over_two, out_two = across(side), outward(over)
    outer_g = dft(pos, table, seg, side, choose=True)
    next_g = dft(pos, table, seg, over, side, choose=True)
    windows = taps_spectra(table, filter_taps, seg)
    side_x, over_x, windows, outer_g, next_g, strip = after((side_x, over_x, windows, outer_g, next_g, strip))

    beside_strip = beside(strip)
    outer_m = dft(pos, table, seg, side_x, choose=True)
    next_m = dft(pos, table, seg, over_x, side_x, choose=True)
    side_x, outer_m, next_m = after((side_x, outer_m, next_m))
    two_x = across(side_x)
    over_two, outer_m, next_m, beside_strip = after((over_two, outer_m, next_m, beside_strip))

    three = outward(over_two)
    pair = strip + beside_strip
    two_g = dft(pos, table, seg, over_two, out_two)
    acc = early(pos, windows, (own_g, outer_g, next_g, two_g), (own_m, outer_m, next_m), seg)
    two_x, acc = after((two_x, acc))

    two_m, partial = back_partial(pos, table, inverse, windows, next_m, two_x, seg)
    partial, pair = after((partial, pair))
    partial = outward(partial)
    other = send(pair, (0, 2), (2, 0), (1, 3), (3, 1))
    three_g = dft(pos, table, seg, three)
    query_grad, filter_grad, back = late(
        pos, inverse, acc, windows, three_g, two_g, own_m, outer_m, next_m, two_m,
        gated, mixed, skip_gain[None, :], upstream,
    )
    key_grad, value_grad, skip_grad = finish(back, key_gate, values, partial, pair, other)
    return (query_grad, key_grad, value_grad, filter_grad, skip_grad[0])


def matmul(left, right):
    return jnp.dot(left, right, preferred_element_type=jnp.float32, precision=lax.Precision.HIGHEST)


def forward_table(seg_len, count, offset):
    num_bins = seg_len + 1
    period = 2 * seg_len
    bin_index = lax.broadcasted_iota(jnp.int32, (num_bins, count), 0)
    pos_index = lax.broadcasted_iota(jnp.int32, (num_bins, count), 1) + offset
    angles = (bin_index * pos_index % period).astype(jnp.float32) * (2.0 * math.pi / period)
    return jnp.concatenate([jnp.cos(angles), -jnp.sin(angles)], axis=0)


def inverse_table(seg_len, count, offset):
    num_bins = seg_len + 1
    period = 2 * seg_len
    pos_index = lax.broadcasted_iota(jnp.int32, (count, num_bins), 0) + offset
    bin_index = lax.broadcasted_iota(jnp.int32, (count, num_bins), 1)
    angles = (bin_index * pos_index % period).astype(jnp.float32) * (2.0 * math.pi / period)
    weights = jnp.where((bin_index == 0) | (bin_index == seg_len), 1.0, 2.0) / period
    return jnp.concatenate([weights * jnp.cos(angles), -weights * jnp.sin(angles)], axis=1)


def times_spec(first, second):
    num_bins = first.shape[0] // 2
    real_a, imag_a = (first[:num_bins], first[num_bins:])
    real_b, imag_b = (second[:num_bins], second[num_bins:])
    return jnp.concatenate(
        [real_a * real_b - imag_a * imag_b, real_a * imag_b + imag_a * real_b], axis=0
    )


def conj_times(first, second):
    num_bins = first.shape[0] // 2
    real_a, imag_a = (first[:num_bins], first[num_bins:])
    real_b, imag_b = (second[:num_bins], second[num_bins:])
    return jnp.concatenate(
        [real_a * real_b + imag_a * imag_b, real_a * imag_b - imag_a * real_b], axis=0
    )


def pick(stack, index):
    return lax.dynamic_index_in_dim(stack, index, 0, keepdims=False)


def local(query_gate, key_gate, values, filter_taps, skip_gain, upstream):
    seg_len, width_dev = values.shape
    cycle_size = lax.axis_size("ctx")
    position = lax.axis_index("ctx")
    history = seg_len * cycle_size
    gated = key_gate * values
    mixed_grad = upstream * query_gate
    table_low = forward_table(seg_len, seg_len, 0)
    table_high = forward_table(seg_len, seg_len, seg_len)
    table_taps = forward_table(seg_len, 2 * seg_len, 0)
    back_low = inverse_table(seg_len, seg_len, 0)
    back_high = inverse_table(seg_len, seg_len, seg_len)
    back_full = inverse_table(seg_len, 2 * seg_len, 0)
    own_grad_spec = matmul(table_high, mixed_grad)
    spec_rows = 2 * (seg_len + 1)

    def taps_spec(lag_block):
        start_row = (lag_block - 1) * seg_len + history
        window = lax.dynamic_slice_in_dim(filter_taps, start_row, 2 * seg_len, 0)
        return matmul(table_taps, window)

    def visit(carry, gated_spec, grad_spec, source):
        acc_conv, acc_back, partial_value = carry
        lag_block = position - source
        acc_conv = acc_conv + times_spec(taps_spec(lag_block), gated_spec)
        acc_back = acc_back + conj_times(taps_spec(-lag_block), grad_spec)
        segment = matmul(back_full, conj_times(gated_spec, own_grad_spec))
        start_row = (lag_block - 1) * seg_len + history
        current = lax.dynamic_slice_in_dim(partial_value, start_row, 2 * seg_len, 0)
        partial_value = lax.dynamic_update_slice_in_dim(
            partial_value, current + segment, start_row, 0
        )
        return (acc_conv, acc_back, partial_value)

    initial = (
        jnp.zeros((spec_rows, width_dev), jnp.float32),
        jnp.zeros((spec_rows, width_dev), jnp.float32),
        jnp.zeros((2 * history, width_dev), jnp.float32),
    )
    own_gated_spec = matmul(table_low, gated)
    pieces = (
        lax.all_gather(own_gated_spec[None], "ctx", axis=0, tiled=True),
        lax.all_gather(own_grad_spec[None], "ctx", axis=0, tiled=True),
    )

    def advance(member, state):
        return visit(state, pick(pieces[0], member), pick(pieces[1], member), member)

    folded = lax.fori_loop(0, pieces[0].shape[0], advance, initial)
    acc_conv, acc_back, partial_value = folded
    filter_grad = lax.psum_scatter(partial_value, "ctx", scatter_dimension=0, tiled=True)
    conv = matmul(back_high, acc_conv)
    back = matmul(back_low, acc_back) + skip_gain[None, :] * mixed_grad
    query_grad = upstream * (conv + skip_gain[None, :] * gated)
    key_grad = back * values
    value_grad = back * key_gate
    skip_grad = lax.psum(jnp.sum(mixed_grad * gated, axis=0), "ctx")
    return (query_grad, key_grad, value_grad, filter_grad, skip_grad)


def solution(mesh):
    in_specs = (
        P(("groups", "ctx"), "chan"),
        P(("groups", "ctx"), "chan"),
        P(("groups", "ctx"), "chan"),
        P(None, "chan"),
        P("chan"),
        P(("groups", "ctx"), "chan"),
    )
    out_specs = (
        P(("groups", "ctx"), "chan"),
        P(("groups", "ctx"), "chan"),
        P(("groups", "ctx"), "chan"),
        P(("groups", "ctx"), "chan"),
        P(("groups", "chan")),
    )
    body = local_line if mesh.shape["ctx"] == 4 else local
    return jax.shard_map(body, mesh=mesh, in_specs=in_specs, out_specs=out_specs, check_vma=False)
```

```python
import functools
import math

import jax
import jax.numpy as jnp
import ml_dtypes
import numpy as np
from jax import lax
from jax.experimental import pallas as pl
from jax.experimental.pallas import tpu as pltpu
from jax.sharding import PartitionSpec as P

COS1, SIN1, HALF = math.cos(math.pi / 8), math.sin(math.pi / 8), math.sqrt(0.5)


def split_np(table):
    high = table.astype(ml_dtypes.bfloat16)
    low = (table - high.astype(np.float64)).astype(ml_dtypes.bfloat16)
    return np.stack([high, low])


def tables(seg):
    sub = seg // 4
    bins, pos = np.arange(sub)[:, None], np.arange(sub)[None, :]
    forward = []
    for group in range(4):
        angle = 2 * np.pi * pos * (8 * bins + group + 0.5) / (2 * seg)
        cos, sin = np.cos(angle), np.sin(angle)
        forward.append(np.block([[cos, -sin], [-sin, -cos]]))
    forward = np.stack(forward)
    inverse = forward.transpose(0, 2, 1) / seg
    return split_np(forward), split_np(inverse)


def split(x):
    high = x.astype(jnp.bfloat16)
    return high, (x - high.astype(jnp.float32)).astype(jnp.bfloat16)


def dot3(table_ref, group, high, low):
    t_high, t_low = table_ref[0, group], table_ref[1, group]
    dot = functools.partial(jnp.dot, preferred_element_type=jnp.float32)
    return dot(t_high, high) + dot(t_high, low) + dot(t_low, high)


def spread(x):
    sub = x.shape[0] // 4
    x0, x1, x2, x3 = (x[i * sub : (i + 1) * sub] for i in range(4))
    u, p, s, q, t = HALF * x2, COS1 * x1, SIN1 * x1, COS1 * x3, SIN1 * x3
    a, b, pt, sq, pmt, spq = x0 + u, x0 - u, p + t, s - q, p - t, s + q
    pairs = ((a + pt, spq + u), (b + sq, pmt + u), (b - sq, pmt - u), (a - pt, spq - u))
    return [jnp.concatenate(pair, axis=0) for pair in pairs]


def gather_quarters(re, im):
    e03, d03, e12, d12 = re[0] + re[3], re[0] - re[3], re[1] + re[2], re[1] - re[2]
    f03, g03, f12, g12 = im[0] + im[3], im[0] - im[3], im[1] + im[2], im[1] - im[2]
    return (
        e03 + e12,
        COS1 * (d03 + f12) + SIN1 * (d12 + f03),
        HALF * (e03 - e12 + g03 + g12),
        SIN1 * (d03 - f12) + COS1 * (f03 - d12),
    )


def transform(x, table_ref, store):
    for group, part in enumerate(spread(x)):
        store(group, dot3(table_ref, group, *split(part)))


def cost(flops, nbytes):
    return pl.CostEstimate(flops=int(flops), bytes_accessed=int(nbytes), transcendentals=0)


def params(mib):
    return pltpu.CompilerParams(vmem_limit_bytes=mib << 20)


def whole_spec(shape):
    return pl.BlockSpec(shape, lambda *_: (0,) * len(shape))


def f32(*shape):
    return jax.ShapeDtypeStruct(shape, jnp.float32)


def block_sums(gated, mixed):
    seg, width = gated.shape
    return jnp.sum((gated * mixed).reshape(seg // 8, 8, width), axis=0)


def sums_kernel(gated_ref, mixed_ref, out_ref):
    out_ref[...] = block_sums(gated_ref[...], mixed_ref[...])


def sums(gated, mixed):
    seg, width = gated.shape
    return pl.pallas_call(
        sums_kernel,
        grid=(1,),
        in_specs=[whole_spec((seg, width))] * 2,
        out_specs=whole_spec((8, width)),
        out_shape=f32(8, width),
        compiler_params=params(8),
        cost_estimate=cost(2 * seg * width, 8 * seg * width),
        name="sums",
    )(gated, mixed)


def mix_kernel(gated_ref, up_ref, query_ref, mixed_ref, sum_ref):
    mixed = up_ref[...] * query_ref[...]
    mixed_ref[...] = mixed
    sum_ref[...] = block_sums(gated_ref[...], mixed)


def mix(gated, upstream, query_gate):
    seg, width = gated.shape
    block = whole_spec((seg, width))
    return pl.pallas_call(
        mix_kernel,
        grid=(1,),
        in_specs=[block] * 3,
        out_specs=[block, whole_spec((8, width))],
        out_shape=[f32(seg, width), f32(8, width)],
        compiler_params=params(12),
        cost_estimate=cost(4 * seg * width, 16 * seg * width),
        name="mix",
    )(gated, upstream, query_gate)


def dft_kernel(choose, pos_ref, table_ref, *refs):
    *x_refs, out_ref = refs
    rows = out_ref.shape[0] // 4
    inner = jnp.logical_or(pos_ref[0] == 1, pos_ref[0] == 2)

    def store(group, value):
        out_ref[group * rows : (group + 1) * rows, :] = value

    x = x_refs[0][...]
    if choose:
        x = jnp.where(inner, x, x_refs[1][...] if len(x_refs) == 2 else 0.0)
    elif len(x_refs) == 2:
        x = x + x_refs[1][...]
    transform(x, table_ref, store)


def dft(pos, table, seg, *xs, choose=False):
    width = xs[0].shape[1]
    return pl.pallas_call(
        functools.partial(dft_kernel, choose),
        grid_spec=pltpu.PrefetchScalarGridSpec(
            num_scalar_prefetch=1,
            grid=(1,),
            in_specs=[whole_spec(table.shape)] + [whole_spec((seg, width))] * len(xs),
            out_specs=whole_spec((2 * seg, width)),
        ),
        out_shape=f32(2 * seg, width),
        compiler_params=params(12),
        cost_estimate=cost(3 * seg * seg * width * 2, 12 * seg * width),
        name="dft",
    )(pos, table, *xs)


def taps_kernel(table_ref, x_ref, out_ref, last_ref):
    step = pl.program_id(0)
    rows = out_ref.shape[1] // 4
    sub = rows // 2

    def store(group, value):
        base = group * rows
        sign = 1.0 if group % 2 == 0 else -1.0
        re, im = slice(base, base + sub), slice(base + sub, base + rows)
        out_ref[0, re, :] = value[:sub] - sign * last_ref[im, :]
        out_ref[0, im, :] = value[sub:] + sign * last_ref[re, :]
        last_ref[base : base + rows, :] = value

    @pl.when(step == 0)
    def _():
        last_ref[...] = jnp.zeros_like(last_ref)

    transform(x_ref[...], table_ref, store)


def taps_spectra(table, taps, seg):
    width = taps.shape[1]
    blocks = taps.shape[0] // seg
    return pl.pallas_call(
        taps_kernel,
        grid=(blocks,),
        in_specs=[whole_spec(table.shape), pl.BlockSpec((seg, width), lambda i: (i, 0))],
        out_specs=pl.BlockSpec((1, 2 * seg, width), lambda i: (jnp.maximum(i - 1, 0), 0, 0)),
        out_shape=jax.ShapeDtypeStruct((blocks - 1, 2 * seg, width), jnp.float32),
        scratch_shapes=[pltpu.VMEM((2 * seg, width), jnp.float32)],
        compiler_params=params(14),
        cost_estimate=cost(blocks * 3 * seg * seg * width * 2, blocks * 12 * seg * width),
        name="taps",
    )(table, taps)


def conj_mul(a, b):
    return a[0] * b[0] + a[1] * b[1], a[0] * b[1] - a[1] * b[0]


def mul(a, b):
    return a[0] * b[0] - a[1] * b[1], a[0] * b[1] + a[1] * b[0]


def add(a, b):
    return a[0] + b[0], a[1] + b[1]


def partial_kernel(
    pos_ref, table_ref, inverse_ref, win_near, win_far, next_ref, x_ref, gated_ref, near_sums, out_ref, z_ref
):
    rows = next_ref.shape[0] // 4
    sub = rows // 2
    for group, part in enumerate(spread(x_ref[...])):
        base = group * rows
        far = dot3(table_ref, group, *split(part))
        re, im = slice(base, base + sub), slice(base + sub, base + rows)
        total = add(
            conj_mul((win_near[0, re, :], win_near[0, im, :]), (next_ref[re, :], next_ref[im, :])),
            conj_mul((win_far[0, re, :], win_far[0, im, :]), (far[:sub], far[sub:])),
        )
        z_ref[group] = dot3(inverse_ref, group, *split(jnp.concatenate(total, axis=0)))
    quarters = gather_quarters([z_ref[g, :sub] for g in range(4)], [z_ref[g, sub:] for g in range(4)])
    for i, quarter in enumerate(quarters):
        out_ref[i * sub : (i + 1) * sub, :] = quarter
    out_ref[4 * sub :, :] = near_sums[...] + block_sums(gated_ref[...], x_ref[...])


def back_partial(pos, table, inverse, windows, next_m, x, gated, near_sums, half, seg):
    width = x.shape[1] // 2
    n = (windows.shape[0] + 1) // 2

    def window(distance):
        return pl.BlockSpec(
            (1, 2 * seg, width),
            lambda i, pos: (jnp.where(pos[0] == 1, n - 1 + distance, n - 1 - distance), 0, half),
        )

    def lanes(rows):
        return pl.BlockSpec((rows, width), lambda i, pos: (0, half))

    return pl.pallas_call(
        partial_kernel,
        grid_spec=pltpu.PrefetchScalarGridSpec(
            num_scalar_prefetch=1,
            grid=(1,),
            in_specs=[
                whole_spec(table.shape),
                whole_spec(inverse.shape),
                window(2),
                window(3),
                lanes(2 * seg),
                lanes(seg),
                lanes(seg),
                lanes(8),
            ],
            out_specs=whole_spec((seg + 8, width)),
            scratch_shapes=[pltpu.VMEM((4, seg // 2, width), jnp.float32)],
        ),
        out_shape=f32(seg + 8, width),
        compiler_params=params(24),
        cost_estimate=cost(6 * seg * seg * width * 2, 24 * seg * width),
        name="partial",
    )(pos, table, inverse, windows, windows, next_m, x, gated, near_sums)


OWN, OUTER, NEXT, TWO, THREE = range(5)
PAIRS = (
    ((), ((OWN, THREE),), ((OWN, TWO), (NEXT, THREE))),
    (
        ((OUTER, NEXT), (OWN, TWO)),
        ((OUTER, OWN), (OWN, NEXT), (NEXT, TWO)),
        ((OUTER, OUTER), (OWN, OWN), (NEXT, NEXT), (TWO, TWO)),
    ),
    (
        ((TWO, TWO), (NEXT, NEXT), (OWN, OWN), (OUTER, OUTER)),
        ((NEXT, TWO), (OWN, NEXT), (OUTER, OWN)),
        ((OWN, TWO), (OUTER, NEXT)),
    ),
    (((NEXT, THREE), (OWN, TWO)), ((OWN, THREE),), ()),
)


def is_late(pair):
    return pair[0] == TWO or pair[1] == THREE


def pair_sums(distances, gated, mixed, sign, late):
    total = []
    for pairs in distances:
        value = None
        for m, g in pairs:
            if is_late((m, g)) == late:
                term = conj_mul(gated[g](), mixed[m]())
                value = term if value is None else add(value, term)
        total.append(value)
    out = []
    for low, high in zip(total[:2], total[1:]):
        if high is not None:
            turned = (sign * high[1], -sign * high[0])
            low = turned if low is None else add(low, turned)
        out.append(low)
    return out


TILE = 16


def tile_reader(tile, sub):
    re = pl.ds(pl.multiple_of(tile * TILE, TILE), TILE)
    im = pl.ds(pl.multiple_of(sub + tile * TILE, TILE), TILE)

    def read(ref, *lead):
        return ref[(*lead, re, slice(None))], ref[(*lead, im, slice(None))]

    return re, im, read


def group_sign():
    return jnp.where(pl.program_id(0) % 2 == 0, 1.0, -1.0)


def early_kernel(
    pos_ref, win_own, win_outer, win_next, win_two, own_g, outer_g, next_g, two_g, own_m, outer_m, next_m, out_ref
):
    pos, sign = pos_ref[0], group_sign()
    rows = own_g.shape[0]
    sub = rows // 2
    count = sub // TILE

    def put(at, slot, value):
        re, im = at
        out_ref[slot, re, :] = value[0]
        out_ref[slot, im, :] = value[1]

    def sums(tile, _):
        re, im, read = tile_reader(tile, sub)
        own, outer, ahead = read(win_own, 0), read(win_outer, 0), read(win_next, 0)
        conv = add(mul(own, read(own_g)), mul(outer, read(outer_g)))
        conv = add(conv, add(mul(ahead, read(next_g)), mul(read(win_two, 0), read(two_g))))
        put((re, im), 0, conv)
        back = add(conj_mul(own, read(own_m)), conj_mul(ahead, read(outer_m)))
        put((re, im), 1, add(back, conj_mul(outer, read(next_m))))
        return _

    lax.fori_loop(0, count, sums, 0)
    for where, distances in enumerate(PAIRS):

        @pl.when(pos == where)
        def _():
            def lags(tile, _):
                re, im, read = tile_reader(tile, sub)
                gated = [functools.partial(read, ref) for ref in (own_g, outer_g, next_g, two_g)]
                mixed = [functools.partial(read, ref) for ref in (own_m, outer_m, next_m)]
                for slot, value in enumerate(pair_sums(distances, gated, mixed, sign, False)):
                    if value is None:
                        value = (jnp.zeros_like(own_g[re, :]),) * 2
                    put((re, im), 2 + slot, value)
                return _

            lax.fori_loop(0, count, lags, 0)


def early(pos, windows, gated, mixed, seg):
    width = gated[0].shape[1]
    rows = seg // 2
    mid = windows.shape[0] // 2

    def window(index):
        return pl.BlockSpec((1, rows, width), lambda i, pos: (index(pos[0]), i, 0))

    group = pl.BlockSpec((rows, width), lambda i, pos: (i, 0))
    return pl.pallas_call(
        early_kernel,
        grid_spec=pltpu.PrefetchScalarGridSpec(
            num_scalar_prefetch=1,
            grid=(4,),
            in_specs=[
                window(lambda p: mid),
                window(lambda p: jnp.where(p < 2, mid + 1, mid - 1)),
                window(lambda p: jnp.where(p < 2, mid - 1, mid + 1)),
                window(lambda p: jnp.where(p < 2, mid - 2, mid + 2)),
            ]
            + [group] * 7,
            out_specs=pl.BlockSpec((4, rows, width), lambda i, pos: (0, i, 0)),
        ),
        out_shape=f32(4, 2 * seg, width),
        compiler_params=params(14),
        cost_estimate=cost(200 * seg * width, 120 * seg * width),
        name="early",
    )(pos, *[windows] * 4, *gated, *mixed)


def late_kernel(
    pos_ref, inverse_ref, acc_ref, win_ref, three_g, two_g, own_m, outer_m, next_m, *rest
):
    two_m, gated_ref, mixed_ref, skip_ref, up_ref, query_out, filter_out, back_out, x_high, x_low, z_ref = rest
    group = pl.program_id(0)
    pos, sign = pos_ref[0], group_sign()
    rows, width = own_m.shape
    sub = rows // 2

    def put(at, slot, value):
        for rows_at, part in zip(at, value):
            high, low = split(part)
            x_high[rows_at, slot * width : (slot + 1) * width] = high
            x_low[rows_at, slot * width : (slot + 1) * width] = low

    for where, distances in enumerate(PAIRS):

        @pl.when(pos == where)
        def _():
            def lags(tile, _):
                re, im, read = tile_reader(tile, sub)

                gated = [None, None, None, functools.partial(read, two_g), functools.partial(read, three_g)]
                mixed = [functools.partial(read, ref) for ref in (own_m, outer_m, next_m, two_m)]
                total = [read(acc_ref, slot) for slot in range(4)]
                if where in (0, 3):
                    total[0] = add(total[0], mul(read(win_ref, 0), gated[THREE]()))
                else:
                    total[1] = add(total[1], conj_mul(read(win_ref, 0), mixed[TWO]()))
                for slot, value in enumerate(pair_sums(distances, gated, mixed, sign, True)):
                    if value is not None:
                        total[2 + slot] = add(total[2 + slot], value)
                for slot, value in enumerate(total):
                    put((re, im), slot, value)
                return _

            lax.fori_loop(0, sub // TILE, lags, 0)

    dot = functools.partial(jnp.dot, preferred_element_type=jnp.float32)
    t_high, t_low = inverse_ref[0, 0], inverse_ref[1, 0]
    for slot in range(4):
        cols = slice(slot * width, (slot + 1) * width)
        z_ref[group, :, cols] = (
            dot(t_high, x_high[:, cols]) + dot(t_high, x_low[:, cols]) + dot(t_low, x_high[:, cols])
        )

    @pl.when(group == 3)
    def _():
        seg = 4 * sub
        for slot in range(4):
            cols = slice(slot * width, (slot + 1) * width)
            quarters = gather_quarters(
                [z_ref[g, :sub, cols] for g in range(4)], [z_ref[g, sub:, cols] for g in range(4)]
            )
            for i, quarter in enumerate(quarters):
                at = slice(i * sub, (i + 1) * sub)
                if slot == 0:
                    query_out[at, :] = up_ref[at, :] * (quarter + skip_ref[...] * gated_ref[at, :])
                elif slot == 1:
                    back_out[at, :] = quarter + skip_ref[...] * mixed_ref[at, :]
                else:
                    base = (slot - 2) * seg + i * sub
                    filter_out[base : base + sub, :] = quarter


def late(pos, inverse, acc, windows, three_g, two_g, own_m, outer_m, next_m, two_m, gated, mixed, skip, upstream):
    seg, width = upstream.shape
    rows = seg // 2
    mid = windows.shape[0] // 2

    def win_at(i, pos):
        p = pos[0]
        ends = jnp.where(p == 0, mid - 3, mid + 3)
        return jnp.where(p == 1, mid + 2, jnp.where(p == 2, mid - 2, ends)), i, 0

    group = pl.BlockSpec((rows, width), lambda i, pos: (i, 0))
    return pl.pallas_call(
        late_kernel,
        grid_spec=pltpu.PrefetchScalarGridSpec(
            num_scalar_prefetch=1,
            grid=(4,),
            in_specs=[
                pl.BlockSpec((2, 1, rows, rows), lambda i, pos: (0, i, 0, 0)),
                pl.BlockSpec((4, rows, width), lambda i, pos: (0, i, 0)),
                pl.BlockSpec((1, rows, width), win_at),
                *[group] * 6,
                whole_spec((seg, width)),
                whole_spec((seg, width)),
                whole_spec((1, width)),
                whole_spec((seg, width)),
            ],
            out_specs=[whole_spec((seg, width)), whole_spec((2 * seg, width)), whole_spec((seg, width))],
            scratch_shapes=[
                pltpu.VMEM((rows, 4 * width), jnp.bfloat16),
                pltpu.VMEM((rows, 4 * width), jnp.bfloat16),
                pltpu.VMEM((4, rows, 4 * width), jnp.float32),
            ],
        ),
        out_shape=[f32(seg, width), f32(2 * seg, width), f32(seg, width)],
        compiler_params=params(20),
        cost_estimate=cost(12 * seg * seg * width * 2, 100 * seg * width),
        name="late",
    )(pos, inverse, acc, windows, three_g, two_g, own_m, outer_m, next_m, two_m, gated, mixed, skip, upstream)


def finish_kernel(back_ref, key_ref, values_ref, made_ref, sent_ref, own_ref, side_ref, *rest):
    key_out, value_out, skip_out = rest[-3:]
    seg = back_ref.shape[0]
    back = back_ref[...] + sent_ref[:seg, :]
    key_out[...] = back * values_ref[...]
    value_out[...] = back * key_ref[...]
    total = (own_ref[...] + side_ref[...]) + (made_ref[seg:, :] + sent_ref[seg:, :])
    skip_out[...] = jnp.sum(total, axis=0, keepdims=True)


def finish(back, key_gate, values, made, sent, own_sums, side_sums, half, before=()):
    seg, full = back.shape
    width = full // 2

    def lanes(rows):
        return pl.BlockSpec((rows, width), lambda i: (0, half))

    held = pl.BlockSpec(memory_space=pl.ANY)
    return pl.pallas_call(
        finish_kernel,
        grid=(1,),
        in_specs=[lanes(seg)] * 3 + [whole_spec((seg + 8, width))] * 2 + [lanes(8)] * 2 + [held] * len(before),
        out_specs=[lanes(seg), lanes(seg), lanes(1)],
        out_shape=[f32(seg, full), f32(seg, full), f32(1, full)],
        input_output_aliases={7 + i: i for i in range(len(before))},
        compiler_params=params(12),
        cost_estimate=cost(3 * seg * width, 24 * seg * width),
        name="finish",
    )(back, key_gate, values, made, sent, own_sums, side_sums, *before)


def send(x, *pairs):
    return lax.ppermute(x, "ctx", list(pairs))


def across(x):
    return send(x, (1, 2), (2, 1))


def outward(x):
    return send(x, (1, 0), (2, 3))


def beside(x):
    return send(x, (0, 1), (1, 0), (2, 3), (3, 2))


def local_line(query_gate, key_gate, values, filter_taps, skip_gain, upstream):
    seg, width = values.shape
    forward_np, inverse_np = tables(seg)
    table, inverse = jnp.asarray(forward_np), jnp.asarray(inverse_np)
    pos = lax.axis_index("ctx").astype(jnp.int32).reshape(1)
    after = lax.optimization_barrier

    gated = key_gate * values
    side, over = beside(gated), across(gated)
    mixed, own_sums = mix(gated, upstream, query_gate)
    side_x, over_x = beside(mixed), across(mixed)
    own_g, own_m = dft(pos, table, seg, gated), dft(pos, table, seg, mixed)
    side, over, filter_taps, own_g, own_m = after((side, over, filter_taps, own_g, own_m))

    over_two, out_two = across(side), outward(over)
    outer_g = dft(pos, table, seg, side, choose=True)
    next_g = dft(pos, table, seg, over, side, choose=True)
    windows = taps_spectra(table, filter_taps, seg)
    side_x, over_x, windows, outer_g, next_g = after((side_x, over_x, windows, outer_g, next_g))

    outer_m = dft(pos, table, seg, side_x, choose=True)
    next_m = dft(pos, table, seg, over_x, side_x, choose=True)
    side_x, outer_m, next_m = after((side_x, outer_m, next_m))
    two_x = across(side_x)
    side_sums, near_sums = sums(side, side_x), sums(over, over_x)
    over_two, outer_m, next_m, side_sums, near_sums = after((over_two, outer_m, next_m, side_sums, near_sums))

    three = outward(over_two)
    two_g = dft(pos, table, seg, over_two, out_two)
    acc = early(pos, windows, (own_g, outer_g, next_g, two_g), (own_m, outer_m, next_m), seg)
    two_x, acc = after((two_x, acc))

    made_0 = back_partial(pos, table, inverse, windows, next_m, two_x, over_two, near_sums, 0, seg)
    two_x, made_0 = after((two_x, made_0))
    sent_0 = outward(made_0)
    made_1 = back_partial(pos, table, inverse, windows, next_m, two_x, over_two, near_sums, 1, seg)
    two_x, made_1 = after((two_x, made_1))
    sent_1 = outward(made_1)
    two_m, three_g = dft(pos, table, seg, two_x), dft(pos, table, seg, three)
    query_grad, filter_grad, back = late(
        pos, inverse, acc, windows, three_g, two_g, own_m, outer_m, next_m, two_m,
        gated, mixed, skip_gain[None, :], upstream,
    )
    done = finish(back, key_gate, values, made_0, sent_0, own_sums, side_sums, 0)
    sent_1, *done = after((sent_1, *done))
    key_grad, value_grad, skip_grad = finish(back, key_gate, values, made_1, sent_1, own_sums, side_sums, 1, done)
    return (query_grad, key_grad, value_grad, filter_grad, skip_grad[0])


def matmul(left, right):
    return jnp.dot(left, right, preferred_element_type=jnp.float32, precision=lax.Precision.HIGHEST)


def forward_table(seg_len, count, offset):
    num_bins = seg_len + 1
    period = 2 * seg_len
    bin_index = lax.broadcasted_iota(jnp.int32, (num_bins, count), 0)
    pos_index = lax.broadcasted_iota(jnp.int32, (num_bins, count), 1) + offset
    angles = (bin_index * pos_index % period).astype(jnp.float32) * (2.0 * math.pi / period)
    return jnp.concatenate([jnp.cos(angles), -jnp.sin(angles)], axis=0)


def inverse_table(seg_len, count, offset):
    num_bins = seg_len + 1
    period = 2 * seg_len
    pos_index = lax.broadcasted_iota(jnp.int32, (count, num_bins), 0) + offset
    bin_index = lax.broadcasted_iota(jnp.int32, (count, num_bins), 1)
    angles = (bin_index * pos_index % period).astype(jnp.float32) * (2.0 * math.pi / period)
    weights = jnp.where((bin_index == 0) | (bin_index == seg_len), 1.0, 2.0) / period
    return jnp.concatenate([weights * jnp.cos(angles), -weights * jnp.sin(angles)], axis=1)


def times_spec(first, second):
    num_bins = first.shape[0] // 2
    real_a, imag_a = (first[:num_bins], first[num_bins:])
    real_b, imag_b = (second[:num_bins], second[num_bins:])
    return jnp.concatenate(
        [real_a * real_b - imag_a * imag_b, real_a * imag_b + imag_a * real_b], axis=0
    )


def conj_times(first, second):
    num_bins = first.shape[0] // 2
    real_a, imag_a = (first[:num_bins], first[num_bins:])
    real_b, imag_b = (second[:num_bins], second[num_bins:])
    return jnp.concatenate(
        [real_a * real_b + imag_a * imag_b, real_a * imag_b - imag_a * real_b], axis=0
    )


def pick(stack, index):
    return lax.dynamic_index_in_dim(stack, index, 0, keepdims=False)


def local(query_gate, key_gate, values, filter_taps, skip_gain, upstream):
    seg_len, width_dev = values.shape
    cycle_size = lax.axis_size("ctx")
    position = lax.axis_index("ctx")
    history = seg_len * cycle_size
    gated = key_gate * values
    mixed_grad = upstream * query_gate
    table_low = forward_table(seg_len, seg_len, 0)
    table_high = forward_table(seg_len, seg_len, seg_len)
    table_taps = forward_table(seg_len, 2 * seg_len, 0)
    back_low = inverse_table(seg_len, seg_len, 0)
    back_high = inverse_table(seg_len, seg_len, seg_len)
    back_full = inverse_table(seg_len, 2 * seg_len, 0)
    own_grad_spec = matmul(table_high, mixed_grad)
    spec_rows = 2 * (seg_len + 1)

    def taps_spec(lag_block):
        start_row = (lag_block - 1) * seg_len + history
        window = lax.dynamic_slice_in_dim(filter_taps, start_row, 2 * seg_len, 0)
        return matmul(table_taps, window)

    def visit(carry, gated_spec, grad_spec, source):
        acc_conv, acc_back, partial_value = carry
        lag_block = position - source
        acc_conv = acc_conv + times_spec(taps_spec(lag_block), gated_spec)
        acc_back = acc_back + conj_times(taps_spec(-lag_block), grad_spec)
        segment = matmul(back_full, conj_times(gated_spec, own_grad_spec))
        start_row = (lag_block - 1) * seg_len + history
        current = lax.dynamic_slice_in_dim(partial_value, start_row, 2 * seg_len, 0)
        partial_value = lax.dynamic_update_slice_in_dim(
            partial_value, current + segment, start_row, 0
        )
        return (acc_conv, acc_back, partial_value)

    initial = (
        jnp.zeros((spec_rows, width_dev), jnp.float32),
        jnp.zeros((spec_rows, width_dev), jnp.float32),
        jnp.zeros((2 * history, width_dev), jnp.float32),
    )
    own_gated_spec = matmul(table_low, gated)
    pieces = (
        lax.all_gather(own_gated_spec[None], "ctx", axis=0, tiled=True),
        lax.all_gather(own_grad_spec[None], "ctx", axis=0, tiled=True),
    )

    def advance(member, state):
        return visit(state, pick(pieces[0], member), pick(pieces[1], member), member)

    folded = lax.fori_loop(0, pieces[0].shape[0], advance, initial)
    acc_conv, acc_back, partial_value = folded
    filter_grad = lax.psum_scatter(partial_value, "ctx", scatter_dimension=0, tiled=True)
    conv = matmul(back_high, acc_conv)
    back = matmul(back_low, acc_back) + skip_gain[None, :] * mixed_grad
    query_grad = upstream * (conv + skip_gain[None, :] * gated)
    key_grad = back * values
    value_grad = back * key_gate
    skip_grad = lax.psum(jnp.sum(mixed_grad * gated, axis=0), "ctx")
    return (query_grad, key_grad, value_grad, filter_grad, skip_grad)


def solution(mesh):
    in_specs = (
        P(("groups", "ctx"), "chan"),
        P(("groups", "ctx"), "chan"),
        P(("groups", "ctx"), "chan"),
        P(None, "chan"),
        P("chan"),
        P(("groups", "ctx"), "chan"),
    )
    out_specs = (
        P(("groups", "ctx"), "chan"),
        P(("groups", "ctx"), "chan"),
        P(("groups", "ctx"), "chan"),
        P(("groups", "ctx"), "chan"),
        P(("groups", "chan")),
    )
    body = local_line if mesh.shape["ctx"] == 4 else local
    return jax.shard_map(body, mesh=mesh, in_specs=in_specs, out_specs=out_specs, check_vma=False)
```

```python
import functools
import math

import jax
import jax.numpy as jnp
import ml_dtypes
import numpy as np
from jax import lax
from jax.experimental import pallas as pl
from jax.experimental.pallas import tpu as pltpu
from jax.sharding import PartitionSpec as P

COS1, SIN1, HALF = math.cos(math.pi / 8), math.sin(math.pi / 8), math.sqrt(0.5)


def split_np(table):
    high = table.astype(ml_dtypes.bfloat16)
    low = (table - high.astype(np.float64)).astype(ml_dtypes.bfloat16)
    return np.stack([high, low])


def tables(seg):
    sub = seg // 4
    bins, pos = np.arange(sub)[:, None], np.arange(sub)[None, :]
    forward = []
    for group in range(4):
        angle = 2 * np.pi * pos * (8 * bins + group + 0.5) / (2 * seg)
        cos, sin = np.cos(angle), np.sin(angle)
        forward.append(np.block([[cos, -sin], [-sin, -cos]]))
    forward = np.stack(forward)
    inverse = forward.transpose(0, 2, 1) / seg
    return split_np(forward), split_np(inverse)


def split(x):
    high = x.astype(jnp.bfloat16)
    return high, (x - high.astype(jnp.float32)).astype(jnp.bfloat16)


def dot3(table_ref, group, high, low):
    t_high, t_low = table_ref[0, group], table_ref[1, group]
    dot = functools.partial(jnp.dot, preferred_element_type=jnp.float32)
    return dot(t_high, high) + dot(t_high, low) + dot(t_low, high)


def spread(x):
    sub = x.shape[0] // 4
    x0, x1, x2, x3 = (x[i * sub : (i + 1) * sub] for i in range(4))
    u, p, s, q, t = HALF * x2, COS1 * x1, SIN1 * x1, COS1 * x3, SIN1 * x3
    a, b, pt, sq, pmt, spq = x0 + u, x0 - u, p + t, s - q, p - t, s + q
    pairs = ((a + pt, spq + u), (b + sq, pmt + u), (b - sq, pmt - u), (a - pt, spq - u))
    return [jnp.concatenate(pair, axis=0) for pair in pairs]


def gather_quarters(re, im):
    e03, d03, e12, d12 = re[0] + re[3], re[0] - re[3], re[1] + re[2], re[1] - re[2]
    f03, g03, f12, g12 = im[0] + im[3], im[0] - im[3], im[1] + im[2], im[1] - im[2]
    return (
        e03 + e12,
        COS1 * (d03 + f12) + SIN1 * (d12 + f03),
        HALF * (e03 - e12 + g03 + g12),
        SIN1 * (d03 - f12) + COS1 * (f03 - d12),
    )


def transform(x, table_ref, store):
    for group, part in enumerate(spread(x)):
        store(group, dot3(table_ref, group, *split(part)))


def cost(flops, nbytes):
    return pl.CostEstimate(flops=int(flops), bytes_accessed=int(nbytes), transcendentals=0)


def params(mib):
    return pltpu.CompilerParams(vmem_limit_bytes=mib << 20)


def whole_spec(shape):
    return pl.BlockSpec(shape, lambda *_: (0,) * len(shape))


def f32(*shape):
    return jax.ShapeDtypeStruct(shape, jnp.float32)


def block_sums(gated, mixed):
    seg, width = gated.shape
    return jnp.sum((gated * mixed).reshape(seg // 8, 8, width), axis=0)


def sums_kernel(gated_ref, mixed_ref, out_ref):
    out_ref[...] = block_sums(gated_ref[...], mixed_ref[...])


def sums(gated, mixed):
    seg, width = gated.shape
    return pl.pallas_call(
        sums_kernel,
        grid=(1,),
        in_specs=[whole_spec((seg, width))] * 2,
        out_specs=whole_spec((8, width)),
        out_shape=f32(8, width),
        compiler_params=params(8),
        cost_estimate=cost(2 * seg * width, 8 * seg * width),
        name="sums",
    )(gated, mixed)


def mix_kernel(gated_ref, up_ref, query_ref, mixed_ref, sum_ref):
    mixed = up_ref[...] * query_ref[...]
    mixed_ref[...] = mixed
    sum_ref[...] = block_sums(gated_ref[...], mixed)


def mix(gated, upstream, query_gate):
    seg, width = gated.shape
    block = whole_spec((seg, width))
    return pl.pallas_call(
        mix_kernel,
        grid=(1,),
        in_specs=[block] * 3,
        out_specs=[block, whole_spec((8, width))],
        out_shape=[f32(seg, width), f32(8, width)],
        compiler_params=params(12),
        cost_estimate=cost(4 * seg * width, 16 * seg * width),
        name="mix",
    )(gated, upstream, query_gate)


def dft_kernel(choose, pos_ref, table_ref, *refs):
    *x_refs, out_ref = refs
    rows = out_ref.shape[0] // 4
    inner = jnp.logical_or(pos_ref[0] == 1, pos_ref[0] == 2)

    def store(group, value):
        out_ref[group * rows : (group + 1) * rows, :] = value

    x = x_refs[0][...]
    if choose:
        x = jnp.where(inner, x, x_refs[1][...] if len(x_refs) == 2 else 0.0)
    elif len(x_refs) == 2:
        x = x + x_refs[1][...]
    transform(x, table_ref, store)


def dft(pos, table, seg, *xs, choose=False):
    width = xs[0].shape[1]
    return pl.pallas_call(
        functools.partial(dft_kernel, choose),
        grid_spec=pltpu.PrefetchScalarGridSpec(
            num_scalar_prefetch=1,
            grid=(1,),
            in_specs=[whole_spec(table.shape)] + [whole_spec((seg, width))] * len(xs),
            out_specs=whole_spec((2 * seg, width)),
        ),
        out_shape=f32(2 * seg, width),
        compiler_params=params(12),
        cost_estimate=cost(3 * seg * seg * width * 2, 12 * seg * width),
        name="dft",
    )(pos, table, *xs)


def taps_kernel(table_ref, x_ref, out_ref, last_ref):
    step = pl.program_id(0)
    rows = out_ref.shape[1] // 4
    sub = rows // 2

    def store(group, value):
        base = group * rows
        sign = 1.0 if group % 2 == 0 else -1.0
        re, im = slice(base, base + sub), slice(base + sub, base + rows)
        out_ref[0, re, :] = value[:sub] - sign * last_ref[im, :]
        out_ref[0, im, :] = value[sub:] + sign * last_ref[re, :]
        last_ref[base : base + rows, :] = value

    @pl.when(step == 0)
    def _():
        last_ref[...] = jnp.zeros_like(last_ref)

    transform(x_ref[...], table_ref, store)


def taps_spectra(table, taps, seg):
    width = taps.shape[1]
    blocks = taps.shape[0] // seg
    return pl.pallas_call(
        taps_kernel,
        grid=(blocks,),
        in_specs=[whole_spec(table.shape), pl.BlockSpec((seg, width), lambda i: (i, 0))],
        out_specs=pl.BlockSpec((1, 2 * seg, width), lambda i: (jnp.maximum(i - 1, 0), 0, 0)),
        out_shape=jax.ShapeDtypeStruct((blocks - 1, 2 * seg, width), jnp.float32),
        scratch_shapes=[pltpu.VMEM((2 * seg, width), jnp.float32)],
        compiler_params=params(14),
        cost_estimate=cost(blocks * 3 * seg * seg * width * 2, blocks * 12 * seg * width),
        name="taps",
    )(table, taps)


def conj_mul(a, b):
    return a[0] * b[0] + a[1] * b[1], a[0] * b[1] - a[1] * b[0]


def mul(a, b):
    return a[0] * b[0] - a[1] * b[1], a[0] * b[1] + a[1] * b[0]


def add(a, b):
    return a[0] + b[0], a[1] + b[1]


def partial_kernel(
    pos_ref, table_ref, inverse_ref, win_near, win_far, next_ref, x_ref, gated_ref, near_sums, out_ref, z_ref
):
    rows = next_ref.shape[0] // 4
    sub = rows // 2
    for group, part in enumerate(spread(x_ref[...])):
        base = group * rows
        far = dot3(table_ref, group, *split(part))
        re, im = slice(base, base + sub), slice(base + sub, base + rows)
        total = add(
            conj_mul((win_near[0, re, :], win_near[0, im, :]), (next_ref[re, :], next_ref[im, :])),
            conj_mul((win_far[0, re, :], win_far[0, im, :]), (far[:sub], far[sub:])),
        )
        z_ref[group] = dot3(inverse_ref, group, *split(jnp.concatenate(total, axis=0)))
    quarters = gather_quarters([z_ref[g, :sub] for g in range(4)], [z_ref[g, sub:] for g in range(4)])
    for i, quarter in enumerate(quarters):
        out_ref[i * sub : (i + 1) * sub, :] = quarter
    out_ref[4 * sub :, :] = near_sums[...] + block_sums(gated_ref[...], x_ref[...])


def back_partial(pos, table, inverse, windows, next_m, x, gated, near_sums, half, seg):
    width = x.shape[1] // 2
    n = (windows.shape[0] + 1) // 2

    def window(distance):
        return pl.BlockSpec(
            (1, 2 * seg, width),
            lambda i, pos: (jnp.where(pos[0] == 1, n - 1 + distance, n - 1 - distance), 0, half),
        )

    def lanes(rows):
        return pl.BlockSpec((rows, width), lambda i, pos: (0, half))

    return pl.pallas_call(
        partial_kernel,
        grid_spec=pltpu.PrefetchScalarGridSpec(
            num_scalar_prefetch=1,
            grid=(1,),
            in_specs=[
                whole_spec(table.shape),
                whole_spec(inverse.shape),
                window(2),
                window(3),
                lanes(2 * seg),
                lanes(seg),
                lanes(seg),
                lanes(8),
            ],
            out_specs=whole_spec((seg + 8, width)),
            scratch_shapes=[pltpu.VMEM((4, seg // 2, width), jnp.float32)],
        ),
        out_shape=f32(seg + 8, width),
        compiler_params=params(24),
        cost_estimate=cost(6 * seg * seg * width * 2, 24 * seg * width),
        name="partial",
    )(pos, table, inverse, windows, windows, next_m, x, gated, near_sums)


OWN, OUTER, NEXT, TWO, THREE = range(5)
PAIRS = (
    ((), ((OWN, THREE),), ((OWN, TWO), (NEXT, THREE))),
    (
        ((OUTER, NEXT), (OWN, TWO)),
        ((OUTER, OWN), (OWN, NEXT), (NEXT, TWO)),
        ((OUTER, OUTER), (OWN, OWN), (NEXT, NEXT), (TWO, TWO)),
    ),
    (
        ((TWO, TWO), (NEXT, NEXT), (OWN, OWN), (OUTER, OUTER)),
        ((NEXT, TWO), (OWN, NEXT), (OUTER, OWN)),
        ((OWN, TWO), (OUTER, NEXT)),
    ),
    (((NEXT, THREE), (OWN, TWO)), ((OWN, THREE),), ()),
)


def is_late(pair):
    return pair[0] == TWO or pair[1] == THREE


def pair_sums(distances, gated, mixed, sign, late):
    total = []
    for pairs in distances:
        value = None
        for m, g in pairs:
            if is_late((m, g)) == late:
                term = conj_mul(gated[g](), mixed[m]())
                value = term if value is None else add(value, term)
        total.append(value)
    out = []
    for low, high in zip(total[:2], total[1:]):
        if high is not None:
            turned = (sign * high[1], -sign * high[0])
            low = turned if low is None else add(low, turned)
        out.append(low)
    return out


TILE = 16


def tile_reader(tile, sub):
    re = pl.ds(pl.multiple_of(tile * TILE, TILE), TILE)
    im = pl.ds(pl.multiple_of(sub + tile * TILE, TILE), TILE)

    def read(ref, *lead):
        return ref[(*lead, re, slice(None))], ref[(*lead, im, slice(None))]

    return re, im, read


def group_sign():
    return jnp.where(pl.program_id(0) % 2 == 0, 1.0, -1.0)


def early_kernel(
    pos_ref, win_own, win_outer, win_next, win_two, own_g, outer_g, next_g, two_g, own_m, outer_m, next_m, out_ref
):
    pos, sign = pos_ref[0], group_sign()
    rows = own_g.shape[0]
    sub = rows // 2
    count = sub // TILE

    def put(at, slot, value):
        re, im = at
        out_ref[slot, re, :] = value[0]
        out_ref[slot, im, :] = value[1]

    def sums(tile, _):
        re, im, read = tile_reader(tile, sub)
        own, outer, ahead = read(win_own, 0), read(win_outer, 0), read(win_next, 0)
        conv = add(mul(own, read(own_g)), mul(outer, read(outer_g)))
        conv = add(conv, add(mul(ahead, read(next_g)), mul(read(win_two, 0), read(two_g))))
        put((re, im), 0, conv)
        back = add(conj_mul(own, read(own_m)), conj_mul(ahead, read(outer_m)))
        put((re, im), 1, add(back, conj_mul(outer, read(next_m))))
        return _

    lax.fori_loop(0, count, sums, 0)
    for where, distances in enumerate(PAIRS):

        @pl.when(pos == where)
        def _():
            def lags(tile, _):
                re, im, read = tile_reader(tile, sub)
                gated = [functools.partial(read, ref) for ref in (own_g, outer_g, next_g, two_g)]
                mixed = [functools.partial(read, ref) for ref in (own_m, outer_m, next_m)]
                for slot, value in enumerate(pair_sums(distances, gated, mixed, sign, False)):
                    if value is None:
                        value = (jnp.zeros_like(own_g[re, :]),) * 2
                    put((re, im), 2 + slot, value)
                return _

            lax.fori_loop(0, count, lags, 0)


def early(pos, windows, gated, mixed, seg):
    width = gated[0].shape[1]
    rows = seg // 2
    mid = windows.shape[0] // 2

    def window(index):
        return pl.BlockSpec((1, rows, width), lambda i, pos: (index(pos[0]), i, 0))

    group = pl.BlockSpec((rows, width), lambda i, pos: (i, 0))
    return pl.pallas_call(
        early_kernel,
        grid_spec=pltpu.PrefetchScalarGridSpec(
            num_scalar_prefetch=1,
            grid=(4,),
            in_specs=[
                window(lambda p: mid),
                window(lambda p: jnp.where(p < 2, mid + 1, mid - 1)),
                window(lambda p: jnp.where(p < 2, mid - 1, mid + 1)),
                window(lambda p: jnp.where(p < 2, mid - 2, mid + 2)),
            ]
            + [group] * 7,
            out_specs=pl.BlockSpec((4, rows, width), lambda i, pos: (0, i, 0)),
        ),
        out_shape=f32(4, 2 * seg, width),
        compiler_params=params(14),
        cost_estimate=cost(200 * seg * width, 120 * seg * width),
        name="early",
    )(pos, *[windows] * 4, *gated, *mixed)


def late_kernel(
    pos_ref, inverse_ref, acc_ref, win_ref, three_g, two_g, own_m, outer_m, next_m, *rest
):
    two_m, gated_ref, mixed_ref, skip_ref, up_ref, query_out, filter_out, back_out, x_high, x_low, z_ref = rest
    group = pl.program_id(0)
    pos, sign = pos_ref[0], group_sign()
    rows, width = own_m.shape
    sub = rows // 2

    def put(at, slot, value):
        for rows_at, part in zip(at, value):
            high, low = split(part)
            x_high[rows_at, slot * width : (slot + 1) * width] = high
            x_low[rows_at, slot * width : (slot + 1) * width] = low

    for where, distances in enumerate(PAIRS):

        @pl.when(pos == where)
        def _():
            def lags(tile, _):
                re, im, read = tile_reader(tile, sub)

                gated = [None, None, None, functools.partial(read, two_g), functools.partial(read, three_g)]
                mixed = [functools.partial(read, ref) for ref in (own_m, outer_m, next_m, two_m)]
                total = [read(acc_ref, slot) for slot in range(4)]
                if where in (0, 3):
                    total[0] = add(total[0], mul(read(win_ref, 0), gated[THREE]()))
                else:
                    total[1] = add(total[1], conj_mul(read(win_ref, 0), mixed[TWO]()))
                for slot, value in enumerate(pair_sums(distances, gated, mixed, sign, True)):
                    if value is not None:
                        total[2 + slot] = add(total[2 + slot], value)
                for slot, value in enumerate(total):
                    put((re, im), slot, value)
                return _

            lax.fori_loop(0, sub // TILE, lags, 0)

    dot = functools.partial(jnp.dot, preferred_element_type=jnp.float32)
    t_high, t_low = inverse_ref[0, 0], inverse_ref[1, 0]
    for slot in range(4):
        cols = slice(slot * width, (slot + 1) * width)
        z_ref[group, :, cols] = (
            dot(t_high, x_high[:, cols]) + dot(t_high, x_low[:, cols]) + dot(t_low, x_high[:, cols])
        )

    @pl.when(group == 3)
    def _():
        seg = 4 * sub
        for slot in range(4):
            cols = slice(slot * width, (slot + 1) * width)
            quarters = gather_quarters(
                [z_ref[g, :sub, cols] for g in range(4)], [z_ref[g, sub:, cols] for g in range(4)]
            )
            for i, quarter in enumerate(quarters):
                at = slice(i * sub, (i + 1) * sub)
                if slot == 0:
                    query_out[at, :] = up_ref[at, :] * (quarter + skip_ref[...] * gated_ref[at, :])
                elif slot == 1:
                    back_out[at, :] = quarter + skip_ref[...] * mixed_ref[at, :]
                else:
                    base = (slot - 2) * seg + i * sub
                    filter_out[base : base + sub, :] = quarter


def late(pos, inverse, acc, windows, three_g, two_g, own_m, outer_m, next_m, two_m, gated, mixed, skip, upstream):
    seg, width = upstream.shape
    rows = seg // 2
    mid = windows.shape[0] // 2

    def win_at(i, pos):
        p = pos[0]
        ends = jnp.where(p == 0, mid - 3, mid + 3)
        return jnp.where(p == 1, mid + 2, jnp.where(p == 2, mid - 2, ends)), i, 0

    group = pl.BlockSpec((rows, width), lambda i, pos: (i, 0))
    return pl.pallas_call(
        late_kernel,
        grid_spec=pltpu.PrefetchScalarGridSpec(
            num_scalar_prefetch=1,
            grid=(4,),
            in_specs=[
                pl.BlockSpec((2, 1, rows, rows), lambda i, pos: (0, i, 0, 0)),
                pl.BlockSpec((4, rows, width), lambda i, pos: (0, i, 0)),
                pl.BlockSpec((1, rows, width), win_at),
                *[group] * 6,
                whole_spec((seg, width)),
                whole_spec((seg, width)),
                whole_spec((1, width)),
                whole_spec((seg, width)),
            ],
            out_specs=[whole_spec((seg, width)), whole_spec((2 * seg, width)), whole_spec((seg, width))],
            scratch_shapes=[
                pltpu.VMEM((rows, 4 * width), jnp.bfloat16),
                pltpu.VMEM((rows, 4 * width), jnp.bfloat16),
                pltpu.VMEM((4, rows, 4 * width), jnp.float32),
            ],
        ),
        out_shape=[f32(seg, width), f32(2 * seg, width), f32(seg, width)],
        compiler_params=params(20),
        cost_estimate=cost(12 * seg * seg * width * 2, 100 * seg * width),
        name="late",
    )(pos, inverse, acc, windows, three_g, two_g, own_m, outer_m, next_m, two_m, gated, mixed, skip, upstream)


def finish_kernel(back_ref, key_ref, values_ref, made_ref, sent_ref, own_ref, side_ref, *rest):
    key_out, value_out, skip_out = rest[-3:]
    seg = back_ref.shape[0]
    back = back_ref[...] + sent_ref[:seg, :]
    key_out[...] = back * values_ref[...]
    value_out[...] = back * key_ref[...]
    total = (own_ref[...] + side_ref[...]) + (made_ref[seg:, :] + sent_ref[seg:, :])
    skip_out[...] = jnp.sum(total, axis=0, keepdims=True)


def finish(back, key_gate, values, made, sent, own_sums, side_sums, half, before=()):
    seg, full = back.shape
    width = full // 2

    def lanes(rows):
        return pl.BlockSpec((rows, width), lambda i: (0, half))

    held = pl.BlockSpec(memory_space=pl.ANY)
    return pl.pallas_call(
        finish_kernel,
        grid=(1,),
        in_specs=[lanes(seg)] * 3 + [whole_spec((seg + 8, width))] * 2 + [lanes(8)] * 2 + [held] * len(before),
        out_specs=[lanes(seg), lanes(seg), lanes(1)],
        out_shape=[f32(seg, full), f32(seg, full), f32(1, full)],
        input_output_aliases={7 + i: i for i in range(len(before))},
        compiler_params=params(12),
        cost_estimate=cost(3 * seg * width, 24 * seg * width),
        name="finish",
    )(back, key_gate, values, made, sent, own_sums, side_sums, *before)


def send(x, *pairs):
    return lax.ppermute(x, "ctx", list(pairs))


def across(x):
    return send(x, (1, 2), (2, 1))


def outward(x):
    return send(x, (1, 0), (2, 3))


def beside(x):
    return send(x, (0, 1), (1, 0), (2, 3), (3, 2))


def local_line(query_gate, key_gate, values, filter_taps, skip_gain, upstream):
    seg, width = values.shape
    forward_np, inverse_np = tables(seg)
    table, inverse = jnp.asarray(forward_np), jnp.asarray(inverse_np)
    pos = lax.axis_index("ctx").astype(jnp.int32).reshape(1)
    after = lax.optimization_barrier

    gated = key_gate * values
    side, over = beside(gated), across(gated)
    mixed, own_sums = mix(gated, upstream, query_gate)
    side_x, over_x = beside(mixed), across(mixed)
    own_g, own_m = dft(pos, table, seg, gated), dft(pos, table, seg, mixed)
    over, side, filter_taps, own_g, own_m = after((over, side, filter_taps, own_g, own_m))

    over_two, out_two = across(side), outward(over)
    outer_g = dft(pos, table, seg, side, choose=True)
    next_g = dft(pos, table, seg, over, side, choose=True)
    windows = taps_spectra(table, filter_taps, seg)
    over_x, side_x, windows, outer_g, next_g = after((over_x, side_x, windows, outer_g, next_g))

    outer_m = dft(pos, table, seg, side_x, choose=True)
    next_m = dft(pos, table, seg, over_x, side_x, choose=True)
    side_x, outer_m, next_m = after((side_x, outer_m, next_m))
    two_x = across(side_x)
    side_sums, near_sums = sums(side, side_x), sums(over, over_x)
    over_two, outer_m, next_m, side_sums, near_sums = after((over_two, outer_m, next_m, side_sums, near_sums))

    three = outward(over_two)
    two_g = dft(pos, table, seg, over_two, out_two)
    acc = early(pos, windows, (own_g, outer_g, next_g, two_g), (own_m, outer_m, next_m), seg)
    two_x, acc = after((two_x, acc))

    made_0 = back_partial(pos, table, inverse, windows, next_m, two_x, over_two, near_sums, 0, seg)
    two_x, made_0 = after((two_x, made_0))
    sent_0 = outward(made_0)
    made_1 = back_partial(pos, table, inverse, windows, next_m, two_x, over_two, near_sums, 1, seg)
    two_x, made_1 = after((two_x, made_1))
    sent_1 = outward(made_1)
    two_m, three_g = dft(pos, table, seg, two_x), dft(pos, table, seg, three)
    query_grad, filter_grad, back = late(
        pos, inverse, acc, windows, three_g, two_g, own_m, outer_m, next_m, two_m,
        gated, mixed, skip_gain[None, :], upstream,
    )
    done = finish(back, key_gate, values, made_0, sent_0, own_sums, side_sums, 0)
    sent_1, *done = after((sent_1, *done))
    key_grad, value_grad, skip_grad = finish(back, key_gate, values, made_1, sent_1, own_sums, side_sums, 1, done)
    return (query_grad, key_grad, value_grad, filter_grad, skip_grad[0])


def matmul(left, right):
    return jnp.dot(left, right, preferred_element_type=jnp.float32, precision=lax.Precision.HIGHEST)


def forward_table(seg_len, count, offset):
    num_bins = seg_len + 1
    period = 2 * seg_len
    bin_index = lax.broadcasted_iota(jnp.int32, (num_bins, count), 0)
    pos_index = lax.broadcasted_iota(jnp.int32, (num_bins, count), 1) + offset
    angles = (bin_index * pos_index % period).astype(jnp.float32) * (2.0 * math.pi / period)
    return jnp.concatenate([jnp.cos(angles), -jnp.sin(angles)], axis=0)


def inverse_table(seg_len, count, offset):
    num_bins = seg_len + 1
    period = 2 * seg_len
    pos_index = lax.broadcasted_iota(jnp.int32, (count, num_bins), 0) + offset
    bin_index = lax.broadcasted_iota(jnp.int32, (count, num_bins), 1)
    angles = (bin_index * pos_index % period).astype(jnp.float32) * (2.0 * math.pi / period)
    weights = jnp.where((bin_index == 0) | (bin_index == seg_len), 1.0, 2.0) / period
    return jnp.concatenate([weights * jnp.cos(angles), -weights * jnp.sin(angles)], axis=1)


def times_spec(first, second):
    num_bins = first.shape[0] // 2
    real_a, imag_a = (first[:num_bins], first[num_bins:])
    real_b, imag_b = (second[:num_bins], second[num_bins:])
    return jnp.concatenate(
        [real_a * real_b - imag_a * imag_b, real_a * imag_b + imag_a * real_b], axis=0
    )


def conj_times(first, second):
    num_bins = first.shape[0] // 2
    real_a, imag_a = (first[:num_bins], first[num_bins:])
    real_b, imag_b = (second[:num_bins], second[num_bins:])
    return jnp.concatenate(
        [real_a * real_b + imag_a * imag_b, real_a * imag_b - imag_a * real_b], axis=0
    )


def pick(stack, index):
    return lax.dynamic_index_in_dim(stack, index, 0, keepdims=False)


def local(query_gate, key_gate, values, filter_taps, skip_gain, upstream):
    seg_len, width_dev = values.shape
    cycle_size = lax.axis_size("ctx")
    position = lax.axis_index("ctx")
    history = seg_len * cycle_size
    gated = key_gate * values
    mixed_grad = upstream * query_gate
    table_low = forward_table(seg_len, seg_len, 0)
    table_high = forward_table(seg_len, seg_len, seg_len)
    table_taps = forward_table(seg_len, 2 * seg_len, 0)
    back_low = inverse_table(seg_len, seg_len, 0)
    back_high = inverse_table(seg_len, seg_len, seg_len)
    back_full = inverse_table(seg_len, 2 * seg_len, 0)
    own_grad_spec = matmul(table_high, mixed_grad)
    spec_rows = 2 * (seg_len + 1)

    def taps_spec(lag_block):
        start_row = (lag_block - 1) * seg_len + history
        window = lax.dynamic_slice_in_dim(filter_taps, start_row, 2 * seg_len, 0)
        return matmul(table_taps, window)

    def visit(carry, gated_spec, grad_spec, source):
        acc_conv, acc_back, partial_value = carry
        lag_block = position - source
        acc_conv = acc_conv + times_spec(taps_spec(lag_block), gated_spec)
        acc_back = acc_back + conj_times(taps_spec(-lag_block), grad_spec)
        segment = matmul(back_full, conj_times(gated_spec, own_grad_spec))
        start_row = (lag_block - 1) * seg_len + history
        current = lax.dynamic_slice_in_dim(partial_value, start_row, 2 * seg_len, 0)
        partial_value = lax.dynamic_update_slice_in_dim(
            partial_value, current + segment, start_row, 0
        )
        return (acc_conv, acc_back, partial_value)

    initial = (
        jnp.zeros((spec_rows, width_dev), jnp.float32),
        jnp.zeros((spec_rows, width_dev), jnp.float32),
        jnp.zeros((2 * history, width_dev), jnp.float32),
    )
    own_gated_spec = matmul(table_low, gated)
    pieces = (
        lax.all_gather(own_gated_spec[None], "ctx", axis=0, tiled=True),
        lax.all_gather(own_grad_spec[None], "ctx", axis=0, tiled=True),
    )

    def advance(member, state):
        return visit(state, pick(pieces[0], member), pick(pieces[1], member), member)

    folded = lax.fori_loop(0, pieces[0].shape[0], advance, initial)
    acc_conv, acc_back, partial_value = folded
    filter_grad = lax.psum_scatter(partial_value, "ctx", scatter_dimension=0, tiled=True)
    conv = matmul(back_high, acc_conv)
    back = matmul(back_low, acc_back) + skip_gain[None, :] * mixed_grad
    query_grad = upstream * (conv + skip_gain[None, :] * gated)
    key_grad = back * values
    value_grad = back * key_gate
    skip_grad = lax.psum(jnp.sum(mixed_grad * gated, axis=0), "ctx")
    return (query_grad, key_grad, value_grad, filter_grad, skip_grad)


def solution(mesh):
    in_specs = (
        P(("groups", "ctx"), "chan"),
        P(("groups", "ctx"), "chan"),
        P(("groups", "ctx"), "chan"),
        P(None, "chan"),
        P("chan"),
        P(("groups", "ctx"), "chan"),
    )
    out_specs = (
        P(("groups", "ctx"), "chan"),
        P(("groups", "ctx"), "chan"),
        P(("groups", "ctx"), "chan"),
        P(("groups", "ctx"), "chan"),
        P(("groups", "chan")),
    )
    body = local_line if mesh.shape["ctx"] == 4 else local
    return jax.shard_map(body, mesh=mesh, in_specs=in_specs, out_specs=out_specs, check_vma=False)
```

```python
import functools
import math

import jax
import jax.numpy as jnp
import ml_dtypes
import numpy as np
from jax import lax
from jax.experimental import pallas as pl
from jax.experimental.pallas import tpu as pltpu
from jax.sharding import PartitionSpec as P

COS1, SIN1, HALF = math.cos(math.pi / 8), math.sin(math.pi / 8), math.sqrt(0.5)


def split_np(table):
    high = table.astype(ml_dtypes.bfloat16)
    low = (table - high.astype(np.float64)).astype(ml_dtypes.bfloat16)
    return np.stack([high, low])


def tables(seg):
    sub = seg // 4
    bins, pos = np.arange(sub)[:, None], np.arange(sub)[None, :]
    forward = []
    for group in range(4):
        angle = 2 * np.pi * pos * (8 * bins + group + 0.5) / (2 * seg)
        cos, sin = np.cos(angle), np.sin(angle)
        forward.append(np.block([[cos, -sin], [-sin, -cos]]))
    forward = np.stack(forward)
    inverse = forward.transpose(0, 2, 1) / seg
    return split_np(forward), split_np(inverse)


def split(x):
    high = x.astype(jnp.bfloat16)
    return high, (x - high.astype(jnp.float32)).astype(jnp.bfloat16)


def dot3(table_ref, group, high, low):
    t_high, t_low = table_ref[0, group], table_ref[1, group]
    dot = functools.partial(jnp.dot, preferred_element_type=jnp.float32)
    width = high.shape[1]
    if width <= 128:
        both = dot(t_high, jnp.concatenate([high, low], axis=1))
        return both[:, :width] + both[:, width:] + dot(t_low, high)
    return dot(t_high, high) + dot(t_high, low) + dot(t_low, high)


def spread(x):
    sub = x.shape[0] // 4
    x0, x1, x2, x3 = (x[i * sub : (i + 1) * sub] for i in range(4))
    u, p, s, q, t = HALF * x2, COS1 * x1, SIN1 * x1, COS1 * x3, SIN1 * x3
    a, b, pt, sq, pmt, spq = x0 + u, x0 - u, p + t, s - q, p - t, s + q
    pairs = ((a + pt, spq + u), (b + sq, pmt + u), (b - sq, pmt - u), (a - pt, spq - u))
    return [jnp.concatenate(pair, axis=0) for pair in pairs]


def gather_quarters(re, im):
    e03, d03, e12, d12 = re[0] + re[3], re[0] - re[3], re[1] + re[2], re[1] - re[2]
    f03, g03, f12, g12 = im[0] + im[3], im[0] - im[3], im[1] + im[2], im[1] - im[2]
    return (
        e03 + e12,
        COS1 * (d03 + f12) + SIN1 * (d12 + f03),
        HALF * (e03 - e12 + g03 + g12),
        SIN1 * (d03 - f12) + COS1 * (f03 - d12),
    )


def transform(x, table_ref, store):
    for group, part in enumerate(spread(x)):
        store(group, dot3(table_ref, group, *split(part)))


def cost(flops, nbytes):
    return pl.CostEstimate(flops=int(flops), bytes_accessed=int(nbytes), transcendentals=0)


def params(mib):
    return pltpu.CompilerParams(vmem_limit_bytes=mib << 20)


def whole_spec(shape):
    return pl.BlockSpec(shape, lambda *_: (0,) * len(shape))


def f32(*shape):
    return jax.ShapeDtypeStruct(shape, jnp.float32)


def block_sums(gated, mixed):
    seg, width = gated.shape
    return jnp.sum((gated * mixed).reshape(seg // 8, 8, width), axis=0)


def sums_kernel(gated_ref, mixed_ref, out_ref):
    out_ref[...] = block_sums(gated_ref[...], mixed_ref[...])


def sums(gated, mixed):
    seg, width = gated.shape
    return pl.pallas_call(
        sums_kernel,
        grid=(1,),
        in_specs=[whole_spec((seg, width))] * 2,
        out_specs=whole_spec((8, width)),
        out_shape=f32(8, width),
        compiler_params=params(8),
        cost_estimate=cost(2 * seg * width, 8 * seg * width),
        name="sums",
    )(gated, mixed)


def mix_kernel(gated_ref, up_ref, query_ref, mixed_ref, sum_ref):
    mixed = up_ref[...] * query_ref[...]
    mixed_ref[...] = mixed
    sum_ref[...] = block_sums(gated_ref[...], mixed)


def mix(gated, upstream, query_gate):
    seg, width = gated.shape
    block = whole_spec((seg, width))
    return pl.pallas_call(
        mix_kernel,
        grid=(1,),
        in_specs=[block] * 3,
        out_specs=[block, whole_spec((8, width))],
        out_shape=[f32(seg, width), f32(8, width)],
        compiler_params=params(12),
        cost_estimate=cost(4 * seg * width, 16 * seg * width),
        name="mix",
    )(gated, upstream, query_gate)


def dft_kernel(choose, pos_ref, table_ref, *refs):
    *x_refs, out_ref = refs
    rows = out_ref.shape[0] // 4
    inner = jnp.logical_or(pos_ref[0] == 1, pos_ref[0] == 2)

    def store(group, value):
        out_ref[group * rows : (group + 1) * rows, :] = value

    x = x_refs[0][...]
    if choose:
        x = jnp.where(inner, x, x_refs[1][...] if len(x_refs) == 2 else 0.0)
    elif len(x_refs) == 2:
        x = x + x_refs[1][...]
    transform(x, table_ref, store)


def dft(pos, table, seg, *xs, choose=False):
    width = xs[0].shape[1]
    return pl.pallas_call(
        functools.partial(dft_kernel, choose),
        grid_spec=pltpu.PrefetchScalarGridSpec(
            num_scalar_prefetch=1,
            grid=(1,),
            in_specs=[whole_spec(table.shape)] + [whole_spec((seg, width))] * len(xs),
            out_specs=whole_spec((2 * seg, width)),
        ),
        out_shape=f32(2 * seg, width),
        compiler_params=params(12),
        cost_estimate=cost(3 * seg * seg * width * 2, 12 * seg * width),
        name="dft",
    )(pos, table, *xs)


def taps_kernel(table_ref, x_ref, out_ref, last_ref):
    step = pl.program_id(0)
    rows = out_ref.shape[1] // 4
    sub = rows // 2

    def store(group, value):
        base = group * rows
        sign = 1.0 if group % 2 == 0 else -1.0
        re, im = slice(base, base + sub), slice(base + sub, base + rows)
        out_ref[0, re, :] = value[:sub] - sign * last_ref[im, :]
        out_ref[0, im, :] = value[sub:] + sign * last_ref[re, :]
        last_ref[base : base + rows, :] = value

    @pl.when(step == 0)
    def _():
        last_ref[...] = jnp.zeros_like(last_ref)

    transform(x_ref[...], table_ref, store)


def taps_spectra(table, taps, seg):
    width = taps.shape[1]
    blocks = taps.shape[0] // seg
    return pl.pallas_call(
        taps_kernel,
        grid=(blocks,),
        in_specs=[whole_spec(table.shape), pl.BlockSpec((seg, width), lambda i: (i, 0))],
        out_specs=pl.BlockSpec((1, 2 * seg, width), lambda i: (jnp.maximum(i - 1, 0), 0, 0)),
        out_shape=jax.ShapeDtypeStruct((blocks - 1, 2 * seg, width), jnp.float32),
        scratch_shapes=[pltpu.VMEM((2 * seg, width), jnp.float32)],
        compiler_params=params(14),
        cost_estimate=cost(blocks * 3 * seg * seg * width * 2, blocks * 12 * seg * width),
        name="taps",
    )(table, taps)


def conj_mul(a, b):
    return a[0] * b[0] + a[1] * b[1], a[0] * b[1] - a[1] * b[0]


def mul(a, b):
    return a[0] * b[0] - a[1] * b[1], a[0] * b[1] + a[1] * b[0]


def add(a, b):
    return a[0] + b[0], a[1] + b[1]


def partial_kernel(
    pos_ref, table_ref, inverse_ref, win_near, win_far, next_ref, x_ref, gated_ref, near_sums, out_ref, z_ref
):
    rows = next_ref.shape[0] // 4
    sub = rows // 2
    for group, part in enumerate(spread(x_ref[...])):
        base = group * rows
        far = dot3(table_ref, group, *split(part))
        re, im = slice(base, base + sub), slice(base + sub, base + rows)
        total = add(
            conj_mul((win_near[0, re, :], win_near[0, im, :]), (next_ref[re, :], next_ref[im, :])),
            conj_mul((win_far[0, re, :], win_far[0, im, :]), (far[:sub], far[sub:])),
        )
        z_ref[group] = dot3(inverse_ref, group, *split(jnp.concatenate(total, axis=0)))
    quarters = gather_quarters([z_ref[g, :sub] for g in range(4)], [z_ref[g, sub:] for g in range(4)])
    for i, quarter in enumerate(quarters):
        out_ref[i * sub : (i + 1) * sub, :] = quarter
    out_ref[4 * sub :, :] = near_sums[...] + block_sums(gated_ref[...], x_ref[...])


def back_partial(pos, table, inverse, windows, next_m, x, gated, near_sums, half, seg):
    width = x.shape[1] // 2
    n = (windows.shape[0] + 1) // 2

    def window(distance):
        return pl.BlockSpec(
            (1, 2 * seg, width),
            lambda i, pos: (jnp.where(pos[0] == 1, n - 1 + distance, n - 1 - distance), 0, half),
        )

    def lanes(rows):
        return pl.BlockSpec((rows, width), lambda i, pos: (0, half))

    return pl.pallas_call(
        partial_kernel,
        grid_spec=pltpu.PrefetchScalarGridSpec(
            num_scalar_prefetch=1,
            grid=(1,),
            in_specs=[
                whole_spec(table.shape),
                whole_spec(inverse.shape),
                window(2),
                window(3),
                lanes(2 * seg),
                lanes(seg),
                lanes(seg),
                lanes(8),
            ],
            out_specs=whole_spec((seg + 8, width)),
            scratch_shapes=[pltpu.VMEM((4, seg // 2, width), jnp.float32)],
        ),
        out_shape=f32(seg + 8, width),
        compiler_params=params(24),
        cost_estimate=cost(6 * seg * seg * width * 2, 24 * seg * width),
        name="partial",
    )(pos, table, inverse, windows, windows, next_m, x, gated, near_sums)


OWN, OUTER, NEXT, TWO, THREE = range(5)
PAIRS = (
    ((), ((OWN, THREE),), ((OWN, TWO), (NEXT, THREE))),
    (
        ((OUTER, NEXT), (OWN, TWO)),
        ((OUTER, OWN), (OWN, NEXT), (NEXT, TWO)),
        ((OUTER, OUTER), (OWN, OWN), (NEXT, NEXT), (TWO, TWO)),
    ),
    (
        ((TWO, TWO), (NEXT, NEXT), (OWN, OWN), (OUTER, OUTER)),
        ((NEXT, TWO), (OWN, NEXT), (OUTER, OWN)),
        ((OWN, TWO), (OUTER, NEXT)),
    ),
    (((NEXT, THREE), (OWN, TWO)), ((OWN, THREE),), ()),
)


def is_late(pair):
    return pair[0] == TWO or pair[1] == THREE


def pair_sums(distances, gated, mixed, sign, late):
    total = []
    for pairs in distances:
        value = None
        for m, g in pairs:
            if is_late((m, g)) == late:
                term = conj_mul(gated[g](), mixed[m]())
                value = term if value is None else add(value, term)
        total.append(value)
    out = []
    for low, high in zip(total[:2], total[1:]):
        if high is not None:
            turned = (sign * high[1], -sign * high[0])
            low = turned if low is None else add(low, turned)
        out.append(low)
    return out


TILE = 16


def tile_reader(tile, sub):
    re = pl.ds(pl.multiple_of(tile * TILE, TILE), TILE)
    im = pl.ds(pl.multiple_of(sub + tile * TILE, TILE), TILE)

    def read(ref, *lead):
        return ref[(*lead, re, slice(None))], ref[(*lead, im, slice(None))]

    return re, im, read


def group_sign():
    return jnp.where(pl.program_id(0) % 2 == 0, 1.0, -1.0)


def early_kernel(
    pos_ref, win_own, win_outer, win_next, win_two, own_g, outer_g, next_g, two_g, own_m, outer_m, next_m, out_ref
):
    pos, sign = pos_ref[0], group_sign()
    rows = own_g.shape[0]
    sub = rows // 2
    count = sub // TILE

    def put(at, slot, value):
        re, im = at
        out_ref[slot, re, :] = value[0]
        out_ref[slot, im, :] = value[1]

    def sums(tile, _):
        re, im, read = tile_reader(tile, sub)
        own, outer, ahead = read(win_own, 0), read(win_outer, 0), read(win_next, 0)
        conv = add(mul(own, read(own_g)), mul(outer, read(outer_g)))
        conv = add(conv, add(mul(ahead, read(next_g)), mul(read(win_two, 0), read(two_g))))
        put((re, im), 0, conv)
        back = add(conj_mul(own, read(own_m)), conj_mul(ahead, read(outer_m)))
        put((re, im), 1, add(back, conj_mul(outer, read(next_m))))
        return _

    lax.fori_loop(0, count, sums, 0)
    for where, distances in enumerate(PAIRS):

        @pl.when(pos == where)
        def _():
            def lags(tile, _):
                re, im, read = tile_reader(tile, sub)
                gated = [functools.partial(read, ref) for ref in (own_g, outer_g, next_g, two_g)]
                mixed = [functools.partial(read, ref) for ref in (own_m, outer_m, next_m)]
                for slot, value in enumerate(pair_sums(distances, gated, mixed, sign, False)):
                    if value is None:
                        value = (jnp.zeros_like(own_g[re, :]),) * 2
                    put((re, im), 2 + slot, value)
                return _

            lax.fori_loop(0, count, lags, 0)


def early(pos, windows, gated, mixed, seg):
    width = gated[0].shape[1]
    rows = seg // 2
    mid = windows.shape[0] // 2

    def window(index):
        return pl.BlockSpec((1, rows, width), lambda i, pos: (index(pos[0]), i, 0))

    group = pl.BlockSpec((rows, width), lambda i, pos: (i, 0))
    return pl.pallas_call(
        early_kernel,
        grid_spec=pltpu.PrefetchScalarGridSpec(
            num_scalar_prefetch=1,
            grid=(4,),
            in_specs=[
                window(lambda p: mid),
                window(lambda p: jnp.where(p < 2, mid + 1, mid - 1)),
                window(lambda p: jnp.where(p < 2, mid - 1, mid + 1)),
                window(lambda p: jnp.where(p < 2, mid - 2, mid + 2)),
            ]
            + [group] * 7,
            out_specs=pl.BlockSpec((4, rows, width), lambda i, pos: (0, i, 0)),
        ),
        out_shape=f32(4, 2 * seg, width),
        compiler_params=params(14),
        cost_estimate=cost(200 * seg * width, 120 * seg * width),
        name="early",
    )(pos, *[windows] * 4, *gated, *mixed)


def late_kernel(
    pos_ref, inverse_ref, acc_ref, win_ref, three_g, two_g, own_m, outer_m, next_m, *rest
):
    two_m, gated_ref, mixed_ref, skip_ref, up_ref, query_out, filter_out, back_out, x_high, x_low, z_ref = rest
    group = pl.program_id(0)
    pos, sign = pos_ref[0], group_sign()
    rows, width = own_m.shape
    sub = rows // 2

    def put(at, slot, value):
        for rows_at, part in zip(at, value):
            high, low = split(part)
            x_high[rows_at, slot * width : (slot + 1) * width] = high
            x_low[rows_at, slot * width : (slot + 1) * width] = low

    for where, distances in enumerate(PAIRS):

        @pl.when(pos == where)
        def _():
            def lags(tile, _):
                re, im, read = tile_reader(tile, sub)

                gated = [None, None, None, functools.partial(read, two_g), functools.partial(read, three_g)]
                mixed = [functools.partial(read, ref) for ref in (own_m, outer_m, next_m, two_m)]
                total = [read(acc_ref, slot) for slot in range(4)]
                if where in (0, 3):
                    total[0] = add(total[0], mul(read(win_ref, 0), gated[THREE]()))
                else:
                    total[1] = add(total[1], conj_mul(read(win_ref, 0), mixed[TWO]()))
                for slot, value in enumerate(pair_sums(distances, gated, mixed, sign, True)):
                    if value is not None:
                        total[2 + slot] = add(total[2 + slot], value)
                for slot, value in enumerate(total):
                    put((re, im), slot, value)
                return _

            lax.fori_loop(0, sub // TILE, lags, 0)

    dot = functools.partial(jnp.dot, preferred_element_type=jnp.float32)
    t_high, t_low = inverse_ref[0, 0], inverse_ref[1, 0]
    for slot in range(4):
        cols = slice(slot * width, (slot + 1) * width)
        z_ref[group, :, cols] = (
            dot(t_high, x_high[:, cols]) + dot(t_high, x_low[:, cols]) + dot(t_low, x_high[:, cols])
        )

    @pl.when(group == 3)
    def _():
        seg = 4 * sub
        for slot in range(4):
            cols = slice(slot * width, (slot + 1) * width)
            quarters = gather_quarters(
                [z_ref[g, :sub, cols] for g in range(4)], [z_ref[g, sub:, cols] for g in range(4)]
            )
            for i, quarter in enumerate(quarters):
                at = slice(i * sub, (i + 1) * sub)
                if slot == 0:
                    query_out[at, :] = up_ref[at, :] * (quarter + skip_ref[...] * gated_ref[at, :])
                elif slot == 1:
                    back_out[at, :] = quarter + skip_ref[...] * mixed_ref[at, :]
                else:
                    base = (slot - 2) * seg + i * sub
                    filter_out[base : base + sub, :] = quarter


def late(pos, inverse, acc, windows, three_g, two_g, own_m, outer_m, next_m, two_m, gated, mixed, skip, upstream):
    seg, width = upstream.shape
    rows = seg // 2
    mid = windows.shape[0] // 2

    def win_at(i, pos):
        p = pos[0]
        ends = jnp.where(p == 0, mid - 3, mid + 3)
        return jnp.where(p == 1, mid + 2, jnp.where(p == 2, mid - 2, ends)), i, 0

    group = pl.BlockSpec((rows, width), lambda i, pos: (i, 0))
    return pl.pallas_call(
        late_kernel,
        grid_spec=pltpu.PrefetchScalarGridSpec(
            num_scalar_prefetch=1,
            grid=(4,),
            in_specs=[
                pl.BlockSpec((2, 1, rows, rows), lambda i, pos: (0, i, 0, 0)),
                pl.BlockSpec((4, rows, width), lambda i, pos: (0, i, 0)),
                pl.BlockSpec((1, rows, width), win_at),
                *[group] * 6,
                whole_spec((seg, width)),
                whole_spec((seg, width)),
                whole_spec((1, width)),
                whole_spec((seg, width)),
            ],
            out_specs=[whole_spec((seg, width)), whole_spec((2 * seg, width)), whole_spec((seg, width))],
            scratch_shapes=[
                pltpu.VMEM((rows, 4 * width), jnp.bfloat16),
                pltpu.VMEM((rows, 4 * width), jnp.bfloat16),
                pltpu.VMEM((4, rows, 4 * width), jnp.float32),
            ],
        ),
        out_shape=[f32(seg, width), f32(2 * seg, width), f32(seg, width)],
        compiler_params=params(20),
        cost_estimate=cost(12 * seg * seg * width * 2, 100 * seg * width),
        name="late",
    )(pos, inverse, acc, windows, three_g, two_g, own_m, outer_m, next_m, two_m, gated, mixed, skip, upstream)


def finish_kernel(back_ref, key_ref, values_ref, made_ref, sent_ref, own_ref, side_ref, *rest):
    key_out, value_out, skip_out = rest[-3:]
    seg = back_ref.shape[0]
    back = back_ref[...] + sent_ref[:seg, :]
    key_out[...] = back * values_ref[...]
    value_out[...] = back * key_ref[...]
    total = (own_ref[...] + side_ref[...]) + (made_ref[seg:, :] + sent_ref[seg:, :])
    skip_out[...] = jnp.sum(total, axis=0, keepdims=True)


def finish(back, key_gate, values, made, sent, own_sums, side_sums, half, before=()):
    seg, full = back.shape
    width = full // 2

    def lanes(rows):
        return pl.BlockSpec((rows, width), lambda i: (0, half))

    held = pl.BlockSpec(memory_space=pl.ANY)
    return pl.pallas_call(
        finish_kernel,
        grid=(1,),
        in_specs=[lanes(seg)] * 3 + [whole_spec((seg + 8, width))] * 2 + [lanes(8)] * 2 + [held] * len(before),
        out_specs=[lanes(seg), lanes(seg), lanes(1)],
        out_shape=[f32(seg, full), f32(seg, full), f32(1, full)],
        input_output_aliases={7 + i: i for i in range(len(before))},
        compiler_params=params(12),
        cost_estimate=cost(3 * seg * width, 24 * seg * width),
        name="finish",
    )(back, key_gate, values, made, sent, own_sums, side_sums, *before)


def send(x, *pairs):
    return lax.ppermute(x, "ctx", list(pairs))


def across(x):
    return send(x, (1, 2), (2, 1))


def outward(x):
    return send(x, (1, 0), (2, 3))


def beside(x):
    return send(x, (0, 1), (1, 0), (2, 3), (3, 2))


def local_line(query_gate, key_gate, values, filter_taps, skip_gain, upstream):
    seg, width = values.shape
    forward_np, inverse_np = tables(seg)
    table, inverse = jnp.asarray(forward_np), jnp.asarray(inverse_np)
    pos = lax.axis_index("ctx").astype(jnp.int32).reshape(1)
    after = lax.optimization_barrier

    gated = key_gate * values
    side, over = beside(gated), across(gated)
    mixed, own_sums = mix(gated, upstream, query_gate)
    side_x, over_x = beside(mixed), across(mixed)
    own_g, own_m = dft(pos, table, seg, gated), dft(pos, table, seg, mixed)
    over, side, filter_taps, own_g, own_m = after((over, side, filter_taps, own_g, own_m))

    over_two, out_two = across(side), outward(over)
    outer_g = dft(pos, table, seg, side, choose=True)
    next_g = dft(pos, table, seg, over, side, choose=True)
    windows = taps_spectra(table, filter_taps, seg)
    over_x, side_x, windows, outer_g, next_g = after((over_x, side_x, windows, outer_g, next_g))

    outer_m = dft(pos, table, seg, side_x, choose=True)
    next_m = dft(pos, table, seg, over_x, side_x, choose=True)
    side_x, outer_m, next_m = after((side_x, outer_m, next_m))
    two_x = across(side_x)
    side_sums, near_sums = sums(side, side_x), sums(over, over_x)
    over_two, outer_m, next_m, side_sums, near_sums = after((over_two, outer_m, next_m, side_sums, near_sums))

    three = outward(over_two)
    two_g = dft(pos, table, seg, over_two, out_two)
    acc = early(pos, windows, (own_g, outer_g, next_g, two_g), (own_m, outer_m, next_m), seg)
    two_x, acc = after((two_x, acc))

    made_0 = back_partial(pos, table, inverse, windows, next_m, two_x, over_two, near_sums, 0, seg)
    two_x, made_0 = after((two_x, made_0))
    sent_0 = outward(made_0)
    made_1 = back_partial(pos, table, inverse, windows, next_m, two_x, over_two, near_sums, 1, seg)
    two_x, made_1 = after((two_x, made_1))
    sent_1 = outward(made_1)
    two_m, three_g = dft(pos, table, seg, two_x), dft(pos, table, seg, three)
    query_grad, filter_grad, back = late(
        pos, inverse, acc, windows, three_g, two_g, own_m, outer_m, next_m, two_m,
        gated, mixed, skip_gain[None, :], upstream,
    )
    done = finish(back, key_gate, values, made_0, sent_0, own_sums, side_sums, 0)
    sent_1, *done = after((sent_1, *done))
    key_grad, value_grad, skip_grad = finish(back, key_gate, values, made_1, sent_1, own_sums, side_sums, 1, done)
    return (query_grad, key_grad, value_grad, filter_grad, skip_grad[0])


def matmul(left, right):
    return jnp.dot(left, right, preferred_element_type=jnp.float32, precision=lax.Precision.HIGHEST)


def forward_table(seg_len, count, offset):
    num_bins = seg_len + 1
    period = 2 * seg_len
    bin_index = lax.broadcasted_iota(jnp.int32, (num_bins, count), 0)
    pos_index = lax.broadcasted_iota(jnp.int32, (num_bins, count), 1) + offset
    angles = (bin_index * pos_index % period).astype(jnp.float32) * (2.0 * math.pi / period)
    return jnp.concatenate([jnp.cos(angles), -jnp.sin(angles)], axis=0)


def inverse_table(seg_len, count, offset):
    num_bins = seg_len + 1
    period = 2 * seg_len
    pos_index = lax.broadcasted_iota(jnp.int32, (count, num_bins), 0) + offset
    bin_index = lax.broadcasted_iota(jnp.int32, (count, num_bins), 1)
    angles = (bin_index * pos_index % period).astype(jnp.float32) * (2.0 * math.pi / period)
    weights = jnp.where((bin_index == 0) | (bin_index == seg_len), 1.0, 2.0) / period
    return jnp.concatenate([weights * jnp.cos(angles), -weights * jnp.sin(angles)], axis=1)


def times_spec(first, second):
    num_bins = first.shape[0] // 2
    real_a, imag_a = (first[:num_bins], first[num_bins:])
    real_b, imag_b = (second[:num_bins], second[num_bins:])
    return jnp.concatenate(
        [real_a * real_b - imag_a * imag_b, real_a * imag_b + imag_a * real_b], axis=0
    )


def conj_times(first, second):
    num_bins = first.shape[0] // 2
    real_a, imag_a = (first[:num_bins], first[num_bins:])
    real_b, imag_b = (second[:num_bins], second[num_bins:])
    return jnp.concatenate(
        [real_a * real_b + imag_a * imag_b, real_a * imag_b - imag_a * real_b], axis=0
    )


def pick(stack, index):
    return lax.dynamic_index_in_dim(stack, index, 0, keepdims=False)


def local(query_gate, key_gate, values, filter_taps, skip_gain, upstream):
    seg_len, width_dev = values.shape
    cycle_size = lax.axis_size("ctx")
    position = lax.axis_index("ctx")
    history = seg_len * cycle_size
    gated = key_gate * values
    mixed_grad = upstream * query_gate
    table_low = forward_table(seg_len, seg_len, 0)
    table_high = forward_table(seg_len, seg_len, seg_len)
    table_taps = forward_table(seg_len, 2 * seg_len, 0)
    back_low = inverse_table(seg_len, seg_len, 0)
    back_high = inverse_table(seg_len, seg_len, seg_len)
    back_full = inverse_table(seg_len, 2 * seg_len, 0)
    own_grad_spec = matmul(table_high, mixed_grad)
    spec_rows = 2 * (seg_len + 1)

    def taps_spec(lag_block):
        start_row = (lag_block - 1) * seg_len + history
        window = lax.dynamic_slice_in_dim(filter_taps, start_row, 2 * seg_len, 0)
        return matmul(table_taps, window)

    def visit(carry, gated_spec, grad_spec, source):
        acc_conv, acc_back, partial_value = carry
        lag_block = position - source
        acc_conv = acc_conv + times_spec(taps_spec(lag_block), gated_spec)
        acc_back = acc_back + conj_times(taps_spec(-lag_block), grad_spec)
        segment = matmul(back_full, conj_times(gated_spec, own_grad_spec))
        start_row = (lag_block - 1) * seg_len + history
        current = lax.dynamic_slice_in_dim(partial_value, start_row, 2 * seg_len, 0)
        partial_value = lax.dynamic_update_slice_in_dim(
            partial_value, current + segment, start_row, 0
        )
        return (acc_conv, acc_back, partial_value)

    initial = (
        jnp.zeros((spec_rows, width_dev), jnp.float32),
        jnp.zeros((spec_rows, width_dev), jnp.float32),
        jnp.zeros((2 * history, width_dev), jnp.float32),
    )
    own_gated_spec = matmul(table_low, gated)
    pieces = (
        lax.all_gather(own_gated_spec[None], "ctx", axis=0, tiled=True),
        lax.all_gather(own_grad_spec[None], "ctx", axis=0, tiled=True),
    )

    def advance(member, state):
        return visit(state, pick(pieces[0], member), pick(pieces[1], member), member)

    folded = lax.fori_loop(0, pieces[0].shape[0], advance, initial)
    acc_conv, acc_back, partial_value = folded
    filter_grad = lax.psum_scatter(partial_value, "ctx", scatter_dimension=0, tiled=True)
    conv = matmul(back_high, acc_conv)
    back = matmul(back_low, acc_back) + skip_gain[None, :] * mixed_grad
    query_grad = upstream * (conv + skip_gain[None, :] * gated)
    key_grad = back * values
    value_grad = back * key_gate
    skip_grad = lax.psum(jnp.sum(mixed_grad * gated, axis=0), "ctx")
    return (query_grad, key_grad, value_grad, filter_grad, skip_grad)


def solution(mesh):
    in_specs = (
        P(("groups", "ctx"), "chan"),
        P(("groups", "ctx"), "chan"),
        P(("groups", "ctx"), "chan"),
        P(None, "chan"),
        P("chan"),
        P(("groups", "ctx"), "chan"),
    )
    out_specs = (
        P(("groups", "ctx"), "chan"),
        P(("groups", "ctx"), "chan"),
        P(("groups", "ctx"), "chan"),
        P(("groups", "ctx"), "chan"),
        P(("groups", "chan")),
    )
    body = local_line if mesh.shape["ctx"] == 4 else local
    return jax.shard_map(body, mesh=mesh, in_specs=in_specs, out_specs=out_specs, check_vma=False)
```

```python
import functools
import math

import jax
import jax.numpy as jnp
import ml_dtypes
import numpy as np
from jax import lax
from jax.experimental import pallas as pl
from jax.experimental.pallas import tpu as pltpu
from jax.sharding import PartitionSpec as P

COS1, SIN1, HALF = math.cos(math.pi / 8), math.sin(math.pi / 8), math.sqrt(0.5)


def split_np(table):
    high = table.astype(ml_dtypes.bfloat16)
    low = (table - high.astype(np.float64)).astype(ml_dtypes.bfloat16)
    return np.stack([high, low])


def tables(seg):
    sub = seg // 4
    bins, pos = np.arange(sub)[:, None], np.arange(sub)[None, :]
    forward = []
    for group in range(4):
        angle = 2 * np.pi * pos * (8 * bins + group + 0.5) / (2 * seg)
        cos, sin = np.cos(angle), np.sin(angle)
        forward.append(np.block([[cos, -sin], [-sin, -cos]]))
    forward = np.stack(forward)
    inverse = forward.transpose(0, 2, 1) / seg
    return split_np(forward), split_np(inverse)


def split(x):
    high = x.astype(jnp.bfloat16)
    return high, (x - high.astype(jnp.float32)).astype(jnp.bfloat16)


def dot3(table_ref, group, high, low):
    t_high, t_low = table_ref[0, group], table_ref[1, group]
    dot = functools.partial(jnp.dot, preferred_element_type=jnp.float32)
    width = high.shape[1]
    if width <= 128:
        both = dot(t_high, jnp.concatenate([high, low], axis=1))
        return both[:, :width] + both[:, width:] + dot(t_low, high)
    return dot(t_high, high) + dot(t_high, low) + dot(t_low, high)


def spread(x):
    sub = x.shape[0] // 4
    x0, x1, x2, x3 = (x[i * sub : (i + 1) * sub] for i in range(4))
    u, p, s, q, t = HALF * x2, COS1 * x1, SIN1 * x1, COS1 * x3, SIN1 * x3
    a, b, pt, sq, pmt, spq = x0 + u, x0 - u, p + t, s - q, p - t, s + q
    pairs = ((a + pt, spq + u), (b + sq, pmt + u), (b - sq, pmt - u), (a - pt, spq - u))
    return [jnp.concatenate(pair, axis=0) for pair in pairs]


def gather_quarters(re, im):
    e03, d03, e12, d12 = re[0] + re[3], re[0] - re[3], re[1] + re[2], re[1] - re[2]
    f03, g03, f12, g12 = im[0] + im[3], im[0] - im[3], im[1] + im[2], im[1] - im[2]
    return (
        e03 + e12,
        COS1 * (d03 + f12) + SIN1 * (d12 + f03),
        HALF * (e03 - e12 + g03 + g12),
        SIN1 * (d03 - f12) + COS1 * (f03 - d12),
    )


def transform(x, table_ref, store):
    for group, part in enumerate(spread(x)):
        store(group, dot3(table_ref, group, *split(part)))


def cost(flops, nbytes):
    return pl.CostEstimate(flops=int(flops), bytes_accessed=int(nbytes), transcendentals=0)


def params(mib):
    return pltpu.CompilerParams(vmem_limit_bytes=mib << 20)


def whole_spec(shape):
    return pl.BlockSpec(shape, lambda *_: (0,) * len(shape))


def f32(*shape):
    return jax.ShapeDtypeStruct(shape, jnp.float32)


def block_sums(gated, mixed):
    seg, width = gated.shape
    return jnp.sum((gated * mixed).reshape(seg // 8, 8, width), axis=0)


def sums_kernel(gated_ref, mixed_ref, out_ref):
    out_ref[...] = block_sums(gated_ref[...], mixed_ref[...])


def sums(gated, mixed):
    seg, width = gated.shape
    return pl.pallas_call(
        sums_kernel,
        grid=(1,),
        in_specs=[whole_spec((seg, width))] * 2,
        out_specs=whole_spec((8, width)),
        out_shape=f32(8, width),
        compiler_params=params(8),
        cost_estimate=cost(2 * seg * width, 8 * seg * width),
        name="sums",
    )(gated, mixed)


def mix_kernel(gated_ref, up_ref, query_ref, mixed_ref, sum_ref):
    mixed = up_ref[...] * query_ref[...]
    mixed_ref[...] = mixed
    sum_ref[...] = block_sums(gated_ref[...], mixed)


def mix(gated, upstream, query_gate):
    seg, width = gated.shape
    block = whole_spec((seg, width))
    return pl.pallas_call(
        mix_kernel,
        grid=(1,),
        in_specs=[block] * 3,
        out_specs=[block, whole_spec((8, width))],
        out_shape=[f32(seg, width), f32(8, width)],
        compiler_params=params(12),
        cost_estimate=cost(4 * seg * width, 16 * seg * width),
        name="mix",
    )(gated, upstream, query_gate)


def dft_kernel(choose, pos_ref, table_ref, *refs):
    *x_refs, out_ref = refs
    rows = out_ref.shape[0] // 4
    inner = jnp.logical_or(pos_ref[0] == 1, pos_ref[0] == 2)

    def store(group, value):
        out_ref[group * rows : (group + 1) * rows, :] = value

    x = x_refs[0][...]
    if choose:
        x = jnp.where(inner, x, x_refs[1][...] if len(x_refs) == 2 else 0.0)
    elif len(x_refs) == 2:
        x = x + x_refs[1][...]
    transform(x, table_ref, store)


def dft(pos, table, seg, *xs, choose=False):
    width = xs[0].shape[1]
    return pl.pallas_call(
        functools.partial(dft_kernel, choose),
        grid_spec=pltpu.PrefetchScalarGridSpec(
            num_scalar_prefetch=1,
            grid=(1,),
            in_specs=[whole_spec(table.shape)] + [whole_spec((seg, width))] * len(xs),
            out_specs=whole_spec((2 * seg, width)),
        ),
        out_shape=f32(2 * seg, width),
        compiler_params=params(12),
        cost_estimate=cost(3 * seg * seg * width * 2, 12 * seg * width),
        name="dft",
    )(pos, table, *xs)


def taps_kernel(table_ref, x_ref, out_ref, last_ref):
    step = pl.program_id(0)
    rows = out_ref.shape[1] // 4
    sub = rows // 2

    def store(group, value):
        base = group * rows
        sign = 1.0 if group % 2 == 0 else -1.0
        re, im = slice(base, base + sub), slice(base + sub, base + rows)
        out_ref[0, re, :] = value[:sub] - sign * last_ref[im, :]
        out_ref[0, im, :] = value[sub:] + sign * last_ref[re, :]
        last_ref[base : base + rows, :] = value

    @pl.when(step == 0)
    def _():
        last_ref[...] = jnp.zeros_like(last_ref)

    transform(x_ref[...], table_ref, store)


def taps_spectra(table, taps, seg):
    width = taps.shape[1]
    blocks = taps.shape[0] // seg
    return pl.pallas_call(
        taps_kernel,
        grid=(blocks,),
        in_specs=[whole_spec(table.shape), pl.BlockSpec((seg, width), lambda i: (i, 0))],
        out_specs=pl.BlockSpec((1, 2 * seg, width), lambda i: (jnp.maximum(i - 1, 0), 0, 0)),
        out_shape=jax.ShapeDtypeStruct((blocks - 1, 2 * seg, width), jnp.float32),
        scratch_shapes=[pltpu.VMEM((2 * seg, width), jnp.float32)],
        compiler_params=params(14),
        cost_estimate=cost(blocks * 3 * seg * seg * width * 2, blocks * 12 * seg * width),
        name="taps",
    )(table, taps)


def conj_mul(a, b):
    return a[0] * b[0] + a[1] * b[1], a[0] * b[1] - a[1] * b[0]


def mul(a, b):
    return a[0] * b[0] - a[1] * b[1], a[0] * b[1] + a[1] * b[0]


def add(a, b):
    return a[0] + b[0], a[1] + b[1]


def ahead_kernel(pos_ref, win_near, win_far, next_ref, near_ref, far_ref):
    rows = next_ref.shape[0]
    sub = rows // 2
    re, im = slice(0, sub), slice(sub, rows)
    near = conj_mul((win_near[0, re, :], win_near[0, im, :]), (next_ref[re, :], next_ref[im, :]))
    near_ref[re, :], near_ref[im, :] = near
    far_ref[...] = win_far[0]


def ahead(pos, windows, next_m, seg):
    width = next_m.shape[1]
    rows = seg // 2
    n = (windows.shape[0] + 1) // 2

    def window(distance):
        return pl.BlockSpec(
            (1, rows, width),
            lambda i, pos: (jnp.where(pos[0] == 1, n - 1 + distance, n - 1 - distance), i, 0),
        )

    group = pl.BlockSpec((rows, width), lambda i, pos: (i, 0))
    return pl.pallas_call(
        ahead_kernel,
        grid_spec=pltpu.PrefetchScalarGridSpec(
            num_scalar_prefetch=1,
            grid=(4,),
            in_specs=[window(2), window(3), group],
            out_specs=[group] * 2,
        ),
        out_shape=[f32(2 * seg, width)] * 2,
        compiler_params=params(8),
        cost_estimate=cost(12 * seg * width, 40 * seg * width),
        name="ahead",
    )(pos, windows, windows, next_m)


def partial_kernel(half, table_ref, inverse_ref, near_ref, win_ref, x_ref, gated_ref, near_sums, out_ref, z_ref):
    rows = near_ref.shape[0] // 4
    sub = rows // 2
    width = out_ref.shape[1]
    lanes = slice(half * width, (half + 1) * width)
    x = x_ref[:, lanes]
    for group, part in enumerate(spread(x)):
        base = group * rows
        far = dot3(table_ref, group, *split(part))
        re, im = slice(base, base + sub), slice(base + sub, base + rows)
        total = add(
            (near_ref[re, lanes], near_ref[im, lanes]),
            conj_mul((win_ref[re, lanes], win_ref[im, lanes]), (far[:sub], far[sub:])),
        )
        z_ref[group] = dot3(inverse_ref, group, *split(jnp.concatenate(total, axis=0)))
    quarters = gather_quarters([z_ref[g, :sub] for g in range(4)], [z_ref[g, sub:] for g in range(4)])
    for i, quarter in enumerate(quarters):
        out_ref[i * sub : (i + 1) * sub, :] = quarter
    out_ref[4 * sub :, :] = near_sums[:, lanes] + block_sums(gated_ref[:, lanes], x)


def back_partial(table, inverse, near, window, x, gated, near_sums, half):
    seg, full = x.shape
    width = full // 2
    whole = (table, inverse, near, window, x, gated, near_sums)
    return pl.pallas_call(
        functools.partial(partial_kernel, half),
        grid=(1,),
        in_specs=[whole_spec(a.shape) for a in whole],
        out_specs=whole_spec((seg + 8, width)),
        out_shape=f32(seg + 8, width),
        scratch_shapes=[pltpu.VMEM((4, seg // 2, width), jnp.float32)],
        compiler_params=params(24),
        cost_estimate=cost(6 * seg * seg * width * 2, 24 * seg * width),
        name="partial",
    )(*whole)


OWN, OUTER, NEXT, TWO, THREE = range(5)
PAIRS = (
    ((), ((OWN, THREE),), ((OWN, TWO), (NEXT, THREE))),
    (
        ((OUTER, NEXT), (OWN, TWO)),
        ((OUTER, OWN), (OWN, NEXT), (NEXT, TWO)),
        ((OUTER, OUTER), (OWN, OWN), (NEXT, NEXT), (TWO, TWO)),
    ),
    (
        ((TWO, TWO), (NEXT, NEXT), (OWN, OWN), (OUTER, OUTER)),
        ((NEXT, TWO), (OWN, NEXT), (OUTER, OWN)),
        ((OWN, TWO), (OUTER, NEXT)),
    ),
    (((NEXT, THREE), (OWN, TWO)), ((OWN, THREE),), ()),
)


def is_late(pair):
    return pair[0] == TWO or pair[1] == THREE


def pair_sums(distances, gated, mixed, sign, late):
    total = []
    for pairs in distances:
        value = None
        for m, g in pairs:
            if is_late((m, g)) == late:
                term = conj_mul(gated[g](), mixed[m]())
                value = term if value is None else add(value, term)
        total.append(value)
    out = []
    for low, high in zip(total[:2], total[1:]):
        if high is not None:
            turned = (sign * high[1], -sign * high[0])
            low = turned if low is None else add(low, turned)
        out.append(low)
    return out


TILE = 16


def tile_reader(tile, sub):
    re = pl.ds(pl.multiple_of(tile * TILE, TILE), TILE)
    im = pl.ds(pl.multiple_of(sub + tile * TILE, TILE), TILE)

    def read(ref, *lead):
        return ref[(*lead, re, slice(None))], ref[(*lead, im, slice(None))]

    return re, im, read


def group_sign():
    return jnp.where(pl.program_id(0) % 2 == 0, 1.0, -1.0)


def early_kernel(
    pos_ref, win_own, win_outer, win_next, win_two, own_g, outer_g, next_g, two_g, own_m, outer_m, next_m, out_ref
):
    pos, sign = pos_ref[0], group_sign()
    rows = own_g.shape[0]
    sub = rows // 2
    count = sub // TILE

    def put(at, slot, value):
        re, im = at
        out_ref[slot, re, :] = value[0]
        out_ref[slot, im, :] = value[1]

    def sums(tile, _):
        re, im, read = tile_reader(tile, sub)
        own, outer, ahead = read(win_own, 0), read(win_outer, 0), read(win_next, 0)
        conv = add(mul(own, read(own_g)), mul(outer, read(outer_g)))
        conv = add(conv, add(mul(ahead, read(next_g)), mul(read(win_two, 0), read(two_g))))
        put((re, im), 0, conv)
        back = add(conj_mul(own, read(own_m)), conj_mul(ahead, read(outer_m)))
        put((re, im), 1, add(back, conj_mul(outer, read(next_m))))
        return _

    lax.fori_loop(0, count, sums, 0)
    for where, distances in enumerate(PAIRS):

        @pl.when(pos == where)
        def _():
            def lags(tile, _):
                re, im, read = tile_reader(tile, sub)
                gated = [functools.partial(read, ref) for ref in (own_g, outer_g, next_g, two_g)]
                mixed = [functools.partial(read, ref) for ref in (own_m, outer_m, next_m)]
                for slot, value in enumerate(pair_sums(distances, gated, mixed, sign, False)):
                    if value is None:
                        value = (jnp.zeros_like(own_g[re, :]),) * 2
                    put((re, im), 2 + slot, value)
                return _

            lax.fori_loop(0, count, lags, 0)


def early(pos, windows, gated, mixed, seg):
    width = gated[0].shape[1]
    rows = seg // 2
    mid = windows.shape[0] // 2

    def window(index):
        return pl.BlockSpec((1, rows, width), lambda i, pos: (index(pos[0]), i, 0))

    group = pl.BlockSpec((rows, width), lambda i, pos: (i, 0))
    return pl.pallas_call(
        early_kernel,
        grid_spec=pltpu.PrefetchScalarGridSpec(
            num_scalar_prefetch=1,
            grid=(4,),
            in_specs=[
                window(lambda p: mid),
                window(lambda p: jnp.where(p < 2, mid + 1, mid - 1)),
                window(lambda p: jnp.where(p < 2, mid - 1, mid + 1)),
                window(lambda p: jnp.where(p < 2, mid - 2, mid + 2)),
            ]
            + [group] * 7,
            out_specs=pl.BlockSpec((4, rows, width), lambda i, pos: (0, i, 0)),
        ),
        out_shape=f32(4, 2 * seg, width),
        compiler_params=params(14),
        cost_estimate=cost(200 * seg * width, 120 * seg * width),
        name="early",
    )(pos, *[windows] * 4, *gated, *mixed)


def late_kernel(
    pos_ref, inverse_ref, acc_ref, win_ref, three_g, two_g, own_m, outer_m, next_m, *rest
):
    two_m, gated_ref, mixed_ref, skip_ref, up_ref, query_out, filter_out, back_out, x_high, x_low, z_ref = rest
    group = pl.program_id(0)
    pos, sign = pos_ref[0], group_sign()
    rows, width = own_m.shape
    sub = rows // 2

    def put(at, slot, value):
        for rows_at, part in zip(at, value):
            high, low = split(part)
            x_high[rows_at, slot * width : (slot + 1) * width] = high
            x_low[rows_at, slot * width : (slot + 1) * width] = low

    for where, distances in enumerate(PAIRS):

        @pl.when(pos == where)
        def _():
            def lags(tile, _):
                re, im, read = tile_reader(tile, sub)

                gated = [None, None, None, functools.partial(read, two_g), functools.partial(read, three_g)]
                mixed = [functools.partial(read, ref) for ref in (own_m, outer_m, next_m, two_m)]
                total = [read(acc_ref, slot) for slot in range(4)]
                if where in (0, 3):
                    total[0] = add(total[0], mul(read(win_ref, 0), gated[THREE]()))
                else:
                    total[1] = add(total[1], conj_mul(read(win_ref, 0), mixed[TWO]()))
                for slot, value in enumerate(pair_sums(distances, gated, mixed, sign, True)):
                    if value is not None:
                        total[2 + slot] = add(total[2 + slot], value)
                for slot, value in enumerate(total):
                    put((re, im), slot, value)
                return _

            lax.fori_loop(0, sub // TILE, lags, 0)

    dot = functools.partial(jnp.dot, preferred_element_type=jnp.float32)
    t_high, t_low = inverse_ref[0, 0], inverse_ref[1, 0]
    for slot in range(4):
        cols = slice(slot * width, (slot + 1) * width)
        z_ref[group, :, cols] = (
            dot(t_high, x_high[:, cols]) + dot(t_high, x_low[:, cols]) + dot(t_low, x_high[:, cols])
        )

    @pl.when(group == 3)
    def _():
        seg = 4 * sub
        for slot in range(4):
            cols = slice(slot * width, (slot + 1) * width)
            quarters = gather_quarters(
                [z_ref[g, :sub, cols] for g in range(4)], [z_ref[g, sub:, cols] for g in range(4)]
            )
            for i, quarter in enumerate(quarters):
                at = slice(i * sub, (i + 1) * sub)
                if slot == 0:
                    query_out[at, :] = up_ref[at, :] * (quarter + skip_ref[...] * gated_ref[at, :])
                elif slot == 1:
                    back_out[at, :] = quarter + skip_ref[...] * mixed_ref[at, :]
                else:
                    base = (slot - 2) * seg + i * sub
                    filter_out[base : base + sub, :] = quarter


def late(pos, inverse, acc, windows, three_g, two_g, own_m, outer_m, next_m, two_m, gated, mixed, skip, upstream):
    seg, width = upstream.shape
    rows = seg // 2
    mid = windows.shape[0] // 2

    def win_at(i, pos):
        p = pos[0]
        ends = jnp.where(p == 0, mid - 3, mid + 3)
        return jnp.where(p == 1, mid + 2, jnp.where(p == 2, mid - 2, ends)), i, 0

    group = pl.BlockSpec((rows, width), lambda i, pos: (i, 0))
    return pl.pallas_call(
        late_kernel,
        grid_spec=pltpu.PrefetchScalarGridSpec(
            num_scalar_prefetch=1,
            grid=(4,),
            in_specs=[
                pl.BlockSpec((2, 1, rows, rows), lambda i, pos: (0, i, 0, 0)),
                pl.BlockSpec((4, rows, width), lambda i, pos: (0, i, 0)),
                pl.BlockSpec((1, rows, width), win_at),
                *[group] * 6,
                whole_spec((seg, width)),
                whole_spec((seg, width)),
                whole_spec((1, width)),
                whole_spec((seg, width)),
            ],
            out_specs=[whole_spec((seg, width)), whole_spec((2 * seg, width)), whole_spec((seg, width))],
            scratch_shapes=[
                pltpu.VMEM((rows, 4 * width), jnp.bfloat16),
                pltpu.VMEM((rows, 4 * width), jnp.bfloat16),
                pltpu.VMEM((4, rows, 4 * width), jnp.float32),
            ],
        ),
        out_shape=[f32(seg, width), f32(2 * seg, width), f32(seg, width)],
        compiler_params=params(20),
        cost_estimate=cost(12 * seg * seg * width * 2, 100 * seg * width),
        name="late",
    )(pos, inverse, acc, windows, three_g, two_g, own_m, outer_m, next_m, two_m, gated, mixed, skip, upstream)


def finish_kernel(back_ref, key_ref, values_ref, made_ref, sent_ref, own_ref, side_ref, *rest):
    key_out, value_out, skip_out = rest[-3:]
    seg = back_ref.shape[0]
    back = back_ref[...] + sent_ref[:seg, :]
    key_out[...] = back * values_ref[...]
    value_out[...] = back * key_ref[...]
    total = (own_ref[...] + side_ref[...]) + (made_ref[seg:, :] + sent_ref[seg:, :])
    skip_out[...] = jnp.sum(total, axis=0, keepdims=True)


def finish(back, key_gate, values, made, sent, own_sums, side_sums, half, before=()):
    seg, full = back.shape
    width = full // 2

    def lanes(rows):
        return pl.BlockSpec((rows, width), lambda i: (0, half))

    held = pl.BlockSpec(memory_space=pl.ANY)
    return pl.pallas_call(
        finish_kernel,
        grid=(1,),
        in_specs=[lanes(seg)] * 3 + [whole_spec((seg + 8, width))] * 2 + [lanes(8)] * 2 + [held] * len(before),
        out_specs=[lanes(seg), lanes(seg), lanes(1)],
        out_shape=[f32(seg, full), f32(seg, full), f32(1, full)],
        input_output_aliases={7 + i: i for i in range(len(before))},
        compiler_params=params(12),
        cost_estimate=cost(3 * seg * width, 24 * seg * width),
        name="finish",
    )(back, key_gate, values, made, sent, own_sums, side_sums, *before)


def send(x, *pairs):
    return lax.ppermute(x, "ctx", list(pairs))


def across(x):
    return send(x, (1, 2), (2, 1))


def outward(x):
    return send(x, (1, 0), (2, 3))


def beside(x):
    return send(x, (0, 1), (1, 0), (2, 3), (3, 2))


def local_line(query_gate, key_gate, values, filter_taps, skip_gain, upstream):
    seg, width = values.shape
    forward_np, inverse_np = tables(seg)
    table, inverse = jnp.asarray(forward_np), jnp.asarray(inverse_np)
    pos = lax.axis_index("ctx").astype(jnp.int32).reshape(1)
    after = lax.optimization_barrier

    gated = key_gate * values
    side, over = beside(gated), across(gated)
    mixed, own_sums = mix(gated, upstream, query_gate)
    side_x, over_x = beside(mixed), across(mixed)
    own_g, own_m = dft(pos, table, seg, gated), dft(pos, table, seg, mixed)
    over, side, filter_taps, own_g, own_m = after((over, side, filter_taps, own_g, own_m))

    over_two, out_two = across(side), outward(over)
    outer_g = dft(pos, table, seg, side, choose=True)
    next_g = dft(pos, table, seg, over, side, choose=True)
    windows = taps_spectra(table, filter_taps, seg)
    over_x, side_x, windows, outer_g, next_g = after((over_x, side_x, windows, outer_g, next_g))

    outer_m = dft(pos, table, seg, side_x, choose=True)
    next_m = dft(pos, table, seg, over_x, side_x, choose=True)
    side_x, outer_m, next_m = after((side_x, outer_m, next_m))
    two_x = across(side_x)
    side_sums, near_sums = sums(side, side_x), sums(over, over_x)
    near, far_window = ahead(pos, windows, next_m, seg)
    over_two, near, far_window, side_sums, near_sums = after((over_two, near, far_window, side_sums, near_sums))

    three = outward(over_two)
    two_g = dft(pos, table, seg, over_two, out_two)
    acc = early(pos, windows, (own_g, outer_g, next_g, two_g), (own_m, outer_m, next_m), seg)
    two_x, acc = after((two_x, acc))

    made_0 = back_partial(table, inverse, near, far_window, two_x, over_two, near_sums, 0)
    two_x, made_0 = after((two_x, made_0))
    sent_0 = outward(made_0)
    made_1 = back_partial(table, inverse, near, far_window, two_x, over_two, near_sums, 1)
    two_x, made_1 = after((two_x, made_1))
    sent_1 = outward(made_1)
    two_m, three_g = dft(pos, table, seg, two_x), dft(pos, table, seg, three)
    query_grad, filter_grad, back = late(
        pos, inverse, acc, windows, three_g, two_g, own_m, outer_m, next_m, two_m,
        gated, mixed, skip_gain[None, :], upstream,
    )
    done = finish(back, key_gate, values, made_0, sent_0, own_sums, side_sums, 0)
    sent_1, *done = after((sent_1, *done))
    key_grad, value_grad, skip_grad = finish(back, key_gate, values, made_1, sent_1, own_sums, side_sums, 1, done)
    return (query_grad, key_grad, value_grad, filter_grad, skip_grad[0])


def matmul(left, right):
    return jnp.dot(left, right, preferred_element_type=jnp.float32, precision=lax.Precision.HIGHEST)


def forward_table(seg_len, count, offset):
    num_bins = seg_len + 1
    period = 2 * seg_len
    bin_index = lax.broadcasted_iota(jnp.int32, (num_bins, count), 0)
    pos_index = lax.broadcasted_iota(jnp.int32, (num_bins, count), 1) + offset
    angles = (bin_index * pos_index % period).astype(jnp.float32) * (2.0 * math.pi / period)
    return jnp.concatenate([jnp.cos(angles), -jnp.sin(angles)], axis=0)


def inverse_table(seg_len, count, offset):
    num_bins = seg_len + 1
    period = 2 * seg_len
    pos_index = lax.broadcasted_iota(jnp.int32, (count, num_bins), 0) + offset
    bin_index = lax.broadcasted_iota(jnp.int32, (count, num_bins), 1)
    angles = (bin_index * pos_index % period).astype(jnp.float32) * (2.0 * math.pi / period)
    weights = jnp.where((bin_index == 0) | (bin_index == seg_len), 1.0, 2.0) / period
    return jnp.concatenate([weights * jnp.cos(angles), -weights * jnp.sin(angles)], axis=1)


def times_spec(first, second):
    num_bins = first.shape[0] // 2
    real_a, imag_a = (first[:num_bins], first[num_bins:])
    real_b, imag_b = (second[:num_bins], second[num_bins:])
    return jnp.concatenate(
        [real_a * real_b - imag_a * imag_b, real_a * imag_b + imag_a * real_b], axis=0
    )


def conj_times(first, second):
    num_bins = first.shape[0] // 2
    real_a, imag_a = (first[:num_bins], first[num_bins:])
    real_b, imag_b = (second[:num_bins], second[num_bins:])
    return jnp.concatenate(
        [real_a * real_b + imag_a * imag_b, real_a * imag_b - imag_a * real_b], axis=0
    )


def pick(stack, index):
    return lax.dynamic_index_in_dim(stack, index, 0, keepdims=False)


def local(query_gate, key_gate, values, filter_taps, skip_gain, upstream):
    seg_len, width_dev = values.shape
    cycle_size = lax.axis_size("ctx")
    position = lax.axis_index("ctx")
    history = seg_len * cycle_size
    gated = key_gate * values
    mixed_grad = upstream * query_gate
    table_low = forward_table(seg_len, seg_len, 0)
    table_high = forward_table(seg_len, seg_len, seg_len)
    table_taps = forward_table(seg_len, 2 * seg_len, 0)
    back_low = inverse_table(seg_len, seg_len, 0)
    back_high = inverse_table(seg_len, seg_len, seg_len)
    back_full = inverse_table(seg_len, 2 * seg_len, 0)
    own_grad_spec = matmul(table_high, mixed_grad)
    spec_rows = 2 * (seg_len + 1)

    def taps_spec(lag_block):
        start_row = (lag_block - 1) * seg_len + history
        window = lax.dynamic_slice_in_dim(filter_taps, start_row, 2 * seg_len, 0)
        return matmul(table_taps, window)

    def visit(carry, gated_spec, grad_spec, source):
        acc_conv, acc_back, partial_value = carry
        lag_block = position - source
        acc_conv = acc_conv + times_spec(taps_spec(lag_block), gated_spec)
        acc_back = acc_back + conj_times(taps_spec(-lag_block), grad_spec)
        segment = matmul(back_full, conj_times(gated_spec, own_grad_spec))
        start_row = (lag_block - 1) * seg_len + history
        current = lax.dynamic_slice_in_dim(partial_value, start_row, 2 * seg_len, 0)
        partial_value = lax.dynamic_update_slice_in_dim(
            partial_value, current + segment, start_row, 0
        )
        return (acc_conv, acc_back, partial_value)

    initial = (
        jnp.zeros((spec_rows, width_dev), jnp.float32),
        jnp.zeros((spec_rows, width_dev), jnp.float32),
        jnp.zeros((2 * history, width_dev), jnp.float32),
    )
    own_gated_spec = matmul(table_low, gated)
    pieces = (
        lax.all_gather(own_gated_spec[None], "ctx", axis=0, tiled=True),
        lax.all_gather(own_grad_spec[None], "ctx", axis=0, tiled=True),
    )

    def advance(member, state):
        return visit(state, pick(pieces[0], member), pick(pieces[1], member), member)

    folded = lax.fori_loop(0, pieces[0].shape[0], advance, initial)
    acc_conv, acc_back, partial_value = folded
    filter_grad = lax.psum_scatter(partial_value, "ctx", scatter_dimension=0, tiled=True)
    conv = matmul(back_high, acc_conv)
    back = matmul(back_low, acc_back) + skip_gain[None, :] * mixed_grad
    query_grad = upstream * (conv + skip_gain[None, :] * gated)
    key_grad = back * values
    value_grad = back * key_gate
    skip_grad = lax.psum(jnp.sum(mixed_grad * gated, axis=0), "ctx")
    return (query_grad, key_grad, value_grad, filter_grad, skip_grad)


def solution(mesh):
    in_specs = (
        P(("groups", "ctx"), "chan"),
        P(("groups", "ctx"), "chan"),
        P(("groups", "ctx"), "chan"),
        P(None, "chan"),
        P("chan"),
        P(("groups", "ctx"), "chan"),
    )
    out_specs = (
        P(("groups", "ctx"), "chan"),
        P(("groups", "ctx"), "chan"),
        P(("groups", "ctx"), "chan"),
        P(("groups", "ctx"), "chan"),
        P(("groups", "chan")),
    )
    body = local_line if mesh.shape["ctx"] == 4 else local
    return jax.shard_map(body, mesh=mesh, in_specs=in_specs, out_specs=out_specs, check_vma=False)
```

```python
import functools
import math

import jax
import jax.numpy as jnp
import ml_dtypes
import numpy as np
from jax import lax
from jax.experimental import pallas as pl
from jax.experimental.pallas import tpu as pltpu
from jax.sharding import PartitionSpec as P

COS1, SIN1, HALF = math.cos(math.pi / 8), math.sin(math.pi / 8), math.sqrt(0.5)


def split_np(table):
    high = table.astype(ml_dtypes.bfloat16)
    low = (table - high.astype(np.float64)).astype(ml_dtypes.bfloat16)
    return np.stack([high, low])


def tables(seg):
    sub = seg // 4
    bins, pos = np.arange(sub)[:, None], np.arange(sub)[None, :]
    forward = []
    for group in range(4):
        angle = 2 * np.pi * pos * (8 * bins + group + 0.5) / (2 * seg)
        cos, sin = np.cos(angle), np.sin(angle)
        forward.append(np.block([[cos, -sin], [-sin, -cos]]))
    forward = np.stack(forward)
    inverse = forward.transpose(0, 2, 1) / seg
    return split_np(forward), split_np(inverse)


def split(x):
    high = x.astype(jnp.bfloat16)
    return high, (x - high.astype(jnp.float32)).astype(jnp.bfloat16)


def dot3(table_ref, group, high, low):
    t_high, t_low = table_ref[0, group], table_ref[1, group]
    dot = functools.partial(jnp.dot, preferred_element_type=jnp.float32)
    width = high.shape[1]
    if width <= 128:
        both = dot(t_high, jnp.concatenate([high, low], axis=1))
        return both[:, :width] + both[:, width:] + dot(t_low, high)
    return dot(t_high, high) + dot(t_high, low) + dot(t_low, high)


def spread(x):
    sub = x.shape[0] // 4
    x0, x1, x2, x3 = (x[i * sub : (i + 1) * sub] for i in range(4))
    u, p, s, q, t = HALF * x2, COS1 * x1, SIN1 * x1, COS1 * x3, SIN1 * x3
    a, b, pt, sq, pmt, spq = x0 + u, x0 - u, p + t, s - q, p - t, s + q
    pairs = ((a + pt, spq + u), (b + sq, pmt + u), (b - sq, pmt - u), (a - pt, spq - u))
    return [jnp.concatenate(pair, axis=0) for pair in pairs]


def gather_quarters(re, im):
    e03, d03, e12, d12 = re[0] + re[3], re[0] - re[3], re[1] + re[2], re[1] - re[2]
    f03, g03, f12, g12 = im[0] + im[3], im[0] - im[3], im[1] + im[2], im[1] - im[2]
    return (
        e03 + e12,
        COS1 * (d03 + f12) + SIN1 * (d12 + f03),
        HALF * (e03 - e12 + g03 + g12),
        SIN1 * (d03 - f12) + COS1 * (f03 - d12),
    )


def transform(x, table_ref, store):
    for group, part in enumerate(spread(x)):
        store(group, dot3(table_ref, group, *split(part)))


def cost(flops, nbytes):
    return pl.CostEstimate(flops=int(flops), bytes_accessed=int(nbytes), transcendentals=0)


def params(mib):
    return pltpu.CompilerParams(vmem_limit_bytes=mib << 20)


def whole_spec(shape):
    return pl.BlockSpec(shape, lambda *_: (0,) * len(shape))


def f32(*shape):
    return jax.ShapeDtypeStruct(shape, jnp.float32)


def block_sums(gated, mixed):
    seg, width = gated.shape
    return jnp.sum((gated * mixed).reshape(seg // 8, 8, width), axis=0)


def sums_kernel(gated_ref, mixed_ref, out_ref):
    out_ref[...] = block_sums(gated_ref[...], mixed_ref[...])


def sums(gated, mixed):
    seg, width = gated.shape
    return pl.pallas_call(
        sums_kernel,
        grid=(1,),
        in_specs=[whole_spec((seg, width))] * 2,
        out_specs=whole_spec((8, width)),
        out_shape=f32(8, width),
        compiler_params=params(8),
        cost_estimate=cost(2 * seg * width, 8 * seg * width),
        name="sums",
    )(gated, mixed)


def mix_kernel(gated_ref, up_ref, query_ref, mixed_ref, sum_ref):
    mixed = up_ref[...] * query_ref[...]
    mixed_ref[...] = mixed
    sum_ref[...] = block_sums(gated_ref[...], mixed)


def mix(gated, upstream, query_gate):
    seg, width = gated.shape
    block = whole_spec((seg, width))
    return pl.pallas_call(
        mix_kernel,
        grid=(1,),
        in_specs=[block] * 3,
        out_specs=[block, whole_spec((8, width))],
        out_shape=[f32(seg, width), f32(8, width)],
        compiler_params=params(12),
        cost_estimate=cost(4 * seg * width, 16 * seg * width),
        name="mix",
    )(gated, upstream, query_gate)


def dft_kernel(choose, pos_ref, table_ref, *refs):
    *x_refs, out_ref = refs
    rows = out_ref.shape[0] // 4
    inner = jnp.logical_or(pos_ref[0] == 1, pos_ref[0] == 2)

    def store(group, value):
        out_ref[group * rows : (group + 1) * rows, :] = value

    x = x_refs[0][...]
    if choose:
        x = jnp.where(inner, x, x_refs[1][...] if len(x_refs) == 2 else 0.0)
    elif len(x_refs) == 2:
        x = x + x_refs[1][...]
    transform(x, table_ref, store)


def dft(pos, table, seg, *xs, choose=False):
    width = xs[0].shape[1]
    return pl.pallas_call(
        functools.partial(dft_kernel, choose),
        grid_spec=pltpu.PrefetchScalarGridSpec(
            num_scalar_prefetch=1,
            grid=(1,),
            in_specs=[whole_spec(table.shape)] + [whole_spec((seg, width))] * len(xs),
            out_specs=whole_spec((2 * seg, width)),
        ),
        out_shape=f32(2 * seg, width),
        compiler_params=params(12),
        cost_estimate=cost(3 * seg * seg * width * 2, 12 * seg * width),
        name="dft",
    )(pos, table, *xs)


def taps_kernel(table_ref, x_ref, out_ref, last_ref):
    step = pl.program_id(0)
    rows = out_ref.shape[1] // 4
    sub = rows // 2

    def store(group, value):
        base = group * rows
        sign = 1.0 if group % 2 == 0 else -1.0
        re, im = slice(base, base + sub), slice(base + sub, base + rows)
        out_ref[0, re, :] = value[:sub] - sign * last_ref[im, :]
        out_ref[0, im, :] = value[sub:] + sign * last_ref[re, :]
        last_ref[base : base + rows, :] = value

    @pl.when(step == 0)
    def _():
        last_ref[...] = jnp.zeros_like(last_ref)

    transform(x_ref[...], table_ref, store)


def taps_spectra(table, taps, seg):
    width = taps.shape[1]
    blocks = taps.shape[0] // seg
    return pl.pallas_call(
        taps_kernel,
        grid=(blocks,),
        in_specs=[whole_spec(table.shape), pl.BlockSpec((seg, width), lambda i: (i, 0))],
        out_specs=pl.BlockSpec((1, 2 * seg, width), lambda i: (jnp.maximum(i - 1, 0), 0, 0)),
        out_shape=jax.ShapeDtypeStruct((blocks - 1, 2 * seg, width), jnp.float32),
        scratch_shapes=[pltpu.VMEM((2 * seg, width), jnp.float32)],
        compiler_params=params(14),
        cost_estimate=cost(blocks * 3 * seg * seg * width * 2, blocks * 12 * seg * width),
        name="taps",
    )(table, taps)


def conj_mul(a, b):
    return a[0] * b[0] + a[1] * b[1], a[0] * b[1] - a[1] * b[0]


def mul(a, b):
    return a[0] * b[0] - a[1] * b[1], a[0] * b[1] + a[1] * b[0]


def add(a, b):
    return a[0] + b[0], a[1] + b[1]


def partial_kernel(
    pos_ref, table_ref, inverse_ref, win_near, win_far, next_ref, x_ref, gated_ref, near_sums, out_ref, z_ref
):
    rows = next_ref.shape[0] // 4
    sub = rows // 2
    for group, part in enumerate(spread(x_ref[...])):
        base = group * rows
        far = dot3(table_ref, group, *split(part))
        re, im = slice(base, base + sub), slice(base + sub, base + rows)
        total = add(
            conj_mul((win_near[0, re, :], win_near[0, im, :]), (next_ref[re, :], next_ref[im, :])),
            conj_mul((win_far[0, re, :], win_far[0, im, :]), (far[:sub], far[sub:])),
        )
        z_ref[group] = dot3(inverse_ref, group, *split(jnp.concatenate(total, axis=0)))
    quarters = gather_quarters([z_ref[g, :sub] for g in range(4)], [z_ref[g, sub:] for g in range(4)])
    for i, quarter in enumerate(quarters):
        out_ref[i * sub : (i + 1) * sub, :] = quarter
    out_ref[4 * sub :, :] = near_sums[...] + block_sums(gated_ref[...], x_ref[...])


def back_partial(pos, table, inverse, windows, next_m, x, gated, near_sums, half, seg):
    width = x.shape[1] // 2
    n = (windows.shape[0] + 1) // 2

    def window(distance):
        return pl.BlockSpec(
            (1, 2 * seg, width),
            lambda i, pos: (jnp.where(pos[0] == 1, n - 1 + distance, n - 1 - distance), 0, half),
        )

    def lanes(rows):
        return pl.BlockSpec((rows, width), lambda i, pos: (0, half))

    return pl.pallas_call(
        partial_kernel,
        grid_spec=pltpu.PrefetchScalarGridSpec(
            num_scalar_prefetch=1,
            grid=(1,),
            in_specs=[
                whole_spec(table.shape),
                whole_spec(inverse.shape),
                window(2),
                window(3),
                lanes(2 * seg),
                lanes(seg),
                lanes(seg),
                lanes(8),
            ],
            out_specs=whole_spec((seg + 8, width)),
            scratch_shapes=[pltpu.VMEM((4, seg // 2, width), jnp.float32)],
        ),
        out_shape=f32(seg + 8, width),
        compiler_params=params(24),
        cost_estimate=cost(6 * seg * seg * width * 2, 24 * seg * width),
        name="partial",
    )(pos, table, inverse, windows, windows, next_m, x, gated, near_sums)


OWN, OUTER, NEXT, TWO, THREE = range(5)
PAIRS = (
    ((), ((OWN, THREE),), ((OWN, TWO), (NEXT, THREE))),
    (
        ((OUTER, NEXT), (OWN, TWO)),
        ((OUTER, OWN), (OWN, NEXT), (NEXT, TWO)),
        ((OUTER, OUTER), (OWN, OWN), (NEXT, NEXT), (TWO, TWO)),
    ),
    (
        ((TWO, TWO), (NEXT, NEXT), (OWN, OWN), (OUTER, OUTER)),
        ((NEXT, TWO), (OWN, NEXT), (OUTER, OWN)),
        ((OWN, TWO), (OUTER, NEXT)),
    ),
    (((NEXT, THREE), (OWN, TWO)), ((OWN, THREE),), ()),
)


def is_late(pair):
    return pair[0] == TWO or pair[1] == THREE


def pair_sums(distances, gated, mixed, sign, late):
    total = []
    for pairs in distances:
        value = None
        for m, g in pairs:
            if is_late((m, g)) == late:
                term = conj_mul(gated[g](), mixed[m]())
                value = term if value is None else add(value, term)
        total.append(value)
    out = []
    for low, high in zip(total[:2], total[1:]):
        if high is not None:
            turned = (sign * high[1], -sign * high[0])
            low = turned if low is None else add(low, turned)
        out.append(low)
    return out


TILE = 16


def tile_reader(tile, sub):
    re = pl.ds(pl.multiple_of(tile * TILE, TILE), TILE)
    im = pl.ds(pl.multiple_of(sub + tile * TILE, TILE), TILE)

    def read(ref, *lead):
        return ref[(*lead, re, slice(None))], ref[(*lead, im, slice(None))]

    return re, im, read


def group_sign():
    return jnp.where(pl.program_id(0) % 2 == 0, 1.0, -1.0)


def early_kernel(
    pos_ref, win_own, win_outer, win_next, win_two, own_g, outer_g, next_g, two_g, own_m, outer_m, next_m, out_ref
):
    pos, sign = pos_ref[0], group_sign()
    rows = own_g.shape[0]
    sub = rows // 2
    count = sub // TILE

    def put(at, slot, value):
        re, im = at
        out_ref[slot, re, :] = value[0]
        out_ref[slot, im, :] = value[1]

    def sums(tile, _):
        re, im, read = tile_reader(tile, sub)
        own, outer, ahead = read(win_own, 0), read(win_outer, 0), read(win_next, 0)
        conv = add(mul(own, read(own_g)), mul(outer, read(outer_g)))
        conv = add(conv, add(mul(ahead, read(next_g)), mul(read(win_two, 0), read(two_g))))
        put((re, im), 0, conv)
        back = add(conj_mul(own, read(own_m)), conj_mul(ahead, read(outer_m)))
        put((re, im), 1, add(back, conj_mul(outer, read(next_m))))
        return _

    lax.fori_loop(0, count, sums, 0)
    for where, distances in enumerate(PAIRS):

        @pl.when(pos == where)
        def _():
            def lags(tile, _):
                re, im, read = tile_reader(tile, sub)
                gated = [functools.partial(read, ref) for ref in (own_g, outer_g, next_g, two_g)]
                mixed = [functools.partial(read, ref) for ref in (own_m, outer_m, next_m)]
                for slot, value in enumerate(pair_sums(distances, gated, mixed, sign, False)):
                    if value is None:
                        value = (jnp.zeros_like(own_g[re, :]),) * 2
                    put((re, im), 2 + slot, value)
                return _

            lax.fori_loop(0, count, lags, 0)


def early(pos, windows, gated, mixed, seg):
    width = gated[0].shape[1]
    rows = seg // 2
    mid = windows.shape[0] // 2

    def window(index):
        return pl.BlockSpec((1, rows, width), lambda i, pos: (index(pos[0]), i, 0))

    group = pl.BlockSpec((rows, width), lambda i, pos: (i, 0))
    return pl.pallas_call(
        early_kernel,
        grid_spec=pltpu.PrefetchScalarGridSpec(
            num_scalar_prefetch=1,
            grid=(4,),
            in_specs=[
                window(lambda p: mid),
                window(lambda p: jnp.where(p < 2, mid + 1, mid - 1)),
                window(lambda p: jnp.where(p < 2, mid - 1, mid + 1)),
                window(lambda p: jnp.where(p < 2, mid - 2, mid + 2)),
            ]
            + [group] * 7,
            out_specs=pl.BlockSpec((4, rows, width), lambda i, pos: (0, i, 0)),
        ),
        out_shape=f32(4, 2 * seg, width),
        compiler_params=params(14),
        cost_estimate=cost(200 * seg * width, 120 * seg * width),
        name="early",
    )(pos, *[windows] * 4, *gated, *mixed)


def late_kernel(
    pos_ref, inverse_ref, acc_ref, win_ref, three_g, two_g, own_m, outer_m, next_m, *rest
):
    two_m, gated_ref, mixed_ref, skip_ref, up_ref, query_out, filter_out, back_out, x_high, x_low, z_ref = rest
    group = pl.program_id(0)
    pos, sign = pos_ref[0], group_sign()
    rows, width = own_m.shape
    sub = rows // 2

    def put(at, slot, value):
        for rows_at, part in zip(at, value):
            high, low = split(part)
            x_high[rows_at, slot * width : (slot + 1) * width] = high
            x_low[rows_at, slot * width : (slot + 1) * width] = low

    for where, distances in enumerate(PAIRS):

        @pl.when(pos == where)
        def _():
            def lags(tile, _):
                re, im, read = tile_reader(tile, sub)

                gated = [None, None, None, functools.partial(read, two_g), functools.partial(read, three_g)]
                mixed = [functools.partial(read, ref) for ref in (own_m, outer_m, next_m, two_m)]
                total = [read(acc_ref, slot) for slot in range(4)]
                if where in (0, 3):
                    total[0] = add(total[0], mul(read(win_ref, 0), gated[THREE]()))
                else:
                    total[1] = add(total[1], conj_mul(read(win_ref, 0), mixed[TWO]()))
                for slot, value in enumerate(pair_sums(distances, gated, mixed, sign, True)):
                    if value is not None:
                        total[2 + slot] = add(total[2 + slot], value)
                for slot, value in enumerate(total):
                    put((re, im), slot, value)
                return _

            lax.fori_loop(0, sub // TILE, lags, 0)

    dot = functools.partial(jnp.dot, preferred_element_type=jnp.float32)
    t_high, t_low = inverse_ref[0, 0], inverse_ref[1, 0]
    for slot in range(4):
        cols = slice(slot * width, (slot + 1) * width)
        z_ref[group, :, cols] = (
            dot(t_high, x_high[:, cols]) + dot(t_high, x_low[:, cols]) + dot(t_low, x_high[:, cols])
        )

    @pl.when(group == 3)
    def _():
        seg = 4 * sub
        for slot in range(4):
            cols = slice(slot * width, (slot + 1) * width)
            quarters = gather_quarters(
                [z_ref[g, :sub, cols] for g in range(4)], [z_ref[g, sub:, cols] for g in range(4)]
            )
            for i, quarter in enumerate(quarters):
                at = slice(i * sub, (i + 1) * sub)
                if slot == 0:
                    query_out[at, :] = up_ref[at, :] * (quarter + skip_ref[...] * gated_ref[at, :])
                elif slot == 1:
                    back_out[at, :] = quarter + skip_ref[...] * mixed_ref[at, :]
                else:
                    base = (slot - 2) * seg + i * sub
                    filter_out[base : base + sub, :] = quarter


def late(pos, inverse, acc, windows, three_g, two_g, own_m, outer_m, next_m, two_m, gated, mixed, skip, upstream):
    seg, width = upstream.shape
    rows = seg // 2
    mid = windows.shape[0] // 2

    def win_at(i, pos):
        p = pos[0]
        ends = jnp.where(p == 0, mid - 3, mid + 3)
        return jnp.where(p == 1, mid + 2, jnp.where(p == 2, mid - 2, ends)), i, 0

    group = pl.BlockSpec((rows, width), lambda i, pos: (i, 0))
    return pl.pallas_call(
        late_kernel,
        grid_spec=pltpu.PrefetchScalarGridSpec(
            num_scalar_prefetch=1,
            grid=(4,),
            in_specs=[
                pl.BlockSpec((2, 1, rows, rows), lambda i, pos: (0, i, 0, 0)),
                pl.BlockSpec((4, rows, width), lambda i, pos: (0, i, 0)),
                pl.BlockSpec((1, rows, width), win_at),
                *[group] * 6,
                whole_spec((seg, width)),
                whole_spec((seg, width)),
                whole_spec((1, width)),
                whole_spec((seg, width)),
            ],
            out_specs=[whole_spec((seg, width)), whole_spec((2 * seg, width)), whole_spec((seg, width))],
            scratch_shapes=[
                pltpu.VMEM((rows, 4 * width), jnp.bfloat16),
                pltpu.VMEM((rows, 4 * width), jnp.bfloat16),
                pltpu.VMEM((4, rows, 4 * width), jnp.float32),
            ],
        ),
        out_shape=[f32(seg, width), f32(2 * seg, width), f32(seg, width)],
        compiler_params=params(20),
        cost_estimate=cost(12 * seg * seg * width * 2, 100 * seg * width),
        name="late",
    )(pos, inverse, acc, windows, three_g, two_g, own_m, outer_m, next_m, two_m, gated, mixed, skip, upstream)


def finish_kernel(half, back_ref, key_ref, values_ref, made_ref, sent_ref, own_ref, side_ref, *rest):
    key_out, value_out, skip_out = rest[-3:]
    seg = back_ref.shape[0]
    width = sent_ref.shape[1]
    lanes = slice(half * width, (half + 1) * width)
    back = back_ref[:, lanes] + sent_ref[:seg, :]
    key_out[...] = back * values_ref[:, lanes]
    value_out[...] = back * key_ref[:, lanes]
    total = (own_ref[:, lanes] + side_ref[:, lanes]) + (made_ref[seg:, :] + sent_ref[seg:, :])
    skip_out[...] = jnp.sum(total, axis=0, keepdims=True)


def finish(back, key_gate, values, made, sent, own_sums, side_sums, half, before=()):
    seg, full = back.shape
    width = full // 2

    def lanes(rows):
        return pl.BlockSpec((rows, width), lambda i: (0, half))

    held = pl.BlockSpec(memory_space=pl.ANY)
    return pl.pallas_call(
        functools.partial(finish_kernel, half),
        grid=(1,),
        in_specs=[whole_spec((seg, full))] * 3
        + [whole_spec((seg + 8, width))] * 2
        + [whole_spec((8, full))] * 2
        + [held] * len(before),
        out_specs=[lanes(seg), lanes(seg), lanes(1)],
        out_shape=[f32(seg, full), f32(seg, full), f32(1, full)],
        input_output_aliases={7 + i: i for i in range(len(before))},
        compiler_params=params(12),
        cost_estimate=cost(3 * seg * width, 24 * seg * width),
        name="finish",
    )(back, key_gate, values, made, sent, own_sums, side_sums, *before)


def send(x, *pairs):
    return lax.ppermute(x, "ctx", list(pairs))


def across(x):
    return send(x, (1, 2), (2, 1))


def outward(x):
    return send(x, (1, 0), (2, 3))


def beside(x):
    return send(x, (0, 1), (1, 0), (2, 3), (3, 2))


def local_line(query_gate, key_gate, values, filter_taps, skip_gain, upstream):
    seg, width = values.shape
    forward_np, inverse_np = tables(seg)
    table, inverse = jnp.asarray(forward_np), jnp.asarray(inverse_np)
    pos = lax.axis_index("ctx").astype(jnp.int32).reshape(1)
    after = lax.optimization_barrier

    gated = key_gate * values
    side, over = beside(gated), across(gated)
    mixed, own_sums = mix(gated, upstream, query_gate)
    side_x, over_x = beside(mixed), across(mixed)
    own_g, own_m = dft(pos, table, seg, gated), dft(pos, table, seg, mixed)
    over, side, filter_taps, own_g, own_m = after((over, side, filter_taps, own_g, own_m))

    over_two, out_two = across(side), outward(over)
    outer_g = dft(pos, table, seg, side, choose=True)
    next_g = dft(pos, table, seg, over, side, choose=True)
    windows = taps_spectra(table, filter_taps, seg)
    over_x, side_x, windows, outer_g, next_g = after((over_x, side_x, windows, outer_g, next_g))

    outer_m = dft(pos, table, seg, side_x, choose=True)
    next_m = dft(pos, table, seg, over_x, side_x, choose=True)
    side_x, outer_m, next_m = after((side_x, outer_m, next_m))
    two_x = across(side_x)
    side_sums, near_sums = sums(side, side_x), sums(over, over_x)
    over_two, outer_m, next_m, side_sums, near_sums = after((over_two, outer_m, next_m, side_sums, near_sums))

    three = outward(over_two)
    two_g = dft(pos, table, seg, over_two, out_two)
    acc = early(pos, windows, (own_g, outer_g, next_g, two_g), (own_m, outer_m, next_m), seg)
    two_x, acc = after((two_x, acc))

    made_0 = back_partial(pos, table, inverse, windows, next_m, two_x, over_two, near_sums, 0, seg)
    two_x, made_0 = after((two_x, made_0))
    sent_0 = outward(made_0)
    made_1 = back_partial(pos, table, inverse, windows, next_m, two_x, over_two, near_sums, 1, seg)
    two_x, made_1 = after((two_x, made_1))
    sent_1 = outward(made_1)
    two_m, three_g = dft(pos, table, seg, two_x), dft(pos, table, seg, three)
    query_grad, filter_grad, back = late(
        pos, inverse, acc, windows, three_g, two_g, own_m, outer_m, next_m, two_m,
        gated, mixed, skip_gain[None, :], upstream,
    )
    done = finish(back, key_gate, values, made_0, sent_0, own_sums, side_sums, 0)
    sent_1, *done = after((sent_1, *done))
    key_grad, value_grad, skip_grad = finish(back, key_gate, values, made_1, sent_1, own_sums, side_sums, 1, done)
    return (query_grad, key_grad, value_grad, filter_grad, skip_grad[0])


def matmul(left, right):
    return jnp.dot(left, right, preferred_element_type=jnp.float32, precision=lax.Precision.HIGHEST)


def forward_table(seg_len, count, offset):
    num_bins = seg_len + 1
    period = 2 * seg_len
    bin_index = lax.broadcasted_iota(jnp.int32, (num_bins, count), 0)
    pos_index = lax.broadcasted_iota(jnp.int32, (num_bins, count), 1) + offset
    angles = (bin_index * pos_index % period).astype(jnp.float32) * (2.0 * math.pi / period)
    return jnp.concatenate([jnp.cos(angles), -jnp.sin(angles)], axis=0)


def inverse_table(seg_len, count, offset):
    num_bins = seg_len + 1
    period = 2 * seg_len
    pos_index = lax.broadcasted_iota(jnp.int32, (count, num_bins), 0) + offset
    bin_index = lax.broadcasted_iota(jnp.int32, (count, num_bins), 1)
    angles = (bin_index * pos_index % period).astype(jnp.float32) * (2.0 * math.pi / period)
    weights = jnp.where((bin_index == 0) | (bin_index == seg_len), 1.0, 2.0) / period
    return jnp.concatenate([weights * jnp.cos(angles), -weights * jnp.sin(angles)], axis=1)


def times_spec(first, second):
    num_bins = first.shape[0] // 2
    real_a, imag_a = (first[:num_bins], first[num_bins:])
    real_b, imag_b = (second[:num_bins], second[num_bins:])
    return jnp.concatenate(
        [real_a * real_b - imag_a * imag_b, real_a * imag_b + imag_a * real_b], axis=0
    )


def conj_times(first, second):
    num_bins = first.shape[0] // 2
    real_a, imag_a = (first[:num_bins], first[num_bins:])
    real_b, imag_b = (second[:num_bins], second[num_bins:])
    return jnp.concatenate(
        [real_a * real_b + imag_a * imag_b, real_a * imag_b - imag_a * real_b], axis=0
    )


def pick(stack, index):
    return lax.dynamic_index_in_dim(stack, index, 0, keepdims=False)


def local(query_gate, key_gate, values, filter_taps, skip_gain, upstream):
    seg_len, width_dev = values.shape
    cycle_size = lax.axis_size("ctx")
    position = lax.axis_index("ctx")
    history = seg_len * cycle_size
    gated = key_gate * values
    mixed_grad = upstream * query_gate
    table_low = forward_table(seg_len, seg_len, 0)
    table_high = forward_table(seg_len, seg_len, seg_len)
    table_taps = forward_table(seg_len, 2 * seg_len, 0)
    back_low = inverse_table(seg_len, seg_len, 0)
    back_high = inverse_table(seg_len, seg_len, seg_len)
    back_full = inverse_table(seg_len, 2 * seg_len, 0)
    own_grad_spec = matmul(table_high, mixed_grad)
    spec_rows = 2 * (seg_len + 1)

    def taps_spec(lag_block):
        start_row = (lag_block - 1) * seg_len + history
        window = lax.dynamic_slice_in_dim(filter_taps, start_row, 2 * seg_len, 0)
        return matmul(table_taps, window)

    def visit(carry, gated_spec, grad_spec, source):
        acc_conv, acc_back, partial_value = carry
        lag_block = position - source
        acc_conv = acc_conv + times_spec(taps_spec(lag_block), gated_spec)
        acc_back = acc_back + conj_times(taps_spec(-lag_block), grad_spec)
        segment = matmul(back_full, conj_times(gated_spec, own_grad_spec))
        start_row = (lag_block - 1) * seg_len + history
        current = lax.dynamic_slice_in_dim(partial_value, start_row, 2 * seg_len, 0)
        partial_value = lax.dynamic_update_slice_in_dim(
            partial_value, current + segment, start_row, 0
        )
        return (acc_conv, acc_back, partial_value)

    initial = (
        jnp.zeros((spec_rows, width_dev), jnp.float32),
        jnp.zeros((spec_rows, width_dev), jnp.float32),
        jnp.zeros((2 * history, width_dev), jnp.float32),
    )
    own_gated_spec = matmul(table_low, gated)
    pieces = (
        lax.all_gather(own_gated_spec[None], "ctx", axis=0, tiled=True),
        lax.all_gather(own_grad_spec[None], "ctx", axis=0, tiled=True),
    )

    def advance(member, state):
        return visit(state, pick(pieces[0], member), pick(pieces[1], member), member)

    folded = lax.fori_loop(0, pieces[0].shape[0], advance, initial)
    acc_conv, acc_back, partial_value = folded
    filter_grad = lax.psum_scatter(partial_value, "ctx", scatter_dimension=0, tiled=True)
    conv = matmul(back_high, acc_conv)
    back = matmul(back_low, acc_back) + skip_gain[None, :] * mixed_grad
    query_grad = upstream * (conv + skip_gain[None, :] * gated)
    key_grad = back * values
    value_grad = back * key_gate
    skip_grad = lax.psum(jnp.sum(mixed_grad * gated, axis=0), "ctx")
    return (query_grad, key_grad, value_grad, filter_grad, skip_grad)


def solution(mesh):
    in_specs = (
        P(("groups", "ctx"), "chan"),
        P(("groups", "ctx"), "chan"),
        P(("groups", "ctx"), "chan"),
        P(None, "chan"),
        P("chan"),
        P(("groups", "ctx"), "chan"),
    )
    out_specs = (
        P(("groups", "ctx"), "chan"),
        P(("groups", "ctx"), "chan"),
        P(("groups", "ctx"), "chan"),
        P(("groups", "ctx"), "chan"),
        P(("groups", "chan")),
    )
    body = local_line if mesh.shape["ctx"] == 4 else local
    return jax.shard_map(body, mesh=mesh, in_specs=in_specs, out_specs=out_specs, check_vma=False)
```

```python
import functools
import math

import jax
import jax.numpy as jnp
import ml_dtypes
import numpy as np
from jax import lax
from jax.experimental import pallas as pl
from jax.experimental.pallas import tpu as pltpu
from jax.sharding import PartitionSpec as P

COS1, SIN1, HALF = math.cos(math.pi / 8), math.sin(math.pi / 8), math.sqrt(0.5)


def split_np(table):
    high = table.astype(ml_dtypes.bfloat16)
    low = (table - high.astype(np.float64)).astype(ml_dtypes.bfloat16)
    return np.stack([high, low])


def tables(seg):
    sub = seg // 4
    bins, pos = np.arange(sub)[:, None], np.arange(sub)[None, :]
    forward = []
    for group in range(4):
        angle = 2 * np.pi * pos * (8 * bins + group + 0.5) / (2 * seg)
        cos, sin = np.cos(angle), np.sin(angle)
        forward.append(np.block([[cos, -sin], [-sin, -cos]]))
    forward = np.stack(forward)
    inverse = forward.transpose(0, 2, 1) / seg
    return split_np(forward), split_np(inverse)


def split(x):
    high = x.astype(jnp.bfloat16)
    return high, (x - high.astype(jnp.float32)).astype(jnp.bfloat16)


def dot3(table_ref, group, high, low):
    t_high, t_low = table_ref[0, group], table_ref[1, group]
    dot = functools.partial(jnp.dot, preferred_element_type=jnp.float32)
    width = high.shape[1]
    if width <= 128:
        both = dot(t_high, jnp.concatenate([high, low], axis=1))
        return both[:, :width] + both[:, width:] + dot(t_low, high)
    return dot(t_high, high) + dot(t_high, low) + dot(t_low, high)


def spread(x):
    sub = x.shape[0] // 4
    x0, x1, x2, x3 = (x[i * sub : (i + 1) * sub] for i in range(4))
    u, p, s, q, t = HALF * x2, COS1 * x1, SIN1 * x1, COS1 * x3, SIN1 * x3
    a, b, pt, sq, pmt, spq = x0 + u, x0 - u, p + t, s - q, p - t, s + q
    pairs = ((a + pt, spq + u), (b + sq, pmt + u), (b - sq, pmt - u), (a - pt, spq - u))
    return [jnp.concatenate(pair, axis=0) for pair in pairs]


def gather_quarters(re, im):
    e03, d03, e12, d12 = re[0] + re[3], re[0] - re[3], re[1] + re[2], re[1] - re[2]
    f03, g03, f12, g12 = im[0] + im[3], im[0] - im[3], im[1] + im[2], im[1] - im[2]
    return (
        e03 + e12,
        COS1 * (d03 + f12) + SIN1 * (d12 + f03),
        HALF * (e03 - e12 + g03 + g12),
        SIN1 * (d03 - f12) + COS1 * (f03 - d12),
    )


def transform(x, table_ref, store):
    for group, part in enumerate(spread(x)):
        store(group, dot3(table_ref, group, *split(part)))


def cost(flops, nbytes):
    return pl.CostEstimate(flops=int(flops), bytes_accessed=int(nbytes), transcendentals=0)


def params(mib):
    return pltpu.CompilerParams(vmem_limit_bytes=mib << 20)


def whole_spec(shape):
    return pl.BlockSpec(shape, lambda *_: (0,) * len(shape))


def f32(*shape):
    return jax.ShapeDtypeStruct(shape, jnp.float32)


def block_sums(gated, mixed):
    seg, width = gated.shape
    return jnp.sum((gated * mixed).reshape(seg // 8, 8, width), axis=0)


def sums_kernel(gated_ref, mixed_ref, out_ref):
    out_ref[...] = block_sums(gated_ref[...], mixed_ref[...])


def sums(gated, mixed):
    seg, width = gated.shape
    return pl.pallas_call(
        sums_kernel,
        grid=(1,),
        in_specs=[whole_spec((seg, width))] * 2,
        out_specs=whole_spec((8, width)),
        out_shape=f32(8, width),
        compiler_params=params(8),
        cost_estimate=cost(2 * seg * width, 8 * seg * width),
        name="sums",
    )(gated, mixed)


def mix_kernel(gated_ref, up_ref, query_ref, mixed_ref, sum_ref):
    mixed = up_ref[...] * query_ref[...]
    mixed_ref[...] = mixed
    sum_ref[...] = block_sums(gated_ref[...], mixed)


def mix(gated, upstream, query_gate):
    seg, width = gated.shape
    block = whole_spec((seg, width))
    return pl.pallas_call(
        mix_kernel,
        grid=(1,),
        in_specs=[block] * 3,
        out_specs=[block, whole_spec((8, width))],
        out_shape=[f32(seg, width), f32(8, width)],
        compiler_params=params(12),
        cost_estimate=cost(4 * seg * width, 16 * seg * width),
        name="mix",
    )(gated, upstream, query_gate)


def dft_kernel(choose, pos_ref, table_ref, *refs):
    *x_refs, out_ref = refs
    rows = out_ref.shape[0] // 4
    inner = jnp.logical_or(pos_ref[0] == 1, pos_ref[0] == 2)

    def store(group, value):
        out_ref[group * rows : (group + 1) * rows, :] = value

    x = x_refs[0][...]
    if choose:
        x = jnp.where(inner, x, x_refs[1][...] if len(x_refs) == 2 else 0.0)
    elif len(x_refs) == 2:
        x = x + x_refs[1][...]
    transform(x, table_ref, store)


def dft(pos, table, seg, *xs, choose=False):
    width = xs[0].shape[1]
    return pl.pallas_call(
        functools.partial(dft_kernel, choose),
        grid_spec=pltpu.PrefetchScalarGridSpec(
            num_scalar_prefetch=1,
            grid=(1,),
            in_specs=[whole_spec(table.shape)] + [whole_spec((seg, width))] * len(xs),
            out_specs=whole_spec((2 * seg, width)),
        ),
        out_shape=f32(2 * seg, width),
        compiler_params=params(12),
        cost_estimate=cost(3 * seg * seg * width * 2, 12 * seg * width),
        name="dft",
    )(pos, table, *xs)


def taps_kernel(table_ref, x_ref, out_ref, last_ref):
    step = pl.program_id(0)
    rows = out_ref.shape[1] // 4
    sub = rows // 2

    def store(group, value):
        base = group * rows
        sign = 1.0 if group % 2 == 0 else -1.0
        re, im = slice(base, base + sub), slice(base + sub, base + rows)
        out_ref[0, re, :] = value[:sub] - sign * last_ref[im, :]
        out_ref[0, im, :] = value[sub:] + sign * last_ref[re, :]
        last_ref[base : base + rows, :] = value

    @pl.when(step == 0)
    def _():
        last_ref[...] = jnp.zeros_like(last_ref)

    transform(x_ref[...], table_ref, store)


def taps_spectra(table, taps, seg):
    width = taps.shape[1]
    blocks = taps.shape[0] // seg
    return pl.pallas_call(
        taps_kernel,
        grid=(blocks,),
        in_specs=[whole_spec(table.shape), pl.BlockSpec((seg, width), lambda i: (i, 0))],
        out_specs=pl.BlockSpec((1, 2 * seg, width), lambda i: (jnp.maximum(i - 1, 0), 0, 0)),
        out_shape=jax.ShapeDtypeStruct((blocks - 1, 2 * seg, width), jnp.float32),
        scratch_shapes=[pltpu.VMEM((2 * seg, width), jnp.float32)],
        compiler_params=params(14),
        cost_estimate=cost(blocks * 3 * seg * seg * width * 2, blocks * 12 * seg * width),
        name="taps",
    )(table, taps)


def conj_mul(a, b):
    return a[0] * b[0] + a[1] * b[1], a[0] * b[1] - a[1] * b[0]


def mul(a, b):
    return a[0] * b[0] - a[1] * b[1], a[0] * b[1] + a[1] * b[0]


def add(a, b):
    return a[0] + b[0], a[1] + b[1]


def partial_kernel(
    pos_ref, table_ref, inverse_ref, win_near, win_far, next_ref, x_ref, gated_ref, near_sums, out_ref, z_ref
):
    rows = next_ref.shape[0] // 4
    sub = rows // 2
    for group, part in enumerate(spread(x_ref[...])):
        base = group * rows
        far = dot3(table_ref, group, *split(part))
        re, im = slice(base, base + sub), slice(base + sub, base + rows)
        total = add(
            conj_mul((win_near[0, re, :], win_near[0, im, :]), (next_ref[re, :], next_ref[im, :])),
            conj_mul((win_far[0, re, :], win_far[0, im, :]), (far[:sub], far[sub:])),
        )
        z_ref[group] = dot3(inverse_ref, group, *split(jnp.concatenate(total, axis=0)))
    quarters = gather_quarters([z_ref[g, :sub] for g in range(4)], [z_ref[g, sub:] for g in range(4)])
    for i, quarter in enumerate(quarters):
        out_ref[i * sub : (i + 1) * sub, :] = quarter
    out_ref[4 * sub :, :] = near_sums[...] + block_sums(gated_ref[...], x_ref[...])


def back_partial(pos, table, inverse, windows, next_m, x, gated, near_sums, half, seg):
    width = x.shape[1] // 2
    n = (windows.shape[0] + 1) // 2

    def window(distance):
        return pl.BlockSpec(
            (1, 2 * seg, width),
            lambda i, pos: (jnp.where(pos[0] == 1, n - 1 + distance, n - 1 - distance), 0, half),
        )

    def lanes(rows):
        return pl.BlockSpec((rows, width), lambda i, pos: (0, half))

    return pl.pallas_call(
        partial_kernel,
        grid_spec=pltpu.PrefetchScalarGridSpec(
            num_scalar_prefetch=1,
            grid=(1,),
            in_specs=[
                whole_spec(table.shape),
                whole_spec(inverse.shape),
                window(2),
                window(3),
                lanes(2 * seg),
                lanes(seg),
                lanes(seg),
                lanes(8),
            ],
            out_specs=whole_spec((seg + 8, width)),
            scratch_shapes=[pltpu.VMEM((4, seg // 2, width), jnp.float32)],
        ),
        out_shape=f32(seg + 8, width),
        compiler_params=params(24),
        cost_estimate=cost(6 * seg * seg * width * 2, 24 * seg * width),
        name="partial",
    )(pos, table, inverse, windows, windows, next_m, x, gated, near_sums)


OWN, OUTER, NEXT, TWO, THREE = range(5)
PAIRS = (
    ((), ((OWN, THREE),), ((OWN, TWO), (NEXT, THREE))),
    (
        ((OUTER, NEXT), (OWN, TWO)),
        ((OUTER, OWN), (OWN, NEXT), (NEXT, TWO)),
        ((OUTER, OUTER), (OWN, OWN), (NEXT, NEXT), (TWO, TWO)),
    ),
    (
        ((TWO, TWO), (NEXT, NEXT), (OWN, OWN), (OUTER, OUTER)),
        ((NEXT, TWO), (OWN, NEXT), (OUTER, OWN)),
        ((OWN, TWO), (OUTER, NEXT)),
    ),
    (((NEXT, THREE), (OWN, TWO)), ((OWN, THREE),), ()),
)


def is_late(pair):
    return pair[0] == TWO or pair[1] == THREE


def pair_sums(distances, gated, mixed, sign, late):
    total = []
    for pairs in distances:
        value = None
        for m, g in pairs:
            if is_late((m, g)) == late:
                term = conj_mul(gated[g](), mixed[m]())
                value = term if value is None else add(value, term)
        total.append(value)
    out = []
    for low, high in zip(total[:2], total[1:]):
        if high is not None:
            turned = (sign * high[1], -sign * high[0])
            low = turned if low is None else add(low, turned)
        out.append(low)
    return out


TILE = 16


def tile_reader(tile, sub):
    re = pl.ds(pl.multiple_of(tile * TILE, TILE), TILE)
    im = pl.ds(pl.multiple_of(sub + tile * TILE, TILE), TILE)

    def read(ref, *lead):
        return ref[(*lead, re, slice(None))], ref[(*lead, im, slice(None))]

    return re, im, read


def group_sign():
    return jnp.where(pl.program_id(0) % 2 == 0, 1.0, -1.0)


def early_kernel(
    pos_ref, win_own, win_outer, win_next, win_two, own_g, outer_g, next_g, two_g, own_m, outer_m, next_m, out_ref
):
    pos, sign = pos_ref[0], group_sign()
    rows = own_g.shape[0]
    sub = rows // 2
    count = sub // TILE

    def put(at, slot, value):
        re, im = at
        out_ref[slot, re, :] = value[0]
        out_ref[slot, im, :] = value[1]

    def sums(tile, _):
        re, im, read = tile_reader(tile, sub)
        own, outer, ahead = read(win_own, 0), read(win_outer, 0), read(win_next, 0)
        conv = add(mul(own, read(own_g)), mul(outer, read(outer_g)))
        conv = add(conv, add(mul(ahead, read(next_g)), mul(read(win_two, 0), read(two_g))))
        put((re, im), 0, conv)
        back = add(conj_mul(own, read(own_m)), conj_mul(ahead, read(outer_m)))
        put((re, im), 1, add(back, conj_mul(outer, read(next_m))))
        return _

    lax.fori_loop(0, count, sums, 0)
    for where, distances in enumerate(PAIRS):

        @pl.when(pos == where)
        def _():
            def lags(tile, _):
                re, im, read = tile_reader(tile, sub)
                gated = [functools.partial(read, ref) for ref in (own_g, outer_g, next_g, two_g)]
                mixed = [functools.partial(read, ref) for ref in (own_m, outer_m, next_m)]
                for slot, value in enumerate(pair_sums(distances, gated, mixed, sign, False)):
                    if value is None:
                        value = (jnp.zeros_like(own_g[re, :]),) * 2
                    put((re, im), 2 + slot, value)
                return _

            lax.fori_loop(0, count, lags, 0)


def early(pos, windows, gated, mixed, seg):
    width = gated[0].shape[1]
    rows = seg // 2
    mid = windows.shape[0] // 2

    def window(index):
        return pl.BlockSpec((1, rows, width), lambda i, pos: (index(pos[0]), i, 0))

    group = pl.BlockSpec((rows, width), lambda i, pos: (i, 0))
    return pl.pallas_call(
        early_kernel,
        grid_spec=pltpu.PrefetchScalarGridSpec(
            num_scalar_prefetch=1,
            grid=(4,),
            in_specs=[
                window(lambda p: mid),
                window(lambda p: jnp.where(p < 2, mid + 1, mid - 1)),
                window(lambda p: jnp.where(p < 2, mid - 1, mid + 1)),
                window(lambda p: jnp.where(p < 2, mid - 2, mid + 2)),
            ]
            + [group] * 7,
            out_specs=pl.BlockSpec((4, rows, width), lambda i, pos: (0, i, 0)),
        ),
        out_shape=f32(4, 2 * seg, width),
        compiler_params=params(14),
        cost_estimate=cost(200 * seg * width, 120 * seg * width),
        name="early",
    )(pos, *[windows] * 4, *gated, *mixed)


def late_kernel(
    pos_ref, inverse_ref, acc_ref, win_ref, three_g, two_g, own_m, outer_m, next_m, *rest
):
    two_m, gated_ref, mixed_ref, skip_ref, up_ref, query_out, filter_out, back_out, x_high, x_low, z_ref = rest
    group = pl.program_id(0)
    pos, sign = pos_ref[0], group_sign()
    rows, width = own_m.shape
    sub = rows // 2

    def put(at, slot, value):
        for rows_at, part in zip(at, value):
            high, low = split(part)
            x_high[rows_at, slot * width : (slot + 1) * width] = high
            x_low[rows_at, slot * width : (slot + 1) * width] = low

    for where, distances in enumerate(PAIRS):

        @pl.when(pos == where)
        def _():
            def lags(tile, _):
                re, im, read = tile_reader(tile, sub)

                gated = [None, None, None, functools.partial(read, two_g), functools.partial(read, three_g)]
                mixed = [functools.partial(read, ref) for ref in (own_m, outer_m, next_m, two_m)]
                total = [read(acc_ref, slot) for slot in range(4)]
                if where in (0, 3):
                    total[0] = add(total[0], mul(read(win_ref, 0), gated[THREE]()))
                else:
                    total[1] = add(total[1], conj_mul(read(win_ref, 0), mixed[TWO]()))
                for slot, value in enumerate(pair_sums(distances, gated, mixed, sign, True)):
                    if value is not None:
                        total[2 + slot] = add(total[2 + slot], value)
                for slot, value in enumerate(total):
                    put((re, im), slot, value)
                return _

            lax.fori_loop(0, sub // TILE, lags, 0)

    dot = functools.partial(jnp.dot, preferred_element_type=jnp.float32)
    t_high, t_low = inverse_ref[0, 0], inverse_ref[1, 0]
    for slot in range(4):
        cols = slice(slot * width, (slot + 1) * width)
        z_ref[group, :, cols] = (
            dot(t_high, x_high[:, cols]) + dot(t_high, x_low[:, cols]) + dot(t_low, x_high[:, cols])
        )

    @pl.when(group == 3)
    def _():
        seg = 4 * sub
        for slot in range(4):
            cols = slice(slot * width, (slot + 1) * width)
            quarters = gather_quarters(
                [z_ref[g, :sub, cols] for g in range(4)], [z_ref[g, sub:, cols] for g in range(4)]
            )
            for i, quarter in enumerate(quarters):
                at = slice(i * sub, (i + 1) * sub)
                if slot == 0:
                    query_out[at, :] = up_ref[at, :] * (quarter + skip_ref[...] * gated_ref[at, :])
                elif slot == 1:
                    back_out[at, :] = quarter + skip_ref[...] * mixed_ref[at, :]
                else:
                    base = (slot - 2) * seg + i * sub
                    filter_out[base : base + sub, :] = quarter


def late(pos, inverse, acc, windows, three_g, two_g, own_m, outer_m, next_m, two_m, gated, mixed, skip, upstream):
    seg, width = upstream.shape
    rows = seg // 2
    mid = windows.shape[0] // 2

    def win_at(i, pos):
        p = pos[0]
        ends = jnp.where(p == 0, mid - 3, mid + 3)
        return jnp.where(p == 1, mid + 2, jnp.where(p == 2, mid - 2, ends)), i, 0

    group = pl.BlockSpec((rows, width), lambda i, pos: (i, 0))
    return pl.pallas_call(
        late_kernel,
        grid_spec=pltpu.PrefetchScalarGridSpec(
            num_scalar_prefetch=1,
            grid=(4,),
            in_specs=[
                pl.BlockSpec((2, 1, rows, rows), lambda i, pos: (0, i, 0, 0)),
                pl.BlockSpec((4, rows, width), lambda i, pos: (0, i, 0)),
                pl.BlockSpec((1, rows, width), win_at),
                *[group] * 6,
                whole_spec((seg, width)),
                whole_spec((seg, width)),
                whole_spec((1, width)),
                whole_spec((seg, width)),
            ],
            out_specs=[whole_spec((seg, width)), whole_spec((2 * seg, width)), whole_spec((seg, width))],
            scratch_shapes=[
                pltpu.VMEM((rows, 4 * width), jnp.bfloat16),
                pltpu.VMEM((rows, 4 * width), jnp.bfloat16),
                pltpu.VMEM((4, rows, 4 * width), jnp.float32),
            ],
        ),
        out_shape=[f32(seg, width), f32(2 * seg, width), f32(seg, width)],
        compiler_params=params(20),
        cost_estimate=cost(12 * seg * seg * width * 2, 100 * seg * width),
        name="late",
    )(pos, inverse, acc, windows, three_g, two_g, own_m, outer_m, next_m, two_m, gated, mixed, skip, upstream)


def finish_kernel(half, back_ref, key_ref, values_ref, made_ref, sent_ref, own_ref, side_ref, *rest):
    key_out, value_out, skip_out = rest[-3:]
    seg = back_ref.shape[0]
    width = sent_ref.shape[1]
    lanes = slice(half * width, (half + 1) * width)
    back = back_ref[:, lanes] + sent_ref[:seg, :]
    key_out[...] = back * values_ref[:, lanes]
    value_out[...] = back * key_ref[:, lanes]
    total = (own_ref[:, lanes] + side_ref[:, lanes]) + (made_ref[seg:, :] + sent_ref[seg:, :])
    skip_out[...] = jnp.sum(total, axis=0, keepdims=True)


def finish(back, key_gate, values, made, sent, own_sums, side_sums, half, before=()):
    seg, full = back.shape
    width = full // 2

    def lanes(rows):
        return pl.BlockSpec((rows, width), lambda i: (0, half))

    held = pl.BlockSpec(memory_space=pl.ANY)
    return pl.pallas_call(
        functools.partial(finish_kernel, half),
        grid=(1,),
        in_specs=[whole_spec((seg, full))] * 3
        + [whole_spec((seg + 8, width))] * 2
        + [whole_spec((8, full))] * 2
        + [held] * len(before),
        out_specs=[lanes(seg), lanes(seg), lanes(1)],
        out_shape=[f32(seg, full), f32(seg, full), f32(1, full)],
        input_output_aliases={7 + i: i for i in range(len(before))},
        compiler_params=params(12),
        cost_estimate=cost(3 * seg * width, 24 * seg * width),
        name="finish",
    )(back, key_gate, values, made, sent, own_sums, side_sums, *before)


def send(x, *pairs):
    return lax.ppermute(x, "ctx", list(pairs))


def across(x):
    return send(x, (1, 2), (2, 1))


def outward(x):
    return send(x, (1, 0), (2, 3))


def beside(x):
    return send(x, (0, 1), (1, 0), (2, 3), (3, 2))


def local_line(query_gate, key_gate, values, filter_taps, skip_gain, upstream):
    seg, width = values.shape
    forward_np, inverse_np = tables(seg)
    table, inverse = jnp.asarray(forward_np), jnp.asarray(inverse_np)
    pos = lax.axis_index("ctx").astype(jnp.int32).reshape(1)
    after = lax.optimization_barrier

    gated = key_gate * values
    side, over = beside(gated), across(gated)
    mixed, own_sums = mix(gated, upstream, query_gate)
    side_x, over_x = beside(mixed), across(mixed)
    own_g, own_m = dft(pos, table, seg, gated), dft(pos, table, seg, mixed)
    over, side, filter_taps, own_g, own_m = after((over, side, filter_taps, own_g, own_m))

    over_two, out_two = across(side), outward(over)
    outer_g = dft(pos, table, seg, side, choose=True)
    next_g = dft(pos, table, seg, over, side, choose=True)
    windows = taps_spectra(table, filter_taps, seg)
    side_x, over_x, windows, outer_g, next_g = after((side_x, over_x, windows, outer_g, next_g))

    outer_m = dft(pos, table, seg, side_x, choose=True)
    next_m = dft(pos, table, seg, over_x, side_x, choose=True)
    side_x, outer_m, next_m = after((side_x, outer_m, next_m))
    two_x = across(side_x)
    side_sums, near_sums = sums(side, side_x), sums(over, over_x)
    over_two, outer_m, next_m, side_sums, near_sums = after((over_two, outer_m, next_m, side_sums, near_sums))

    three = outward(over_two)
    two_g = dft(pos, table, seg, over_two, out_two)
    acc = early(pos, windows, (own_g, outer_g, next_g, two_g), (own_m, outer_m, next_m), seg)
    two_x, acc = after((two_x, acc))

    made_0 = back_partial(pos, table, inverse, windows, next_m, two_x, over_two, near_sums, 0, seg)
    two_x, made_0 = after((two_x, made_0))
    sent_0 = outward(made_0)
    made_1 = back_partial(pos, table, inverse, windows, next_m, two_x, over_two, near_sums, 1, seg)
    two_x, made_1 = after((two_x, made_1))
    sent_1 = outward(made_1)
    two_m, three_g = dft(pos, table, seg, two_x), dft(pos, table, seg, three)
    query_grad, filter_grad, back = late(
        pos, inverse, acc, windows, three_g, two_g, own_m, outer_m, next_m, two_m,
        gated, mixed, skip_gain[None, :], upstream,
    )
    done = finish(back, key_gate, values, made_0, sent_0, own_sums, side_sums, 0)
    sent_1, *done = after((sent_1, *done))
    key_grad, value_grad, skip_grad = finish(back, key_gate, values, made_1, sent_1, own_sums, side_sums, 1, done)
    return (query_grad, key_grad, value_grad, filter_grad, skip_grad[0])


def matmul(left, right):
    return jnp.dot(left, right, preferred_element_type=jnp.float32, precision=lax.Precision.HIGHEST)


def forward_table(seg_len, count, offset):
    num_bins = seg_len + 1
    period = 2 * seg_len
    bin_index = lax.broadcasted_iota(jnp.int32, (num_bins, count), 0)
    pos_index = lax.broadcasted_iota(jnp.int32, (num_bins, count), 1) + offset
    angles = (bin_index * pos_index % period).astype(jnp.float32) * (2.0 * math.pi / period)
    return jnp.concatenate([jnp.cos(angles), -jnp.sin(angles)], axis=0)


def inverse_table(seg_len, count, offset):
    num_bins = seg_len + 1
    period = 2 * seg_len
    pos_index = lax.broadcasted_iota(jnp.int32, (count, num_bins), 0) + offset
    bin_index = lax.broadcasted_iota(jnp.int32, (count, num_bins), 1)
    angles = (bin_index * pos_index % period).astype(jnp.float32) * (2.0 * math.pi / period)
    weights = jnp.where((bin_index == 0) | (bin_index == seg_len), 1.0, 2.0) / period
    return jnp.concatenate([weights * jnp.cos(angles), -weights * jnp.sin(angles)], axis=1)


def times_spec(first, second):
    num_bins = first.shape[0] // 2
    real_a, imag_a = (first[:num_bins], first[num_bins:])
    real_b, imag_b = (second[:num_bins], second[num_bins:])
    return jnp.concatenate(
        [real_a * real_b - imag_a * imag_b, real_a * imag_b + imag_a * real_b], axis=0
    )


def conj_times(first, second):
    num_bins = first.shape[0] // 2
    real_a, imag_a = (first[:num_bins], first[num_bins:])
    real_b, imag_b = (second[:num_bins], second[num_bins:])
    return jnp.concatenate(
        [real_a * real_b + imag_a * imag_b, real_a * imag_b - imag_a * real_b], axis=0
    )


def pick(stack, index):
    return lax.dynamic_index_in_dim(stack, index, 0, keepdims=False)


def local(query_gate, key_gate, values, filter_taps, skip_gain, upstream):
    seg_len, width_dev = values.shape
    cycle_size = lax.axis_size("ctx")
    position = lax.axis_index("ctx")
    history = seg_len * cycle_size
    gated = key_gate * values
    mixed_grad = upstream * query_gate
    table_low = forward_table(seg_len, seg_len, 0)
    table_high = forward_table(seg_len, seg_len, seg_len)
    table_taps = forward_table(seg_len, 2 * seg_len, 0)
    back_low = inverse_table(seg_len, seg_len, 0)
    back_high = inverse_table(seg_len, seg_len, seg_len)
    back_full = inverse_table(seg_len, 2 * seg_len, 0)
    own_grad_spec = matmul(table_high, mixed_grad)
    spec_rows = 2 * (seg_len + 1)

    def taps_spec(lag_block):
        start_row = (lag_block - 1) * seg_len + history
        window = lax.dynamic_slice_in_dim(filter_taps, start_row, 2 * seg_len, 0)
        return matmul(table_taps, window)

    def visit(carry, gated_spec, grad_spec, source):
        acc_conv, acc_back, partial_value = carry
        lag_block = position - source
        acc_conv = acc_conv + times_spec(taps_spec(lag_block), gated_spec)
        acc_back = acc_back + conj_times(taps_spec(-lag_block), grad_spec)
        segment = matmul(back_full, conj_times(gated_spec, own_grad_spec))
        start_row = (lag_block - 1) * seg_len + history
        current = lax.dynamic_slice_in_dim(partial_value, start_row, 2 * seg_len, 0)
        partial_value = lax.dynamic_update_slice_in_dim(
            partial_value, current + segment, start_row, 0
        )
        return (acc_conv, acc_back, partial_value)

    initial = (
        jnp.zeros((spec_rows, width_dev), jnp.float32),
        jnp.zeros((spec_rows, width_dev), jnp.float32),
        jnp.zeros((2 * history, width_dev), jnp.float32),
    )
    own_gated_spec = matmul(table_low, gated)
    pieces = (
        lax.all_gather(own_gated_spec[None], "ctx", axis=0, tiled=True),
        lax.all_gather(own_grad_spec[None], "ctx", axis=0, tiled=True),
    )

    def advance(member, state):
        return visit(state, pick(pieces[0], member), pick(pieces[1], member), member)

    folded = lax.fori_loop(0, pieces[0].shape[0], advance, initial)
    acc_conv, acc_back, partial_value = folded
    filter_grad = lax.psum_scatter(partial_value, "ctx", scatter_dimension=0, tiled=True)
    conv = matmul(back_high, acc_conv)
    back = matmul(back_low, acc_back) + skip_gain[None, :] * mixed_grad
    query_grad = upstream * (conv + skip_gain[None, :] * gated)
    key_grad = back * values
    value_grad = back * key_gate
    skip_grad = lax.psum(jnp.sum(mixed_grad * gated, axis=0), "ctx")
    return (query_grad, key_grad, value_grad, filter_grad, skip_grad)


def solution(mesh):
    in_specs = (
        P(("groups", "ctx"), "chan"),
        P(("groups", "ctx"), "chan"),
        P(("groups", "ctx"), "chan"),
        P(None, "chan"),
        P("chan"),
        P(("groups", "ctx"), "chan"),
    )
    out_specs = (
        P(("groups", "ctx"), "chan"),
        P(("groups", "ctx"), "chan"),
        P(("groups", "ctx"), "chan"),
        P(("groups", "ctx"), "chan"),
        P(("groups", "chan")),
    )
    body = local_line if mesh.shape["ctx"] == 4 else local
    return jax.shard_map(body, mesh=mesh, in_specs=in_specs, out_specs=out_specs, check_vma=False)
```

```python
import functools
import math

import jax
import jax.numpy as jnp
import ml_dtypes
import numpy as np
from jax import lax
from jax.experimental import pallas as pl
from jax.experimental.pallas import tpu as pltpu
from jax.sharding import PartitionSpec as P

COS1, SIN1, HALF = math.cos(math.pi / 8), math.sin(math.pi / 8), math.sqrt(0.5)


def split_np(table):
    high = table.astype(ml_dtypes.bfloat16)
    low = (table - high.astype(np.float64)).astype(ml_dtypes.bfloat16)
    return np.stack([high, low])


def tables(seg):
    sub = seg // 4
    bins, pos = np.arange(sub)[:, None], np.arange(sub)[None, :]
    forward = []
    for group in range(4):
        angle = 2 * np.pi * pos * (8 * bins + group + 0.5) / (2 * seg)
        cos, sin = np.cos(angle), np.sin(angle)
        forward.append(np.block([[cos, -sin], [-sin, -cos]]))
    forward = np.stack(forward)
    inverse = forward.transpose(0, 2, 1) / seg
    return split_np(forward), split_np(inverse)


def split(x):
    high = x.astype(jnp.bfloat16)
    return high, (x - high.astype(jnp.float32)).astype(jnp.bfloat16)


def dot3(table_ref, group, high, low):
    t_high, t_low = table_ref[0, group], table_ref[1, group]
    dot = functools.partial(jnp.dot, preferred_element_type=jnp.float32)
    width = high.shape[1]
    if width <= 128:
        both = dot(t_high, jnp.concatenate([high, low], axis=1))
        return both[:, :width] + both[:, width:] + dot(t_low, high)
    return dot(t_high, high) + dot(t_high, low) + dot(t_low, high)


def spread(x):
    sub = x.shape[0] // 4
    x0, x1, x2, x3 = (x[i * sub : (i + 1) * sub] for i in range(4))
    u, p, s, q, t = HALF * x2, COS1 * x1, SIN1 * x1, COS1 * x3, SIN1 * x3
    a, b, pt, sq, pmt, spq = x0 + u, x0 - u, p + t, s - q, p - t, s + q
    pairs = ((a + pt, spq + u), (b + sq, pmt + u), (b - sq, pmt - u), (a - pt, spq - u))
    return [jnp.concatenate(pair, axis=0) for pair in pairs]


def gather_quarters(re, im):
    e03, d03, e12, d12 = re[0] + re[3], re[0] - re[3], re[1] + re[2], re[1] - re[2]
    f03, g03, f12, g12 = im[0] + im[3], im[0] - im[3], im[1] + im[2], im[1] - im[2]
    return (
        e03 + e12,
        COS1 * (d03 + f12) + SIN1 * (d12 + f03),
        HALF * (e03 - e12 + g03 + g12),
        SIN1 * (d03 - f12) + COS1 * (f03 - d12),
    )


def transform(x, table_ref, store):
    for group, part in enumerate(spread(x)):
        store(group, dot3(table_ref, group, *split(part)))


def cost(flops, nbytes):
    return pl.CostEstimate(flops=int(flops), bytes_accessed=int(nbytes), transcendentals=0)


def params(mib):
    return pltpu.CompilerParams(vmem_limit_bytes=mib << 20)


def whole_spec(shape):
    return pl.BlockSpec(shape, lambda *_: (0,) * len(shape))


def f32(*shape):
    return jax.ShapeDtypeStruct(shape, jnp.float32)


def block_sums(gated, mixed):
    seg, width = gated.shape
    return jnp.sum((gated * mixed).reshape(seg // 8, 8, width), axis=0)


def sums_kernel(gated_ref, mixed_ref, out_ref):
    out_ref[...] = block_sums(gated_ref[...], mixed_ref[...])


def sums(gated, mixed):
    seg, width = gated.shape
    return pl.pallas_call(
        sums_kernel,
        grid=(1,),
        in_specs=[whole_spec((seg, width))] * 2,
        out_specs=whole_spec((8, width)),
        out_shape=f32(8, width),
        compiler_params=params(8),
        cost_estimate=cost(2 * seg * width, 8 * seg * width),
        name="sums",
    )(gated, mixed)


def mix_kernel(gated_ref, up_ref, query_ref, mixed_ref, sum_ref):
    mixed = up_ref[...] * query_ref[...]
    mixed_ref[...] = mixed
    sum_ref[...] = block_sums(gated_ref[...], mixed)


def mix(gated, upstream, query_gate):
    seg, width = gated.shape
    block = whole_spec((seg, width))
    return pl.pallas_call(
        mix_kernel,
        grid=(1,),
        in_specs=[block] * 3,
        out_specs=[block, whole_spec((8, width))],
        out_shape=[f32(seg, width), f32(8, width)],
        compiler_params=params(12),
        cost_estimate=cost(4 * seg * width, 16 * seg * width),
        name="mix",
    )(gated, upstream, query_gate)


def dft_kernel(choose, pos_ref, table_ref, *refs):
    *x_refs, out_ref = refs
    rows = out_ref.shape[0] // 4
    inner = jnp.logical_or(pos_ref[0] == 1, pos_ref[0] == 2)

    def store(group, value):
        out_ref[group * rows : (group + 1) * rows, :] = value

    x = x_refs[0][...]
    if choose:
        x = jnp.where(inner, x, x_refs[1][...] if len(x_refs) == 2 else 0.0)
    elif len(x_refs) == 2:
        x = x + x_refs[1][...]
    transform(x, table_ref, store)


def dft(pos, table, seg, *xs, choose=False):
    width = xs[0].shape[1]
    return pl.pallas_call(
        functools.partial(dft_kernel, choose),
        grid_spec=pltpu.PrefetchScalarGridSpec(
            num_scalar_prefetch=1,
            grid=(1,),
            in_specs=[whole_spec(table.shape)] + [whole_spec((seg, width))] * len(xs),
            out_specs=whole_spec((2 * seg, width)),
        ),
        out_shape=f32(2 * seg, width),
        compiler_params=params(12),
        cost_estimate=cost(3 * seg * seg * width * 2, 12 * seg * width),
        name="dft",
    )(pos, table, *xs)


def taps_kernel(table_ref, x_ref, out_ref, last_ref):
    step = pl.program_id(0)
    rows = out_ref.shape[1] // 4
    sub = rows // 2

    def store(group, value):
        base = group * rows
        sign = 1.0 if group % 2 == 0 else -1.0
        re, im = slice(base, base + sub), slice(base + sub, base + rows)
        out_ref[0, re, :] = value[:sub] - sign * last_ref[im, :]
        out_ref[0, im, :] = value[sub:] + sign * last_ref[re, :]
        last_ref[base : base + rows, :] = value

    @pl.when(step == 0)
    def _():
        last_ref[...] = jnp.zeros_like(last_ref)

    transform(x_ref[...], table_ref, store)


def taps_spectra(table, taps, seg):
    width = taps.shape[1]
    blocks = taps.shape[0] // seg
    return pl.pallas_call(
        taps_kernel,
        grid=(blocks,),
        in_specs=[whole_spec(table.shape), pl.BlockSpec((seg, width), lambda i: (i, 0))],
        out_specs=pl.BlockSpec((1, 2 * seg, width), lambda i: (jnp.maximum(i - 1, 0), 0, 0)),
        out_shape=jax.ShapeDtypeStruct((blocks - 1, 2 * seg, width), jnp.float32),
        scratch_shapes=[pltpu.VMEM((2 * seg, width), jnp.float32)],
        compiler_params=params(14),
        cost_estimate=cost(blocks * 3 * seg * seg * width * 2, blocks * 12 * seg * width),
        name="taps",
    )(table, taps)


def conj_mul(a, b):
    return a[0] * b[0] + a[1] * b[1], a[0] * b[1] - a[1] * b[0]


def mul(a, b):
    return a[0] * b[0] - a[1] * b[1], a[0] * b[1] + a[1] * b[0]


def add(a, b):
    return a[0] + b[0], a[1] + b[1]


def partial_kernel(
    pos_ref, table_ref, inverse_ref, win_near, win_far, next_ref, x_ref, gated_ref, near_sums, out_ref, z_ref
):
    rows = next_ref.shape[0] // 4
    sub = rows // 2
    for group, part in enumerate(spread(x_ref[...])):
        base = group * rows
        far = dot3(table_ref, group, *split(part))
        re, im = slice(base, base + sub), slice(base + sub, base + rows)
        total = add(
            conj_mul((win_near[0, re, :], win_near[0, im, :]), (next_ref[re, :], next_ref[im, :])),
            conj_mul((win_far[0, re, :], win_far[0, im, :]), (far[:sub], far[sub:])),
        )
        z_ref[group] = dot3(inverse_ref, group, *split(jnp.concatenate(total, axis=0)))
    quarters = gather_quarters([z_ref[g, :sub] for g in range(4)], [z_ref[g, sub:] for g in range(4)])
    for i, quarter in enumerate(quarters):
        out_ref[i * sub : (i + 1) * sub, :] = quarter
    out_ref[4 * sub :, :] = near_sums[...] + block_sums(gated_ref[...], x_ref[...])


def back_partial(pos, table, inverse, windows, next_m, x, gated, near_sums, half, seg):
    width = x.shape[1] // 2
    n = (windows.shape[0] + 1) // 2

    def window(distance):
        return pl.BlockSpec(
            (1, 2 * seg, width),
            lambda i, pos: (jnp.where(pos[0] == 1, n - 1 + distance, n - 1 - distance), 0, half),
        )

    def lanes(rows):
        return pl.BlockSpec((rows, width), lambda i, pos: (0, half))

    return pl.pallas_call(
        partial_kernel,
        grid_spec=pltpu.PrefetchScalarGridSpec(
            num_scalar_prefetch=1,
            grid=(1,),
            in_specs=[
                whole_spec(table.shape),
                whole_spec(inverse.shape),
                window(2),
                window(3),
                lanes(2 * seg),
                lanes(seg),
                lanes(seg),
                lanes(8),
            ],
            out_specs=whole_spec((seg + 8, width)),
            scratch_shapes=[pltpu.VMEM((4, seg // 2, width), jnp.float32)],
        ),
        out_shape=f32(seg + 8, width),
        compiler_params=params(24),
        cost_estimate=cost(6 * seg * seg * width * 2, 24 * seg * width),
        name="partial",
    )(pos, table, inverse, windows, windows, next_m, x, gated, near_sums)


OWN, OUTER, NEXT, TWO, THREE = range(5)
PAIRS = (
    ((), ((OWN, THREE),), ((OWN, TWO), (NEXT, THREE))),
    (
        ((OUTER, NEXT), (OWN, TWO)),
        ((OUTER, OWN), (OWN, NEXT), (NEXT, TWO)),
        ((OUTER, OUTER), (OWN, OWN), (NEXT, NEXT), (TWO, TWO)),
    ),
    (
        ((TWO, TWO), (NEXT, NEXT), (OWN, OWN), (OUTER, OUTER)),
        ((NEXT, TWO), (OWN, NEXT), (OUTER, OWN)),
        ((OWN, TWO), (OUTER, NEXT)),
    ),
    (((NEXT, THREE), (OWN, TWO)), ((OWN, THREE),), ()),
)


def is_late(pair):
    return pair[0] == TWO or pair[1] == THREE


def pair_sums(distances, gated, mixed, sign, late):
    total = []
    for pairs in distances:
        value = None
        for m, g in pairs:
            if is_late((m, g)) == late:
                term = conj_mul(gated[g](), mixed[m]())
                value = term if value is None else add(value, term)
        total.append(value)
    out = []
    for low, high in zip(total[:2], total[1:]):
        if high is not None:
            turned = (sign * high[1], -sign * high[0])
            low = turned if low is None else add(low, turned)
        out.append(low)
    return out


TILE = 16


def tile_reader(tile, sub):
    re = pl.ds(pl.multiple_of(tile * TILE, TILE), TILE)
    im = pl.ds(pl.multiple_of(sub + tile * TILE, TILE), TILE)

    def read(ref, *lead):
        return ref[(*lead, re, slice(None))], ref[(*lead, im, slice(None))]

    return re, im, read


def group_sign():
    return jnp.where(pl.program_id(0) % 2 == 0, 1.0, -1.0)


def early_kernel(
    pos_ref, win_own, win_outer, win_next, win_two, own_g, outer_g, next_g, two_g, own_m, outer_m, next_m, out_ref
):
    pos, sign = pos_ref[0], group_sign()
    rows = own_g.shape[0]
    sub = rows // 2
    count = sub // TILE

    def put(at, slot, value):
        re, im = at
        out_ref[slot, re, :] = value[0]
        out_ref[slot, im, :] = value[1]

    def sums(tile, _):
        re, im, read = tile_reader(tile, sub)
        own, outer, ahead = read(win_own, 0), read(win_outer, 0), read(win_next, 0)
        conv = add(mul(own, read(own_g)), mul(outer, read(outer_g)))
        conv = add(conv, add(mul(ahead, read(next_g)), mul(read(win_two, 0), read(two_g))))
        put((re, im), 0, conv)
        back = add(conj_mul(own, read(own_m)), conj_mul(ahead, read(outer_m)))
        put((re, im), 1, add(back, conj_mul(outer, read(next_m))))
        return _

    lax.fori_loop(0, count, sums, 0)
    for where, distances in enumerate(PAIRS):

        @pl.when(pos == where)
        def _():
            def lags(tile, _):
                re, im, read = tile_reader(tile, sub)
                gated = [functools.partial(read, ref) for ref in (own_g, outer_g, next_g, two_g)]
                mixed = [functools.partial(read, ref) for ref in (own_m, outer_m, next_m)]
                for slot, value in enumerate(pair_sums(distances, gated, mixed, sign, False)):
                    if value is None:
                        value = (jnp.zeros_like(own_g[re, :]),) * 2
                    put((re, im), 2 + slot, value)
                return _

            lax.fori_loop(0, count, lags, 0)


def early(pos, windows, gated, mixed, seg):
    width = gated[0].shape[1]
    rows = seg // 2
    mid = windows.shape[0] // 2

    def window(index):
        return pl.BlockSpec((1, rows, width), lambda i, pos: (index(pos[0]), i, 0))

    group = pl.BlockSpec((rows, width), lambda i, pos: (i, 0))
    return pl.pallas_call(
        early_kernel,
        grid_spec=pltpu.PrefetchScalarGridSpec(
            num_scalar_prefetch=1,
            grid=(4,),
            in_specs=[
                window(lambda p: mid),
                window(lambda p: jnp.where(p < 2, mid + 1, mid - 1)),
                window(lambda p: jnp.where(p < 2, mid - 1, mid + 1)),
                window(lambda p: jnp.where(p < 2, mid - 2, mid + 2)),
            ]
            + [group] * 7,
            out_specs=pl.BlockSpec((4, rows, width), lambda i, pos: (0, i, 0)),
        ),
        out_shape=f32(4, 2 * seg, width),
        compiler_params=params(14),
        cost_estimate=cost(200 * seg * width, 120 * seg * width),
        name="early",
    )(pos, *[windows] * 4, *gated, *mixed)


def late_kernel(
    pos_ref, inverse_ref, acc_ref, win_ref, three_g, two_g, own_m, outer_m, next_m, *rest
):
    two_m, gated_ref, mixed_ref, skip_ref, up_ref, query_out, filter_out, back_out, x_high, x_low, z_ref = rest
    group = pl.program_id(0)
    pos, sign = pos_ref[0], group_sign()
    rows, width = own_m.shape
    sub = rows // 2

    def put(at, slot, value):
        for rows_at, part in zip(at, value):
            high, low = split(part)
            x_high[rows_at, slot * width : (slot + 1) * width] = high
            x_low[rows_at, slot * width : (slot + 1) * width] = low

    for where, distances in enumerate(PAIRS):

        @pl.when(pos == where)
        def _():
            def lags(tile, _):
                re, im, read = tile_reader(tile, sub)

                gated = [None, None, None, functools.partial(read, two_g), functools.partial(read, three_g)]
                mixed = [functools.partial(read, ref) for ref in (own_m, outer_m, next_m, two_m)]
                total = [read(acc_ref, slot) for slot in range(4)]
                if where in (0, 3):
                    total[0] = add(total[0], mul(read(win_ref, 0), gated[THREE]()))
                else:
                    total[1] = add(total[1], conj_mul(read(win_ref, 0), mixed[TWO]()))
                for slot, value in enumerate(pair_sums(distances, gated, mixed, sign, True)):
                    if value is not None:
                        total[2 + slot] = add(total[2 + slot], value)
                for slot, value in enumerate(total):
                    put((re, im), slot, value)
                return _

            lax.fori_loop(0, sub // TILE, lags, 0)

    dot = functools.partial(jnp.dot, preferred_element_type=jnp.float32)
    t_high, t_low = inverse_ref[0, 0], inverse_ref[1, 0]
    for slot in range(4):
        cols = slice(slot * width, (slot + 1) * width)
        z_ref[group, :, cols] = (
            dot(t_high, x_high[:, cols]) + dot(t_high, x_low[:, cols]) + dot(t_low, x_high[:, cols])
        )

    @pl.when(group == 3)
    def _():
        seg = 4 * sub
        for slot in range(4):
            cols = slice(slot * width, (slot + 1) * width)
            quarters = gather_quarters(
                [z_ref[g, :sub, cols] for g in range(4)], [z_ref[g, sub:, cols] for g in range(4)]
            )
            for i, quarter in enumerate(quarters):
                at = slice(i * sub, (i + 1) * sub)
                if slot == 0:
                    query_out[at, :] = up_ref[at, :] * (quarter + skip_ref[...] * gated_ref[at, :])
                elif slot == 1:
                    back_out[at, :] = quarter + skip_ref[...] * mixed_ref[at, :]
                else:
                    base = (slot - 2) * seg + i * sub
                    filter_out[base : base + sub, :] = quarter


def late(pos, inverse, acc, windows, three_g, two_g, own_m, outer_m, next_m, two_m, gated, mixed, skip, upstream):
    seg, width = upstream.shape
    rows = seg // 2
    mid = windows.shape[0] // 2

    def win_at(i, pos):
        p = pos[0]
        ends = jnp.where(p == 0, mid - 3, mid + 3)
        return jnp.where(p == 1, mid + 2, jnp.where(p == 2, mid - 2, ends)), i, 0

    group = pl.BlockSpec((rows, width), lambda i, pos: (i, 0))
    return pl.pallas_call(
        late_kernel,
        grid_spec=pltpu.PrefetchScalarGridSpec(
            num_scalar_prefetch=1,
            grid=(4,),
            in_specs=[
                pl.BlockSpec((2, 1, rows, rows), lambda i, pos: (0, i, 0, 0)),
                pl.BlockSpec((4, rows, width), lambda i, pos: (0, i, 0)),
                pl.BlockSpec((1, rows, width), win_at),
                *[group] * 6,
                whole_spec((seg, width)),
                whole_spec((seg, width)),
                whole_spec((1, width)),
                whole_spec((seg, width)),
            ],
            out_specs=[whole_spec((seg, width)), whole_spec((2 * seg, width)), whole_spec((seg, width))],
            scratch_shapes=[
                pltpu.VMEM((rows, 4 * width), jnp.bfloat16),
                pltpu.VMEM((rows, 4 * width), jnp.bfloat16),
                pltpu.VMEM((4, rows, 4 * width), jnp.float32),
            ],
        ),
        out_shape=[f32(seg, width), f32(2 * seg, width), f32(seg, width)],
        compiler_params=params(20),
        cost_estimate=cost(12 * seg * seg * width * 2, 100 * seg * width),
        name="late",
    )(pos, inverse, acc, windows, three_g, two_g, own_m, outer_m, next_m, two_m, gated, mixed, skip, upstream)


def finish_kernel(half, back_ref, key_ref, values_ref, sent_ref, made_sums, sent_sums, own_ref, side_ref, *rest):
    key_out, value_out, skip_out = rest[-3:]
    width = sent_ref.shape[1]
    lanes = slice(half * width, (half + 1) * width)
    back = back_ref[:, lanes] + sent_ref[...]
    key_out[...] = back * values_ref[:, lanes]
    value_out[...] = back * key_ref[:, lanes]
    total = (own_ref[:, lanes] + side_ref[:, lanes]) + (made_sums[...] + sent_sums[...])
    skip_out[...] = jnp.sum(total, axis=0, keepdims=True)


def finish(back, key_gate, values, made, sent, own_sums, side_sums, half, before=()):
    seg, full = back.shape
    width = full // 2

    rows = seg // 2
    block = pl.BlockSpec((rows, width), lambda i: (i, half))
    below = pl.BlockSpec((8, width), lambda i: (seg // 8, 0))
    held = pl.BlockSpec(memory_space=pl.ANY)
    return pl.pallas_call(
        functools.partial(finish_kernel, half),
        grid=(seg // rows,),
        in_specs=[pl.BlockSpec((rows, full), lambda i: (i, 0))] * 3
        + [pl.BlockSpec((rows, width), lambda i: (i, 0)), below, below]
        + [whole_spec((8, full))] * 2
        + [held] * len(before),
        out_specs=[block, block, pl.BlockSpec((1, width), lambda i: (0, half))],
        out_shape=[f32(seg, full), f32(seg, full), f32(1, full)],
        input_output_aliases={8 + i: i for i in range(len(before))},
        compiler_params=params(12),
        cost_estimate=cost(3 * seg * width, 24 * seg * width),
        name="finish",
    )(back, key_gate, values, sent, made, sent, own_sums, side_sums, *before)


def send(x, *pairs):
    return lax.ppermute(x, "ctx", list(pairs))


def across(x):
    return send(x, (1, 2), (2, 1))


def outward(x):
    return send(x, (1, 0), (2, 3))


def beside(x):
    return send(x, (0, 1), (1, 0), (2, 3), (3, 2))


def local_line(query_gate, key_gate, values, filter_taps, skip_gain, upstream):
    seg, width = values.shape
    forward_np, inverse_np = tables(seg)
    table, inverse = jnp.asarray(forward_np), jnp.asarray(inverse_np)
    pos = lax.axis_index("ctx").astype(jnp.int32).reshape(1)
    after = lax.optimization_barrier

    gated = key_gate * values
    side, over = beside(gated), across(gated)
    mixed, own_sums = mix(gated, upstream, query_gate)
    side_x, over_x = beside(mixed), across(mixed)
    own_g, own_m = dft(pos, table, seg, gated), dft(pos, table, seg, mixed)
    over, side, filter_taps, own_g, own_m = after((over, side, filter_taps, own_g, own_m))

    over_two, out_two = across(side), outward(over)
    outer_g = dft(pos, table, seg, side, choose=True)
    next_g = dft(pos, table, seg, over, side, choose=True)
    windows = taps_spectra(table, filter_taps, seg)
    over_x, side_x, windows, outer_g, next_g = after((over_x, side_x, windows, outer_g, next_g))

    outer_m = dft(pos, table, seg, side_x, choose=True)
    next_m = dft(pos, table, seg, over_x, side_x, choose=True)
    side_x, outer_m, next_m = after((side_x, outer_m, next_m))
    two_x = across(side_x)
    side_sums, near_sums = sums(side, side_x), sums(over, over_x)
    over_two, outer_m, next_m, side_sums, near_sums = after((over_two, outer_m, next_m, side_sums, near_sums))

    three = outward(over_two)
    two_g = dft(pos, table, seg, over_two, out_two)
    acc = early(pos, windows, (own_g, outer_g, next_g, two_g), (own_m, outer_m, next_m), seg)
    two_x, acc = after((two_x, acc))

    made_0 = back_partial(pos, table, inverse, windows, next_m, two_x, over_two, near_sums, 0, seg)
    two_x, made_0 = after((two_x, made_0))
    sent_0 = outward(made_0)
    made_1 = back_partial(pos, table, inverse, windows, next_m, two_x, over_two, near_sums, 1, seg)
    two_x, made_1 = after((two_x, made_1))
    sent_1 = outward(made_1)
    two_m, three_g = dft(pos, table, seg, two_x), dft(pos, table, seg, three)
    query_grad, filter_grad, back = late(
        pos, inverse, acc, windows, three_g, two_g, own_m, outer_m, next_m, two_m,
        gated, mixed, skip_gain[None, :], upstream,
    )
    done = finish(back, key_gate, values, made_0, sent_0, own_sums, side_sums, 0)
    sent_1, *done = after((sent_1, *done))
    key_grad, value_grad, skip_grad = finish(back, key_gate, values, made_1, sent_1, own_sums, side_sums, 1, done)
    return (query_grad, key_grad, value_grad, filter_grad, skip_grad[0])


def matmul(left, right):
    return jnp.dot(left, right, preferred_element_type=jnp.float32, precision=lax.Precision.HIGHEST)


def forward_table(seg_len, count, offset):
    num_bins = seg_len + 1
    period = 2 * seg_len
    bin_index = lax.broadcasted_iota(jnp.int32, (num_bins, count), 0)
    pos_index = lax.broadcasted_iota(jnp.int32, (num_bins, count), 1) + offset
    angles = (bin_index * pos_index % period).astype(jnp.float32) * (2.0 * math.pi / period)
    return jnp.concatenate([jnp.cos(angles), -jnp.sin(angles)], axis=0)


def inverse_table(seg_len, count, offset):
    num_bins = seg_len + 1
    period = 2 * seg_len
    pos_index = lax.broadcasted_iota(jnp.int32, (count, num_bins), 0) + offset
    bin_index = lax.broadcasted_iota(jnp.int32, (count, num_bins), 1)
    angles = (bin_index * pos_index % period).astype(jnp.float32) * (2.0 * math.pi / period)
    weights = jnp.where((bin_index == 0) | (bin_index == seg_len), 1.0, 2.0) / period
    return jnp.concatenate([weights * jnp.cos(angles), -weights * jnp.sin(angles)], axis=1)


def times_spec(first, second):
    num_bins = first.shape[0] // 2
    real_a, imag_a = (first[:num_bins], first[num_bins:])
    real_b, imag_b = (second[:num_bins], second[num_bins:])
    return jnp.concatenate(
        [real_a * real_b - imag_a * imag_b, real_a * imag_b + imag_a * real_b], axis=0
    )


def conj_times(first, second):
    num_bins = first.shape[0] // 2
    real_a, imag_a = (first[:num_bins], first[num_bins:])
    real_b, imag_b = (second[:num_bins], second[num_bins:])
    return jnp.concatenate(
        [real_a * real_b + imag_a * imag_b, real_a * imag_b - imag_a * real_b], axis=0
    )


def pick(stack, index):
    return lax.dynamic_index_in_dim(stack, index, 0, keepdims=False)


def local(query_gate, key_gate, values, filter_taps, skip_gain, upstream):
    seg_len, width_dev = values.shape
    cycle_size = lax.axis_size("ctx")
    position = lax.axis_index("ctx")
    history = seg_len * cycle_size
    gated = key_gate * values
    mixed_grad = upstream * query_gate
    table_low = forward_table(seg_len, seg_len, 0)
    table_high = forward_table(seg_len, seg_len, seg_len)
    table_taps = forward_table(seg_len, 2 * seg_len, 0)
    back_low = inverse_table(seg_len, seg_len, 0)
    back_high = inverse_table(seg_len, seg_len, seg_len)
    back_full = inverse_table(seg_len, 2 * seg_len, 0)
    own_grad_spec = matmul(table_high, mixed_grad)
    spec_rows = 2 * (seg_len + 1)

    def taps_spec(lag_block):
        start_row = (lag_block - 1) * seg_len + history
        window = lax.dynamic_slice_in_dim(filter_taps, start_row, 2 * seg_len, 0)
        return matmul(table_taps, window)

    def visit(carry, gated_spec, grad_spec, source):
        acc_conv, acc_back, partial_value = carry
        lag_block = position - source
        acc_conv = acc_conv + times_spec(taps_spec(lag_block), gated_spec)
        acc_back = acc_back + conj_times(taps_spec(-lag_block), grad_spec)
        segment = matmul(back_full, conj_times(gated_spec, own_grad_spec))
        start_row = (lag_block - 1) * seg_len + history
        current = lax.dynamic_slice_in_dim(partial_value, start_row, 2 * seg_len, 0)
        partial_value = lax.dynamic_update_slice_in_dim(
            partial_value, current + segment, start_row, 0
        )
        return (acc_conv, acc_back, partial_value)

    initial = (
        jnp.zeros((spec_rows, width_dev), jnp.float32),
        jnp.zeros((spec_rows, width_dev), jnp.float32),
        jnp.zeros((2 * history, width_dev), jnp.float32),
    )
    own_gated_spec = matmul(table_low, gated)
    pieces = (
        lax.all_gather(own_gated_spec[None], "ctx", axis=0, tiled=True),
        lax.all_gather(own_grad_spec[None], "ctx", axis=0, tiled=True),
    )

    def advance(member, state):
        return visit(state, pick(pieces[0], member), pick(pieces[1], member), member)

    folded = lax.fori_loop(0, pieces[0].shape[0], advance, initial)
    acc_conv, acc_back, partial_value = folded
    filter_grad = lax.psum_scatter(partial_value, "ctx", scatter_dimension=0, tiled=True)
    conv = matmul(back_high, acc_conv)
    back = matmul(back_low, acc_back) + skip_gain[None, :] * mixed_grad
    query_grad = upstream * (conv + skip_gain[None, :] * gated)
    key_grad = back * values
    value_grad = back * key_gate
    skip_grad = lax.psum(jnp.sum(mixed_grad * gated, axis=0), "ctx")
    return (query_grad, key_grad, value_grad, filter_grad, skip_grad)


def solution(mesh):
    in_specs = (
        P(("groups", "ctx"), "chan"),
        P(("groups", "ctx"), "chan"),
        P(("groups", "ctx"), "chan"),
        P(None, "chan"),
        P("chan"),
        P(("groups", "ctx"), "chan"),
    )
    out_specs = (
        P(("groups", "ctx"), "chan"),
        P(("groups", "ctx"), "chan"),
        P(("groups", "ctx"), "chan"),
        P(("groups", "ctx"), "chan"),
        P(("groups", "chan")),
    )
    body = local_line if mesh.shape["ctx"] == 4 else local
    return jax.shard_map(body, mesh=mesh, in_specs=in_specs, out_specs=out_specs, check_vma=False)
```
